32 devices in a mesh: dp: 4 (over y, core), fsdp: 8 (over z, x).
Axes of the slice: x: 2, y: 2, z: 4, core: 2. Of those that a mesh axis runs over, the one named last changes fastest.
Arguments:
- tokens: bfloat16 [36864, 512], P(('dp', 'fsdp')), may hold values from -6 to 6
- cotangent: bfloat16 [36864, 512], P(('dp', 'fsdp')), may hold values from -6 to 6
- project_weight: bfloat16 [512, 1536], P('dp', 'fsdp'), may hold values from -0.25 to 0.25
- position_weight: bfloat16 [512, 512], P('dp', 'fsdp'), may hold values from -0.25 to 0.25
- mixing_weight: bfloat16 [512, 512], P('dp', 'fsdp'), may hold values from -2 to 2
- expand_weight: bfloat16 [512, 2048], P('dp', 'fsdp'), may hold values from -0.25 to 0.25
- contract_weight: bfloat16 [2048, 512], P('dp', 'fsdp'), may hold values from -0.125 to 0.125
- pooling_weight: bfloat16 [1536, 512], P('dp', 'fsdp'), may hold values from -0.15625 to 0.15625
- upsample_weight: bfloat16 [512, 1536], P('dp', 'fsdp'), may hold values from -0.25 to 0.25
- first_gain: bfloat16 [512], P(('dp', 'fsdp')), may hold values from 0.25 to 1.75
- first_shift: bfloat16 [512], P(('dp', 'fsdp')), may hold values from -3 to 3
- content_bias: bfloat16 [512], P(('dp', 'fsdp')), may hold values from -3 to 3
- position_bias: bfloat16 [512], P(('dp', 'fsdp')), may hold values from -3 to 3
- mixing_bias: bfloat16 [512], P(('dp', 'fsdp')), may hold values from -3 to 3
- second_gain: bfloat16 [512], P(('dp', 'fsdp')), may hold values from 0.25 to 1.75
- second_shift: bfloat16 [512], P(('dp', 'fsdp')), may hold values from -3 to 3
- hidden_units_bias: bfloat16 [2048], P(('dp', 'fsdp')), may hold values from -3 to 3
- contract_bias: bfloat16 [512], P(('dp', 'fsdp')), may hold values from -3 to 3
- pooling_bias: bfloat16 [512], P(('dp', 'fsdp')), may hold values from -3 to 3
- upsampling_bias: bfloat16 [1536], P(('dp', 'fsdp')), may hold values from -3 to 3
Outputs:
- output: bfloat16 [36864, 512], P(('dp', 'fsdp'))
- token_grad: float32 [36864, 512], P(('dp', 'fsdp'))
- project_grad: float32 [512, 1536], P('dp', 'fsdp')
- position_grad: float32 [512, 512], P('dp', 'fsdp')
- mixing_grad: float32 [512, 512], P('dp', 'fsdp')
- expand_grad: float32 [512, 2048], P('dp', 'fsdp')
- contract_grad: float32 [2048, 512], P('dp', 'fsdp')
- pooling_grad: float32 [1536, 512], P('dp', 'fsdp')
- upsample_grad: float32 [512, 1536], P('dp', 'fsdp')
- first_gain_grad: float32 [512], P(('dp', 'fsdp'))
- first_shift_grad: float32 [512], P(('dp', 'fsdp'))
- content_bias_grad: float32 [512], P(('dp', 'fsdp'))
- position_bias_grad: float32 [512], P(('dp', 'fsdp'))
- mixing_bias_grad: float32 [512], P(('dp', 'fsdp'))
- second_gain_grad: float32 [512], P(('dp', 'fsdp'))
- second_shift_grad: float32 [512], P(('dp', 'fsdp'))
- expand_bias_grad: float32 [2048], P(('dp', 'fsdp'))
- contract_bias_grad: float32 [512], P(('dp', 'fsdp'))
- pooling_bias_grad: float32 [512], P(('dp', 'fsdp'))
- upsample_bias_grad: float32 [1536], P(('dp', 'fsdp'))
The draws below stay inside these ranges and needn't reach their ends.
All inputs are finite; a program needn't handle non-finite values.
Results may differ from the reference program's by a relative error of at most 0.02.
Values may be sent and summed in bfloat16 or wider, within the bound.
A program may use at most 256 MiB of HBM per device.

```python
import jax
import jax.numpy as jnp
from jax import lax

D = 512
HEADS = 8
HEAD_DIM = 64
FF = 2048
SEQ = 1152
TOKENS = 36864


def with_spikes(values, stream_key, source, target, parts, factor):
    def block_of(dim):
        return (jnp.arange(values.shape[dim]) // (values.shape[dim] // parts)).reshape((-1,) + (1,) * (values.ndim - 1 - dim))

    one_side = jax.random.permutation(stream_key, parts)[block_of(target)]
    far = (block_of(target) + parts // 2) % parts
    return jnp.where((block_of(source) == one_side) | (block_of(source) == far), factor * values, values)


def levels(key, extent, split, low, largest):
    def one(position, shards_of):
        steps = jax.random.uniform(jax.random.fold_in(jax.random.fold_in(key, 6), position), (shards_of,), jnp.float32, low / len(split), largest / len(split))
        return jnp.repeat(jnp.exp(steps), extent[position] // shards_of).reshape((-1,) + (1,) * (len(extent) - position - 1))

    factor_of = one(*split[0])
    for cut in split[1:]:
        factor_of = factor_of * one(*cut)
    return factor_of


def scatter_about(own_key, shape, width, most, pieces=(), kind=jnp.bfloat16):
    drawn = jax.random.normal(own_key, shape, jnp.float32) * width
    if len(pieces) > 0:
        drawn = levels(own_key, shape, pieces, -0.22, 0.18) * drawn
    return jnp.clip(drawn, min=-most, max=most).astype(kind)


def bell_draw_with(own_key, shape, width, limit, pieces, heavy, kind=jnp.bfloat16):
    values = width * jax.random.normal(own_key, shape, jnp.float32)
    if pieces:
        values = values * levels(own_key, shape, pieces, -0.22, 0.18)
    return jnp.clip(with_spikes(values, jax.random.fold_in(own_key, 3), *heavy), -limit, limit).astype(kind)


def setup_inputs(seed: int = 0) -> dict:
    key_list = jax.random.split(jax.random.key(seed), 21)
    return {
        "tokens": scatter_about(key_list[0], (TOKENS, D), 1.0, 6.0, ((0, 32),)),
        "cotangent": bell_draw_with(key_list[1], (TOKENS, D), 1.0, 6.0, ((0, 32),), (0, 1, 32, 2.75)),
        "project_weight": scatter_about(key_list[2], (D, 3 * D), D ** -0.5, 0.25, ((0, 4), (1, 8))),
        "position_weight": scatter_about(key_list[3], (D, D), D ** -0.5, 0.25, ((0, 4), (1, 8))),
        "mixing_weight": scatter_about(key_list[4], (D, D), (D // 64) ** -0.5, 2.0, ((0, 4), (1, 8))),
        "expand_weight": scatter_about(key_list[5], (D, FF), D ** -0.5, 0.25, ((0, 4), (1, 8))),
        "contract_weight": scatter_about(key_list[6], (FF, D), FF ** -0.5, 0.125, ((0, 4), (1, 8))),
        "pooling_weight": scatter_about(key_list[7], (3 * D, D), (3 * D) ** -0.5, 0.15625, ((0, 4), (1, 8))),
        "upsample_weight": scatter_about(key_list[8], (D, 3 * D), D ** -0.5, 0.25, ((0, 4), (1, 8))),
        "first_gain": jnp.clip(1.0 + 0.15 * jax.random.normal(key_list[9], (D,), jnp.float32), 0.25, 1.75).astype(jnp.bfloat16),
        "first_shift": scatter_about(key_list[10], (D,), 0.3, 3.0, ((0, 32),)),
        "content_bias": scatter_about(key_list[11], (D,), 0.5, 3.0, ((0, 32),)),
        "position_bias": scatter_about(key_list[12], (D,), 0.5, 3.0, ((0, 32),)),
        "mixing_bias": scatter_about(key_list[13], (D,), 0.3, 3.0, ((0, 32),)),
        "second_gain": jnp.clip(1.0 + 0.15 * jax.random.normal(key_list[14], (D,), jnp.float32), 0.25, 1.75).astype(jnp.bfloat16),
        "second_shift": scatter_about(key_list[15], (D,), 0.3, 3.0, ((0, 32),)),
        "hidden_units_bias": scatter_about(key_list[16], (FF,), 0.5, 3.0, ((0, 32),)),
        "contract_bias": scatter_about(key_list[17], (D,), 0.3, 3.0, ((0, 32),)),
        "pooling_bias": scatter_about(key_list[18], (D,), 0.3, 3.0, ((0, 32),)),
        "upsampling_bias": scatter_about(key_list[19], (3 * D,), 0.3, 3.0, ((0, 32),)),
    }


@jax.custom_vjp
def low(v):
    return lax.optimization_barrier(v.astype(jnp.bfloat16)).astype(jnp.float32)

@jax.custom_vjp
def low_back(v):
    return v

def low_keep(v):
    return (low(v), None)

def low_pass(kept, grad):
    return (grad,)

def back_keep(v):
    return (v, None)

def back_low(kept, grad):
    return (low(grad),)
low.defvjp(low_keep, low_pass)
low_back.defvjp(back_keep, back_low)
epsilon = 1e-05
highest_accuracy = lax.Precision.HIGHEST
masked_fill = -1e+30

def product(factor_left, factor_right):
    return jnp.dot(factor_left, factor_right, precision=highest_accuracy, preferred_element_type=jnp.float32)

def layer_norm(values, norm_gain, norm_shift):
    row_mean = lax.optimization_barrier(jnp.mean(values, axis=-1, keepdims=True))
    centred = values - row_mean
    variance = lax.optimization_barrier(jnp.mean(centred * centred, axis=-1, keepdims=True))
    return centred * lax.rsqrt(variance + epsilon) * norm_gain + norm_shift

def distance_table(length, columns):
    ratios = jnp.arange(0, columns, 2).astype(jnp.float32) / columns
    inverse = 1.0 / 10000.0 ** ratios
    places = jnp.arange(length).astype(jnp.float32)
    angles = places[:, None] * inverse[None, :]
    return jnp.concatenate([jnp.sin(angles), jnp.cos(angles)], axis=1)

def attention(queries_u, queries_v, keys_all, values_all, positions):
    shaped_u = queries_u.reshape(SEQ, HEADS, HEAD_DIM)
    reshaped_value_offsets = queries_v.reshape(SEQ, HEADS, HEAD_DIM)
    shaped_keys = keys_all.reshape(SEQ, HEADS, HEAD_DIM)
    shaped_values = values_all.reshape(SEQ, HEADS, HEAD_DIM)
    reshaped_positions = positions.reshape(SEQ, HEADS, HEAD_DIM)
    content = jnp.einsum('ihd,jhd->hij', shaped_u, shaped_keys, precision=highest_accuracy, preferred_element_type=jnp.float32)
    cross_window = jnp.einsum('ebp,qbp->beq', reshaped_value_offsets, reshaped_positions, precision=highest_accuracy, preferred_element_type=jnp.float32)
    places = jnp.arange(SEQ)
    distance = places[:, None] - places[None, :]
    causal = distance >= 0
    gather_index = jnp.broadcast_to(jnp.clip(distance, 0, SEQ - 1).astype(jnp.int32)[None], (HEADS, SEQ, SEQ))
    relative = jnp.take_along_axis(cross_window, gather_index, axis=2)
    score_total = low_back(content + relative)
    scores = jnp.where(causal[None], score_total * HEAD_DIM ** (-0.5), masked_fill)
    top_score = lax.optimization_barrier(jnp.max(scores, axis=-1, keepdims=True))
    exp_scores = jnp.exp(scores - top_score)
    soft_probs = exp_scores / lax.optimization_barrier(jnp.sum(exp_scores, axis=-1, keepdims=True))
    mixed_out = jnp.einsum('hij,jhd->ihd', low(soft_probs), shaped_values, precision=highest_accuracy, preferred_element_type=jnp.float32)
    return low(low_back(mixed_out.reshape(SEQ, D)))

def forward(inputs, matrices, vectors):
    project_weight, position_weight, mixing_weight, expand_weight, contract_weight, pooling_weight, upsample_weight = matrices
    first_gain, first_shift, content_bias, position_bias, mixing_bias, second_gain, second_shift, hidden_units_bias, contract_bias, pooling_bias, upsampling_bias = vectors
    normed_one = low(layer_norm(inputs, first_gain, first_shift))
    joined = low_back(product(normed_one, project_weight))
    queries = joined[:, :D]
    keys_all = joined[:, D:2 * D]
    values_all = joined[:, 2 * D:]
    table_low = low(distance_table(SEQ, D))
    positions = low(low_back(product(table_low, position_weight)))
    mixed_out = attention(low(queries + content_bias), low(queries + position_bias), low(keys_all), low(values_all), positions)
    attended = low_back(product(mixed_out, mixing_weight) + mixing_bias)
    first_sum = inputs + attended
    normed_two = low(layer_norm(first_sum, second_gain, second_shift))
    inner_act = low_back(product(normed_two, expand_weight) + hidden_units_bias)
    activated = low(jax.nn.gelu(inner_act, approximate=False))
    branch = low_back(product(activated, contract_weight) + contract_bias)
    block_out = first_sum + branch
    shifted = jnp.concatenate([jnp.zeros((2, D), jnp.float32), low(block_out)[:-2]], axis=0)
    grouped = shifted.reshape(SEQ // 3, 3 * D)
    pooled = low(low_back(product(grouped, pooling_weight) + pooling_bias))
    upward = low_back(product(pooled, upsample_weight) + upsampling_bias)
    return block_out + upward.reshape(SEQ, D)

def reference(tokens, cotangent, project_weight, position_weight, mixing_weight, expand_weight, contract_weight, pooling_weight, upsample_weight, first_gain, first_shift, content_bias, position_bias, mixing_bias, second_gain, second_shift, hidden_units_bias, contract_bias, pooling_bias, upsampling_bias):
    matrices = tuple((weight.astype(jnp.float32) for weight in (project_weight, position_weight, mixing_weight, expand_weight, contract_weight, pooling_weight, upsample_weight)))
    vectors = tuple((weight.astype(jnp.float32) for weight in (first_gain, first_shift, content_bias, position_bias, mixing_bias, second_gain, second_shift, hidden_units_bias, contract_bias, pooling_bias, upsampling_bias)))
    inputs = tokens.astype(jnp.float32).reshape(-1, SEQ, D)
    upstream = cotangent.astype(jnp.float32).reshape(-1, SEQ, D)

    def one_window(totals, window_pair):
        result, pullback = jax.vjp(forward, window_pair[0], matrices, vectors)
        input_gradient, matrix_grads, vector_grads = pullback(window_pair[1])
        totals = jax.tree.map(jnp.add, totals, (matrix_grads, vector_grads))
        return (totals, (result, input_gradient))
    start_totals = jax.tree.map(jnp.zeros_like, (matrices, vectors))
    (matrix_sums, vector_sums), (results, input_grads) = lax.scan(one_window, start_totals, (inputs, upstream))
    output = results.reshape(-1, D).astype(jnp.bfloat16)
    token_grad = input_grads.reshape(-1, D)
    return (output, token_grad, matrix_sums[0], matrix_sums[1], matrix_sums[2], matrix_sums[3], matrix_sums[4], matrix_sums[5], matrix_sums[6], vector_sums[0], vector_sums[1], vector_sums[2], vector_sums[3], vector_sums[4], vector_sums[5], vector_sums[6], vector_sums[7], vector_sums[8], vector_sums[9], vector_sums[10])
```

```python
import math
from types import SimpleNamespace

import jax
import jax.numpy as jnp
from jax import lax
from jax.experimental import pallas as pl
from jax.experimental.pallas import tpu as pltpu
from jax.sharding import PartitionSpec as P

D = 512
HALF = D // 2
HEADS = 8
HEAD_DIM = 64
FF = 2048
SEQ = 1152
THIRD = SEQ // 3
QB = 384
SB = 128
CH = 16
RB = 128
BLOCKS = SEQ // QB
POFF = [sum((b + 1) * QB for b in range(n)) for n in range(BLOCKS + 1)]
PW = POFF[BLOCKS]
EXP_SCALE = HEAD_DIM ** (-0.5) * math.log2(math.e)
ANGLE_STEP = 32
epsilon = 1e-05
bf16 = jnp.bfloat16
f32 = jnp.float32
MESH = pl.DeviceIdType.MESH
VMEM_LIMIT = 63 << 20

WEIGHTS = ("project", "position", "mixing", "expand", "contract", "pooling", "upsample")
WEIGHT_SHAPE = {
    "project": (D, 3 * D),
    "position": (D, D),
    "mixing": (D, D),
    "expand": (D, FF),
    "contract": (FF, D),
    "pooling": (3 * D, D),
    "upsample": (D, 3 * D),
}
VECTORS = (
    "gain_one",
    "shift_one",
    "content",
    "position_bias",
    "mixing_bias",
    "gain_two",
    "shift_two",
    "hidden",
    "contract_bias",
    "pooling_bias",
    "upsample_bias",
)
VECTOR_SIZE = {n: D for n in VECTORS} | {"hidden": FF, "upsample_bias": 3 * D}
VECTOR_ROW = {n: i for i, n in enumerate(VECTORS)}
PACKED_VECTORS = ("hidden", "upsample_bias", "gain_one") + tuple(
    n for n in VECTORS if n not in ("hidden", "upsample_bias", "gain_one")
)


def nn(a, b):
    return lax.dot_general(a, b, (((1,), (0,)), ((), ())), preferred_element_type=f32)


def nt(a, b):
    return lax.dot_general(a, b, (((1,), (1,)), ((), ())), preferred_element_type=f32)


def tn(a, b):
    return lax.dot_general(a, b, (((0,), (0,)), ((), ())), preferred_element_type=f32)


def at_rows(step, rows):
    return pl.ds(pl.multiple_of(step * rows, rows), rows)


def eight_rows(values):
    rows, columns = values.shape
    return jnp.sum(values.reshape(rows // 8, 8, columns), axis=0)


def call(body, ins, outs, scratch, **params):
    names = [*ins, *outs, *scratch]

    def kernel(*refs):
        body(SimpleNamespace(**dict(zip(names, refs))))

    results = pl.pallas_call(
        kernel,
        out_shape=[jax.ShapeDtypeStruct(s, t) for s, t, _ in outs.values()],
        in_specs=[pl.BlockSpec(memory_space=m) for _, m in ins.values()],
        out_specs=[pl.BlockSpec(memory_space=m) for _, _, m in outs.values()],
        scratch_shapes=list(scratch.values()),
        compiler_params=pltpu.CompilerParams(vmem_limit_bytes=VMEM_LIMIT, **params),
    )(*[a for a, _ in ins.values()])
    return SimpleNamespace(**dict(zip(outs, results)))


VMEM = pltpu.VMEM
ANY = pl.ANY


BIT_AXIS = ("fsdp", "fsdp", "fsdp", "dp", "dp")
BIT_MASK = (4, 2, 1, 2, 1)
GATHER_ORDER = ((0, 1, 2, 3, 4), (0, 1, 3, 2, 4))
SCATTER_ORDER = ((4, 3, 2, 1, 0), (4, 2, 3, 1, 0))
CUBE = (2,) * 5


def my_bits():
    fs = lax.axis_index("fsdp")
    dp = lax.axis_index("dp")
    return (
        lax.rem(fs // 4, 2),
        lax.rem(fs // 2, 2),
        lax.rem(fs, 2),
        lax.rem(dp // 2, 2),
        lax.rem(dp, 2),
    )


def partner(bit):
    fs = lax.axis_index("fsdp")
    dp = lax.axis_index("dp")
    step = BIT_MASK[bit] * (1 - 2 * my_bits()[bit])
    if BIT_AXIS[bit] == "fsdp":
        return (dp, fs + step)
    return (dp + step, fs)


def partner_barrier():
    sem = pltpu.get_barrier_semaphore()
    for bit in range(5):
        pl.semaphore_signal(sem, inc=1, device_id=partner(bit), device_id_type=MESH)
    pl.semaphore_wait(sem, 5)


class Gather:
    def __init__(self, buf, pieces, send_sem, recv_sem):
        self.buf, self.pieces = buf, pieces
        self.send_sem, self.recv_sem = send_sem, recv_sem
        self.bits = my_bits()

    def copy(self, i, stage):
        row, rows, kind = self.pieces[i]
        order = GATHER_ORDER[kind]
        index = tuple(slice(None) if k in order[:stage] else self.bits[k] for k in range(5))
        ref = self.buf.at[index + (pl.ds(row, rows),)]
        return pltpu.make_async_remote_copy(
            src_ref=ref,
            dst_ref=ref,
            send_sem=self.send_sem.at[i * 5 + stage],
            recv_sem=self.recv_sem.at[i * 5 + stage],
            device_id=partner(order[stage]),
            device_id_type=MESH,
        )

    def advance(self, i, stage):
        if stage > 0:
            self.copy(i, stage - 1).wait_recv()
        if stage < 5:
            self.copy(i, stage).start()

    def drain(self):
        for i in range(len(self.pieces)):
            for stage in range(5):
                self.copy(i, stage).wait_send()


class Scatter:
    def __init__(self, own, land, out, pieces, send_sem, recv_sem, first=0):
        self.own, self.land, self.out, self.pieces = own, land, out, pieces
        self.send_sem, self.recv_sem, self.first = send_sem, recv_sem, first
        self.bits = my_bits()

    def index(self, order, stage, side):
        out = []
        for k in range(5):
            if k in order[:stage]:
                out.append(1 - self.bits[k] if side in ("land", "target") else self.bits[k])
            elif k == order[stage]:
                out.append(1 - self.bits[k] if side in ("send", "target") else self.bits[k])
            else:
                out.append(slice(None))
        return tuple(out)

    def copy(self, i, stage):
        row, rows, kind = self.pieces[i]
        order = SCATTER_ORDER[kind]
        part = (pl.ds(row, rows),)
        sem = self.first + i * 5 + stage
        return pltpu.make_async_remote_copy(
            src_ref=self.own.at[self.index(order, stage, "send") + part],
            dst_ref=self.land.at[self.index(order, stage, "target") + part],
            send_sem=self.send_sem.at[sem],
            recv_sem=self.recv_sem.at[sem],
            device_id=partner(order[stage]),
            device_id_type=MESH,
        )

    def add(self, i, stage):
        row, rows, kind = self.pieces[i]
        order = SCATTER_ORDER[kind]
        part = (pl.ds(row, rows), slice(None))
        mine = self.own.at[self.index(order, stage, "own")]
        came = self.land.at[self.index(order, stage, "land")]
        if stage == 4:
            self.out[pl.ds(row, rows), :] = mine[part].astype(f32) + came[part].astype(f32)
            return
        free = 4 - stage

        def body(j, carry):
            at = tuple(lax.rem(j // 2 ** (free - 1 - q), 2) for q in range(free)) + part
            mine[at] = mine[at] + came[at]
            return carry

        lax.fori_loop(0, 2**free, body, 0)

    def advance(self, i, stage):
        if stage > 0:
            self.copy(i, stage - 1).wait()
            self.add(i, stage - 1)
        if stage < 5:
            self.copy(i, stage).start()


def split_pieces(chunks):
    pieces = []
    for row, rows in chunks:
        half = (rows // 2 + 15) // 16 * 16
        pieces.append((row, half, 0))
        pieces.append((row + half, rows - half, 1))
    return pieces


def tick_events(chunks, ticks):
    return [
        [
            (2 * c + half, t - c)
            for c in range(chunks)
            if 0 <= t - c <= 5
            for half in range(2)
        ]
        for t in ticks
    ]


class Plan:
    def __init__(self, dp, fsdp):
        self.shard = {n: (WEIGHT_SHAPE[n][0] // dp, WEIGHT_SHAPE[n][1] // fsdp) for n in WEIGHTS}
        self.row, at = {}, 0
        for name in WEIGHTS:
            self.row[name] = at
            at += self.shard[name][0] * self.shard[name][1] // 128
        self.rows = at

    def span(self, first, last, shift):
        r, c = self.shard[last]
        end = self.row[last] + r * c // 128
        return (self.row[first] + shift, end - self.row[first])

    def full_shape(self, name):
        return (2, 2, 2, self.shard[name][1], WEIGHT_SHAPE[name][0])

    def blocks(self, name, shift):
        r, c = self.shard[name]
        return [
            (y, core, shift + self.row[name] + q * c, (y * 2 + core) * r + q * 128)
            for y in range(2)
            for core in range(2)
            for q in range(r // 128)
        ]


def load_weight(plan, name, buf, target, sem, shift):
    c = plan.shard[name][1]
    for y, core, row, column in plan.blocks(name, shift):
        pltpu.make_async_copy(
            buf.at[:, :, :, y, core, pl.ds(row, c), :],
            target.at[:, :, :, :, pl.ds(column, 128)],
            sem,
        ).start()


def wait_whole(target, sem):
    pltpu.make_async_copy(target, target, sem).wait()


def full(ref):
    values = ref[...]
    return values.reshape(-1, values.shape[-1])


def vector_places():
    places, at = {}, 0
    for name in PACKED_VECTORS:
        size = VECTOR_SIZE[name] // 32
        places[name] = (at // 128, at % 128, size)
        at += size
    return places


def block_owner(columns, size):
    row = lax.broadcasted_iota(jnp.int32, (32, columns), 0)
    lane = lax.broadcasted_iota(jnp.int32, (32, columns), 1)
    return lane // size == lax.rem(row, 4) * 8 + row // 4


def unpack_vectors(blocks, target):
    flat = blocks[...].reshape(32 * 16, 128)
    for name, (line, offset, size) in vector_places().items():
        columns = VECTOR_SIZE[name]
        row = lax.broadcasted_iota(jnp.int32, (32, 512), 0)
        lane = lax.broadcasted_iota(jnp.int32, (32, 512), 1)
        pick = (lane == row * 16 + line).astype(bf16)
        own = nn(pick, flat).astype(bf16)
        source = lax.broadcasted_iota(jnp.int32, (128, columns), 0)
        lane = lax.broadcasted_iota(jnp.int32, (128, columns), 1)
        spread = (source - offset == lax.rem(lane, size)).astype(bf16)
        spread_own = jnp.where(block_owner(columns, size), nn(own, spread), 0.0)
        r = VECTOR_ROW[name]
        target[r : r + 1, :columns] = jnp.sum(spread_own, axis=0, keepdims=True)


def pack_vectors(source, target):
    lines = [jnp.zeros((32, 128), f32), jnp.zeros((32, 128), f32)]
    for name, (line, offset, size) in vector_places().items():
        columns = VECTOR_SIZE[name]
        r = VECTOR_ROW[name]
        values = jnp.broadcast_to(source[r : r + 1, :columns], (32, columns))
        values = jnp.where(block_owner(columns, size), values, 0.0)
        lane = lax.broadcasted_iota(jnp.int32, (columns, 128), 0)
        goal = lax.broadcasted_iota(jnp.int32, (columns, 128), 1)
        gather = (goal - offset == lax.rem(lane, size)).astype(bf16)
        for _ in range(3):
            term = values.astype(bf16)
            lines[line] += nn(term, gather)
            values = values - term.astype(f32)
    both = jnp.concatenate([lines[0][:, None, :], lines[1][:, None, :]], axis=1)
    both = jnp.concatenate([both, jnp.zeros((32, 6, 128), f32)], axis=1)
    target[...] = both.reshape(CUBE + (8, 128))


def coarse_angles():
    ratios = jnp.arange(0, D, 2).astype(f32) / D
    inverse = 1.0 / 10000.0**ratios
    steps = SEQ // ANGLE_STEP
    places = jnp.concatenate(
        [jnp.arange(steps) * ANGLE_STEP, jnp.zeros((-steps % 8,), jnp.int32), jnp.arange(ANGLE_STEP)]
    ).astype(f32)
    angles = places[:, None] * inverse[None, :]
    return jnp.concatenate([jnp.sin(angles), jnp.cos(angles)], axis=1)


def expand_angles(coarse, angles, table_of):
    steps = SEQ // ANGLE_STEP
    start = steps + -steps % 8

    def body(q, carry):
        high_sin, high_cos = coarse[pl.ds(q, 1), :HALF], coarse[pl.ds(q, 1), HALF:]
        low_sin, low_cos = coarse[start:, :HALF], coarse[start:, HALF:]
        sine = high_sin * low_cos + high_cos * low_sin
        cosine = high_cos * low_cos - high_sin * low_sin
        rows = at_rows(q, ANGLE_STEP)
        angles[rows, :HALF] = sine
        angles[rows, HALF:] = cosine
        table_of(rows, sine.astype(bf16), cosine.astype(bf16))
        return carry

    lax.fori_loop(0, steps, body, 0)


def head_lanes(rows, head):
    return (lax.broadcasted_iota(jnp.int32, (rows, 128), 1) // HEAD_DIM) == head


def keep_head(values, head):
    return jnp.where(head_lanes(values.shape[0], head), values, 0).astype(bf16)


def rotate(pair, sines, cosines):
    low, high = pair[:, :HALF], pair[:, HALF:]
    return high * sines - low * cosines, low * sines + high * cosines


def norm_parts(values):
    row_mean = jnp.mean(values, axis=-1, keepdims=True)
    centred = values - row_mean
    variance = jnp.mean(centred * centred, axis=-1, keepdims=True)
    inv_std = lax.rsqrt(variance + epsilon)
    return centred * inv_std, inv_std


def norm_backward(normal, inv_std, gain, upstream):
    scaled = upstream * gain
    scaled_mean = jnp.mean(scaled, axis=-1, keepdims=True)
    cross_mean = jnp.mean(scaled * normal, axis=-1, keepdims=True)
    return inv_std * (scaled - scaled_mean - normal * cross_mean)


def vec(ref, name):
    r = VECTOR_ROW[name]
    return ref[r : r + 1, : VECTOR_SIZE[name]]


VECTOR_ROWS = 16


def front(plan, linked, ins):
    outs = {
        "vectors": ((16, FF), f32, VMEM),
        "query_u": ((SEQ, D), bf16, VMEM),
        "query_v": ((SEQ, D), bf16, VMEM),
        "key": ((SEQ, D), bf16, VMEM),
        "value": ((SEQ, D), bf16, VMEM),
        "mixed": ((SEQ, D), bf16, VMEM),
        "probs_out": ((HEADS, QB, PW), bf16, ANY),
    }
    scratch = {
        "normal": VMEM((SEQ, D), f32),
        "angles": VMEM((SEQ, D), f32),
        "key_table": VMEM((SEQ, 128 + D), bf16),
        "score": VMEM((2, QB, SEQ), f32),
        "turned": VMEM((2, QB, 128 + D), bf16),
        "probs": VMEM((2, QB, PW), bf16),
        "probs_sem": pltpu.SemaphoreType.DMA((2,)),
    }
    params = {}
    if linked:
        rows = VECTOR_ROWS + plan.rows
        chunks = [
            (0, VECTOR_ROWS + plan.span("project", "project", 0)[1]),
            plan.span("position", "mixing", VECTOR_ROWS),
            plan.span("expand", "expand", VECTOR_ROWS),
            plan.span("contract", "contract", VECTOR_ROWS),
            plan.span("pooling", "pooling", VECTOR_ROWS),
            plan.span("upsample", "upsample", VECTOR_ROWS),
        ]
        pieces = split_pieces(chunks)
        outs["blocks"] = (CUBE + (rows, 128), bf16, ANY)
        scratch |= {
            "mine": VMEM((rows, 128), bf16),
            "project": VMEM(plan.full_shape("project"), bf16),
            "position": VMEM(plan.full_shape("position"), bf16),
            "vector_blocks": VMEM(CUBE + (VECTOR_ROWS, 128), bf16),
            "send_sem": pltpu.SemaphoreType.DMA((5 * len(pieces),)),
            "recv_sem": pltpu.SemaphoreType.DMA((5 * len(pieces),)),
            "load_sem": pltpu.SemaphoreType.DMA((4,)),
        }
        params = dict(collective_id=0, has_side_effects=True)

    def body(ref):
        events = []
        if linked:
            gather = Gather(ref.blocks, pieces, ref.send_sem, ref.recv_sem)

            def run(tick_list):
                for batch in tick_list:
                    for piece, stage in batch:
                        gather.advance(piece, stage)

            ref.mine[:VECTOR_ROWS, :] = ref.packed[...]
            for name in WEIGHTS:
                r, c = plan.shard[name]
                shard = getattr(ref, name + "_shard")
                for q in range(r // 128):
                    at = VECTOR_ROWS + plan.row[name] + q * c
                    ref.mine[at : at + c, :] = shard[q * 128 : (q + 1) * 128, :].T
            own = pltpu.make_async_copy(
                ref.mine, ref.blocks.at[gather.bits], ref.load_sem.at[0]
            )
            own.start()
            partner_barrier()
            own.wait()
            run(tick_events(6, [0]))
            events = tick_events(6, range(7, 11))

        def first_norm(i, carry):
            rows = at_rows(i, RB)
            ref.normal[rows, :] = norm_parts(ref.tokens[rows, :].astype(f32))[0]
            return carry

        lax.fori_loop(0, SEQ // RB, first_norm, 0)

        def table_of(rows, sine, cosine):
            ref.key_table[rows, 128 : 128 + HALF] = sine
            ref.key_table[rows, 128 + HALF :] = cosine

        expand_angles(ref.coarse, ref.angles, table_of)

        if linked:
            run(tick_events(6, [1, 2, 3, 4, 5]))
            load_weight(plan, "project", ref.blocks, ref.project, ref.load_sem.at[1], VECTOR_ROWS)
            small = pltpu.make_async_copy(
                ref.blocks.at[:, :, :, :, :, pl.ds(0, VECTOR_ROWS), :],
                ref.vector_blocks,
                ref.load_sem.at[2],
            )
            small.start()
            small.wait()
            unpack_vectors(ref.vector_blocks, ref.vectors)
            wait_whole(ref.project, ref.load_sem.at[1])
        else:
            ref.vectors[...] = ref.given_vectors[...]

        for b in range(BLOCKS):
            rows = slice(b * QB, (b + 1) * QB)
            normed = ref.normal[rows, :] * vec(ref.vectors, "gain_one") + vec(
                ref.vectors, "shift_one"
            )
            joined = nt(normed.astype(bf16), full(ref.project))
            ref.query_u[rows, :] = (joined[:, :D] + vec(ref.vectors, "content")).astype(bf16)
            ref.query_v[rows, :] = (joined[:, :D] + vec(ref.vectors, "position_bias")).astype(bf16)
            ref.key[rows, :] = joined[:, D : 2 * D].astype(bf16)
            ref.value[rows, :] = joined[:, 2 * D :].astype(bf16)

        if linked:
            run(tick_events(6, [6]))
            load_weight(plan, "position", ref.blocks, ref.position, ref.load_sem.at[3], VECTOR_ROWS)
            wait_whole(ref.position, ref.load_sem.at[3])
            position = ref.position.reshape(D, D)
        else:
            position = ref.position

        def out_copy(head, slot):
            return pltpu.make_async_copy(
                ref.probs.at[slot], ref.probs_out.at[head], ref.probs_sem.at[slot]
            )

        def scores(lanes, b, e):
            row, width = b * QB, (b + 1) * QB
            rows = slice(row, row + QB)
            spread = nn(keep_head(ref.query_v[rows, lanes], e), position[lanes, :])
            low, high = rotate(spread, ref.angles[rows, :HALF], ref.angles[rows, HALF:])
            ref.turned[e, :, :128] = keep_head(ref.query_u[rows, lanes], e)
            ref.turned[e, :, 128 : 128 + HALF] = low.astype(bf16)
            ref.turned[e, :, 128 + HALF :] = high.astype(bf16)
            ref.score[e, :, :width] = nt(ref.turned[e], ref.key_table[:width, :])

        def softmax(b, e):
            row, width = b * QB, (b + 1) * QB
            for sub in range(QB // SB):
                used = row + (sub + 1) * SB
                for g in range(SB // CH):
                    at = slice(sub * SB + g * CH, sub * SB + (g + 1) * CH)
                    tiles = [
                        ref.score[e, at, i * 128 : (i + 1) * 128] for i in range(used // 128)
                    ]
                    lane = lax.broadcasted_iota(jnp.int32, (CH, SB), 1)
                    place = lax.broadcasted_iota(jnp.int32, (CH, SB), 0) + g * CH
                    tiles[-1] = jnp.where(lane <= place, tiles[-1], -1e30)
                    top = tiles[0]
                    for tile in tiles[1:]:
                        top = jnp.maximum(top, tile)
                    top = jnp.max(top, axis=1, keepdims=True)
                    tiles = [jnp.exp2((tile - top) * EXP_SCALE) for tile in tiles]
                    total = tiles[0]
                    for tile in tiles[1:]:
                        total = total + tile
                    scale = 1.0 / jnp.sum(total, axis=1, keepdims=True)
                    for i, tile in enumerate(tiles):
                        lanes = slice(POFF[b] + i * 128, POFF[b] + (i + 1) * 128)
                        ref.probs[e, at, lanes] = (tile * scale).astype(bf16)
                if used < width:
                    ref.probs[e, sub * SB : (sub + 1) * SB, POFF[b] + used : POFF[b] + width] = (
                        jnp.zeros((SB, width - used), bf16)
                    )

        def pair(hp, carry):
            lanes = pl.ds(pl.multiple_of(hp * 128, 128), 128)
            ref.key_table[:, :128] = ref.key[:, lanes]

            @pl.when(hp > 0)
            def _():
                for e in range(2):
                    out_copy(0, e).wait()

            for b in range(BLOCKS):
                for e in range(2):
                    scores(lanes, b, e)
                    softmax(b, e)
                    point = b * 2 + e
                    for number, batch in enumerate(events):
                        when = 4 + number * 5
                        if when % 6 == point:

                            @pl.when(hp == when // 6)
                            def _(batch=batch):
                                run([batch])

                row, width = b * QB, (b + 1) * QB
                values = ref.value[:width, lanes]
                span = slice(POFF[b], POFF[b] + width)
                ref.mixed[row : row + QB, lanes] = jnp.where(
                    head_lanes(QB, 0),
                    nn(ref.probs[0, :, span], values),
                    nn(ref.probs[1, :, span], values),
                ).astype(bf16)
            for e in range(2):
                out_copy(hp * 2 + e, e).start()
            return carry

        lax.fori_loop(0, HEADS // 2, pair, 0)
        for e in range(2):
            out_copy(0, e).wait()
        if linked:
            gather.drain()

    return call(body, ins, outs, scratch, **params)


MIDDLE = ("mixing", "expand", "contract", "pooling", "upsample")


def middle(plan, linked, ins):
    def weight_shape(name):
        return plan.full_shape(name) if linked else WEIGHT_SHAPE[name][::-1]

    outs = {
        "output": ((SEQ, D), bf16, VMEM),
        "first_grad": ((SEQ, D), f32, VMEM),
        "mixed_grad": ((SEQ, D), bf16, VMEM),
        "sums": ((16, FF), f32, VMEM),
    }
    outs |= {n + "_grad": (weight_shape(n), bf16, VMEM) for n in MIDDLE}
    scratch = {n: VMEM(weight_shape(n), bf16) for n in MIDDLE}
    scratch |= {
        "normal": VMEM((SEQ, D), f32),
        "inverse": VMEM((SEQ, 128), f32),
        "second_low": VMEM((SEQ, D), bf16),
        "activated": VMEM((SEQ, FF), bf16),
        "slope": VMEM((SEQ, FF), bf16),
        "tiles": VMEM((D // 128, SEQ + 16, 128), f32),
        "grouped": VMEM((THIRD, 3 * D), bf16),
        "up_rows": VMEM((THIRD, 3 * D), bf16),
        "branch_grad": VMEM((SEQ, D), bf16),
        "attended_grad": VMEM((SEQ, D), bf16),
        "parts": VMEM((5, 8, FF), f32),
        "sem": pltpu.SemaphoreType.DMA((len(MIDDLE),)),
    }

    def body(ref):
        weight = {}
        for i, name in enumerate(MIDDLE):
            if linked:
                load_weight(plan, name, ref.blocks, getattr(ref, name), ref.sem.at[i], VECTOR_ROWS)
            else:
                pltpu.make_async_copy(
                    getattr(ref, name + "_full"), getattr(ref, name), ref.sem.at[i]
                ).start()

        def ready(name):
            wait_whole(getattr(ref, name), ref.sem.at[MIDDLE.index(name)])

        def get(name):
            return full(getattr(ref, name))

        def put(name, values):
            target = getattr(ref, name + "_grad")
            target[...] = values.astype(bf16).reshape(target.shape)

        def third(start, k):
            return jnp.concatenate(
                [ref.tiles[t, pl.ds(start + k, THIRD, stride=3), :] for t in range(D // 128)],
                axis=1,
            )

        def put_third(start, k, values):
            for t in range(D // 128):
                ref.tiles[t, pl.ds(start + k, THIRD, stride=3), :] = values[
                    :, t * 128 : (t + 1) * 128
                ]

        def rows_of(rows):
            return jnp.concatenate([ref.tiles[t, rows, :] for t in range(D // 128)], axis=1)

        def put_rows(rows, values):
            for t in range(D // 128):
                ref.tiles[t, rows, :] = values[:, t * 128 : (t + 1) * 128]

        def shifted_rows(i):
            return pl.ds(pl.multiple_of(i * RB + 8, 8), RB)

        ref.parts[...] = jnp.zeros_like(ref.parts)
        ref.sums[...] = jnp.zeros_like(ref.sums)

        def add_part(slot, values):
            columns = values.shape[1]
            ref.parts[slot, :, :columns] += eight_rows(values)

        def put_sum(name, values):
            r = VECTOR_ROW[name]
            ref.sums[r : r + 1, : values.shape[1]] = values

        def put_part(name, slot):
            columns = VECTOR_SIZE[name]
            put_sum(name, jnp.sum(ref.parts[slot, :, :columns], axis=0, keepdims=True))

        for name in ("mixing", "expand", "contract"):
            ready(name)

        def forward(i, carry):
            rows = at_rows(i, RB)
            attended = nt(ref.mixed[rows, :], get("mixing")) + vec(ref.vectors, "mixing_bias")
            first = ref.tokens[rows, :].astype(f32) + attended
            normal, inverse = norm_parts(first)
            ref.normal[rows, :] = normal
            ref.inverse[rows, :] = jnp.broadcast_to(inverse, (RB, 128))
            low = (
                normal * vec(ref.vectors, "gain_two") + vec(ref.vectors, "shift_two")
            ).astype(bf16)
            ref.second_low[rows, :] = low
            inner = nt(low, get("expand")) + vec(ref.vectors, "hidden")
            phi = 0.5 * (1.0 + lax.erf(inner * 2.0 ** (-0.5)))
            act = (inner * phi).astype(bf16)
            ref.activated[rows, :] = act
            bell = jnp.exp(-0.5 * inner * inner) * (2.0 * math.pi) ** (-0.5)
            ref.slope[rows, :] = (phi + inner * bell).astype(bf16)
            block = first + nt(act, get("contract")) + vec(ref.vectors, "contract_bias")
            put_rows(shifted_rows(i), block)
            return carry

        lax.fori_loop(0, SEQ // RB, forward, 0)

        put_rows(slice(0, 8), jnp.zeros((8, D), f32))
        for k in range(3):
            ref.grouped[:, k * D : (k + 1) * D] = third(6, k).astype(bf16)
        ready("pooling")
        pooled = (
            nt(ref.grouped[...], get("pooling")) + vec(ref.vectors, "pooling_bias")
        ).astype(bf16)
        ready("upsample")
        for k in range(3):
            columns = slice(k * D, (k + 1) * D)
            upward = nt(pooled, get("upsample")[columns, :]) + vec(ref.vectors, "upsample_bias")[
                :, columns
            ]
            put_third(8, k, third(8, k) + upward)

        def write_output(i, carry):
            ref.output[at_rows(i, RB), :] = rows_of(shifted_rows(i)).astype(bf16)
            put_rows(shifted_rows(i), ref.cotangent[at_rows(i, RB), :].astype(f32))
            return carry

        lax.fori_loop(0, SEQ // RB, write_output, 0)

        for k in range(3):
            ref.up_rows[:, k * D : (k + 1) * D] = third(8, k).astype(bf16)
        up_rows = ref.up_rows[...]
        put_sum("upsample_bias", jnp.sum(up_rows.astype(f32), axis=0, keepdims=True))
        put("upsample", tn(up_rows, pooled))
        pooled_grad = nn(up_rows, get("upsample")).astype(bf16)
        put_sum("pooling_bias", jnp.sum(pooled_grad.astype(f32), axis=0, keepdims=True))
        put("pooling", tn(pooled_grad, ref.grouped[...]))
        for k in range(3):
            put_third(
                6, k, nn(pooled_grad, get("pooling")[:, k * D : (k + 1) * D])
            )
        put_rows(slice(SEQ + 6, SEQ + 8), jnp.zeros((2, D), f32))

        def backward(i, carry):
            rows = at_rows(i, RB)
            block_grad = ref.cotangent[rows, :].astype(f32) + rows_of(shifted_rows(i))
            branch_grad = block_grad.astype(bf16)
            ref.branch_grad[rows, :] = branch_grad
            add_part(0, branch_grad.astype(f32))
            inner_grad = (nn(branch_grad, get("contract")) * ref.slope[rows, :].astype(f32)).astype(
                bf16
            )
            ref.slope[rows, :] = inner_grad
            add_part(1, inner_grad.astype(f32))
            second_grad = nn(inner_grad, get("expand"))
            normal = ref.normal[rows, :]
            add_part(2, second_grad * normal)
            add_part(3, second_grad)
            first_grad = block_grad + norm_backward(
                normal, ref.inverse[rows, :1], vec(ref.vectors, "gain_two"), second_grad
            )
            ref.first_grad[rows, :] = first_grad
            attended_grad = first_grad.astype(bf16)
            ref.attended_grad[rows, :] = attended_grad
            add_part(4, attended_grad.astype(f32))
            ref.mixed_grad[rows, :] = nn(attended_grad, get("mixing")).astype(bf16)
            return carry

        lax.fori_loop(0, SEQ // RB, backward, 0)
        put_part("contract_bias", 0)
        put_part("hidden", 1)
        put_part("gain_two", 2)
        put_part("shift_two", 3)
        put_part("mixing_bias", 4)
        put("contract", tn(ref.branch_grad[...], ref.activated[...]))
        put("expand", tn(ref.slope[...], ref.second_low[...]))
        put("mixing", tn(ref.attended_grad[...], ref.mixed[...]))

    return call(body, ins, outs, scratch)


def back(plan, linked, ins):
    outs = {"token_grad": ((SEQ, D), f32, VMEM)}
    scratch = {
        "angles": VMEM((SEQ, D), f32),
        "key_table": VMEM((SEQ, 128 + D), bf16),
        "prob_grad": VMEM((2, QB, SEQ), f32),
        "total_grad": VMEM((2, QB, SEQ), bf16),
        "probs": VMEM((4, QB, PW), bf16),
        "key_acc": VMEM((128, SEQ), f32),
        "value_acc": VMEM((128, SEQ), f32),
        "joined_grad": VMEM((SEQ, 3 * D), bf16),
        "normed_low": VMEM((SEQ, D), bf16),
        "position_grad": VMEM((D, D), f32),
        "parts": VMEM((2, 8, D), f32),
        "all_sums": VMEM((16, FF), f32),
        "probs_sem": pltpu.SemaphoreType.DMA((4,)),
        "load_sem": pltpu.SemaphoreType.DMA((2,)),
    }
    params = {}
    project_shape = plan.full_shape("project") if linked else (3 * D, D)
    position_shape = plan.full_shape("position") if linked else (D, D)
    scratch |= {"project": VMEM(project_shape, bf16), "position": VMEM(position_shape, bf16)}
    if linked:
        early = [
            plan.span(n, n, 0) for n in ("upsample", "pooling", "contract", "expand", "mixing")
        ]
        late = [plan.span("project", "position", 0)]
        pieces = split_pieces(early + late)
        count = 5 * len(pieces) + 5
        for n in WEIGHTS:
            outs[n + "_out"] = (plan.shard[n], f32, VMEM)
        outs["vector_out"] = ((8, 128), f32, VMEM)
        scratch |= {
            "own": VMEM(CUBE + (plan.rows, 128), bf16),
            "land": VMEM(CUBE + (plan.rows, 128), bf16),
            "flat": VMEM((plan.rows, 128), f32),
            "vector_own": VMEM(CUBE + (8, 128), f32),
            "vector_land": VMEM(CUBE + (8, 128), f32),
            "send_sem": pltpu.SemaphoreType.DMA((count,)),
            "recv_sem": pltpu.SemaphoreType.DMA((count,)),
            "own_sem": pltpu.SemaphoreType.DMA((5,)),
        }
        params = dict(collective_id=1, has_side_effects=True)
    else:
        outs["project_grad"] = ((3 * D, D), bf16, VMEM)
        outs["position_grad_out"] = ((D, D), bf16, VMEM)
        outs["sums_out"] = ((16, FF), f32, VMEM)

    def body(ref):
        events = []
        if linked:
            load_weight(plan, "project", ref.blocks, ref.project, ref.load_sem.at[0], VECTOR_ROWS)
            load_weight(plan, "position", ref.blocks, ref.position, ref.load_sem.at[1], VECTOR_ROWS)
            matrix = Scatter(ref.own, ref.land, ref.flat, pieces, ref.send_sem, ref.recv_sem)
            vector = Scatter(
                ref.vector_own,
                ref.vector_land,
                ref.vector_out,
                [(0, 8, 0)],
                ref.send_sem,
                ref.recv_sem,
                count - 5,
            )

            def run(tick_list):
                for batch in tick_list:
                    for piece, stage in batch:
                        matrix.advance(piece, stage)

            order = ("upsample", "pooling", "contract", "expand", "mixing")
            for i, name in enumerate(order):
                c = plan.shard[name][1]
                for y, core, row, column in plan.blocks(name, 0):
                    pltpu.make_async_copy(
                        getattr(ref, name + "_grad").at[:, :, :, :, pl.ds(column, 128)],
                        ref.own.at[:, :, :, y, core, pl.ds(row, c), :],
                        ref.own_sem.at[i],
                    ).start()
            partner_barrier()
            for i, name in enumerate(order):
                row, rows = plan.span(name, name, 0)
                whole = ref.own.at[:, :, :, :, :, pl.ds(row, rows), :]
                wait_whole(whole, ref.own_sem.at[i])
            run(tick_events(5, [0]))
            events = tick_events(5, range(1, 10))
        else:
            for i, name in enumerate(("project", "position")):
                pltpu.make_async_copy(
                    getattr(ref, name + "_full"), getattr(ref, name), ref.load_sem.at[i]
                ).start()

        def in_copy(head, slot):
            return pltpu.make_async_copy(
                ref.probs_in.at[head], ref.probs.at[slot], ref.probs_sem.at[slot]
            )

        for e in range(2):
            in_copy(e, e).start()

        def table_of(rows, sine, cosine):
            ref.key_table[rows, 128 : 128 + HALF] = sine
            ref.key_table[rows, 128 + HALF :] = cosine

        expand_angles(ref.coarse, ref.angles, table_of)
        ref.all_sums[...] = ref.sums[...]
        ref.parts[...] = jnp.zeros_like(ref.parts)
        wait_whole(ref.project, ref.load_sem.at[0])
        wait_whole(ref.position, ref.load_sem.at[1])
        position = ref.position.reshape(D, D)

        def pair(hp, carry):
            start = pl.multiple_of(hp * 128, 128)
            lanes = pl.ds(start, 128)
            base = lax.rem(hp, 2) * 2
            for e in range(2):
                in_copy(0, base + e).wait()

            @pl.when(hp < HEADS // 2 - 1)
            def _():
                for e in range(2):
                    in_copy(hp * 2 + 2 + e, 2 - base + e).start()

            ref.key_table[:, :128] = ref.key[:, lanes]
            content_sum = jnp.zeros((1, 128), f32)
            position_sum = jnp.zeros((1, 128), f32)
            for b in range(BLOCKS):
                row, width = b * QB, (b + 1) * QB
                rows = slice(row, row + QB)
                span = slice(POFF[b], POFF[b] + width)
                by_content, by_position = [], None
                for e in range(2):
                    upstream = keep_head(ref.mixed_grad[rows, lanes], e)
                    row_dot = jnp.sum(
                        upstream.astype(f32) * ref.mixed[rows, lanes].astype(f32),
                        axis=1,
                        keepdims=True,
                    )
                    ref.prob_grad[e, :, :width] = nt(upstream, ref.value[:width, lanes]) - row_dot
                    for sub in range(QB // SB):
                        used = row + (sub + 1) * SB
                        for g in range(SB // CH):
                            at = slice(sub * SB + g * CH, sub * SB + (g + 1) * CH)
                            p = ref.probs[base + e, at, POFF[b] : POFF[b] + used].astype(f32)
                            ref.total_grad[e, at, :used] = (
                                p * ref.prob_grad[e, at, :used] * HEAD_DIM ** (-0.5)
                            ).astype(bf16)
                        if used < width:
                            ref.total_grad[e, sub * SB : (sub + 1) * SB, used:width] = jnp.zeros(
                                (SB, width - used), bf16
                            )
                    scored = ref.total_grad[e, :, :width]
                    turned = nn(scored, ref.key_table[:width, :])
                    by_content.append(turned[:, :128])
                    low, high = rotate(
                        turned[:, 128:], ref.angles[rows, :HALF], ref.angles[rows, HALF:]
                    )
                    spread = jnp.concatenate([low, high], axis=1).astype(bf16)
                    own = (lax.broadcasted_iota(jnp.int32, (128, D), 0) // HEAD_DIM) == e
                    part = nt(spread, jnp.where(own, position[lanes, :], 0).astype(bf16))
                    by_position = part if by_position is None else by_position + part
                    part = tn(keep_head(ref.query_v[rows, lanes], e), spread)
                    if b == 0 and e == 0:
                        ref.position_grad[lanes, :] = part
                    else:
                        ref.position_grad[lanes, :] += part
                    to_key = tn(keep_head(ref.query_u[rows, lanes], e), scored)
                    to_value = tn(upstream, ref.probs[base + e, :, span])
                    if e == 0:
                        if b > 0:
                            ref.key_acc[:, :row] += to_key[:, :row]
                            ref.value_acc[:, :row] += to_value[:, :row]
                        ref.key_acc[:, row:width] = to_key[:, row:]
                        ref.value_acc[:, row:width] = to_value[:, row:]
                    else:
                        ref.key_acc[:, :width] += to_key
                        ref.value_acc[:, :width] += to_value
                    point = b * 2 + e
                    for number, batch in enumerate(events):
                        when = 2 + (number * 5) // 2
                        if when % 6 == point:

                            @pl.when(hp == when // 6)
                            def _(batch=batch):
                                run([batch])

                by_content = jnp.where(head_lanes(QB, 0), by_content[0], by_content[1])
                ref.joined_grad[rows, lanes] = (by_content + by_position).astype(bf16)
                content_sum += jnp.sum(by_content, axis=0, keepdims=True)
                position_sum += jnp.sum(by_position, axis=0, keepdims=True)
            ref.joined_grad[:, pl.ds(start + D, 128)] = ref.key_acc[...].T.astype(bf16)
            ref.joined_grad[:, pl.ds(start + 2 * D, 128)] = ref.value_acc[...].T.astype(bf16)
            r = VECTOR_ROW["content"]
            ref.all_sums[r : r + 1, lanes] = content_sum
            r = VECTOR_ROW["position_bias"]
            ref.all_sums[r : r + 1, lanes] = position_sum
            return carry

        lax.fori_loop(0, HEADS // 2, pair, 0)

        def norm_rows(rows):
            return norm_parts(ref.tokens[rows, :].astype(f32))

        def low_rows(i, carry):
            rows = at_rows(i, RB)
            normal, _ = norm_rows(rows)
            ref.normed_low[rows, :] = (
                normal * vec(ref.vectors, "gain_one") + vec(ref.vectors, "shift_one")
            ).astype(bf16)
            return carry

        lax.fori_loop(0, SEQ // RB, low_rows, 0)
        for part in range(3):
            columns = slice(part * D, (part + 1) * D)
            grad = tn(ref.joined_grad[:, columns], ref.normed_low[...]).astype(bf16)
            if linked:
                ref.project_full[columns, :] = grad
            else:
                ref.project_grad[columns, :] = grad
        if linked:
            for name, source in (("project", ref.project_full), ("position", ref.position_grad)):
                r, c = plan.shard[name]
                for y, core, at, column in plan.blocks(name, 0):
                    values = source[:, column : column + 128].astype(bf16)
                    ref.own[:, :, :, y, core, at : at + c, :] = values.reshape(2, 2, 2, c, 128)
            tail = len(early) * 2
            for piece in (tail, tail + 1):
                matrix.advance(piece, 0)
        else:
            ref.position_grad_out[...] = ref.position_grad[...].astype(bf16)

        def norm_back(i, carry):
            rows = at_rows(i, RB)
            normal, inverse = norm_rows(rows)
            upstream = nn(ref.joined_grad[rows, :], full(ref.project))
            ref.parts[0, :, :] += eight_rows(upstream * normal)
            ref.parts[1, :, :] += eight_rows(upstream)
            ref.token_grad[rows, :] = ref.first_grad[rows, :] + norm_backward(
                normal, inverse, vec(ref.vectors, "gain_one"), upstream
            )
            return carry

        lax.fori_loop(0, SEQ // RB, norm_back, 0)
        for slot, name in enumerate(("gain_one", "shift_one")):
            r = VECTOR_ROW[name]
            ref.all_sums[r : r + 1, :D] = jnp.sum(ref.parts[slot], axis=0, keepdims=True)
        if linked:
            pack_vectors(ref.all_sums, ref.vector_own)
            for stage in range(1, 6):
                vector.advance(0, stage - 1)
                for piece in (tail, tail + 1):
                    matrix.advance(piece, stage)
            vector.advance(0, 5)
            for name in WEIGHTS:
                r, c = plan.shard[name]
                target = getattr(ref, name + "_out")
                for q in range(r // 128):
                    at = plan.row[name] + q * c
                    target[q * 128 : (q + 1) * 128, :] = ref.flat[at : at + c, :].T
        else:
            ref.sums_out[...] = ref.all_sums[...]

    if linked:
        scratch["project_full"] = VMEM((3 * D, D), bf16)
    return call(body, ins, outs, scratch, **params)


def make_local(dp, fsdp):
    plan = Plan(dp, fsdp)
    linked = (dp, fsdp) == (4, 8)

    def gathered(weights):
        out = {}
        for name, shard in zip(WEIGHTS, weights):
            part = lax.all_gather(shard, "dp", axis=0, tiled=True)
            out[name + "_full"] = lax.all_gather(part, "fsdp", axis=1, tiled=True).T
        return out

    def gathered_vectors(vectors):
        rows = []
        for name, shard in zip(VECTORS, vectors):
            whole = lax.all_gather(shard, ("dp", "fsdp"), axis=0, tiled=True).astype(f32)
            rows.append(jnp.pad(whole, (0, FF - VECTOR_SIZE[name])))
        rows += [jnp.zeros((FF,), f32)] * (16 - len(rows))
        return jnp.stack(rows)

    def local(tokens, cotangent, *params):
        assert tokens.shape[0] == SEQ
        weights, vectors = params[:7], params[7:]
        given = dict(zip(VECTORS, vectors))
        coarse = coarse_angles()
        ins = {"tokens": (tokens, VMEM), "coarse": (coarse, VMEM)}
        if linked:
            packed = jnp.concatenate([given[n] for n in PACKED_VECTORS])
            packed = jnp.pad(packed, (0, VECTOR_ROWS * 128 - packed.shape[0]))
            ins["packed"] = (packed.reshape(VECTOR_ROWS, 128), VMEM)
            ins |= {n + "_shard": (w, VMEM) for n, w in zip(WEIGHTS, weights)}
        else:
            whole = gathered(weights)
            ins["given_vectors"] = (gathered_vectors(vectors), VMEM)
            ins["project"] = (whole["project_full"], VMEM)
            ins["position"] = (whole["position_full"], VMEM)
        one = front(plan, linked, ins)

        ins = {
            "tokens": (tokens, VMEM),
            "cotangent": (cotangent, VMEM),
            "mixed": (one.mixed, VMEM),
            "vectors": (one.vectors, VMEM),
        }
        if linked:
            ins["blocks"] = (one.blocks, ANY)
        else:
            ins |= {n + "_full": (whole[n + "_full"], ANY) for n in MIDDLE}
        two = middle(plan, linked, ins)

        ins = {
            "tokens": (tokens, VMEM),
            "coarse": (coarse, VMEM),
            "vectors": (one.vectors, VMEM),
            "query_u": (one.query_u, VMEM),
            "query_v": (one.query_v, VMEM),
            "key": (one.key, VMEM),
            "value": (one.value, VMEM),
            "mixed": (one.mixed, VMEM),
            "mixed_grad": (two.mixed_grad, VMEM),
            "first_grad": (two.first_grad, VMEM),
            "sums": (two.sums, VMEM),
            "probs_in": (one.probs_out, ANY),
        }
        if linked:
            ins["blocks"] = (one.blocks, ANY)
            ins |= {n + "_grad": (getattr(two, n + "_grad"), ANY) for n in MIDDLE}
        else:
            ins |= {n + "_full": (whole[n + "_full"], ANY) for n in ("project", "position")}
        three = back(plan, linked, ins)

        if linked:
            matrices = [getattr(three, n + "_out") for n in WEIGHTS]
            places = vector_places()
            small = []
            for name in VECTORS:
                line, offset, size = places[name]
                small.append(three.vector_out[line, offset : offset + size])
        else:
            grads = {n: getattr(two, n + "_grad") for n in MIDDLE}
            grads["project"] = three.project_grad
            grads["position"] = three.position_grad_out
            matrices = []
            for name in WEIGHTS:
                part = lax.psum_scatter(
                    grads[name].T, "fsdp", scatter_dimension=1, tiled=True
                )
                part = lax.psum_scatter(part, "dp", scatter_dimension=0, tiled=True)
                matrices.append(part.astype(f32))
            small = []
            for name in VECTORS:
                sums = three.sums_out[VECTOR_ROW[name], : VECTOR_SIZE[name]]
                small.append(
                    lax.psum_scatter(sums, ("dp", "fsdp"), scatter_dimension=0, tiled=True)
                )
        return (two.output, three.token_grad, *matrices, *small)

    return local


def solution(mesh):
    rows = P(("dp", "fsdp"), None)
    matrix = P("dp", "fsdp")
    vector = P(("dp", "fsdp"))
    return jax.shard_map(
        make_local(mesh.shape["dp"], mesh.shape["fsdp"]),
        mesh=mesh,
        in_specs=(rows,) * 2 + (matrix,) * 7 + (vector,) * 11,
        out_specs=(rows,) * 2 + (matrix,) * 7 + (vector,) * 11,
        check_vma=False,
    )
```

```python
import math
from types import SimpleNamespace

import jax
import jax.numpy as jnp
from jax import lax
from jax.experimental import pallas as pl
from jax.experimental.pallas import tpu as pltpu
from jax.sharding import PartitionSpec as P

D = 512
HALF = D // 2
HEADS = 8
HEAD_DIM = 64
FF = 2048
SEQ = 1152
THIRD = SEQ // 3
QB = 384
SB = 128
CH = 16
RB = 192
BLOCKS = SEQ // QB
POFF = [sum((b + 1) * QB for b in range(n)) for n in range(BLOCKS + 1)]
PW = POFF[BLOCKS]
EXP_SCALE = HEAD_DIM ** (-0.5) * math.log2(math.e)
ANGLE_STEP = 32
epsilon = 1e-05
bf16 = jnp.bfloat16
f32 = jnp.float32
MESH = pl.DeviceIdType.MESH
VMEM_LIMIT = 63 << 20

WEIGHTS = ("project", "position", "mixing", "expand", "contract", "pooling", "upsample")
WEIGHT_SHAPE = {
    "project": (D, 3 * D),
    "position": (D, D),
    "mixing": (D, D),
    "expand": (D, FF),
    "contract": (FF, D),
    "pooling": (3 * D, D),
    "upsample": (D, 3 * D),
}
VECTORS = (
    "gain_one",
    "shift_one",
    "content",
    "position_bias",
    "mixing_bias",
    "gain_two",
    "shift_two",
    "hidden",
    "contract_bias",
    "pooling_bias",
    "upsample_bias",
)
VECTOR_SIZE = {n: D for n in VECTORS} | {"hidden": FF, "upsample_bias": 3 * D}
VECTOR_ROW = {n: i for i, n in enumerate(VECTORS)}
PACKED_VECTORS = ("hidden", "upsample_bias", "gain_one") + tuple(
    n for n in VECTORS if n not in ("hidden", "upsample_bias", "gain_one")
)


def nn(a, b):
    return lax.dot_general(a, b, (((1,), (0,)), ((), ())), preferred_element_type=f32)


def nt(a, b):
    return lax.dot_general(a, b, (((1,), (1,)), ((), ())), preferred_element_type=f32)


def tn(a, b):
    return lax.dot_general(a, b, (((0,), (0,)), ((), ())), preferred_element_type=f32)


def at_rows(step, rows):
    return pl.ds(pl.multiple_of(step * rows, rows), rows)


def eight_rows(values):
    rows, columns = values.shape
    return jnp.sum(values.reshape(rows // 8, 8, columns), axis=0)


def call(body, ins, outs, scratch, alias=None, **params):
    names = [*ins, *outs, *scratch]

    def kernel(*refs):
        body(SimpleNamespace(**dict(zip(names, refs))))

    results = pl.pallas_call(
        kernel,
        out_shape=[jax.ShapeDtypeStruct(s, t) for s, t, _ in outs.values()],
        in_specs=[pl.BlockSpec(memory_space=m) for _, m in ins.values()],
        out_specs=[pl.BlockSpec(memory_space=m) for _, _, m in outs.values()],
        scratch_shapes=list(scratch.values()),
        input_output_aliases=alias or {},
        compiler_params=pltpu.CompilerParams(vmem_limit_bytes=VMEM_LIMIT, **params),
    )(*[a for a, _ in ins.values()])
    return SimpleNamespace(**dict(zip(outs, results)))


VMEM = pltpu.VMEM
ANY = pl.ANY


BIT_AXIS = ("fsdp", "fsdp", "fsdp", "dp", "dp")
BIT_MASK = (4, 2, 1, 2, 1)
GATHER_ORDER = ((0, 1, 2, 3, 4), (0, 1, 3, 2, 4))
SCATTER_ORDER = ((4, 3, 2, 1, 0), (4, 2, 3, 1, 0))
CUBE = (2,) * 5


def my_bits():
    fs = lax.axis_index("fsdp")
    dp = lax.axis_index("dp")
    return (
        lax.rem(fs // 4, 2),
        lax.rem(fs // 2, 2),
        lax.rem(fs, 2),
        lax.rem(dp // 2, 2),
        lax.rem(dp, 2),
    )


def partner(bit):
    fs = lax.axis_index("fsdp")
    dp = lax.axis_index("dp")
    step = BIT_MASK[bit] * (1 - 2 * my_bits()[bit])
    if BIT_AXIS[bit] == "fsdp":
        return (dp, fs + step)
    return (dp + step, fs)


def partner_signal():
    sem = pltpu.get_barrier_semaphore()
    for bit in range(5):
        pl.semaphore_signal(sem, inc=1, device_id=partner(bit), device_id_type=MESH)


def partner_wait():
    pl.semaphore_wait(pltpu.get_barrier_semaphore(), 5)


def run_at(step, number, action):
    @pl.when(step == number)
    def _():
        action()


class Gather:
    def __init__(self, buf, pieces, send_sem, recv_sem):
        self.buf, self.pieces = buf, pieces
        self.send_sem, self.recv_sem = send_sem, recv_sem
        self.bits = my_bits()

    def copy(self, i, stage):
        row, rows, kind = self.pieces[i]
        order = GATHER_ORDER[kind]
        index = tuple(slice(None) if k in order[:stage] else self.bits[k] for k in range(5))
        ref = self.buf.at[index + (pl.ds(row, rows),)]
        return pltpu.make_async_remote_copy(
            src_ref=ref,
            dst_ref=ref,
            send_sem=self.send_sem.at[i * 5 + stage],
            recv_sem=self.recv_sem.at[i * 5 + stage],
            device_id=partner(order[stage]),
            device_id_type=MESH,
        )

    def advance(self, i, stage, first=0, last=5):
        if stage > first:
            self.copy(i, stage - 1).wait_recv()
        if stage < last:
            self.copy(i, stage).start()

    def drain(self, i, first=0, last=5):
        for stage in range(first, last):
            self.copy(i, stage).wait_send()


class Scatter:
    def __init__(self, own, land, out, pieces, send_sem, recv_sem, first=0):
        self.own, self.land, self.out, self.pieces = own, land, out, pieces
        self.send_sem, self.recv_sem, self.first = send_sem, recv_sem, first
        self.bits = my_bits()

    def index(self, order, stage, side):
        out = []
        for k in range(5):
            if k in order[:stage]:
                out.append(1 - self.bits[k] if side in ("land", "target") else self.bits[k])
            elif k == order[stage]:
                out.append(1 - self.bits[k] if side in ("send", "target") else self.bits[k])
            else:
                out.append(slice(None))
        return tuple(out)

    def copy(self, i, stage):
        row, rows, kind = self.pieces[i]
        order = SCATTER_ORDER[kind]
        part = (pl.ds(row, rows),)
        sem = self.first + i * 5 + stage
        return pltpu.make_async_remote_copy(
            src_ref=self.own.at[self.index(order, stage, "send") + part],
            dst_ref=self.land.at[self.index(order, stage, "target") + part],
            send_sem=self.send_sem.at[sem],
            recv_sem=self.recv_sem.at[sem],
            device_id=partner(order[stage]),
            device_id_type=MESH,
        )

    def add(self, i, stage):
        row, rows, kind = self.pieces[i]
        order = SCATTER_ORDER[kind]
        part = (pl.ds(row, rows), slice(None))
        mine = self.own.at[self.index(order, stage, "own")]
        came = self.land.at[self.index(order, stage, "land")]
        if stage == 4:
            self.out[pl.ds(row, rows), :] = mine[part].astype(f32) + came[part].astype(f32)
            return
        free = 4 - stage

        def body(j, carry):
            at = tuple(lax.rem(j // 2 ** (free - 1 - q), 2) for q in range(free)) + part
            mine[at] = mine[at] + came[at]
            return carry

        lax.fori_loop(0, 2**free, body, 0)

    def advance(self, i, stage, first=0, last=5):
        if stage > first:
            self.copy(i, stage - 1).wait()
            self.add(i, stage - 1)
        if stage < last:
            self.copy(i, stage).start()


def split_pieces(chunks):
    pieces = []
    for row, rows in chunks:
        half = (rows // 2 + 15) // 16 * 16
        pieces.append((row, half, 0))
        pieces.append((row + half, rows - half, 1))
    return pieces


class AxisScatter:
    def __init__(self, own, land_dp, land_fsdp, out, sems):
        self.own, self.land_dp, self.land_fsdp, self.out = own, land_dp, land_fsdp, out
        self.sems = sems
        self.fs, self.dp = lax.axis_index("fsdp"), lax.axis_index("dp")

    def bits(self, fs, dp):
        return (lax.rem(fs // 4, 2), lax.rem(fs // 2, 2), lax.rem(fs, 2)), (
            lax.rem(dp // 2, 2),
            lax.rem(dp, 2),
        )

    def dp_copy(self, step):
        other = lax.rem(self.dp + step, 4)
        _, (y, core) = self.bits(self.fs, other)
        return pltpu.make_async_remote_copy(
            src_ref=self.own.at[:, :, :, y, core],
            dst_ref=self.land_dp.at[step - 1],
            send_sem=self.sems.at[0, step],
            recv_sem=self.sems.at[1, step],
            device_id=(other, self.fs),
            device_id_type=MESH,
        )

    def fsdp_copy(self, step):
        other = lax.rem(self.fs + step, 8)
        (zh, zl, x), (y, core) = self.bits(other, self.dp)
        return pltpu.make_async_remote_copy(
            src_ref=self.own.at[zh, zl, x, y, core],
            dst_ref=self.land_fsdp.at[step - 1],
            send_sem=self.sems.at[2, step],
            recv_sem=self.sems.at[3, step],
            device_id=(self.dp, other),
            device_id_type=MESH,
        )

    def first(self):
        for step in range(1, 4):
            self.dp_copy(step).start()

    def second(self):
        for step in range(1, 4):
            self.dp_copy(step).wait()
        _, (y, core) = self.bits(self.fs, self.dp)
        mine = self.own.at[:, :, :, y, core]
        mine[...] = mine[...] + self.land_dp[0] + self.land_dp[1] + self.land_dp[2]
        for step in range(1, 8):
            self.fsdp_copy(step).start()

    def last(self):
        for step in range(1, 8):
            self.fsdp_copy(step).wait()
        (zh, zl, x), (y, core) = self.bits(self.fs, self.dp)
        total = self.own[zh, zl, x, y, core]
        for step in range(7):
            total = total + self.land_fsdp[step]
        self.out[...] = total


def axis_signal():
    fs, dp = lax.axis_index("fsdp"), lax.axis_index("dp")
    sem = pltpu.get_barrier_semaphore()
    for step in range(1, 4):
        to = (lax.rem(dp + step, 4), fs)
        pl.semaphore_signal(sem, inc=1, device_id=to, device_id_type=MESH)
    for step in range(1, 8):
        to = (dp, lax.rem(fs + step, 8))
        pl.semaphore_signal(sem, inc=1, device_id=to, device_id_type=MESH)


def axis_wait():
    pl.semaphore_wait(pltpu.get_barrier_semaphore(), 10)


class Plan:
    def __init__(self, dp, fsdp):
        self.shard = {n: (WEIGHT_SHAPE[n][0] // dp, WEIGHT_SHAPE[n][1] // fsdp) for n in WEIGHTS}
        self.row, at = {}, 0
        for name in WEIGHTS:
            self.row[name] = at
            at += self.shard[name][0] * self.shard[name][1] // 128
        self.rows = at

    def span(self, first, last, shift):
        r, c = self.shard[last]
        end = self.row[last] + r * c // 128
        return (self.row[first] + shift, end - self.row[first])

    def full_shape(self, name):
        return (2, 2, 2, self.shard[name][1], WEIGHT_SHAPE[name][0])

    def held_shape(self, name):
        r, c = self.shard[name]
        return (c, r) if c % 128 else (r, c)

    def blocks(self, name, shift):
        r, c = self.shard[name]
        return [
            (y, core, shift + self.row[name] + q * c, (y * 2 + core) * r + q * 128)
            for y in range(2)
            for core in range(2)
            for q in range(r // 128)
        ]


def put_blocks(plan, name, own, shift, values_of):
    c = plan.shard[name][1]
    for y, core, at, column in plan.blocks(name, shift):
        values = values_of(slice(column, column + 128)).astype(bf16)
        own[:, :, :, y, core, at : at + c, :] = values.reshape(2, 2, 2, c, 128)


def put_shard(plan, name, flat, shift, target):
    r, c = plan.shard[name]
    for q in range(r // 128):
        at = shift + plan.row[name] + q * c
        if c % 128:
            target[:, q * 128 : (q + 1) * 128] = flat[at : at + c, :]
        else:
            target[q * 128 : (q + 1) * 128, :] = flat[at : at + c, :].T


def load_weight(plan, name, buf, target, sem, shift):
    c = plan.shard[name][1]
    for y, core, row, column in plan.blocks(name, shift):
        pltpu.make_async_copy(
            buf.at[:, :, :, y, core, pl.ds(row, c), :],
            target.at[:, :, :, :, pl.ds(column, 128)],
            sem,
        ).start()


def wait_whole(target, sem):
    pltpu.make_async_copy(target, target, sem).wait()


def full(ref):
    values = ref[...]
    return values.reshape(-1, values.shape[-1])


def vector_places():
    places, at = {}, 0
    for name in PACKED_VECTORS:
        size = VECTOR_SIZE[name] // 32
        places[name] = (at // 128, at % 128, size)
        at += size
    return places


def block_owner(columns, size):
    row = lax.broadcasted_iota(jnp.int32, (32, columns), 0)
    lane = lax.broadcasted_iota(jnp.int32, (32, columns), 1)
    return lane // size == lax.rem(row, 4) * 8 + row // 4


def unpack_vectors(blocks, target):
    flat = blocks[...].reshape(32 * 16, 128)
    for name, (line, offset, size) in vector_places().items():
        columns = VECTOR_SIZE[name]
        row = lax.broadcasted_iota(jnp.int32, (32, 512), 0)
        lane = lax.broadcasted_iota(jnp.int32, (32, 512), 1)
        pick = (lane == row * 16 + line).astype(bf16)
        own = nn(pick, flat).astype(bf16)
        source = lax.broadcasted_iota(jnp.int32, (128, columns), 0)
        lane = lax.broadcasted_iota(jnp.int32, (128, columns), 1)
        spread = (source - offset == lax.rem(lane, size)).astype(bf16)
        spread_own = jnp.where(block_owner(columns, size), nn(own, spread), 0.0)
        r = VECTOR_ROW[name]
        target[r : r + 1, :columns] = jnp.sum(spread_own, axis=0, keepdims=True)


def pack_vectors(source, target):
    lines = [jnp.zeros((32, 128), f32), jnp.zeros((32, 128), f32)]
    for name, (line, offset, size) in vector_places().items():
        columns = VECTOR_SIZE[name]
        r = VECTOR_ROW[name]
        values = jnp.broadcast_to(source[r : r + 1, :columns], (32, columns))
        values = jnp.where(block_owner(columns, size), values, 0.0)
        lane = lax.broadcasted_iota(jnp.int32, (columns, 128), 0)
        goal = lax.broadcasted_iota(jnp.int32, (columns, 128), 1)
        gather = (goal - offset == lax.rem(lane, size)).astype(bf16)
        for _ in range(3):
            term = values.astype(bf16)
            lines[line] += nn(term, gather)
            values = values - term.astype(f32)
    both = jnp.concatenate([lines[0][:, None, :], lines[1][:, None, :]], axis=1)
    both = jnp.concatenate([both, jnp.zeros((32, 6, 128), f32)], axis=1)
    target[...] = both.reshape(CUBE + (8, 128))


def coarse_angles():
    ratios = jnp.arange(0, D, 2).astype(f32) / D
    inverse = 1.0 / 10000.0**ratios
    steps = SEQ // ANGLE_STEP
    places = jnp.concatenate(
        [jnp.arange(steps) * ANGLE_STEP, jnp.zeros((-steps % 8,), jnp.int32), jnp.arange(ANGLE_STEP)]
    ).astype(f32)
    angles = places[:, None] * inverse[None, :]
    return jnp.concatenate([jnp.sin(angles), jnp.cos(angles)], axis=1)


def expand_angles(coarse, angles, table_of):
    steps = SEQ // ANGLE_STEP
    start = steps + -steps % 8

    def body(q, carry):
        high_sin, high_cos = coarse[pl.ds(q, 1), :HALF], coarse[pl.ds(q, 1), HALF:]
        low_sin, low_cos = coarse[start:, :HALF], coarse[start:, HALF:]
        sine = high_sin * low_cos + high_cos * low_sin
        cosine = high_cos * low_cos - high_sin * low_sin
        rows = at_rows(q, ANGLE_STEP)
        angles[rows, :HALF] = sine
        angles[rows, HALF:] = cosine
        table_of(rows, sine.astype(bf16), cosine.astype(bf16))
        return carry

    lax.fori_loop(0, steps, body, 0)


def head_lanes(rows, head):
    return (lax.broadcasted_iota(jnp.int32, (rows, 128), 1) // HEAD_DIM) == head


def keep_head(values, head):
    return jnp.where(head_lanes(values.shape[0], head), values, 0).astype(bf16)


def rotate(pair, sines, cosines):
    low, high = pair[:, :HALF], pair[:, HALF:]
    return high * sines - low * cosines, low * sines + high * cosines


def norm_parts(values):
    row_mean = jnp.mean(values, axis=-1, keepdims=True)
    centred = values - row_mean
    variance = jnp.mean(centred * centred, axis=-1, keepdims=True)
    inv_std = lax.rsqrt(variance + epsilon)
    return centred * inv_std, inv_std


def norm_backward(normal, inv_std, gain, upstream):
    scaled = upstream * gain
    scaled_mean = jnp.mean(scaled, axis=-1, keepdims=True)
    cross_mean = jnp.mean(scaled * normal, axis=-1, keepdims=True)
    return inv_std * (scaled - scaled_mean - normal * cross_mean)


def vec(ref, name):
    r = VECTOR_ROW[name]
    return ref[r : r + 1, : VECTOR_SIZE[name]]


VECTOR_ROWS = 16


FRONT_ROWS = ("query_u", "query_v", "key", "value", "mixed")
CHUNK_LAST = (5, 5, 5, 5, 2, 2)
BEFORE = ((0, 1), (1, 0), (0, 2), (1, 1), (2, 0), (0, 3), (1, 2), (2, 1), (0, 4), (1, 3), (3, 0), (0, 5), (1, 4))
AFTER = ((1, 5), (2, 2), (3, 1))
DURING = {
    1: ((2, 3), (4, 0)),
    2: ((3, 2),),
    4: ((4, 1), (5, 0)),
    6: ((2, 4),),
    8: ((2, 5), (3, 3), (5, 1)),
    12: ((4, 2), (5, 2)),
    13: ((3, 4),),
    16: ((3, 5),),
}


def front(plan, linked, ins):
    outs = {
        "vectors": ((16, FF), f32, VMEM),
    }
    outs |= {n + "_out": ((SEQ, D), bf16, ANY) for n in FRONT_ROWS}
    outs |= {
        "probs_out": ((HEADS, QB, PW), bf16, ANY),
    }
    scratch = {
        "normal": VMEM((SEQ, D), f32),
        "angles": VMEM((SEQ, D), f32),
        "key_table": VMEM((SEQ, 128 + D), bf16),
        "score": VMEM((2, QB, SEQ), f32),
        "turned": VMEM((2, QB, 128 + D), bf16),
        "probs": VMEM((2, QB, PW), bf16),
        "probs_sem": pltpu.SemaphoreType.DMA((2,)),
        "out_sem": pltpu.SemaphoreType.DMA((len(FRONT_ROWS),)),
    }
    scratch |= {n: VMEM((SEQ, D), bf16) for n in FRONT_ROWS}
    params = {}
    if linked:
        rows = VECTOR_ROWS + plan.rows
        chunks = [
            (0, VECTOR_ROWS + plan.span("project", "project", 0)[1]),
            plan.span("position", "position", VECTOR_ROWS),
            plan.span("mixing", "expand", VECTOR_ROWS),
            plan.span("contract", "contract", VECTOR_ROWS),
            plan.span("pooling", "pooling", VECTOR_ROWS),
            plan.span("upsample", "upsample", VECTOR_ROWS),
        ]
        pieces = split_pieces(chunks)
        outs["blocks"] = (CUBE + (rows, 128), bf16, ANY)
        scratch |= {
            "mine": VMEM((rows, 128), bf16),
            "project": VMEM(plan.full_shape("project"), bf16),
            "position": VMEM(plan.full_shape("position"), bf16),
            "vector_blocks": VMEM(CUBE + (VECTOR_ROWS, 128), bf16),
            "send_sem": pltpu.SemaphoreType.DMA((5 * len(pieces),)),
            "recv_sem": pltpu.SemaphoreType.DMA((5 * len(pieces),)),
            "load_sem": pltpu.SemaphoreType.DMA((4,)),
        }
        params = dict(collective_id=0, has_side_effects=True)

    def body(ref):
        if linked:
            partner_signal()
            gather = Gather(ref.blocks, pieces, ref.send_sem, ref.recv_sem)

            def run(events):
                for chunk, stage in events:
                    for piece in (2 * chunk, 2 * chunk + 1):
                        gather.advance(piece, stage, last=CHUNK_LAST[chunk])

            ref.mine[:VECTOR_ROWS, :] = ref.packed[...]
            for name in WEIGHTS:
                r, c = plan.shard[name]
                shard = getattr(ref, name + "_shard")
                for q in range(r // 128):
                    at = VECTOR_ROWS + plan.row[name] + q * c
                    if c % 128:
                        ref.mine[at : at + c, :] = shard[:, q * 128 : (q + 1) * 128]
                    else:
                        ref.mine[at : at + c, :] = shard[q * 128 : (q + 1) * 128, :].T
            own = pltpu.make_async_copy(
                ref.mine, ref.blocks.at[gather.bits], ref.load_sem.at[0]
            )
            own.start()
            partner_wait()
            own.wait()
            run([(0, 0)])

        def first_norm(i, carry):
            rows = at_rows(i, RB)
            ref.normal[rows, :] = norm_parts(ref.tokens[rows, :].astype(f32))[0]
            return carry

        lax.fori_loop(0, SEQ // RB, first_norm, 0)

        def table_of(rows, sine, cosine):
            ref.key_table[rows, 128 : 128 + HALF] = sine
            ref.key_table[rows, 128 + HALF :] = cosine

        expand_angles(ref.coarse, ref.angles, table_of)

        if linked:
            run(BEFORE)
            load_weight(plan, "project", ref.blocks, ref.project, ref.load_sem.at[1], VECTOR_ROWS)
            small = pltpu.make_async_copy(
                ref.blocks.at[:, :, :, :, :, pl.ds(0, VECTOR_ROWS), :],
                ref.vector_blocks,
                ref.load_sem.at[2],
            )
            small.start()
            small.wait()
            unpack_vectors(ref.vector_blocks, ref.vectors)
            wait_whole(ref.project, ref.load_sem.at[1])
        else:
            ref.vectors[...] = ref.given_vectors[...]

        for b in range(BLOCKS):
            rows = slice(b * QB, (b + 1) * QB)
            normed = ref.normal[rows, :] * vec(ref.vectors, "gain_one") + vec(
                ref.vectors, "shift_one"
            )
            joined = nt(normed.astype(bf16), full(ref.project))
            ref.query_u[rows, :] = (joined[:, :D] + vec(ref.vectors, "content")).astype(bf16)
            ref.query_v[rows, :] = (joined[:, :D] + vec(ref.vectors, "position_bias")).astype(bf16)
            ref.key[rows, :] = joined[:, D : 2 * D].astype(bf16)
            ref.value[rows, :] = joined[:, 2 * D :].astype(bf16)

        def row_copy(i):
            name = FRONT_ROWS[i]
            return pltpu.make_async_copy(
                getattr(ref, name), getattr(ref, name + "_out"), ref.out_sem.at[i]
            )

        for i in range(4):
            row_copy(i).start()

        if linked:
            run(AFTER)
            load_weight(plan, "position", ref.blocks, ref.position, ref.load_sem.at[3], VECTOR_ROWS)
            wait_whole(ref.position, ref.load_sem.at[3])
            position = ref.position.reshape(D, D)
        else:
            position = ref.position

        def out_copy(head, slot):
            return pltpu.make_async_copy(
                ref.probs.at[slot], ref.probs_out.at[head], ref.probs_sem.at[slot]
            )

        def scores(lanes, b, e):
            row, width = b * QB, (b + 1) * QB
            rows = slice(row, row + QB)
            spread = nn(keep_head(ref.query_v[rows, lanes], e), position[lanes, :])
            low, high = rotate(spread, ref.angles[rows, :HALF], ref.angles[rows, HALF:])
            ref.turned[e, :, :128] = keep_head(ref.query_u[rows, lanes], e)
            ref.turned[e, :, 128 : 128 + HALF] = low.astype(bf16)
            ref.turned[e, :, 128 + HALF :] = high.astype(bf16)
            ref.score[e, :, :width] = nt(ref.turned[e], ref.key_table[:width, :])

        def softmax(b, e):
            row, width = b * QB, (b + 1) * QB
            for sub in range(QB // SB):
                used = row + (sub + 1) * SB
                for g in range(SB // CH):
                    at = slice(sub * SB + g * CH, sub * SB + (g + 1) * CH)
                    tiles = [
                        ref.score[e, at, i * 128 : (i + 1) * 128] for i in range(used // 128)
                    ]
                    lane = lax.broadcasted_iota(jnp.int32, (CH, SB), 1)
                    place = lax.broadcasted_iota(jnp.int32, (CH, SB), 0) + g * CH
                    tiles[-1] = jnp.where(lane <= place, tiles[-1], -1e30)
                    top = tiles[0]
                    for tile in tiles[1:]:
                        top = jnp.maximum(top, tile)
                    top = jnp.max(top, axis=1, keepdims=True)
                    tiles = [jnp.exp2((tile - top) * EXP_SCALE) for tile in tiles]
                    total = tiles[0]
                    for tile in tiles[1:]:
                        total = total + tile
                    scale = 1.0 / jnp.sum(total, axis=1, keepdims=True)
                    for i, tile in enumerate(tiles):
                        lanes = slice(POFF[b] + i * 128, POFF[b] + (i + 1) * 128)
                        ref.probs[e, at, lanes] = (tile * scale).astype(bf16)
                if used < width:
                    ref.probs[e, sub * SB : (sub + 1) * SB, POFF[b] + used : POFF[b] + width] = (
                        jnp.zeros((SB, width - used), bf16)
                    )

        def pair(hp, carry):
            lanes = pl.ds(pl.multiple_of(hp * 128, 128), 128)
            ref.key_table[:, :128] = ref.key[:, lanes]

            @pl.when(hp > 0)
            def _():
                for e in range(2):
                    out_copy(0, e).wait()

            for b in range(BLOCKS):
                for e in range(2):
                    scores(lanes, b, e)
                    softmax(b, e)
                    for when, events in DURING.items():
                        if linked and when % 6 == b * 2 + e:
                            run_at(hp, when // 6, lambda events=events: run(events))
                row, width = b * QB, (b + 1) * QB
                values = ref.value[:width, lanes]
                span = slice(POFF[b], POFF[b] + width)
                ref.mixed[row : row + QB, lanes] = jnp.where(
                    head_lanes(QB, 0),
                    nn(ref.probs[0, :, span], values),
                    nn(ref.probs[1, :, span], values),
                ).astype(bf16)
            for e in range(2):
                out_copy(hp * 2 + e, e).start()
            return carry

        lax.fori_loop(0, HEADS // 2, pair, 0)
        row_copy(4).start()
        for e in range(2):
            out_copy(0, e).wait()
        if linked:
            for i in range(len(pieces)):
                gather.drain(i, last=CHUNK_LAST[i // 2])
        for i in range(5):
            row_copy(i).wait()

    return call(body, ins, outs, scratch, **params)


MIDDLE = ("mixing", "expand", "contract", "pooling", "upsample")


def middle(plan, linked, ins):
    def weight_shape(name):
        return plan.full_shape(name) if linked else WEIGHT_SHAPE[name][::-1]

    outs = {
        "output_out": ((SEQ, D), bf16, ANY),
        "first_grad_out": ((SEQ, D), f32, ANY),
        "mixed_grad_out": ((SEQ, D), bf16, ANY),
        "sums": ((16, FF), f32, VMEM),
    }
    summed = ("pooling", "upsample") if linked else ()
    kept = [n for n in MIDDLE if n not in summed]
    outs |= {n + "_grad_out": (weight_shape(n), bf16, ANY) for n in kept}
    params = {}
    scratch = {n: VMEM(weight_shape(n), bf16) for n in MIDDLE}
    scratch |= {
        "normal": VMEM((SEQ, D), f32),
        "inverse": VMEM((SEQ, 128), f32),
        "second_low": VMEM((SEQ, D), bf16),
        "activated": VMEM((SEQ, FF), bf16),
        "slope": VMEM((SEQ, FF), bf16),
        "tiles": VMEM((D // 128, SEQ + 16, 128), f32),
        "grouped": VMEM((THIRD, 3 * D), bf16),
        "up_rows": VMEM((THIRD, 3 * D), bf16),
        "branch_grad": VMEM((SEQ, D), bf16),
        "attended_grad": VMEM((SEQ, D), bf16),
        "parts": VMEM((5, 8, FF), f32),
        "output": VMEM((SEQ, D), bf16),
        "first_grad": VMEM((SEQ, D), f32),
        "mixed_grad": VMEM((SEQ, D), bf16),
        "sem": pltpu.SemaphoreType.DMA((len(MIDDLE),)),
        "out_sem": pltpu.SemaphoreType.DMA((3 + len(kept),)),
    }
    scratch |= {n + "_grad": VMEM(weight_shape(n), bf16) for n in kept}
    if linked:
        gather_pieces = split_pieces(
            [plan.span(n, n, VECTOR_ROWS) for n in ("pooling", "upsample")]
        )
        base = -plan.row["pooling"]
        pieces = split_pieces([plan.span("pooling", "upsample", base)])
        rows = plan.span("pooling", "upsample", base)[1]
        outs["blocks_out"] = (CUBE + (VECTOR_ROWS + plan.rows, 128), bf16, ANY)
        outs["partial"] = ((2, 2, rows, 128), bf16, ANY)
        scratch |= {
            "own": VMEM(CUBE + (rows, 128), bf16),
            "land": VMEM(CUBE + (rows, 128), bf16),
            "partial_sem": pltpu.SemaphoreType.DMA,
            "gather_send": pltpu.SemaphoreType.DMA((20,)),
            "gather_recv": pltpu.SemaphoreType.DMA((20,)),
            "send_sem": pltpu.SemaphoreType.DMA((10,)),
            "recv_sem": pltpu.SemaphoreType.DMA((10,)),
        }
        params = dict(
            collective_id=1,
            has_side_effects=True,
            alias={list(ins).index("blocks"): list(outs).index("blocks_out")},
        )

    def body(ref):
        def fetch(name):
            i = MIDDLE.index(name)
            if linked:
                load_weight(
                    plan, name, ref.blocks_out, getattr(ref, name), ref.sem.at[i], VECTOR_ROWS
                )
            else:
                pltpu.make_async_copy(
                    getattr(ref, name + "_full"), getattr(ref, name), ref.sem.at[i]
                ).start()

        gather_stage = scatter_stage = None
        if linked:
            gather = Gather(ref.blocks_out, gather_pieces, ref.gather_send, ref.gather_recv)
            scatter = Scatter(ref.own, ref.land, None, pieces, ref.send_sem, ref.recv_sem)
            partner_signal()

            def gather_stage(stage):
                for i in range(4):
                    gather.advance(i, stage, first=2)

            def scatter_stage(stage):
                for i in range(2):
                    scatter.advance(i, stage, last=3)

        for name in ("mixing", "expand", "contract"):
            fetch(name)
        if linked:
            partner_wait()
            gather_stage(2)
        else:
            fetch("pooling")
            fetch("upsample")

        outgoing = ["output", "first_grad", "mixed_grad"] + [n + "_grad" for n in kept]

        def send_out(name):
            return pltpu.make_async_copy(
                getattr(ref, name),
                getattr(ref, name + "_out"),
                ref.out_sem.at[outgoing.index(name)],
            )

        def at_step(i, number, action, *args):
            if linked:
                run_at(i, number, lambda: action(*args))

        def ready(name):
            wait_whole(getattr(ref, name), ref.sem.at[MIDDLE.index(name)])

        def get(name):
            return full(getattr(ref, name))

        def put(name, values):
            if name in summed:
                put_blocks(plan, name, ref.own, base, lambda columns: values[:, columns])
                return
            target = getattr(ref, name + "_grad")
            target[...] = values.astype(bf16).reshape(target.shape)
            send_out(name + "_grad").start()

        def third(start, k):
            return jnp.concatenate(
                [ref.tiles[t, pl.ds(start + k, THIRD, stride=3), :] for t in range(D // 128)],
                axis=1,
            )

        def put_third(start, k, values):
            for t in range(D // 128):
                ref.tiles[t, pl.ds(start + k, THIRD, stride=3), :] = values[
                    :, t * 128 : (t + 1) * 128
                ]

        def rows_of(rows):
            return jnp.concatenate([ref.tiles[t, rows, :] for t in range(D // 128)], axis=1)

        def put_rows(rows, values):
            for t in range(D // 128):
                ref.tiles[t, rows, :] = values[:, t * 128 : (t + 1) * 128]

        def shifted_rows(i):
            return pl.ds(pl.multiple_of(i * RB + 8, 8), RB)

        ref.parts[...] = jnp.zeros_like(ref.parts)
        ref.sums[...] = jnp.zeros_like(ref.sums)

        def add_part(slot, values):
            columns = values.shape[1]
            ref.parts[slot, :, :columns] += eight_rows(values)

        def put_sum(name, values):
            r = VECTOR_ROW[name]
            ref.sums[r : r + 1, : values.shape[1]] = values

        def put_part(name, slot):
            columns = VECTOR_SIZE[name]
            put_sum(name, jnp.sum(ref.parts[slot, :, :columns], axis=0, keepdims=True))

        for name in ("mixing", "expand", "contract"):
            ready(name)

        def forward(i, carry):
            rows = at_rows(i, RB)
            attended = nt(ref.mixed[rows, :], get("mixing")) + vec(ref.vectors, "mixing_bias")
            first = ref.tokens[rows, :].astype(f32) + attended
            normal, inverse = norm_parts(first)
            ref.normal[rows, :] = normal
            ref.inverse[rows, :] = jnp.broadcast_to(inverse, (RB, 128))
            low = (
                normal * vec(ref.vectors, "gain_two") + vec(ref.vectors, "shift_two")
            ).astype(bf16)
            ref.second_low[rows, :] = low
            inner = nt(low, get("expand")) + vec(ref.vectors, "hidden")
            phi = 0.5 * (1.0 + lax.erf(inner * 2.0 ** (-0.5)))
            act = (inner * phi).astype(bf16)
            ref.activated[rows, :] = act
            bell = jnp.exp(-0.5 * inner * inner) * (2.0 * math.pi) ** (-0.5)
            ref.slope[rows, :] = (phi + inner * bell).astype(bf16)
            block = first + nt(act, get("contract")) + vec(ref.vectors, "contract_bias")
            put_rows(shifted_rows(i), block)
            at_step(i, 1, gather_stage, 3)
            at_step(i, 4, gather_stage, 4)
            return carry

        lax.fori_loop(0, SEQ // RB, forward, 0)

        put_rows(slice(0, 8), jnp.zeros((8, D), f32))
        for k in range(3):
            ref.grouped[:, k * D : (k + 1) * D] = third(6, k).astype(bf16)
        if linked:
            gather_stage(5)
            fetch("pooling")
            fetch("upsample")
        ready("pooling")
        pooled = (
            nt(ref.grouped[...], get("pooling")) + vec(ref.vectors, "pooling_bias")
        ).astype(bf16)
        ready("upsample")
        for k in range(3):
            columns = slice(k * D, (k + 1) * D)
            upward = nt(pooled, get("upsample")[columns, :]) + vec(ref.vectors, "upsample_bias")[
                :, columns
            ]
            put_third(8, k, third(8, k) + upward)

        def write_output(i, carry):
            ref.output[at_rows(i, RB), :] = rows_of(shifted_rows(i)).astype(bf16)
            put_rows(shifted_rows(i), ref.cotangent[at_rows(i, RB), :].astype(f32))
            return carry

        lax.fori_loop(0, SEQ // RB, write_output, 0)

        send_out("output").start()

        for k in range(3):
            ref.up_rows[:, k * D : (k + 1) * D] = third(8, k).astype(bf16)
        up_rows = ref.up_rows[...]
        put_sum("upsample_bias", jnp.sum(up_rows.astype(f32), axis=0, keepdims=True))
        put("upsample", tn(up_rows, pooled))
        pooled_grad = nn(up_rows, get("upsample")).astype(bf16)
        put_sum("pooling_bias", jnp.sum(pooled_grad.astype(f32), axis=0, keepdims=True))
        put("pooling", tn(pooled_grad, ref.grouped[...]))
        for k in range(3):
            put_third(
                6, k, nn(pooled_grad, get("pooling")[:, k * D : (k + 1) * D])
            )
        put_rows(slice(SEQ + 6, SEQ + 8), jnp.zeros((2, D), f32))
        if linked:
            scatter_stage(0)

        def backward(i, carry):
            rows = at_rows(i, RB)
            block_grad = ref.cotangent[rows, :].astype(f32) + rows_of(shifted_rows(i))
            branch_grad = block_grad.astype(bf16)
            ref.branch_grad[rows, :] = branch_grad
            add_part(0, branch_grad.astype(f32))
            inner_grad = (nn(branch_grad, get("contract")) * ref.slope[rows, :].astype(f32)).astype(
                bf16
            )
            ref.slope[rows, :] = inner_grad
            add_part(1, inner_grad.astype(f32))
            second_grad = nn(inner_grad, get("expand"))
            normal = ref.normal[rows, :]
            add_part(2, second_grad * normal)
            add_part(3, second_grad)
            first_grad = block_grad + norm_backward(
                normal, ref.inverse[rows, :1], vec(ref.vectors, "gain_two"), second_grad
            )
            ref.first_grad[rows, :] = first_grad
            attended_grad = first_grad.astype(bf16)
            ref.attended_grad[rows, :] = attended_grad
            add_part(4, attended_grad.astype(f32))
            ref.mixed_grad[rows, :] = nn(attended_grad, get("mixing")).astype(bf16)
            at_step(i, 1, scatter_stage, 1)
            return carry

        lax.fori_loop(0, SEQ // RB, backward, 0)
        send_out("first_grad").start()
        send_out("mixed_grad").start()
        put_part("contract_bias", 0)
        put_part("hidden", 1)
        put_part("gain_two", 2)
        put_part("shift_two", 3)
        put_part("mixing_bias", 4)
        put("contract", tn(ref.branch_grad[...], ref.activated[...]))
        if linked:
            scatter_stage(2)
        put("expand", tn(ref.slope[...], ref.second_low[...]))
        put("mixing", tn(ref.attended_grad[...], ref.mixed[...]))
        if linked:
            scatter_stage(3)
            _, _, x, y, core = scatter.bits
            partial = pltpu.make_async_copy(
                ref.own.at[:, :, x, y, core], ref.partial, ref.partial_sem
            )
            partial.start()
            partial.wait()
            for i in range(4):
                gather.drain(i, first=2)
        for name in outgoing:
            send_out(name).wait()

    return call(body, ins, outs, scratch, **params)


BACK_FIRST = (0, 0, 0, 3, 0)
BACK_DURING = {
    1: ((0, 1),),
    3: ((3, 4),),
    4: ((1, 1),),
    6: ((0, 2), (2, 1), (3, 5)),
    9: ((0, 3), (1, 2)),
    11: ((2, 2),),
    12: ((0, 4), (1, 3)),
    14: ((2, 3),),
    15: ((1, 4),),
    16: ((0, 5),),
    18: ((2, 4),),
    19: ((1, 5),),
    21: ((2, 5),),
}


def back(plan, linked, ins):
    outs = {"token_grad": ((SEQ, D), f32, VMEM)}
    late_rows = ("tokens", "mixed_grad", "mixed", "value", "key", "query_u", "query_v", "first_grad")
    scratch = {
        "angles": VMEM((SEQ, D), f32),
        "key_table": VMEM((SEQ, 128 + D), bf16),
        "prob_grad": VMEM((2, QB, SEQ), f32),
        "total_grad": VMEM((2, QB, SEQ), bf16),
        "probs": VMEM((4, QB, PW), bf16),
        "key_acc": VMEM((128, SEQ), f32),
        "value_acc": VMEM((128, SEQ), f32),
        "joined_grad": VMEM((SEQ, 3 * D), bf16),
        "normed_low": VMEM((SEQ, D), bf16),
        "position_grad": VMEM((D, D), f32),
        "parts": VMEM((2, 8, D), f32),
        "all_sums": VMEM((16, FF), f32),
        "probs_sem": pltpu.SemaphoreType.DMA((4,)),
        "load_sem": pltpu.SemaphoreType.DMA((2,)),
        "row_sem": pltpu.SemaphoreType.DMA((len(late_rows),)),
    }
    scratch |= {n: VMEM((SEQ, D), f32 if n == "first_grad" else bf16) for n in late_rows}
    params = {}
    project_shape = plan.full_shape("project") if linked else (3 * D, D)
    position_shape = plan.full_shape("position") if linked else (D, D)
    scratch |= {"project": VMEM(project_shape, bf16), "position": VMEM(position_shape, bf16)}
    if linked:
        early_names = ("contract", "expand", "mixing")
        early = [plan.span(n, n, 0) for n in early_names]
        late = [plan.span("pooling", "upsample", 0), plan.span("project", "position", 0)]
        pieces = split_pieces(early + late)
        count = 5 * len(pieces)
        own_rows = plan.rows
        for n in WEIGHTS:
            outs[n + "_out"] = (plan.held_shape(n), f32, VMEM)
        outs["vector_out"] = ((8, 128), f32, VMEM)
        scratch |= {
            "own": VMEM(CUBE + (own_rows, 128), bf16),
            "land": VMEM(CUBE + (own_rows, 128), bf16),
            "flat": VMEM((own_rows, 128), f32),
            "vector_own": VMEM(CUBE + (8, 128), f32),
            "land_dp": VMEM((3, 2, 2, 2, 8, 128), f32),
            "land_fsdp": VMEM((7, 8, 128), f32),
            "vector_sem": pltpu.SemaphoreType.DMA((4, 8)),
            "send_sem": pltpu.SemaphoreType.DMA((count,)),
            "recv_sem": pltpu.SemaphoreType.DMA((count,)),
            "own_sem": pltpu.SemaphoreType.DMA((4,)),
        }
        params = dict(collective_id=2, has_side_effects=True)
    else:
        outs["project_grad"] = ((3 * D, D), bf16, VMEM)
        outs["position_grad_out"] = ((D, D), bf16, VMEM)
        outs["sums_out"] = ((16, FF), f32, VMEM)

    def body(ref):
        def row_copy(name):
            return pltpu.make_async_copy(
                getattr(ref, name + "_in"), getattr(ref, name), ref.row_sem.at[late_rows.index(name)]
            )

        for name in late_rows[:7]:
            row_copy(name).start()
        if linked:
            load_weight(plan, "project", ref.blocks, ref.project, ref.load_sem.at[0], VECTOR_ROWS)
            load_weight(plan, "position", ref.blocks, ref.position, ref.load_sem.at[1], VECTOR_ROWS)
            matrix = Scatter(ref.own, ref.land, ref.flat, pieces, ref.send_sem, ref.recv_sem)
            vector = AxisScatter(
                ref.vector_own, ref.land_dp, ref.land_fsdp, ref.vector_out, ref.vector_sem
            )
            axis_signal()

            def run(events):
                for chunk, stage in events:
                    for piece in (2 * chunk, 2 * chunk + 1):
                        matrix.advance(piece, stage, first=BACK_FIRST[chunk])

            for i, name in enumerate(early_names):
                c = plan.shard[name][1]
                for y, core, row, column in plan.blocks(name, 0):
                    pltpu.make_async_copy(
                        getattr(ref, name + "_grad").at[:, :, :, :, pl.ds(column, 128)],
                        ref.own.at[:, :, :, y, core, pl.ds(row, c), :],
                        ref.own_sem.at[i],
                    ).start()
            _, _, x, y, core = matrix.bits
            row, rows = late[0]
            partial = pltpu.make_async_copy(
                ref.partial, ref.own.at[:, :, x, y, core, pl.ds(row, rows), :], ref.own_sem.at[3]
            )
            partial.start()
        else:
            for i, name in enumerate(("project", "position")):
                pltpu.make_async_copy(
                    getattr(ref, name + "_full"), getattr(ref, name), ref.load_sem.at[i]
                ).start()

        def in_copy(head, slot):
            return pltpu.make_async_copy(
                ref.probs_in.at[head], ref.probs.at[slot], ref.probs_sem.at[slot]
            )

        for e in range(2):
            in_copy(e, e).start()

        def table_of(rows, sine, cosine):
            ref.key_table[rows, 128 : 128 + HALF] = sine
            ref.key_table[rows, 128 + HALF :] = cosine

        expand_angles(ref.coarse, ref.angles, table_of)

        def norm_rows(rows):
            return norm_parts(ref.tokens[rows, :].astype(f32))

        def low_rows(i, carry):
            rows = at_rows(i, RB)
            normal, _ = norm_rows(rows)
            ref.normed_low[rows, :] = (
                normal * vec(ref.vectors, "gain_one") + vec(ref.vectors, "shift_one")
            ).astype(bf16)
            return carry

        row_copy("tokens").wait()
        lax.fori_loop(0, SEQ // RB, low_rows, 0)
        ref.all_sums[...] = ref.sums[...]
        ref.parts[...] = jnp.zeros_like(ref.parts)
        if linked:
            axis_wait()
            partial.wait()
            run([(3, 3)])
            for i, name in enumerate(early_names):
                row, rows = plan.span(name, name, 0)
                whole = ref.own.at[:, :, :, :, :, pl.ds(row, rows), :]
                wait_whole(whole, ref.own_sem.at[i])
                run([(i, 0)])
        wait_whole(ref.project, ref.load_sem.at[0])
        wait_whole(ref.position, ref.load_sem.at[1])
        position = ref.position.reshape(D, D)
        for name in late_rows[1:7]:
            row_copy(name).wait()
        row_copy("first_grad").start()

        def pair(hp, carry):
            start = pl.multiple_of(hp * 128, 128)
            lanes = pl.ds(start, 128)
            base = lax.rem(hp, 2) * 2
            for e in range(2):
                in_copy(0, base + e).wait()

            @pl.when(hp < HEADS // 2 - 1)
            def _():
                for e in range(2):
                    in_copy(hp * 2 + 2 + e, 2 - base + e).start()

            ref.key_table[:, :128] = ref.key[:, lanes]
            content_sum = jnp.zeros((1, 128), f32)
            position_sum = jnp.zeros((1, 128), f32)
            for b in range(BLOCKS):
                row, width = b * QB, (b + 1) * QB
                rows = slice(row, row + QB)
                span = slice(POFF[b], POFF[b] + width)
                by_content, by_position = [], None
                for e in range(2):
                    upstream = keep_head(ref.mixed_grad[rows, lanes], e)
                    row_dot = jnp.sum(
                        upstream.astype(f32) * ref.mixed[rows, lanes].astype(f32),
                        axis=1,
                        keepdims=True,
                    )
                    ref.prob_grad[e, :, :width] = nt(upstream, ref.value[:width, lanes]) - row_dot
                    for sub in range(QB // SB):
                        used = row + (sub + 1) * SB
                        for g in range(SB // CH):
                            at = slice(sub * SB + g * CH, sub * SB + (g + 1) * CH)
                            p = ref.probs[base + e, at, POFF[b] : POFF[b] + used].astype(f32)
                            ref.total_grad[e, at, :used] = (
                                p * ref.prob_grad[e, at, :used] * HEAD_DIM ** (-0.5)
                            ).astype(bf16)
                        if used < width:
                            ref.total_grad[e, sub * SB : (sub + 1) * SB, used:width] = jnp.zeros(
                                (SB, width - used), bf16
                            )
                    scored = ref.total_grad[e, :, :width]
                    turned = nn(scored, ref.key_table[:width, :])
                    by_content.append(turned[:, :128])
                    low, high = rotate(
                        turned[:, 128:], ref.angles[rows, :HALF], ref.angles[rows, HALF:]
                    )
                    spread = jnp.concatenate([low, high], axis=1).astype(bf16)
                    own = (lax.broadcasted_iota(jnp.int32, (128, D), 0) // HEAD_DIM) == e
                    part = nt(spread, jnp.where(own, position[lanes, :], 0).astype(bf16))
                    by_position = part if by_position is None else by_position + part
                    part = tn(keep_head(ref.query_v[rows, lanes], e), spread)
                    if b == 0 and e == 0:
                        ref.position_grad[lanes, :] = part
                    else:
                        ref.position_grad[lanes, :] += part
                    to_key = tn(keep_head(ref.query_u[rows, lanes], e), scored)
                    to_value = tn(upstream, ref.probs[base + e, :, span])
                    if e == 0:
                        if b > 0:
                            ref.key_acc[:, :row] += to_key[:, :row]
                            ref.value_acc[:, :row] += to_value[:, :row]
                        ref.key_acc[:, row:width] = to_key[:, row:]
                        ref.value_acc[:, row:width] = to_value[:, row:]
                    else:
                        ref.key_acc[:, :width] += to_key
                        ref.value_acc[:, :width] += to_value
                    for when, events in BACK_DURING.items():
                        if linked and when % 6 == b * 2 + e:
                            run_at(hp, when // 6, lambda events=events: run(events))
                by_content = jnp.where(head_lanes(QB, 0), by_content[0], by_content[1])
                ref.joined_grad[rows, lanes] = (by_content + by_position).astype(bf16)
                content_sum += jnp.sum(by_content, axis=0, keepdims=True)
                position_sum += jnp.sum(by_position, axis=0, keepdims=True)
            ref.joined_grad[:, pl.ds(start + D, 128)] = ref.key_acc[...].T.astype(bf16)
            ref.joined_grad[:, pl.ds(start + 2 * D, 128)] = ref.value_acc[...].T.astype(bf16)
            r = VECTOR_ROW["content"]
            ref.all_sums[r : r + 1, lanes] = content_sum
            r = VECTOR_ROW["position_bias"]
            ref.all_sums[r : r + 1, lanes] = position_sum
            return carry

        lax.fori_loop(0, HEADS // 2, pair, 0)

        row_copy("first_grad").wait()
        for part in range(3):
            columns = slice(part * D, (part + 1) * D)
            grad = tn(ref.joined_grad[:, columns], ref.normed_low[...]).astype(bf16)
            if linked:
                ref.project_full[columns, :] = grad
            else:
                ref.project_grad[columns, :] = grad
        if linked:
            put_blocks(plan, "project", ref.own, 0, lambda columns: ref.project_full[:, columns])
            put_blocks(plan, "position", ref.own, 0, lambda columns: ref.position_grad[:, columns])
            run([(4, 0)])
        else:
            ref.position_grad_out[...] = ref.position_grad[...].astype(bf16)

        def norm_back(i, carry):
            rows = at_rows(i, RB)
            normal, inverse = norm_rows(rows)
            upstream = nn(ref.joined_grad[rows, :], full(ref.project))
            ref.parts[0, :, :] += eight_rows(upstream * normal)
            ref.parts[1, :, :] += eight_rows(upstream)
            ref.token_grad[rows, :] = ref.first_grad[rows, :] + norm_backward(
                normal, inverse, vec(ref.vectors, "gain_one"), upstream
            )
            if linked:
                run_at(i, 3, lambda: run([(4, 1)]))
            return carry

        lax.fori_loop(0, SEQ // RB, norm_back, 0)
        for slot, name in enumerate(("gain_one", "shift_one")):
            r = VECTOR_ROW[name]
            ref.all_sums[r : r + 1, :D] = jnp.sum(ref.parts[slot], axis=0, keepdims=True)
        if linked:
            pack_vectors(ref.all_sums, ref.vector_own)
            vector.first()
            run([(4, 2)])
            vector.second()
            run([(4, 3), (4, 4)])
            vector.last()
            run([(4, 5)])
            for name in WEIGHTS:
                put_shard(plan, name, ref.flat, 0, getattr(ref, name + "_out"))
        else:
            ref.sums_out[...] = ref.all_sums[...]

    if linked:
        scratch["project_full"] = VMEM((3 * D, D), bf16)
    return call(body, ins, outs, scratch, **params)


def make_local(dp, fsdp):
    plan = Plan(dp, fsdp)
    linked = (dp, fsdp) == (4, 8)

    def gathered(weights):
        out = {}
        for name, shard in zip(WEIGHTS, weights):
            part = lax.all_gather(shard, "dp", axis=0, tiled=True)
            out[name + "_full"] = lax.all_gather(part, "fsdp", axis=1, tiled=True).T
        return out

    def gathered_vectors(vectors):
        rows = []
        for name, shard in zip(VECTORS, vectors):
            whole = lax.all_gather(shard, ("dp", "fsdp"), axis=0, tiled=True).astype(f32)
            rows.append(jnp.pad(whole, (0, FF - VECTOR_SIZE[name])))
        rows += [jnp.zeros((FF,), f32)] * (16 - len(rows))
        return jnp.stack(rows)

    def local(tokens, cotangent, *params):
        assert tokens.shape[0] == SEQ
        weights, vectors = params[:7], params[7:]
        given = dict(zip(VECTORS, vectors))
        coarse = coarse_angles()
        ins = {"tokens": (tokens, VMEM), "coarse": (coarse, VMEM)}
        if linked:
            packed, at = jnp.zeros((VECTOR_ROWS * 128,), bf16), 0
            for n in PACKED_VECTORS:
                size = given[n].shape[0]
                packed += lax.pad(
                    given[n], jnp.zeros((), bf16), [(at, packed.shape[0] - at - size, 0)]
                )
                at += size
            ins["packed"] = (packed.reshape(VECTOR_ROWS, 128), VMEM)
            for n, w in zip(WEIGHTS, weights):
                ins[n + "_shard"] = (w.T if w.shape[1] % 128 else w, VMEM)
        else:
            whole = gathered(weights)
            ins["given_vectors"] = (gathered_vectors(vectors), VMEM)
            ins["project"] = (whole["project_full"], VMEM)
            ins["position"] = (whole["position_full"], VMEM)
        one = front(plan, linked, ins)

        ins = {
            "tokens": (tokens, VMEM),
            "cotangent": (cotangent, VMEM),
            "mixed": (one.mixed_out, VMEM),
            "vectors": (one.vectors, VMEM),
        }
        if linked:
            ins["blocks"] = (one.blocks, ANY)
        else:
            ins |= {n + "_full": (whole[n + "_full"], ANY) for n in MIDDLE}
        two = middle(plan, linked, ins)

        ins = {
            "tokens_in": (tokens, ANY),
            "coarse": (coarse, VMEM),
            "vectors": (one.vectors, VMEM),
            "query_u_in": (one.query_u_out, ANY),
            "query_v_in": (one.query_v_out, ANY),
            "key_in": (one.key_out, ANY),
            "value_in": (one.value_out, ANY),
            "mixed_in": (one.mixed_out, ANY),
            "mixed_grad_in": (two.mixed_grad_out, ANY),
            "first_grad_in": (two.first_grad_out, ANY),
            "sums": (two.sums, VMEM),
            "probs_in": (one.probs_out, ANY),
        }
        if linked:
            ins["blocks"] = (two.blocks_out, ANY)
            for n in ("contract", "expand", "mixing"):
                ins[n + "_grad"] = (getattr(two, n + "_grad_out"), ANY)
            ins["partial"] = (two.partial, ANY)
        else:
            ins |= {n + "_full": (whole[n + "_full"], ANY) for n in ("project", "position")}
        three = back(plan, linked, ins)

        if linked:
            matrices = []
            for n in WEIGHTS:
                grad = getattr(three, n + "_out")
                matrices.append(grad if grad.shape == plan.shard[n] else grad.T)
            places = vector_places()
            small = []
            for name in VECTORS:
                line, offset, size = places[name]
                small.append(three.vector_out[line, offset : offset + size])
        else:
            grads = {n: getattr(two, n + "_grad_out") for n in MIDDLE}
            grads["project"] = three.project_grad
            grads["position"] = three.position_grad_out
            matrices = []
            for name in WEIGHTS:
                part = lax.psum_scatter(
                    grads[name].T, "fsdp", scatter_dimension=1, tiled=True
                )
                part = lax.psum_scatter(part, "dp", scatter_dimension=0, tiled=True)
                matrices.append(part.astype(f32))
            small = []
            for name in VECTORS:
                sums = three.sums_out[VECTOR_ROW[name], : VECTOR_SIZE[name]]
                small.append(
                    lax.psum_scatter(sums, ("dp", "fsdp"), scatter_dimension=0, tiled=True)
                )
        return (two.output_out, three.token_grad, *matrices, *small)

    return local


def solution(mesh):
    rows = P(("dp", "fsdp"), None)
    matrix = P("dp", "fsdp")
    vector = P(("dp", "fsdp"))
    return jax.shard_map(
        make_local(mesh.shape["dp"], mesh.shape["fsdp"]),
        mesh=mesh,
        in_specs=(rows,) * 2 + (matrix,) * 7 + (vector,) * 11,
        out_specs=(rows,) * 2 + (matrix,) * 7 + (vector,) * 11,
        check_vma=False,
    )
```

```python
import math
from types import SimpleNamespace

import jax
import jax.numpy as jnp
from jax import lax
from jax.experimental import pallas as pl
from jax.experimental.pallas import tpu as pltpu
from jax.sharding import PartitionSpec as P

D = 512
HALF = D // 2
HEADS = 8
HEAD_DIM = 64
FF = 2048
SEQ = 1152
THIRD = SEQ // 3
QB = 384
SB = 128
CH = 16
RB = 192
BLOCKS = SEQ // QB
POFF = [sum((b + 1) * QB for b in range(n)) for n in range(BLOCKS + 1)]
PW = POFF[BLOCKS]
EXP_SCALE = HEAD_DIM ** (-0.5) * math.log2(math.e)
ANGLE_STEP = 32
epsilon = 1e-05
bf16 = jnp.bfloat16
f32 = jnp.float32
MESH = pl.DeviceIdType.MESH
VMEM_LIMIT = 63 << 20

WEIGHTS = ("project", "position", "mixing", "expand", "contract", "pooling", "upsample")
WEIGHT_SHAPE = {
    "project": (D, 3 * D),
    "position": (D, D),
    "mixing": (D, D),
    "expand": (D, FF),
    "contract": (FF, D),
    "pooling": (3 * D, D),
    "upsample": (D, 3 * D),
}
VECTORS = (
    "gain_one",
    "shift_one",
    "content",
    "position_bias",
    "mixing_bias",
    "gain_two",
    "shift_two",
    "hidden",
    "contract_bias",
    "pooling_bias",
    "upsample_bias",
)
VECTOR_SIZE = {n: D for n in VECTORS} | {"hidden": FF, "upsample_bias": 3 * D}
VECTOR_ROW = {n: i for i, n in enumerate(VECTORS)}
PACKED_VECTORS = ("hidden", "upsample_bias", "gain_one") + tuple(
    n for n in VECTORS if n not in ("hidden", "upsample_bias", "gain_one")
)


def nn(a, b):
    return lax.dot_general(a, b, (((1,), (0,)), ((), ())), preferred_element_type=f32)


def nt(a, b):
    return lax.dot_general(a, b, (((1,), (1,)), ((), ())), preferred_element_type=f32)


def tn(a, b):
    return lax.dot_general(a, b, (((0,), (0,)), ((), ())), preferred_element_type=f32)


def at_rows(step, rows):
    return pl.ds(pl.multiple_of(step * rows, rows), rows)


def eight_rows(values):
    rows, columns = values.shape
    return jnp.sum(values.reshape(rows // 8, 8, columns), axis=0)


def call(body, ins, outs, scratch, alias=None, **params):
    names = [*ins, *outs, *scratch]

    def kernel(*refs):
        body(SimpleNamespace(**dict(zip(names, refs))))

    results = pl.pallas_call(
        kernel,
        out_shape=[jax.ShapeDtypeStruct(s, t) for s, t, _ in outs.values()],
        in_specs=[pl.BlockSpec(memory_space=m) for _, m in ins.values()],
        out_specs=[pl.BlockSpec(memory_space=m) for _, _, m in outs.values()],
        scratch_shapes=list(scratch.values()),
        input_output_aliases=alias or {},
        compiler_params=pltpu.CompilerParams(vmem_limit_bytes=VMEM_LIMIT, **params),
    )(*[a for a, _ in ins.values()])
    return SimpleNamespace(**dict(zip(outs, results)))


VMEM = pltpu.VMEM
ANY = pl.ANY


BIT_AXIS = ("fsdp", "fsdp", "fsdp", "dp", "dp")
BIT_MASK = (4, 2, 1, 2, 1)
CUBE = (2,) * 5
GATHER_ORDER = ((2, 3, 4), (3, 2, 4))
SCATTER_ORDER = ((4, 3, 2), (4, 2, 3))
STAGES = 4
COPIES = 6


def my_bits():
    fs = lax.axis_index("fsdp")
    dp = lax.axis_index("dp")
    return (
        lax.rem(fs // 4, 2),
        lax.rem(fs // 2, 2),
        lax.rem(fs, 2),
        lax.rem(dp // 2, 2),
        lax.rem(dp, 2),
    )


def partner(*flipped):
    place = {"fsdp": lax.axis_index("fsdp"), "dp": lax.axis_index("dp")}
    bits = my_bits()
    for bit in flipped:
        place[BIT_AXIS[bit]] += BIT_MASK[bit] * (1 - 2 * bits[bit])
    return (place["dp"], place["fsdp"])


LINE_FLIPS = ((1,), (0,), (0, 1))


def flipped_bits(flips):
    return tuple(1 - b if k in flips else b for k, b in enumerate(my_bits()))


def partner_signal():
    sem = pltpu.get_barrier_semaphore()
    for flips in LINE_FLIPS + ((2,), (3,), (4,)):
        pl.semaphore_signal(sem, inc=1, device_id=partner(*flips), device_id_type=MESH)


def partner_wait():
    pl.semaphore_wait(pltpu.get_barrier_semaphore(), 6)


def run_at(step, number, action):
    @pl.when(step == number)
    def _():
        action()


class Gather:
    def __init__(self, buf, pieces, send_sem, recv_sem, mine=None):
        self.buf, self.pieces, self.mine = buf, pieces, mine
        self.send_sem, self.recv_sem = send_sem, recv_sem
        self.bits = my_bits()

    def copy(self, source, target, sem, device):
        return pltpu.make_async_remote_copy(
            src_ref=source,
            dst_ref=target,
            send_sem=self.send_sem.at[sem],
            recv_sem=self.recv_sem.at[sem],
            device_id=device,
            device_id_type=MESH,
        )

    def copies(self, i, stage):
        row, rows, kind = self.pieces[i]
        part = (pl.ds(row, rows),)
        if stage == 0:
            target = self.buf.at[self.bits + part]
            source = target if self.mine is None else self.mine.at[part]
            return [
                self.copy(source, target, i * COPIES + n, partner(*flips))
                for n, flips in enumerate(LINE_FLIPS)
            ]
        order = GATHER_ORDER[kind]
        free = (0, 1) + order[: stage - 1]
        index = tuple(slice(None) if k in free else self.bits[k] for k in range(5))
        ref = self.buf.at[index + part]
        return [self.copy(ref, ref, i * COPIES + 2 + stage, partner(order[stage - 1]))]

    def advance(self, i, stage, first=0, last=STAGES):
        if stage > first:
            for copy in self.copies(i, stage - 1):
                copy.wait_recv()
        if stage < last:
            for copy in self.copies(i, stage):
                copy.start()

    def drain(self, i, first=0, last=STAGES):
        for stage in range(first, last):
            for copy in self.copies(i, stage):
                copy.wait_send()


class Scatter:
    def __init__(self, own, land, out, pieces, send_sem, recv_sem):
        self.own, self.land, self.out, self.pieces = own, land, out, pieces
        self.send_sem, self.recv_sem = send_sem, recv_sem
        self.bits = my_bits()

    def index(self, order, stage, side):
        out = []
        for k in range(5):
            if k in order[:stage]:
                out.append(1 - self.bits[k] if side in ("land", "target") else self.bits[k])
            elif k in order[stage : stage + 1]:
                out.append(1 - self.bits[k] if side in ("send", "target") else self.bits[k])
            else:
                out.append(slice(None))
        return tuple(out)

    def copy(self, source, target, sem, device):
        return pltpu.make_async_remote_copy(
            src_ref=source,
            dst_ref=target,
            send_sem=self.send_sem.at[sem],
            recv_sem=self.recv_sem.at[sem],
            device_id=device,
            device_id_type=MESH,
        )

    def copies(self, i, stage):
        row, rows, kind = self.pieces[i]
        order = SCATTER_ORDER[kind]
        part = (pl.ds(row, rows),)
        if stage == 3:
            place = self.bits[:2] + tuple(1 - b for b in self.bits[2:])
            return [
                self.copy(
                    self.own.at[flipped_bits(flips) + part],
                    self.land.at[place + part],
                    i * COPIES + 3 + n,
                    partner(*flips),
                )
                for n, flips in enumerate(LINE_FLIPS)
            ]
        return [
            self.copy(
                self.own.at[self.index(order, stage, "send") + part],
                self.land.at[self.index(order, stage, "target") + part],
                i * COPIES + stage,
                partner(order[stage]),
            )
        ]

    def add(self, i, stage):
        row, rows, kind = self.pieces[i]
        order = SCATTER_ORDER[kind]
        part = (pl.ds(row, rows), slice(None))
        if stage == 3:
            total = self.own[self.bits + part].astype(f32)
            for flips in LINE_FLIPS:
                place = flipped_bits(flips)[:2] + tuple(1 - b for b in self.bits[2:])
                total = total + self.land[place + part].astype(f32)
            self.out[pl.ds(row, rows), :] = total
            return
        mine = self.own.at[self.index(order, stage, "own")]
        came = self.land.at[self.index(order, stage, "land")]
        free = 4 - stage

        def body(j, carry):
            at = tuple(lax.rem(j // 2 ** (free - 1 - q), 2) for q in range(free)) + part
            mine[at] = mine[at] + came[at]
            return carry

        lax.fori_loop(0, 2**free, body, 0)

    def advance(self, i, stage, first=0, last=STAGES):
        if stage > first:
            for copy in self.copies(i, stage - 1):
                copy.wait()
            self.add(i, stage - 1)
        if stage < last:
            for copy in self.copies(i, stage):
                copy.start()


def split_pieces(chunks):
    pieces = []
    for row, rows in chunks:
        half = (rows // 2 + 15) // 16 * 16
        pieces.append((row, half, 0))
        pieces.append((row + half, rows - half, 1))
    return pieces


class AxisScatter:
    def __init__(self, own, land_dp, land_fsdp, out, sems):
        self.own, self.land_dp, self.land_fsdp, self.out = own, land_dp, land_fsdp, out
        self.sems = sems
        self.fs, self.dp = lax.axis_index("fsdp"), lax.axis_index("dp")

    def bits(self, fs, dp):
        return (lax.rem(fs // 4, 2), lax.rem(fs // 2, 2), lax.rem(fs, 2)), (
            lax.rem(dp // 2, 2),
            lax.rem(dp, 2),
        )

    def dp_copy(self, step):
        other = lax.rem(self.dp + step, 4)
        _, (y, core) = self.bits(self.fs, other)
        return pltpu.make_async_remote_copy(
            src_ref=self.own.at[:, :, :, y, core],
            dst_ref=self.land_dp.at[step - 1],
            send_sem=self.sems.at[0, step],
            recv_sem=self.sems.at[1, step],
            device_id=(other, self.fs),
            device_id_type=MESH,
        )

    def fsdp_copy(self, step):
        other = lax.rem(self.fs + step, 8)
        (zh, zl, x), (y, core) = self.bits(other, self.dp)
        return pltpu.make_async_remote_copy(
            src_ref=self.own.at[zh, zl, x, y, core],
            dst_ref=self.land_fsdp.at[step - 1],
            send_sem=self.sems.at[2, step],
            recv_sem=self.sems.at[3, step],
            device_id=(self.dp, other),
            device_id_type=MESH,
        )

    def first(self):
        for step in range(1, 4):
            self.dp_copy(step).start()

    def second(self):
        for step in range(1, 4):
            self.dp_copy(step).wait()
        _, (y, core) = self.bits(self.fs, self.dp)
        mine = self.own.at[:, :, :, y, core]
        mine[...] = mine[...] + self.land_dp[0] + self.land_dp[1] + self.land_dp[2]
        for step in range(1, 8):
            self.fsdp_copy(step).start()

    def last(self):
        for step in range(1, 8):
            self.fsdp_copy(step).wait()
        (zh, zl, x), (y, core) = self.bits(self.fs, self.dp)
        total = self.own[zh, zl, x, y, core]
        for step in range(7):
            total = total + self.land_fsdp[step]
        self.out[...] = total


def axis_signal():
    fs, dp = lax.axis_index("fsdp"), lax.axis_index("dp")
    sem = pltpu.get_barrier_semaphore()
    for step in range(1, 4):
        to = (lax.rem(dp + step, 4), fs)
        pl.semaphore_signal(sem, inc=1, device_id=to, device_id_type=MESH)
    for step in range(1, 8):
        to = (dp, lax.rem(fs + step, 8))
        pl.semaphore_signal(sem, inc=1, device_id=to, device_id_type=MESH)


def axis_wait():
    pl.semaphore_wait(pltpu.get_barrier_semaphore(), 10)


class Plan:
    def __init__(self, dp, fsdp):
        self.shard = {n: (WEIGHT_SHAPE[n][0] // dp, WEIGHT_SHAPE[n][1] // fsdp) for n in WEIGHTS}
        self.row, at = {}, 0
        for name in WEIGHTS:
            self.row[name] = at
            at += self.shard[name][0] * self.shard[name][1] // 128
        self.rows = at

    def span(self, first, last, shift):
        r, c = self.shard[last]
        end = self.row[last] + r * c // 128
        return (self.row[first] + shift, end - self.row[first])

    def full_shape(self, name):
        return (2, 2, 2, self.shard[name][1], WEIGHT_SHAPE[name][0])

    def held_shape(self, name):
        r, c = self.shard[name]
        return (c, r) if c % 128 else (r, c)

    def blocks(self, name, shift):
        r, c = self.shard[name]
        return [
            (y, core, shift + self.row[name] + q * c, (y * 2 + core) * r + q * 128)
            for y in range(2)
            for core in range(2)
            for q in range(r // 128)
        ]


def put_blocks(plan, name, own, shift, values_of):
    c = plan.shard[name][1]
    for y, core, at, column in plan.blocks(name, shift):
        values = values_of(slice(column, column + 128)).astype(bf16)
        own[:, :, :, y, core, at : at + c, :] = values.reshape(2, 2, 2, c, 128)


def put_shard(plan, name, flat, shift, target):
    r, c = plan.shard[name]
    for q in range(r // 128):
        at = shift + plan.row[name] + q * c
        if c % 128:
            target[:, q * 128 : (q + 1) * 128] = flat[at : at + c, :]
        else:
            target[q * 128 : (q + 1) * 128, :] = flat[at : at + c, :].T


def load_weight(plan, name, buf, target, sem, shift):
    c = plan.shard[name][1]
    for y, core, row, column in plan.blocks(name, shift):
        pltpu.make_async_copy(
            buf.at[:, :, :, y, core, pl.ds(row, c), :],
            target.at[:, :, :, :, pl.ds(column, 128)],
            sem,
        ).start()


def wait_whole(target, sem):
    pltpu.make_async_copy(target, target, sem).wait()


def full(ref):
    values = ref[...]
    return values.reshape(-1, values.shape[-1])


def vector_places():
    places, at = {}, 0
    for name in PACKED_VECTORS:
        size = VECTOR_SIZE[name] // 32
        places[name] = (at // 128, at % 128, size)
        at += size
    return places


def block_owner(columns, size):
    row = lax.broadcasted_iota(jnp.int32, (32, columns), 0)
    lane = lax.broadcasted_iota(jnp.int32, (32, columns), 1)
    return lane // size == lax.rem(row, 4) * 8 + row // 4


def unpack_vectors(blocks, target):
    flat = blocks[...].reshape(32 * 16, 128)
    for name, (line, offset, size) in vector_places().items():
        columns = VECTOR_SIZE[name]
        row = lax.broadcasted_iota(jnp.int32, (32, 512), 0)
        lane = lax.broadcasted_iota(jnp.int32, (32, 512), 1)
        pick = (lane == row * 16 + line).astype(bf16)
        own = nn(pick, flat).astype(bf16)
        source = lax.broadcasted_iota(jnp.int32, (128, columns), 0)
        lane = lax.broadcasted_iota(jnp.int32, (128, columns), 1)
        spread = (source - offset == lax.rem(lane, size)).astype(bf16)
        spread_own = jnp.where(block_owner(columns, size), nn(own, spread), 0.0)
        r = VECTOR_ROW[name]
        target[r : r + 1, :columns] = jnp.sum(spread_own, axis=0, keepdims=True)


def pack_vectors(source, target):
    lines = [jnp.zeros((32, 128), f32), jnp.zeros((32, 128), f32)]
    for name, (line, offset, size) in vector_places().items():
        columns = VECTOR_SIZE[name]
        r = VECTOR_ROW[name]
        values = jnp.broadcast_to(source[r : r + 1, :columns], (32, columns))
        values = jnp.where(block_owner(columns, size), values, 0.0)
        lane = lax.broadcasted_iota(jnp.int32, (columns, 128), 0)
        goal = lax.broadcasted_iota(jnp.int32, (columns, 128), 1)
        gather = (goal - offset == lax.rem(lane, size)).astype(bf16)
        for _ in range(3):
            term = values.astype(bf16)
            lines[line] += nn(term, gather)
            values = values - term.astype(f32)
    both = jnp.concatenate([lines[0][:, None, :], lines[1][:, None, :]], axis=1)
    both = jnp.concatenate([both, jnp.zeros((32, 6, 128), f32)], axis=1)
    target[...] = both.reshape(CUBE + (8, 128))


def coarse_angles():
    ratios = jnp.arange(0, D, 2).astype(f32) / D
    inverse = 1.0 / 10000.0**ratios
    steps = SEQ // ANGLE_STEP
    places = jnp.concatenate(
        [jnp.arange(steps) * ANGLE_STEP, jnp.zeros((-steps % 8,), jnp.int32), jnp.arange(ANGLE_STEP)]
    ).astype(f32)
    angles = places[:, None] * inverse[None, :]
    return jnp.concatenate([jnp.sin(angles), jnp.cos(angles)], axis=1)


def expand_angles(coarse, angles, table_of):
    steps = SEQ // ANGLE_STEP
    start = steps + -steps % 8

    def body(q, carry):
        high_sin, high_cos = coarse[pl.ds(q, 1), :HALF], coarse[pl.ds(q, 1), HALF:]
        low_sin, low_cos = coarse[start:, :HALF], coarse[start:, HALF:]
        sine = high_sin * low_cos + high_cos * low_sin
        cosine = high_cos * low_cos - high_sin * low_sin
        rows = at_rows(q, ANGLE_STEP)
        angles[rows, :HALF] = sine
        angles[rows, HALF:] = cosine
        table_of(rows, sine.astype(bf16), cosine.astype(bf16))
        return carry

    lax.fori_loop(0, steps, body, 0)


def head_lanes(rows, head):
    return (lax.broadcasted_iota(jnp.int32, (rows, 128), 1) // HEAD_DIM) == head


def keep_head(values, head):
    return jnp.where(head_lanes(values.shape[0], head), values, 0).astype(bf16)


def rotate(pair, sines, cosines):
    low, high = pair[:, :HALF], pair[:, HALF:]
    return high * sines - low * cosines, low * sines + high * cosines


def norm_parts(values):
    row_mean = jnp.mean(values, axis=-1, keepdims=True)
    centred = values - row_mean
    variance = jnp.mean(centred * centred, axis=-1, keepdims=True)
    inv_std = lax.rsqrt(variance + epsilon)
    return centred * inv_std, inv_std


def norm_backward(normal, inv_std, gain, upstream):
    scaled = upstream * gain
    scaled_mean = jnp.mean(scaled, axis=-1, keepdims=True)
    cross_mean = jnp.mean(scaled * normal, axis=-1, keepdims=True)
    return inv_std * (scaled - scaled_mean - normal * cross_mean)


def vec(ref, name):
    r = VECTOR_ROW[name]
    return ref[r : r + 1, : VECTOR_SIZE[name]]


VECTOR_ROWS = 16


FRONT_ROWS = ("query_u", "query_v", "key", "value", "mixed")
CHUNK_LAST = (4, 4, 4, 1, 1)
BEFORE = ((0, 1), (1, 0), (0, 2), (0, 3), (1, 1), (2, 0), (0, 4))
AFTER = ((1, 2), (2, 1), (3, 0), (4, 0))
DURING = {
    7: ((1, 3),),
    8: ((3, 1), (4, 1)),
    9: ((2, 2),),
    10: ((1, 4),),
    16: ((2, 3),),
    19: ((2, 4),),
}


def front(plan, linked, ins):
    outs = {
        "vectors": ((16, FF), f32, VMEM),
    }
    outs |= {n + "_out": ((SEQ, D), bf16, ANY) for n in FRONT_ROWS}
    outs |= {
        "probs_out": ((HEADS, QB, PW), bf16, ANY),
    }
    scratch = {
        "normal": VMEM((SEQ, D), f32),
        "angles": VMEM((SEQ, D), f32),
        "key_table": VMEM((SEQ, 128 + D), bf16),
        "score": VMEM((2, QB, SEQ), f32),
        "turned": VMEM((2, QB, 128 + D), bf16),
        "probs": VMEM((2, QB, PW), bf16),
        "probs_sem": pltpu.SemaphoreType.DMA((2,)),
        "out_sem": pltpu.SemaphoreType.DMA((len(FRONT_ROWS),)),
    }
    scratch |= {n: VMEM((SEQ, D), bf16) for n in FRONT_ROWS}
    params = {}
    if linked:
        rows = VECTOR_ROWS + plan.rows
        chunks = [
            (0, VECTOR_ROWS + plan.span("project", "position", 0)[1]),
            plan.span("mixing", "expand", VECTOR_ROWS),
            plan.span("contract", "contract", VECTOR_ROWS),
            plan.span("pooling", "pooling", VECTOR_ROWS),
            plan.span("upsample", "upsample", VECTOR_ROWS),
        ]
        pieces = split_pieces(chunks)
        outs["blocks"] = (CUBE + (rows, 128), bf16, ANY)
        scratch |= {
            "mine": VMEM((rows, 128), bf16),
            "project": VMEM(plan.full_shape("project"), bf16),
            "position": VMEM(plan.full_shape("position"), bf16),
            "vector_blocks": VMEM(CUBE + (VECTOR_ROWS, 128), bf16),
            "vector_lines": VMEM((VECTOR_ROWS, 128), f32),
            "send_sem": pltpu.SemaphoreType.DMA((COPIES * len(pieces),)),
            "recv_sem": pltpu.SemaphoreType.DMA((COPIES * len(pieces),)),
            "load_sem": pltpu.SemaphoreType.DMA((4,)),
        }
        params = dict(collective_id=0, has_side_effects=True)

    def body(ref):
        if linked:
            partner_signal()
            gather = Gather(ref.blocks, pieces, ref.send_sem, ref.recv_sem, ref.mine)

            def run(events):
                for chunk, stage in events:
                    for piece in (2 * chunk, 2 * chunk + 1):
                        gather.advance(piece, stage, last=CHUNK_LAST[chunk])

            def pack(name):
                r, c = plan.shard[name]
                shard = getattr(ref, name + "_shard")
                for q in range(r // 128):
                    at = VECTOR_ROWS + plan.row[name] + q * c
                    if c % 128:
                        ref.mine[at : at + c, :] = shard[:, q * 128 : (q + 1) * 128]
                    else:
                        ref.mine[at : at + c, :] = shard[q * 128 : (q + 1) * 128, :].T

            ref.vector_lines[...] = jnp.zeros_like(ref.vector_lines)
            for name, (line, offset, size) in vector_places().items():
                entries = getattr(ref, name + "_shard")[...].astype(f32).reshape(1, size)
                ref.vector_lines[line : line + 1, offset : offset + size] = entries
            ref.mine[:VECTOR_ROWS, :] = ref.vector_lines[...].astype(bf16)
            for name in ("project", "position"):
                pack(name)
            partner_wait()
            run([(0, 0)])
            for name in WEIGHTS[2:]:
                pack(name)
            own = pltpu.make_async_copy(
                ref.mine, ref.blocks.at[gather.bits], ref.load_sem.at[0]
            )
            own.start()

        def first_norm(i, carry):
            rows = at_rows(i, RB)
            ref.normal[rows, :] = norm_parts(ref.tokens[rows, :].astype(f32))[0]
            return carry

        lax.fori_loop(0, SEQ // RB, first_norm, 0)

        def table_of(rows, sine, cosine):
            ref.key_table[rows, 128 : 128 + HALF] = sine
            ref.key_table[rows, 128 + HALF :] = cosine

        expand_angles(ref.coarse, ref.angles, table_of)

        if linked:
            own.wait()
            run(BEFORE)
            load_weight(plan, "project", ref.blocks, ref.project, ref.load_sem.at[1], VECTOR_ROWS)
            load_weight(plan, "position", ref.blocks, ref.position, ref.load_sem.at[3], VECTOR_ROWS)
            small = pltpu.make_async_copy(
                ref.blocks.at[:, :, :, :, :, pl.ds(0, VECTOR_ROWS), :],
                ref.vector_blocks,
                ref.load_sem.at[2],
            )
            small.start()
            small.wait()
            unpack_vectors(ref.vector_blocks, ref.vectors)
            wait_whole(ref.project, ref.load_sem.at[1])
        else:
            ref.vectors[...] = ref.given_vectors[...]

        for b in range(BLOCKS):
            rows = slice(b * QB, (b + 1) * QB)
            normed = ref.normal[rows, :] * vec(ref.vectors, "gain_one") + vec(
                ref.vectors, "shift_one"
            )
            joined = nt(normed.astype(bf16), full(ref.project))
            ref.query_u[rows, :] = (joined[:, :D] + vec(ref.vectors, "content")).astype(bf16)
            ref.query_v[rows, :] = (joined[:, :D] + vec(ref.vectors, "position_bias")).astype(bf16)
            ref.key[rows, :] = joined[:, D : 2 * D].astype(bf16)
            ref.value[rows, :] = joined[:, 2 * D :].astype(bf16)

        def row_copy(i):
            name = FRONT_ROWS[i]
            return pltpu.make_async_copy(
                getattr(ref, name), getattr(ref, name + "_out"), ref.out_sem.at[i]
            )

        for i in range(4):
            row_copy(i).start()

        if linked:
            run(AFTER)
            wait_whole(ref.position, ref.load_sem.at[3])
            position = ref.position.reshape(D, D)
        else:
            position = ref.position

        def out_copy(head, slot):
            return pltpu.make_async_copy(
                ref.probs.at[slot], ref.probs_out.at[head], ref.probs_sem.at[slot]
            )

        def scores(lanes, b, e):
            row, width = b * QB, (b + 1) * QB
            rows = slice(row, row + QB)
            spread = nn(keep_head(ref.query_v[rows, lanes], e), position[lanes, :])
            low, high = rotate(spread, ref.angles[rows, :HALF], ref.angles[rows, HALF:])
            ref.turned[e, :, :128] = keep_head(ref.query_u[rows, lanes], e)
            ref.turned[e, :, 128 : 128 + HALF] = low.astype(bf16)
            ref.turned[e, :, 128 + HALF :] = high.astype(bf16)
            ref.score[e, :, :width] = nt(ref.turned[e], ref.key_table[:width, :])

        def softmax(b, e):
            row, width = b * QB, (b + 1) * QB
            for sub in range(QB // SB):
                used = row + (sub + 1) * SB
                for g in range(SB // CH):
                    at = slice(sub * SB + g * CH, sub * SB + (g + 1) * CH)
                    tiles = [
                        ref.score[e, at, i * 128 : (i + 1) * 128] for i in range(used // 128)
                    ]
                    lane = lax.broadcasted_iota(jnp.int32, (CH, SB), 1)
                    place = lax.broadcasted_iota(jnp.int32, (CH, SB), 0) + g * CH
                    tiles[-1] = jnp.where(lane <= place, tiles[-1], -1e30)
                    top = tiles[0]
                    for tile in tiles[1:]:
                        top = jnp.maximum(top, tile)
                    top = jnp.max(top, axis=1, keepdims=True)
                    tiles = [jnp.exp2((tile - top) * EXP_SCALE) for tile in tiles]
                    total = tiles[0]
                    for tile in tiles[1:]:
                        total = total + tile
                    scale = 1.0 / jnp.sum(total, axis=1, keepdims=True)
                    for i, tile in enumerate(tiles):
                        lanes = slice(POFF[b] + i * 128, POFF[b] + (i + 1) * 128)
                        ref.probs[e, at, lanes] = (tile * scale).astype(bf16)
                if used < width:
                    ref.probs[e, sub * SB : (sub + 1) * SB, POFF[b] + used : POFF[b] + width] = (
                        jnp.zeros((SB, width - used), bf16)
                    )

        def pair(hp, carry):
            lanes = pl.ds(pl.multiple_of(hp * 128, 128), 128)
            ref.key_table[:, :128] = ref.key[:, lanes]

            @pl.when(hp > 0)
            def _():
                for e in range(2):
                    out_copy(0, e).wait()

            for b in range(BLOCKS):
                for e in range(2):
                    scores(lanes, b, e)
                    softmax(b, e)
                    for when, events in DURING.items():
                        if linked and when % 6 == b * 2 + e:
                            run_at(hp, when // 6, lambda events=events: run(events))
                row, width = b * QB, (b + 1) * QB
                values = ref.value[:width, lanes]
                span = slice(POFF[b], POFF[b] + width)
                ref.mixed[row : row + QB, lanes] = jnp.where(
                    head_lanes(QB, 0),
                    nn(ref.probs[0, :, span], values),
                    nn(ref.probs[1, :, span], values),
                ).astype(bf16)
            for e in range(2):
                out_copy(hp * 2 + e, e).start()
            return carry

        lax.fori_loop(0, HEADS // 2, pair, 0)
        row_copy(4).start()
        for e in range(2):
            out_copy(0, e).wait()
        if linked:
            for i in range(len(pieces)):
                gather.drain(i, last=CHUNK_LAST[i // 2])
        for i in range(5):
            row_copy(i).wait()

    return call(body, ins, outs, scratch, **params)


MIDDLE = ("mixing", "expand", "contract", "pooling", "upsample")


def middle(plan, linked, ins):
    def weight_shape(name):
        return plan.full_shape(name) if linked else WEIGHT_SHAPE[name][::-1]

    outs = {
        "output_out": ((SEQ, D), bf16, ANY),
        "first_grad_out": ((SEQ, D), f32, ANY),
        "mixed_grad_out": ((SEQ, D), bf16, ANY),
        "sums": ((16, FF), f32, VMEM),
    }
    summed = ("pooling", "upsample") if linked else ()
    kept = [n for n in MIDDLE if n not in summed]
    outs |= {n + "_grad_out": (weight_shape(n), bf16, ANY) for n in kept}
    params = {}
    scratch = {n: VMEM(weight_shape(n), bf16) for n in MIDDLE}
    scratch |= {
        "normal": VMEM((SEQ, D), f32),
        "inverse": VMEM((SEQ, 128), f32),
        "second_low": VMEM((SEQ, D), bf16),
        "activated": VMEM((SEQ, FF), bf16),
        "slope": VMEM((SEQ, FF), bf16),
        "tiles": VMEM((D // 128, SEQ + 16, 128), f32),
        "grouped": VMEM((THIRD, 3 * D), bf16),
        "up_rows": VMEM((THIRD, 3 * D), bf16),
        "branch_grad": VMEM((SEQ, D), bf16),
        "attended_grad": VMEM((SEQ, D), bf16),
        "parts": VMEM((5, 8, FF), f32),
        "output": VMEM((SEQ, D), bf16),
        "first_grad": VMEM((SEQ, D), f32),
        "mixed_grad": VMEM((SEQ, D), bf16),
        "sem": pltpu.SemaphoreType.DMA((len(MIDDLE),)),
        "out_sem": pltpu.SemaphoreType.DMA((3 + len(kept),)),
    }
    scratch |= {n + "_grad": VMEM(weight_shape(n), bf16) for n in kept}
    if linked:
        gather_pieces = split_pieces(
            [plan.span(n, n, VECTOR_ROWS) for n in ("pooling", "upsample")]
        )
        base = -plan.row["pooling"]
        pieces = split_pieces([plan.span("pooling", "upsample", base)])
        rows = plan.span("pooling", "upsample", base)[1]
        outs["blocks_out"] = (CUBE + (VECTOR_ROWS + plan.rows, 128), bf16, ANY)
        outs["partial"] = ((2, 2, rows, 128), bf16, ANY)
        scratch |= {
            "own": VMEM(CUBE + (rows, 128), bf16),
            "land": VMEM(CUBE + (rows, 128), bf16),
            "partial_sem": pltpu.SemaphoreType.DMA,
            "gather_send": pltpu.SemaphoreType.DMA((4 * COPIES,)),
            "gather_recv": pltpu.SemaphoreType.DMA((4 * COPIES,)),
            "send_sem": pltpu.SemaphoreType.DMA((2 * COPIES,)),
            "recv_sem": pltpu.SemaphoreType.DMA((2 * COPIES,)),
        }
        params = dict(
            collective_id=1,
            has_side_effects=True,
            alias={list(ins).index("blocks"): list(outs).index("blocks_out")},
        )

    def body(ref):
        def fetch(name):
            i = MIDDLE.index(name)
            if linked:
                load_weight(
                    plan, name, ref.blocks_out, getattr(ref, name), ref.sem.at[i], VECTOR_ROWS
                )
            else:
                pltpu.make_async_copy(
                    getattr(ref, name + "_full"), getattr(ref, name), ref.sem.at[i]
                ).start()

        gather_stage = scatter_stage = None
        if linked:
            gather = Gather(ref.blocks_out, gather_pieces, ref.gather_send, ref.gather_recv)
            scatter = Scatter(ref.own, ref.land, None, pieces, ref.send_sem, ref.recv_sem)
            partner_signal()

            def gather_stage(stage):
                for i in range(4):
                    gather.advance(i, stage, first=1)

            def scatter_stage(stage):
                for i in range(2):
                    scatter.advance(i, stage, last=3)

        for name in ("mixing", "expand", "contract"):
            fetch(name)
        if linked:
            partner_wait()
            gather_stage(1)
        else:
            fetch("pooling")
            fetch("upsample")

        outgoing = ["output", "first_grad", "mixed_grad"] + [n + "_grad" for n in kept]

        def send_out(name):
            return pltpu.make_async_copy(
                getattr(ref, name),
                getattr(ref, name + "_out"),
                ref.out_sem.at[outgoing.index(name)],
            )

        def at_step(i, number, action, *args):
            if linked:
                run_at(i, number, lambda: action(*args))

        def ready(name):
            wait_whole(getattr(ref, name), ref.sem.at[MIDDLE.index(name)])

        def get(name):
            return full(getattr(ref, name))

        def put(name, values):
            if name in summed:
                put_blocks(plan, name, ref.own, base, lambda columns: values[:, columns])
                return
            target = getattr(ref, name + "_grad")
            target[...] = values.astype(bf16).reshape(target.shape)
            send_out(name + "_grad").start()

        def third(start, k):
            return jnp.concatenate(
                [ref.tiles[t, pl.ds(start + k, THIRD, stride=3), :] for t in range(D // 128)],
                axis=1,
            )

        def put_third(start, k, values):
            for t in range(D // 128):
                ref.tiles[t, pl.ds(start + k, THIRD, stride=3), :] = values[
                    :, t * 128 : (t + 1) * 128
                ]

        def rows_of(rows):
            return jnp.concatenate([ref.tiles[t, rows, :] for t in range(D // 128)], axis=1)

        def put_rows(rows, values):
            for t in range(D // 128):
                ref.tiles[t, rows, :] = values[:, t * 128 : (t + 1) * 128]

        def shifted_rows(i):
            return pl.ds(pl.multiple_of(i * RB + 8, 8), RB)

        ref.parts[...] = jnp.zeros_like(ref.parts)
        ref.sums[...] = jnp.zeros_like(ref.sums)

        def add_part(slot, values):
            columns = values.shape[1]
            ref.parts[slot, :, :columns] += eight_rows(values)

        def put_sum(name, values):
            r = VECTOR_ROW[name]
            ref.sums[r : r + 1, : values.shape[1]] = values

        def put_part(name, slot):
            columns = VECTOR_SIZE[name]
            put_sum(name, jnp.sum(ref.parts[slot, :, :columns], axis=0, keepdims=True))

        for name in ("mixing", "expand", "contract"):
            ready(name)

        def forward(i, carry):
            rows = at_rows(i, RB)
            attended = nt(ref.mixed[rows, :], get("mixing")) + vec(ref.vectors, "mixing_bias")
            first = ref.tokens[rows, :].astype(f32) + attended
            normal, inverse = norm_parts(first)
            ref.normal[rows, :] = normal
            ref.inverse[rows, :] = jnp.broadcast_to(inverse, (RB, 128))
            low = (
                normal * vec(ref.vectors, "gain_two") + vec(ref.vectors, "shift_two")
            ).astype(bf16)
            ref.second_low[rows, :] = low
            inner = nt(low, get("expand")) + vec(ref.vectors, "hidden")
            phi = 0.5 * (1.0 + lax.erf(inner * 2.0 ** (-0.5)))
            act = (inner * phi).astype(bf16)
            ref.activated[rows, :] = act
            bell = jnp.exp(-0.5 * inner * inner) * (2.0 * math.pi) ** (-0.5)
            ref.slope[rows, :] = (phi + inner * bell).astype(bf16)
            block = first + nt(act, get("contract")) + vec(ref.vectors, "contract_bias")
            put_rows(shifted_rows(i), block)
            at_step(i, 1, gather_stage, 2)
            at_step(i, 4, gather_stage, 3)
            return carry

        lax.fori_loop(0, SEQ // RB, forward, 0)

        put_rows(slice(0, 8), jnp.zeros((8, D), f32))
        for k in range(3):
            ref.grouped[:, k * D : (k + 1) * D] = third(6, k).astype(bf16)
        if linked:
            gather_stage(4)
            fetch("pooling")
            fetch("upsample")
        ready("pooling")
        pooled = (
            nt(ref.grouped[...], get("pooling")) + vec(ref.vectors, "pooling_bias")
        ).astype(bf16)
        ready("upsample")
        for k in range(3):
            columns = slice(k * D, (k + 1) * D)
            upward = nt(pooled, get("upsample")[columns, :]) + vec(ref.vectors, "upsample_bias")[
                :, columns
            ]
            put_third(8, k, third(8, k) + upward)

        def write_output(i, carry):
            ref.output[at_rows(i, RB), :] = rows_of(shifted_rows(i)).astype(bf16)
            put_rows(shifted_rows(i), ref.cotangent[at_rows(i, RB), :].astype(f32))
            return carry

        lax.fori_loop(0, SEQ // RB, write_output, 0)

        send_out("output").start()

        for k in range(3):
            ref.up_rows[:, k * D : (k + 1) * D] = third(8, k).astype(bf16)
        up_rows = ref.up_rows[...]
        put_sum("upsample_bias", jnp.sum(up_rows.astype(f32), axis=0, keepdims=True))
        put("upsample", tn(up_rows, pooled))
        pooled_grad = nn(up_rows, get("upsample")).astype(bf16)
        put_sum("pooling_bias", jnp.sum(pooled_grad.astype(f32), axis=0, keepdims=True))
        put("pooling", tn(pooled_grad, ref.grouped[...]))
        for k in range(3):
            put_third(
                6, k, nn(pooled_grad, get("pooling")[:, k * D : (k + 1) * D])
            )
        put_rows(slice(SEQ + 6, SEQ + 8), jnp.zeros((2, D), f32))
        if linked:
            scatter_stage(0)

        def backward(i, carry):
            rows = at_rows(i, RB)
            block_grad = ref.cotangent[rows, :].astype(f32) + rows_of(shifted_rows(i))
            branch_grad = block_grad.astype(bf16)
            ref.branch_grad[rows, :] = branch_grad
            add_part(0, branch_grad.astype(f32))
            inner_grad = (nn(branch_grad, get("contract")) * ref.slope[rows, :].astype(f32)).astype(
                bf16
            )
            ref.slope[rows, :] = inner_grad
            add_part(1, inner_grad.astype(f32))
            second_grad = nn(inner_grad, get("expand"))
            normal = ref.normal[rows, :]
            add_part(2, second_grad * normal)
            add_part(3, second_grad)
            first_grad = block_grad + norm_backward(
                normal, ref.inverse[rows, :1], vec(ref.vectors, "gain_two"), second_grad
            )
            ref.first_grad[rows, :] = first_grad
            attended_grad = first_grad.astype(bf16)
            ref.attended_grad[rows, :] = attended_grad
            add_part(4, attended_grad.astype(f32))
            ref.mixed_grad[rows, :] = nn(attended_grad, get("mixing")).astype(bf16)
            at_step(i, 1, scatter_stage, 1)
            return carry

        lax.fori_loop(0, SEQ // RB, backward, 0)
        send_out("first_grad").start()
        send_out("mixed_grad").start()
        put_part("contract_bias", 0)
        put_part("hidden", 1)
        put_part("gain_two", 2)
        put_part("shift_two", 3)
        put_part("mixing_bias", 4)
        put("contract", tn(ref.branch_grad[...], ref.activated[...]))
        if linked:
            scatter_stage(2)
        put("expand", tn(ref.slope[...], ref.second_low[...]))
        put("mixing", tn(ref.attended_grad[...], ref.mixed[...]))
        if linked:
            scatter_stage(3)
            _, _, x, y, core = scatter.bits
            partial = pltpu.make_async_copy(
                ref.own.at[:, :, x, y, core], ref.partial, ref.partial_sem
            )
            partial.start()
            partial.wait()
            for i in range(4):
                gather.drain(i, first=1)
        for name in outgoing:
            send_out(name).wait()

    return call(body, ins, outs, scratch, **params)


BACK_FIRST = (0, 0, 0, 3, 0)
BACK_DURING = {
    1: ((0, 1),),
    4: ((1, 1),),
    5: ((3, 4),),
    6: ((0, 2), (2, 1)),
    9: ((0, 3), (1, 2)),
    11: ((2, 2),),
    13: ((0, 4), (1, 3)),
    15: ((2, 3),),
    17: ((1, 4),),
    19: ((2, 4),),
}


def back(plan, linked, ins):
    outs = {"token_grad": ((SEQ, D), f32, VMEM)}
    late_rows = ("tokens", "mixed_grad", "mixed", "value", "key", "query_u", "query_v", "first_grad")
    scratch = {
        "angles": VMEM((SEQ, D), f32),
        "key_table": VMEM((SEQ, 128 + D), bf16),
        "prob_grad": VMEM((2, QB, SEQ), f32),
        "total_grad": VMEM((2, QB, SEQ), bf16),
        "probs": VMEM((4, QB, PW), bf16),
        "key_acc": VMEM((128, SEQ), f32),
        "value_acc": VMEM((128, SEQ), f32),
        "joined_grad": VMEM((SEQ, 3 * D), bf16),
        "normed_low": VMEM((SEQ, D), bf16),
        "position_grad": VMEM((D, D), f32),
        "parts": VMEM((2, 8, D), f32),
        "all_sums": VMEM((16, FF), f32),
        "probs_sem": pltpu.SemaphoreType.DMA((4,)),
        "load_sem": pltpu.SemaphoreType.DMA((2,)),
        "row_sem": pltpu.SemaphoreType.DMA((len(late_rows),)),
    }
    scratch |= {n: VMEM((SEQ, D), f32 if n == "first_grad" else bf16) for n in late_rows}
    params = {}
    project_shape = plan.full_shape("project") if linked else (3 * D, D)
    position_shape = plan.full_shape("position") if linked else (D, D)
    scratch |= {"project": VMEM(project_shape, bf16), "position": VMEM(position_shape, bf16)}
    if linked:
        early_names = ("contract", "expand", "mixing")
        early = [plan.span(n, n, 0) for n in early_names]
        late = [plan.span("pooling", "upsample", 0), plan.span("project", "position", 0)]
        pieces = split_pieces(early + late)
        count = COPIES * len(pieces)
        own_rows = plan.rows
        outs["vector_out"] = ((8, 128), f32, VMEM)
        outs["flat_out"] = ((own_rows, 128), f32, ANY)
        scratch |= {
            "own": VMEM(CUBE + (own_rows, 128), bf16),
            "land": VMEM(CUBE + (own_rows, 128), bf16),
            "flat": VMEM((own_rows, 128), f32),
            "vector_own": VMEM(CUBE + (8, 128), f32),
            "land_dp": VMEM((3, 2, 2, 2, 8, 128), f32),
            "land_fsdp": VMEM((7, 8, 128), f32),
            "vector_sem": pltpu.SemaphoreType.DMA((4, 8)),
            "send_sem": pltpu.SemaphoreType.DMA((count,)),
            "recv_sem": pltpu.SemaphoreType.DMA((count,)),
            "own_sem": pltpu.SemaphoreType.DMA((4,)),
        }
        params = dict(collective_id=2, has_side_effects=True)
    else:
        outs["project_grad"] = ((3 * D, D), bf16, VMEM)
        outs["position_grad_out"] = ((D, D), bf16, VMEM)
        outs["sums_out"] = ((16, FF), f32, VMEM)

    def body(ref):
        def row_copy(name):
            return pltpu.make_async_copy(
                getattr(ref, name + "_in"), getattr(ref, name), ref.row_sem.at[late_rows.index(name)]
            )

        for name in late_rows[:7]:
            row_copy(name).start()
        if linked:
            load_weight(plan, "project", ref.blocks, ref.project, ref.load_sem.at[0], VECTOR_ROWS)
            load_weight(plan, "position", ref.blocks, ref.position, ref.load_sem.at[1], VECTOR_ROWS)
            matrix = Scatter(ref.own, ref.land, ref.flat, pieces, ref.send_sem, ref.recv_sem)
            vector = AxisScatter(
                ref.vector_own, ref.land_dp, ref.land_fsdp, ref.vector_out, ref.vector_sem
            )
            axis_signal()

            def run(events):
                for chunk, stage in events:
                    for piece in (2 * chunk, 2 * chunk + 1):
                        matrix.advance(piece, stage, first=BACK_FIRST[chunk])

            for i, name in enumerate(early_names):
                c = plan.shard[name][1]
                for y, core, row, column in plan.blocks(name, 0):
                    pltpu.make_async_copy(
                        getattr(ref, name + "_grad").at[:, :, :, :, pl.ds(column, 128)],
                        ref.own.at[:, :, :, y, core, pl.ds(row, c), :],
                        ref.own_sem.at[i],
                    ).start()
            _, _, x, y, core = matrix.bits
            row, rows = late[0]
            partial = pltpu.make_async_copy(
                ref.partial, ref.own.at[:, :, x, y, core, pl.ds(row, rows), :], ref.own_sem.at[3]
            )
            partial.start()
        else:
            for i, name in enumerate(("project", "position")):
                pltpu.make_async_copy(
                    getattr(ref, name + "_full"), getattr(ref, name), ref.load_sem.at[i]
                ).start()

        def in_copy(head, slot):
            return pltpu.make_async_copy(
                ref.probs_in.at[head], ref.probs.at[slot], ref.probs_sem.at[slot]
            )

        for e in range(2):
            in_copy(e, e).start()

        def table_of(rows, sine, cosine):
            ref.key_table[rows, 128 : 128 + HALF] = sine
            ref.key_table[rows, 128 + HALF :] = cosine

        expand_angles(ref.coarse, ref.angles, table_of)

        def norm_rows(rows):
            return norm_parts(ref.tokens[rows, :].astype(f32))

        def low_rows(i, carry):
            rows = at_rows(i, RB)
            normal, _ = norm_rows(rows)
            ref.normed_low[rows, :] = (
                normal * vec(ref.vectors, "gain_one") + vec(ref.vectors, "shift_one")
            ).astype(bf16)
            return carry

        row_copy("tokens").wait()
        lax.fori_loop(0, SEQ // RB, low_rows, 0)
        ref.all_sums[...] = ref.sums[...]
        ref.parts[...] = jnp.zeros_like(ref.parts)
        if linked:
            axis_wait()
            partial.wait()
            run([(3, 3)])
            for i, name in enumerate(early_names):
                row, rows = plan.span(name, name, 0)
                whole = ref.own.at[:, :, :, :, :, pl.ds(row, rows), :]
                wait_whole(whole, ref.own_sem.at[i])
                run([(i, 0)])
        wait_whole(ref.project, ref.load_sem.at[0])
        wait_whole(ref.position, ref.load_sem.at[1])
        position = ref.position.reshape(D, D)
        for name in late_rows[1:7]:
            row_copy(name).wait()
        row_copy("first_grad").start()

        def pair(hp, carry):
            start = pl.multiple_of(hp * 128, 128)
            lanes = pl.ds(start, 128)
            base = lax.rem(hp, 2) * 2
            for e in range(2):
                in_copy(0, base + e).wait()

            @pl.when(hp < HEADS // 2 - 1)
            def _():
                for e in range(2):
                    in_copy(hp * 2 + 2 + e, 2 - base + e).start()

            ref.key_table[:, :128] = ref.key[:, lanes]
            content_sum = jnp.zeros((1, 128), f32)
            position_sum = jnp.zeros((1, 128), f32)
            for b in range(BLOCKS):
                row, width = b * QB, (b + 1) * QB
                rows = slice(row, row + QB)
                span = slice(POFF[b], POFF[b] + width)
                by_content, by_position = [], None
                for e in range(2):
                    upstream = keep_head(ref.mixed_grad[rows, lanes], e)
                    row_dot = jnp.sum(
                        upstream.astype(f32) * ref.mixed[rows, lanes].astype(f32),
                        axis=1,
                        keepdims=True,
                    )
                    ref.prob_grad[e, :, :width] = nt(upstream, ref.value[:width, lanes]) - row_dot
                    for sub in range(QB // SB):
                        used = row + (sub + 1) * SB
                        for g in range(SB // CH):
                            at = slice(sub * SB + g * CH, sub * SB + (g + 1) * CH)
                            p = ref.probs[base + e, at, POFF[b] : POFF[b] + used].astype(f32)
                            ref.total_grad[e, at, :used] = (
                                p * ref.prob_grad[e, at, :used] * HEAD_DIM ** (-0.5)
                            ).astype(bf16)
                        if used < width:
                            ref.total_grad[e, sub * SB : (sub + 1) * SB, used:width] = jnp.zeros(
                                (SB, width - used), bf16
                            )
                    scored = ref.total_grad[e, :, :width]
                    turned = nn(scored, ref.key_table[:width, :])
                    by_content.append(turned[:, :128])
                    low, high = rotate(
                        turned[:, 128:], ref.angles[rows, :HALF], ref.angles[rows, HALF:]
                    )
                    spread = jnp.concatenate([low, high], axis=1).astype(bf16)
                    own = (lax.broadcasted_iota(jnp.int32, (128, D), 0) // HEAD_DIM) == e
                    part = nt(spread, jnp.where(own, position[lanes, :], 0).astype(bf16))
                    by_position = part if by_position is None else by_position + part
                    part = tn(keep_head(ref.query_v[rows, lanes], e), spread)
                    if b == 0 and e == 0:
                        ref.position_grad[lanes, :] = part
                    else:
                        ref.position_grad[lanes, :] += part
                    to_key = tn(keep_head(ref.query_u[rows, lanes], e), scored)
                    to_value = tn(upstream, ref.probs[base + e, :, span])
                    if e == 0:
                        if b > 0:
                            ref.key_acc[:, :row] += to_key[:, :row]
                            ref.value_acc[:, :row] += to_value[:, :row]
                        ref.key_acc[:, row:width] = to_key[:, row:]
                        ref.value_acc[:, row:width] = to_value[:, row:]
                    else:
                        ref.key_acc[:, :width] += to_key
                        ref.value_acc[:, :width] += to_value
                    for when, events in BACK_DURING.items():
                        if linked and when % 6 == b * 2 + e:
                            run_at(hp, when // 6, lambda events=events: run(events))
                by_content = jnp.where(head_lanes(QB, 0), by_content[0], by_content[1])
                ref.joined_grad[rows, lanes] = (by_content + by_position).astype(bf16)
                content_sum += jnp.sum(by_content, axis=0, keepdims=True)
                position_sum += jnp.sum(by_position, axis=0, keepdims=True)
            ref.joined_grad[:, pl.ds(start + D, 128)] = ref.key_acc[...].T.astype(bf16)
            ref.joined_grad[:, pl.ds(start + 2 * D, 128)] = ref.value_acc[...].T.astype(bf16)
            r = VECTOR_ROW["content"]
            ref.all_sums[r : r + 1, lanes] = content_sum
            r = VECTOR_ROW["position_bias"]
            ref.all_sums[r : r + 1, lanes] = position_sum
            return carry

        lax.fori_loop(0, HEADS // 2, pair, 0)

        row_copy("first_grad").wait()
        for part in range(3):
            columns = slice(part * D, (part + 1) * D)
            grad = tn(ref.joined_grad[:, columns], ref.normed_low[...]).astype(bf16)
            if linked:
                ref.project_full[columns, :] = grad
            else:
                ref.project_grad[columns, :] = grad
        if linked:
            put_blocks(plan, "project", ref.own, 0, lambda columns: ref.project_full[:, columns])
            put_blocks(plan, "position", ref.own, 0, lambda columns: ref.position_grad[:, columns])
            run([(4, 0)])
        else:
            ref.position_grad_out[...] = ref.position_grad[...].astype(bf16)

        def norm_back(i, carry):
            rows = at_rows(i, RB)
            normal, inverse = norm_rows(rows)
            upstream = nn(ref.joined_grad[rows, :], full(ref.project))
            ref.parts[0, :, :] += eight_rows(upstream * normal)
            ref.parts[1, :, :] += eight_rows(upstream)
            ref.token_grad[rows, :] = ref.first_grad[rows, :] + norm_backward(
                normal, inverse, vec(ref.vectors, "gain_one"), upstream
            )
            if linked:
                run_at(i, 3, lambda: run([(4, 1)]))
            return carry

        lax.fori_loop(0, SEQ // RB, norm_back, 0)
        for slot, name in enumerate(("gain_one", "shift_one")):
            r = VECTOR_ROW[name]
            ref.all_sums[r : r + 1, :D] = jnp.sum(ref.parts[slot], axis=0, keepdims=True)
        if linked:
            pack_vectors(ref.all_sums, ref.vector_own)
            vector.first()
            run([(4, 2)])
            vector.second()
            run([(4, 3)])
            vector.last()
            run([(4, 4)])
            done = pltpu.make_async_copy(ref.flat, ref.flat_out, ref.own_sem.at[0])
            done.start()
            done.wait()
        else:
            ref.sums_out[...] = ref.all_sums[...]

    if linked:
        scratch["project_full"] = VMEM((3 * D, D), bf16)
    return call(body, ins, outs, scratch, **params)


PARTS = 4


def finish(plan, flat, vectors, rows):
    outs = {n + "_out": (plan.held_shape(n), f32, VMEM) for n in WEIGHTS}
    outs |= {n + "_out": ((VECTOR_SIZE[n] // 32,), f32, VMEM) for n in VECTORS}
    outs |= {n + "_copy": (v.shape, v.dtype, ANY) for n, v in rows.items()}
    ins = {"flat": (flat, VMEM), "vectors": (vectors, VMEM)}
    ins |= {n: (v, ANY) for n, v in rows.items()}
    scratch = {n + "_held": VMEM(v.shape, v.dtype) for n, v in rows.items()}
    scratch["in_sem"] = pltpu.SemaphoreType.DMA((len(rows) * PARTS,))
    scratch["out_sem"] = pltpu.SemaphoreType.DMA((len(rows) * PARTS,))

    def body(ref):
        loads, copies = [], []
        for n in rows:
            for part in range(PARTS):
                at = pl.ds(part * (SEQ // PARTS), SEQ // PARTS)
                held = getattr(ref, n + "_held").at[at]
                slot = len(loads)
                loads.append(
                    pltpu.make_async_copy(getattr(ref, n).at[at], held, ref.in_sem.at[slot])
                )
                copies.append(
                    pltpu.make_async_copy(
                        held, getattr(ref, n + "_copy").at[at], ref.out_sem.at[slot]
                    )
                )
        for load in loads:
            load.start()
        for load, copy in zip(loads, copies):
            load.wait()
            copy.start()
        for name in WEIGHTS:
            put_shard(plan, name, ref.flat, 0, getattr(ref, name + "_out"))
        for name, (line, offset, size) in vector_places().items():
            getattr(ref, name + "_out")[...] = ref.vectors[line, offset : offset + size]
        for copy in copies:
            copy.wait()

    return call(body, ins, outs, scratch)


def make_local(dp, fsdp):
    plan = Plan(dp, fsdp)
    linked = (dp, fsdp) == (4, 8)

    def gathered(weights):
        out = {}
        for name, shard in zip(WEIGHTS, weights):
            part = lax.all_gather(shard, "dp", axis=0, tiled=True)
            out[name + "_full"] = lax.all_gather(part, "fsdp", axis=1, tiled=True).T
        return out

    def gathered_vectors(vectors):
        rows = []
        for name, shard in zip(VECTORS, vectors):
            whole = lax.all_gather(shard, ("dp", "fsdp"), axis=0, tiled=True).astype(f32)
            rows.append(jnp.pad(whole, (0, FF - VECTOR_SIZE[name])))
        rows += [jnp.zeros((FF,), f32)] * (16 - len(rows))
        return jnp.stack(rows)

    def local(tokens, cotangent, *params):
        assert tokens.shape[0] == SEQ
        weights, vectors = params[:7], params[7:]
        given = dict(zip(VECTORS, vectors))
        coarse = coarse_angles()
        ins = {"tokens": (tokens, VMEM), "coarse": (coarse, VMEM)}
        if linked:
            ins |= {n + "_shard": (given[n], VMEM) for n in VECTORS}
            for n, w in zip(WEIGHTS, weights):
                ins[n + "_shard"] = (w.T if w.shape[1] % 128 else w, VMEM)
        else:
            whole = gathered(weights)
            ins["given_vectors"] = (gathered_vectors(vectors), VMEM)
            ins["project"] = (whole["project_full"], VMEM)
            ins["position"] = (whole["position_full"], VMEM)
        one = front(plan, linked, ins)

        ins = {
            "tokens": (tokens, VMEM),
            "cotangent": (cotangent, VMEM),
            "mixed": (one.mixed_out, VMEM),
            "vectors": (one.vectors, VMEM),
        }
        if linked:
            ins["blocks"] = (one.blocks, ANY)
        else:
            ins |= {n + "_full": (whole[n + "_full"], ANY) for n in MIDDLE}
        two = middle(plan, linked, ins)

        ins = {
            "tokens_in": (tokens, ANY),
            "coarse": (coarse, VMEM),
            "vectors": (one.vectors, VMEM),
            "query_u_in": (one.query_u_out, ANY),
            "query_v_in": (one.query_v_out, ANY),
            "key_in": (one.key_out, ANY),
            "value_in": (one.value_out, ANY),
            "mixed_in": (one.mixed_out, ANY),
            "mixed_grad_in": (two.mixed_grad_out, ANY),
            "first_grad_in": (two.first_grad_out, ANY),
            "sums": (two.sums, VMEM),
            "probs_in": (one.probs_out, ANY),
        }
        if linked:
            ins["blocks"] = (two.blocks_out, ANY)
            for n in ("contract", "expand", "mixing"):
                ins[n + "_grad"] = (getattr(two, n + "_grad_out"), ANY)
            ins["partial"] = (two.partial, ANY)
        else:
            ins |= {n + "_full": (whole[n + "_full"], ANY) for n in ("project", "position")}
        three = back(plan, linked, ins)

        if linked:
            last = finish(
                plan,
                three.flat_out,
                three.vector_out,
                {"output": two.output_out, "token_grad": three.token_grad},
            )
            output, token_grad = last.output_copy, last.token_grad_copy
            matrices = []
            for n in WEIGHTS:
                grad = getattr(last, n + "_out")
                matrices.append(grad if grad.shape == plan.shard[n] else grad.T)
            small = [getattr(last, n + "_out") for n in VECTORS]
        else:
            output, token_grad = two.output_out, three.token_grad
            grads = {n: getattr(two, n + "_grad_out") for n in MIDDLE}
            grads["project"] = three.project_grad
            grads["position"] = three.position_grad_out
            matrices = []
            for name in WEIGHTS:
                part = lax.psum_scatter(
                    grads[name].T, "fsdp", scatter_dimension=1, tiled=True
                )
                part = lax.psum_scatter(part, "dp", scatter_dimension=0, tiled=True)
                matrices.append(part.astype(f32))
            small = []
            for name in VECTORS:
                sums = three.sums_out[VECTOR_ROW[name], : VECTOR_SIZE[name]]
                small.append(
                    lax.psum_scatter(sums, ("dp", "fsdp"), scatter_dimension=0, tiled=True)
                )
        return (output, token_grad, *matrices, *small)

    return local


def solution(mesh):
    rows = P(("dp", "fsdp"), None)
    matrix = P("dp", "fsdp")
    vector = P(("dp", "fsdp"))
    return jax.shard_map(
        make_local(mesh.shape["dp"], mesh.shape["fsdp"]),
        mesh=mesh,
        in_specs=(rows,) * 2 + (matrix,) * 7 + (vector,) * 11,
        out_specs=(rows,) * 2 + (matrix,) * 7 + (vector,) * 11,
        check_vma=False,
    )
```

```python
import math
from types import SimpleNamespace

import jax
import jax.numpy as jnp
from jax import lax
from jax.experimental import pallas as pl
from jax.experimental.pallas import tpu as pltpu
from jax.sharding import PartitionSpec as P

D = 512
HALF = D // 2
HEADS = 8
HEAD_DIM = 64
FF = 2048
SEQ = 1152
THIRD = SEQ // 3
QB = 384
SB = 128
CH = 16
RB = 192
BLOCKS = SEQ // QB
POFF = [sum((b + 1) * QB for b in range(n)) for n in range(BLOCKS + 1)]
PW = POFF[BLOCKS]
EXP_SCALE = HEAD_DIM ** (-0.5) * math.log2(math.e)
ANGLE_STEP = 32
epsilon = 1e-05
bf16 = jnp.bfloat16
f32 = jnp.float32
MESH = pl.DeviceIdType.MESH
VMEM_LIMIT = 63 << 20

WEIGHTS = ("project", "position", "mixing", "expand", "contract", "pooling", "upsample")
WEIGHT_SHAPE = {
    "project": (D, 3 * D),
    "position": (D, D),
    "mixing": (D, D),
    "expand": (D, FF),
    "contract": (FF, D),
    "pooling": (3 * D, D),
    "upsample": (D, 3 * D),
}
VECTORS = (
    "gain_one",
    "shift_one",
    "content",
    "position_bias",
    "mixing_bias",
    "gain_two",
    "shift_two",
    "hidden",
    "contract_bias",
    "pooling_bias",
    "upsample_bias",
)
VECTOR_SIZE = {n: D for n in VECTORS} | {"hidden": FF, "upsample_bias": 3 * D}
VECTOR_ROW = {n: i for i, n in enumerate(VECTORS)}
PACKED_VECTORS = ("hidden", "upsample_bias", "gain_one") + tuple(
    n for n in VECTORS if n not in ("hidden", "upsample_bias", "gain_one")
)


def nn(a, b):
    return lax.dot_general(a, b, (((1,), (0,)), ((), ())), preferred_element_type=f32)


def nt(a, b):
    return lax.dot_general(a, b, (((1,), (1,)), ((), ())), preferred_element_type=f32)


def tn(a, b):
    return lax.dot_general(a, b, (((0,), (0,)), ((), ())), preferred_element_type=f32)


def at_rows(step, rows):
    return pl.ds(pl.multiple_of(step * rows, rows), rows)


def eight_rows(values):
    rows, columns = values.shape
    return jnp.sum(values.reshape(rows // 8, 8, columns), axis=0)


def call(body, ins, outs, scratch, alias=None, **params):
    names = [*ins, *outs, *scratch]

    def kernel(*refs):
        body(SimpleNamespace(**dict(zip(names, refs))))

    results = pl.pallas_call(
        kernel,
        out_shape=[jax.ShapeDtypeStruct(s, t) for s, t, _ in outs.values()],
        in_specs=[pl.BlockSpec(memory_space=m) for _, m in ins.values()],
        out_specs=[pl.BlockSpec(memory_space=m) for _, _, m in outs.values()],
        scratch_shapes=list(scratch.values()),
        input_output_aliases=alias or {},
        compiler_params=pltpu.CompilerParams(vmem_limit_bytes=VMEM_LIMIT, **params),
    )(*[a for a, _ in ins.values()])
    return SimpleNamespace(**dict(zip(outs, results)))


VMEM = pltpu.VMEM
ANY = pl.ANY


BIT_AXIS = ("fsdp", "fsdp", "fsdp", "dp", "dp")
BIT_MASK = (4, 2, 1, 2, 1)
CUBE = (2,) * 5
GATHER_ORDER = ((2, 3, 4), (3, 2, 4))
SCATTER_ORDER = ((4, 3, 2), (4, 2, 3))
STAGES = 4
COPIES = 6


def my_bits():
    fs = lax.axis_index("fsdp")
    dp = lax.axis_index("dp")
    return (
        lax.rem(fs // 4, 2),
        lax.rem(fs // 2, 2),
        lax.rem(fs, 2),
        lax.rem(dp // 2, 2),
        lax.rem(dp, 2),
    )


def partner(*flipped):
    place = {"fsdp": lax.axis_index("fsdp"), "dp": lax.axis_index("dp")}
    bits = my_bits()
    for bit in flipped:
        place[BIT_AXIS[bit]] += BIT_MASK[bit] * (1 - 2 * bits[bit])
    return (place["dp"], place["fsdp"])


LINE_FLIPS = ((1,), (0,), (0, 1))


def flipped_bits(flips):
    return tuple(1 - b if k in flips else b for k, b in enumerate(my_bits()))


def partner_signal():
    sem = pltpu.get_barrier_semaphore()
    for flips in LINE_FLIPS + ((2,), (3,), (4,)):
        pl.semaphore_signal(sem, inc=1, device_id=partner(*flips), device_id_type=MESH)


def partner_wait():
    pl.semaphore_wait(pltpu.get_barrier_semaphore(), 6)


def run_at(step, number, action):
    if isinstance(step, int):
        if step == number:
            action()
        return

    @pl.when(step == number)
    def _():
        action()


class Gather:
    def __init__(self, buf, pieces, send_sem, recv_sem, mine=None):
        self.buf, self.pieces, self.mine = buf, pieces, mine
        self.send_sem, self.recv_sem = send_sem, recv_sem
        self.bits = my_bits()

    def copy(self, source, target, sem, device):
        return pltpu.make_async_remote_copy(
            src_ref=source,
            dst_ref=target,
            send_sem=self.send_sem.at[sem],
            recv_sem=self.recv_sem.at[sem],
            device_id=device,
            device_id_type=MESH,
        )

    def copies(self, i, stage):
        row, rows, kind = self.pieces[i]
        part = (pl.ds(row, rows),)
        if stage == 0:
            target = self.buf.at[self.bits + part]
            source = target if self.mine is None else self.mine.at[part]
            return [
                self.copy(source, target, i * COPIES + n, partner(*flips))
                for n, flips in enumerate(LINE_FLIPS)
            ]
        order = GATHER_ORDER[kind]
        free = (0, 1) + order[: stage - 1]
        index = tuple(slice(None) if k in free else self.bits[k] for k in range(5))
        ref = self.buf.at[index + part]
        return [self.copy(ref, ref, i * COPIES + 2 + stage, partner(order[stage - 1]))]

    def advance(self, i, stage, first=0, last=STAGES):
        if stage > first:
            for copy in self.copies(i, stage - 1):
                copy.wait_recv()
        if stage < last:
            for copy in self.copies(i, stage):
                copy.start()

    def drain(self, i, first=0, last=STAGES):
        for stage in range(first, last):
            for copy in self.copies(i, stage):
                copy.wait_send()


class Scatter:
    def __init__(self, own, land, out, pieces, send_sem, recv_sem):
        self.own, self.land, self.out, self.pieces = own, land, out, pieces
        self.send_sem, self.recv_sem = send_sem, recv_sem
        self.bits = my_bits()

    def index(self, order, stage, side):
        out = []
        for k in range(5):
            if k in order[:stage]:
                out.append(1 - self.bits[k] if side in ("land", "target") else self.bits[k])
            elif k in order[stage : stage + 1]:
                out.append(1 - self.bits[k] if side in ("send", "target") else self.bits[k])
            else:
                out.append(slice(None))
        return tuple(out)

    def copy(self, source, target, sem, device):
        return pltpu.make_async_remote_copy(
            src_ref=source,
            dst_ref=target,
            send_sem=self.send_sem.at[sem],
            recv_sem=self.recv_sem.at[sem],
            device_id=device,
            device_id_type=MESH,
        )

    def copies(self, i, stage):
        row, rows, kind = self.pieces[i]
        order = SCATTER_ORDER[kind]
        part = (pl.ds(row, rows),)
        if stage == 3:
            place = self.bits[:2] + tuple(1 - b for b in self.bits[2:])
            return [
                self.copy(
                    self.own.at[flipped_bits(flips) + part],
                    self.land.at[place + part],
                    i * COPIES + 3 + n,
                    partner(*flips),
                )
                for n, flips in enumerate(LINE_FLIPS)
            ]
        return [
            self.copy(
                self.own.at[self.index(order, stage, "send") + part],
                self.land.at[self.index(order, stage, "target") + part],
                i * COPIES + stage,
                partner(order[stage]),
            )
        ]

    def add(self, i, stage):
        row, rows, kind = self.pieces[i]
        order = SCATTER_ORDER[kind]
        part = (pl.ds(row, rows), slice(None))
        if stage == 3:
            total = self.own[self.bits + part].astype(f32)
            for flips in LINE_FLIPS:
                place = flipped_bits(flips)[:2] + tuple(1 - b for b in self.bits[2:])
                total = total + self.land[place + part].astype(f32)
            self.out[pl.ds(row, rows), :] = total
            return
        mine = self.own.at[self.index(order, stage, "own")]
        came = self.land.at[self.index(order, stage, "land")]
        free = 4 - stage

        def body(j, carry):
            at = tuple(lax.rem(j // 2 ** (free - 1 - q), 2) for q in range(free)) + part
            mine[at] = mine[at] + came[at]
            return carry

        lax.fori_loop(0, 2**free, body, 0)

    def advance(self, i, stage, first=0, last=STAGES):
        if stage > first:
            for copy in self.copies(i, stage - 1):
                copy.wait()
            self.add(i, stage - 1)
        if stage < last:
            for copy in self.copies(i, stage):
                copy.start()


def split_pieces(chunks):
    pieces = []
    for row, rows in chunks:
        half = (rows // 2 + 15) // 16 * 16
        pieces.append((row, half, 0))
        pieces.append((row + half, rows - half, 1))
    return pieces


class AxisScatter:
    def __init__(self, own, land_dp, land_fsdp, out, sems):
        self.own, self.land_dp, self.land_fsdp, self.out = own, land_dp, land_fsdp, out
        self.sems = sems
        self.fs, self.dp = lax.axis_index("fsdp"), lax.axis_index("dp")

    def bits(self, fs, dp):
        return (lax.rem(fs // 4, 2), lax.rem(fs // 2, 2), lax.rem(fs, 2)), (
            lax.rem(dp // 2, 2),
            lax.rem(dp, 2),
        )

    def dp_copy(self, step):
        other = lax.rem(self.dp + step, 4)
        _, (y, core) = self.bits(self.fs, other)
        return pltpu.make_async_remote_copy(
            src_ref=self.own.at[:, :, :, y, core],
            dst_ref=self.land_dp.at[step - 1],
            send_sem=self.sems.at[0, step],
            recv_sem=self.sems.at[1, step],
            device_id=(other, self.fs),
            device_id_type=MESH,
        )

    def fsdp_copy(self, step):
        other = lax.rem(self.fs + step, 8)
        (zh, zl, x), (y, core) = self.bits(other, self.dp)
        return pltpu.make_async_remote_copy(
            src_ref=self.own.at[zh, zl, x, y, core],
            dst_ref=self.land_fsdp.at[step - 1],
            send_sem=self.sems.at[2, step],
            recv_sem=self.sems.at[3, step],
            device_id=(self.dp, other),
            device_id_type=MESH,
        )

    def first(self):
        for step in range(1, 4):
            self.dp_copy(step).start()

    def second(self):
        for step in range(1, 4):
            self.dp_copy(step).wait()
        _, (y, core) = self.bits(self.fs, self.dp)
        mine = self.own.at[:, :, :, y, core]
        mine[...] = mine[...] + self.land_dp[0] + self.land_dp[1] + self.land_dp[2]
        for step in range(1, 8):
            self.fsdp_copy(step).start()

    def last(self):
        for step in range(1, 8):
            self.fsdp_copy(step).wait()
        (zh, zl, x), (y, core) = self.bits(self.fs, self.dp)
        total = self.own[zh, zl, x, y, core]
        for step in range(7):
            total = total + self.land_fsdp[step]
        self.out[...] = total


def axis_signal():
    fs, dp = lax.axis_index("fsdp"), lax.axis_index("dp")
    sem = pltpu.get_barrier_semaphore()
    for step in range(1, 4):
        to = (lax.rem(dp + step, 4), fs)
        pl.semaphore_signal(sem, inc=1, device_id=to, device_id_type=MESH)
    for step in range(1, 8):
        to = (dp, lax.rem(fs + step, 8))
        pl.semaphore_signal(sem, inc=1, device_id=to, device_id_type=MESH)


def axis_wait():
    pl.semaphore_wait(pltpu.get_barrier_semaphore(), 10)


class Plan:
    def __init__(self, dp, fsdp):
        self.shard = {n: (WEIGHT_SHAPE[n][0] // dp, WEIGHT_SHAPE[n][1] // fsdp) for n in WEIGHTS}
        self.row, at = {}, 0
        for name in WEIGHTS:
            self.row[name] = at
            at += self.shard[name][0] * self.shard[name][1] // 128
        self.rows = at

    def span(self, first, last, shift):
        r, c = self.shard[last]
        end = self.row[last] + r * c // 128
        return (self.row[first] + shift, end - self.row[first])

    def full_shape(self, name):
        return (2, 2, 2, self.shard[name][1], WEIGHT_SHAPE[name][0])

    def held_shape(self, name):
        r, c = self.shard[name]
        return (c, r) if c % 128 else (r, c)

    def blocks(self, name, shift):
        r, c = self.shard[name]
        return [
            (y, core, shift + self.row[name] + q * c, (y * 2 + core) * r + q * 128)
            for y in range(2)
            for core in range(2)
            for q in range(r // 128)
        ]


def put_blocks(plan, name, own, shift, values_of):
    c = plan.shard[name][1]
    for y, core, at, column in plan.blocks(name, shift):
        values = values_of(slice(column, column + 128)).astype(bf16)
        own[:, :, :, y, core, at : at + c, :] = values.reshape(2, 2, 2, c, 128)


def put_shard(plan, name, flat, shift, target):
    r, c = plan.shard[name]
    for q in range(r // 128):
        at = shift + plan.row[name] + q * c
        if c % 128:
            target[:, q * 128 : (q + 1) * 128] = flat[at : at + c, :]
        else:
            target[q * 128 : (q + 1) * 128, :] = flat[at : at + c, :].T


def load_weight(plan, name, buf, target, sem, shift):
    c = plan.shard[name][1]
    for y, core, row, column in plan.blocks(name, shift):
        pltpu.make_async_copy(
            buf.at[:, :, :, y, core, pl.ds(row, c), :],
            target.at[:, :, :, :, pl.ds(column, 128)],
            sem,
        ).start()


def wait_whole(target, sem):
    pltpu.make_async_copy(target, target, sem).wait()


def full(ref):
    values = ref[...]
    return values.reshape(-1, values.shape[-1])


def vector_places():
    places, at = {}, 0
    for name in PACKED_VECTORS:
        size = VECTOR_SIZE[name] // 32
        places[name] = (at // 128, at % 128, size)
        at += size
    return places


def block_owner(columns, size):
    row = lax.broadcasted_iota(jnp.int32, (32, columns), 0)
    lane = lax.broadcasted_iota(jnp.int32, (32, columns), 1)
    return lane // size == lax.rem(row, 4) * 8 + row // 4


def unpack_vectors(blocks, target):
    flat = blocks[...].reshape(32 * 16, 128)
    for name, (line, offset, size) in vector_places().items():
        columns = VECTOR_SIZE[name]
        row = lax.broadcasted_iota(jnp.int32, (32, 512), 0)
        lane = lax.broadcasted_iota(jnp.int32, (32, 512), 1)
        pick = (lane == row * 16 + line).astype(bf16)
        own = nn(pick, flat).astype(bf16)
        source = lax.broadcasted_iota(jnp.int32, (128, columns), 0)
        lane = lax.broadcasted_iota(jnp.int32, (128, columns), 1)
        spread = (source - offset == lax.rem(lane, size)).astype(bf16)
        spread_own = jnp.where(block_owner(columns, size), nn(own, spread), 0.0)
        r = VECTOR_ROW[name]
        target[r : r + 1, :columns] = jnp.sum(spread_own, axis=0, keepdims=True)


def pack_vectors(source, target):
    lines = [jnp.zeros((32, 128), f32), jnp.zeros((32, 128), f32)]
    for name, (line, offset, size) in vector_places().items():
        columns = VECTOR_SIZE[name]
        r = VECTOR_ROW[name]
        values = jnp.broadcast_to(source[r : r + 1, :columns], (32, columns))
        values = jnp.where(block_owner(columns, size), values, 0.0)
        lane = lax.broadcasted_iota(jnp.int32, (columns, 128), 0)
        goal = lax.broadcasted_iota(jnp.int32, (columns, 128), 1)
        gather = (goal - offset == lax.rem(lane, size)).astype(bf16)
        for _ in range(3):
            term = values.astype(bf16)
            lines[line] += nn(term, gather)
            values = values - term.astype(f32)
    both = jnp.concatenate([lines[0][:, None, :], lines[1][:, None, :]], axis=1)
    both = jnp.concatenate([both, jnp.zeros((32, 6, 128), f32)], axis=1)
    target[...] = both.reshape(CUBE + (8, 128))


def coarse_angles():
    ratios = jnp.arange(0, D, 2).astype(f32) / D
    inverse = 1.0 / 10000.0**ratios
    steps = SEQ // ANGLE_STEP
    places = jnp.concatenate(
        [jnp.arange(steps) * ANGLE_STEP, jnp.zeros((-steps % 8,), jnp.int32), jnp.arange(ANGLE_STEP)]
    ).astype(f32)
    angles = places[:, None] * inverse[None, :]
    return jnp.concatenate([jnp.sin(angles), jnp.cos(angles)], axis=1)


def expand_angles(coarse, angles, table_of):
    steps = SEQ // ANGLE_STEP
    start = steps + -steps % 8

    def body(q, carry):
        high_sin, high_cos = coarse[pl.ds(q, 1), :HALF], coarse[pl.ds(q, 1), HALF:]
        low_sin, low_cos = coarse[start:, :HALF], coarse[start:, HALF:]
        sine = high_sin * low_cos + high_cos * low_sin
        cosine = high_cos * low_cos - high_sin * low_sin
        rows = at_rows(q, ANGLE_STEP)
        angles[rows, :HALF] = sine
        angles[rows, HALF:] = cosine
        table_of(rows, sine.astype(bf16), cosine.astype(bf16))
        return carry

    lax.fori_loop(0, steps, body, 0)


def head_lanes(rows, head):
    return (lax.broadcasted_iota(jnp.int32, (rows, 128), 1) // HEAD_DIM) == head


def keep_head(values, head):
    return jnp.where(head_lanes(values.shape[0], head), values, 0).astype(bf16)


def rotate(pair, sines, cosines):
    low, high = pair[:, :HALF], pair[:, HALF:]
    return high * sines - low * cosines, low * sines + high * cosines


def norm_parts(values):
    row_mean = jnp.mean(values, axis=-1, keepdims=True)
    centred = values - row_mean
    variance = jnp.mean(centred * centred, axis=-1, keepdims=True)
    inv_std = lax.rsqrt(variance + epsilon)
    return centred * inv_std, inv_std


def norm_backward(normal, inv_std, gain, upstream):
    scaled = upstream * gain
    scaled_mean = jnp.mean(scaled, axis=-1, keepdims=True)
    cross_mean = jnp.mean(scaled * normal, axis=-1, keepdims=True)
    return inv_std * (scaled - scaled_mean - normal * cross_mean)


def vec(ref, name):
    r = VECTOR_ROW[name]
    return ref[r : r + 1, : VECTOR_SIZE[name]]


VECTOR_ROWS = 16


FRONT_ROWS = ("query_u", "query_v", "key", "value", "mixed")
CHUNK_LAST = (4, 4, 4, 4, 1, 1)
FIRST = ((0, 0), (1, 0))
BEFORE = ((0, 1), (1, 1), (2, 0), (0, 2), (1, 2), (0, 3), (1, 3), (2, 1), (3, 0), (0, 4), (1, 4))
AFTER = ((2, 2), (3, 1), (4, 0), (5, 0))
DURING = {
    8: ((2, 3), (3, 2), (4, 1), (5, 1)),
    16: ((3, 3),),
    23: ((2, 4), (3, 4)),
}


def front(plan, linked, ins):
    outs = {
        "vectors": ((16, FF), f32, VMEM),
    }
    outs |= {n + "_out": ((SEQ, D), bf16, ANY) for n in FRONT_ROWS}
    outs |= {
        "probs_out": ((HEADS, QB, PW), bf16, ANY),
    }
    scratch = {
        "normal": VMEM((SEQ, D), f32),
        "angles": VMEM((SEQ, D), f32),
        "key_table": VMEM((SEQ, 128 + D), bf16),
        "score": VMEM((2, QB, SEQ), f32),
        "turned": VMEM((2, QB, 128 + D), bf16),
        "probs": VMEM((2, QB, PW), bf16),
        "probs_sem": pltpu.SemaphoreType.DMA((2,)),
        "out_sem": pltpu.SemaphoreType.DMA((len(FRONT_ROWS),)),
    }
    scratch |= {n: VMEM((SEQ, D), bf16) for n in FRONT_ROWS}
    params = {}
    if linked:
        rows = VECTOR_ROWS + plan.rows
        chunks = [
            (0, 128),
            (128, VECTOR_ROWS + plan.span("project", "position", 0)[1] - 128),
            plan.span("mixing", "expand", VECTOR_ROWS),
            plan.span("contract", "contract", VECTOR_ROWS),
            plan.span("pooling", "pooling", VECTOR_ROWS),
            plan.span("upsample", "upsample", VECTOR_ROWS),
        ]
        pieces = split_pieces(chunks)
        outs["blocks"] = (CUBE + (rows, 128), bf16, ANY)
        scratch |= {
            "mine": VMEM((rows, 128), bf16),
            "project": VMEM(plan.full_shape("project"), bf16),
            "position": VMEM(plan.full_shape("position"), bf16),
            "vector_blocks": VMEM(CUBE + (VECTOR_ROWS, 128), bf16),
            "vector_lines": VMEM((VECTOR_ROWS, 128), f32),
            "send_sem": pltpu.SemaphoreType.DMA((COPIES * len(pieces),)),
            "recv_sem": pltpu.SemaphoreType.DMA((COPIES * len(pieces),)),
            "load_sem": pltpu.SemaphoreType.DMA((4,)),
        }
        params = dict(collective_id=0, has_side_effects=True)

    def body(ref):
        if linked:
            partner_signal()
            gather = Gather(ref.blocks, pieces, ref.send_sem, ref.recv_sem, ref.mine)

            def run(events):
                for chunk, stage in events:
                    for piece in (2 * chunk, 2 * chunk + 1):
                        gather.advance(piece, stage, last=CHUNK_LAST[chunk])

            def pack(name):
                r, c = plan.shard[name]
                shard = getattr(ref, name + "_shard")
                for q in range(r // 128):
                    at = VECTOR_ROWS + plan.row[name] + q * c
                    if c % 128:
                        ref.mine[at : at + c, :] = shard[:, q * 128 : (q + 1) * 128]
                    else:
                        ref.mine[at : at + c, :] = shard[q * 128 : (q + 1) * 128, :].T

            ref.vector_lines[...] = jnp.zeros_like(ref.vector_lines)
            for name, (line, offset, size) in vector_places().items():
                entries = getattr(ref, name + "_shard")[...].astype(f32).reshape(1, size)
                ref.vector_lines[line : line + 1, offset : offset + size] = entries
            ref.mine[:VECTOR_ROWS, :] = ref.vector_lines[...].astype(bf16)
            for name in ("project", "position"):
                pack(name)
            partner_wait()
            run(FIRST)
            for name in WEIGHTS[2:]:
                pack(name)
            own = pltpu.make_async_copy(
                ref.mine, ref.blocks.at[gather.bits], ref.load_sem.at[0]
            )
            own.start()

        def first_norm(i, carry):
            rows = at_rows(i, RB)
            ref.normal[rows, :] = norm_parts(ref.tokens[rows, :].astype(f32))[0]
            return carry

        lax.fori_loop(0, SEQ // RB, first_norm, 0)

        def table_of(rows, sine, cosine):
            ref.key_table[rows, 128 : 128 + HALF] = sine
            ref.key_table[rows, 128 + HALF :] = cosine

        expand_angles(ref.coarse, ref.angles, table_of)

        if linked:
            own.wait()
            run(BEFORE)
            load_weight(plan, "project", ref.blocks, ref.project, ref.load_sem.at[1], VECTOR_ROWS)
            load_weight(plan, "position", ref.blocks, ref.position, ref.load_sem.at[3], VECTOR_ROWS)
            small = pltpu.make_async_copy(
                ref.blocks.at[:, :, :, :, :, pl.ds(0, VECTOR_ROWS), :],
                ref.vector_blocks,
                ref.load_sem.at[2],
            )
            small.start()
            small.wait()
            unpack_vectors(ref.vector_blocks, ref.vectors)
            wait_whole(ref.project, ref.load_sem.at[1])
        else:
            ref.vectors[...] = ref.given_vectors[...]

        for b in range(BLOCKS):
            rows = slice(b * QB, (b + 1) * QB)
            normed = ref.normal[rows, :] * vec(ref.vectors, "gain_one") + vec(
                ref.vectors, "shift_one"
            )
            joined = nt(normed.astype(bf16), full(ref.project))
            ref.query_u[rows, :] = (joined[:, :D] + vec(ref.vectors, "content")).astype(bf16)
            ref.query_v[rows, :] = (joined[:, :D] + vec(ref.vectors, "position_bias")).astype(bf16)
            ref.key[rows, :] = joined[:, D : 2 * D].astype(bf16)
            ref.value[rows, :] = joined[:, 2 * D :].astype(bf16)

        def row_copy(i):
            name = FRONT_ROWS[i]
            return pltpu.make_async_copy(
                getattr(ref, name), getattr(ref, name + "_out"), ref.out_sem.at[i]
            )

        for i in range(4):
            row_copy(i).start()

        if linked:
            run(AFTER)
            wait_whole(ref.position, ref.load_sem.at[3])
            position = ref.position.reshape(D, D)
        else:
            position = ref.position

        def out_copy(head, slot):
            return pltpu.make_async_copy(
                ref.probs.at[slot], ref.probs_out.at[head], ref.probs_sem.at[slot]
            )

        def scores(lanes, b, e):
            row, width = b * QB, (b + 1) * QB
            rows = slice(row, row + QB)
            spread = nn(keep_head(ref.query_v[rows, lanes], e), position[lanes, :])
            low, high = rotate(spread, ref.angles[rows, :HALF], ref.angles[rows, HALF:])
            ref.turned[e, :, :128] = keep_head(ref.query_u[rows, lanes], e)
            ref.turned[e, :, 128 : 128 + HALF] = low.astype(bf16)
            ref.turned[e, :, 128 + HALF :] = high.astype(bf16)
            ref.score[e, :, :width] = nt(ref.turned[e], ref.key_table[:width, :])

        def softmax(b, e):
            row, width = b * QB, (b + 1) * QB
            for sub in range(QB // SB):
                used = row + (sub + 1) * SB
                for g in range(SB // CH):
                    at = slice(sub * SB + g * CH, sub * SB + (g + 1) * CH)
                    tiles = [
                        ref.score[e, at, i * 128 : (i + 1) * 128] for i in range(used // 128)
                    ]
                    lane = lax.broadcasted_iota(jnp.int32, (CH, SB), 1)
                    place = lax.broadcasted_iota(jnp.int32, (CH, SB), 0) + g * CH
                    tiles[-1] = jnp.where(lane <= place, tiles[-1], -1e30)
                    top = tiles[0]
                    for tile in tiles[1:]:
                        top = jnp.maximum(top, tile)
                    top = jnp.max(top, axis=1, keepdims=True)
                    tiles = [jnp.exp2((tile - top) * EXP_SCALE) for tile in tiles]
                    total = tiles[0]
                    for tile in tiles[1:]:
                        total = total + tile
                    scale = 1.0 / jnp.sum(total, axis=1, keepdims=True)
                    for i, tile in enumerate(tiles):
                        lanes = slice(POFF[b] + i * 128, POFF[b] + (i + 1) * 128)
                        ref.probs[e, at, lanes] = (tile * scale).astype(bf16)
                if used < width:
                    ref.probs[e, sub * SB : (sub + 1) * SB, POFF[b] + used : POFF[b] + width] = (
                        jnp.zeros((SB, width - used), bf16)
                    )

        def pair(hp):
            lanes = slice(hp * 128, (hp + 1) * 128)
            ref.key_table[:, :128] = ref.key[:, lanes]

            if hp > 0:
                for e in range(2):
                    out_copy(0, e).wait()

            for b in range(BLOCKS):
                for e in range(2):
                    scores(lanes, b, e)
                    softmax(b, e)
                    for when, events in DURING.items():
                        if linked and when % 6 == b * 2 + e:
                            run_at(hp, when // 6, lambda events=events: run(events))
                row, width = b * QB, (b + 1) * QB
                values = ref.value[:width, lanes]
                span = slice(POFF[b], POFF[b] + width)
                ref.mixed[row : row + QB, lanes] = jnp.where(
                    head_lanes(QB, 0),
                    nn(ref.probs[0, :, span], values),
                    nn(ref.probs[1, :, span], values),
                ).astype(bf16)
            for e in range(2):
                out_copy(hp * 2 + e, e).start()

        for hp in range(HEADS // 2):
            pair(hp)
        row_copy(4).start()
        for e in range(2):
            out_copy(0, e).wait()
        if linked:
            for i in range(len(pieces)):
                gather.drain(i, last=CHUNK_LAST[i // 2])
        for i in range(5):
            row_copy(i).wait()

    return call(body, ins, outs, scratch, **params)


MIDDLE = ("mixing", "expand", "contract", "pooling", "upsample")


def middle(plan, linked, ins):
    def weight_shape(name):
        return plan.full_shape(name) if linked else WEIGHT_SHAPE[name][::-1]

    outs = {
        "output_out": ((SEQ, D), bf16, ANY),
        "first_grad_out": ((SEQ, D), f32, ANY),
        "mixed_grad_out": ((SEQ, D), bf16, ANY),
        "sums": ((16, FF), f32, VMEM),
    }
    summed = ("pooling", "upsample") if linked else ()
    kept = [n for n in MIDDLE if n not in summed]
    outs |= {n + "_grad_out": (weight_shape(n), bf16, ANY) for n in kept}
    params = {}
    scratch = {n: VMEM(weight_shape(n), bf16) for n in MIDDLE}
    scratch |= {
        "normal": VMEM((SEQ, D), f32),
        "inverse": VMEM((SEQ, 128), f32),
        "second_low": VMEM((SEQ, D), bf16),
        "activated": VMEM((SEQ, FF), bf16),
        "slope": VMEM((SEQ, FF), bf16),
        "tiles": VMEM((D // 128, SEQ + 16, 128), f32),
        "grouped": VMEM((THIRD, 3 * D), bf16),
        "up_rows": VMEM((THIRD, 3 * D), bf16),
        "branch_grad": VMEM((SEQ, D), bf16),
        "attended_grad": VMEM((SEQ, D), bf16),
        "parts": VMEM((5, 8, FF), f32),
        "output": VMEM((SEQ, D), bf16),
        "first_grad": VMEM((SEQ, D), f32),
        "mixed_grad": VMEM((SEQ, D), bf16),
        "sem": pltpu.SemaphoreType.DMA((len(MIDDLE),)),
        "out_sem": pltpu.SemaphoreType.DMA((3 + len(kept),)),
    }
    scratch |= {n + "_grad": VMEM(weight_shape(n), bf16) for n in kept}
    if linked:
        gather_pieces = split_pieces(
            [plan.span(n, n, VECTOR_ROWS) for n in ("pooling", "upsample")]
        )
        base = -plan.row["pooling"]
        pieces = split_pieces([plan.span(n, n, base) for n in summed])
        rows = plan.span("pooling", "upsample", base)[1]
        outs["blocks_out"] = (CUBE + (VECTOR_ROWS + plan.rows, 128), bf16, ANY)
        outs["partial"] = ((2, 2, rows, 128), bf16, ANY)
        scratch |= {
            "own": VMEM(CUBE + (rows, 128), bf16),
            "land": VMEM(CUBE + (rows, 128), bf16),
            "partial_sem": pltpu.SemaphoreType.DMA,
            "gather_send": pltpu.SemaphoreType.DMA((4 * COPIES,)),
            "gather_recv": pltpu.SemaphoreType.DMA((4 * COPIES,)),
            "send_sem": pltpu.SemaphoreType.DMA((4 * COPIES,)),
            "recv_sem": pltpu.SemaphoreType.DMA((4 * COPIES,)),
        }
        params = dict(
            collective_id=1,
            has_side_effects=True,
            alias={list(ins).index("blocks"): list(outs).index("blocks_out")},
        )

    def body(ref):
        def fetch(name):
            i = MIDDLE.index(name)
            if linked:
                load_weight(
                    plan, name, ref.blocks_out, getattr(ref, name), ref.sem.at[i], VECTOR_ROWS
                )
            else:
                pltpu.make_async_copy(
                    getattr(ref, name + "_full"), getattr(ref, name), ref.sem.at[i]
                ).start()

        gather_stage = scatter_stage = None
        if linked:
            gather = Gather(ref.blocks_out, gather_pieces, ref.gather_send, ref.gather_recv)
            scatter = Scatter(ref.own, ref.land, None, pieces, ref.send_sem, ref.recv_sem)
            partner_signal()

            def gather_stage(stage):
                for i in range(4):
                    gather.advance(i, stage, first=1)

            def scatter_stage(name, stage):
                for half in range(2):
                    scatter.advance(summed.index(name) * 2 + half, stage, last=3)

        for name in ("mixing", "expand", "contract"):
            fetch(name)
        if linked:
            partner_wait()
            gather_stage(1)
        else:
            fetch("pooling")
            fetch("upsample")

        outgoing = ["output", "first_grad", "mixed_grad"] + [n + "_grad" for n in kept]

        def send_out(name):
            return pltpu.make_async_copy(
                getattr(ref, name),
                getattr(ref, name + "_out"),
                ref.out_sem.at[outgoing.index(name)],
            )

        def at_step(i, number, action, *args):
            if linked:
                run_at(i, number, lambda: action(*args))

        def ready(name):
            wait_whole(getattr(ref, name), ref.sem.at[MIDDLE.index(name)])

        def get(name):
            return full(getattr(ref, name))

        def put(name, values):
            if name in summed:
                put_blocks(plan, name, ref.own, base, lambda columns: values[:, columns])
                return
            target = getattr(ref, name + "_grad")
            target[...] = values.astype(bf16).reshape(target.shape)
            send_out(name + "_grad").start()

        def third(start, k):
            return jnp.concatenate(
                [ref.tiles[t, pl.ds(start + k, THIRD, stride=3), :] for t in range(D // 128)],
                axis=1,
            )

        def put_third(start, k, values):
            for t in range(D // 128):
                ref.tiles[t, pl.ds(start + k, THIRD, stride=3), :] = values[
                    :, t * 128 : (t + 1) * 128
                ]

        def rows_of(rows):
            return jnp.concatenate([ref.tiles[t, rows, :] for t in range(D // 128)], axis=1)

        def put_rows(rows, values):
            for t in range(D // 128):
                ref.tiles[t, rows, :] = values[:, t * 128 : (t + 1) * 128]

        def shifted_rows(i):
            return pl.ds(pl.multiple_of(i * RB + 8, 8), RB)

        ref.parts[...] = jnp.zeros_like(ref.parts)
        ref.sums[...] = jnp.zeros_like(ref.sums)

        def add_part(slot, values):
            columns = values.shape[1]
            ref.parts[slot, :, :columns] += eight_rows(values)

        def put_sum(name, values):
            r = VECTOR_ROW[name]
            ref.sums[r : r + 1, : values.shape[1]] = values

        def put_part(name, slot):
            columns = VECTOR_SIZE[name]
            put_sum(name, jnp.sum(ref.parts[slot, :, :columns], axis=0, keepdims=True))

        for name in ("mixing", "expand", "contract"):
            ready(name)

        def forward(i, carry):
            rows = at_rows(i, RB)
            attended = nt(ref.mixed[rows, :], get("mixing")) + vec(ref.vectors, "mixing_bias")
            first = ref.tokens[rows, :].astype(f32) + attended
            normal, inverse = norm_parts(first)
            ref.normal[rows, :] = normal
            ref.inverse[rows, :] = jnp.broadcast_to(inverse, (RB, 128))
            low = (
                normal * vec(ref.vectors, "gain_two") + vec(ref.vectors, "shift_two")
            ).astype(bf16)
            ref.second_low[rows, :] = low
            inner = nt(low, get("expand")) + vec(ref.vectors, "hidden")
            phi = 0.5 * (1.0 + lax.erf(inner * 2.0 ** (-0.5)))
            act = (inner * phi).astype(bf16)
            ref.activated[rows, :] = act
            bell = jnp.exp(-0.5 * inner * inner) * (2.0 * math.pi) ** (-0.5)
            ref.slope[rows, :] = (phi + inner * bell).astype(bf16)
            block = first + nt(act, get("contract")) + vec(ref.vectors, "contract_bias")
            put_rows(shifted_rows(i), block)
            at_step(i, 1, gather_stage, 2)
            at_step(i, 4, gather_stage, 3)
            return carry

        lax.fori_loop(0, SEQ // RB, forward, 0)

        put_rows(slice(0, 8), jnp.zeros((8, D), f32))
        for k in range(3):
            ref.grouped[:, k * D : (k + 1) * D] = third(6, k).astype(bf16)
        if linked:
            gather_stage(4)
            fetch("pooling")
            fetch("upsample")
        ready("pooling")
        pooled = (
            nt(ref.grouped[...], get("pooling")) + vec(ref.vectors, "pooling_bias")
        ).astype(bf16)
        ready("upsample")
        for k in range(3):
            columns = slice(k * D, (k + 1) * D)
            upward = nt(pooled, get("upsample")[columns, :]) + vec(ref.vectors, "upsample_bias")[
                :, columns
            ]
            put_third(8, k, third(8, k) + upward)

        def write_output(i, carry):
            ref.output[at_rows(i, RB), :] = rows_of(shifted_rows(i)).astype(bf16)
            put_rows(shifted_rows(i), ref.cotangent[at_rows(i, RB), :].astype(f32))
            return carry

        lax.fori_loop(0, SEQ // RB, write_output, 0)

        send_out("output").start()

        for k in range(3):
            ref.up_rows[:, k * D : (k + 1) * D] = third(8, k).astype(bf16)
        up_rows = ref.up_rows[...]
        put_sum("upsample_bias", jnp.sum(up_rows.astype(f32), axis=0, keepdims=True))
        put("upsample", tn(up_rows, pooled))
        if linked:
            scatter_stage("upsample", 0)
        pooled_grad = nn(up_rows, get("upsample")).astype(bf16)
        put_sum("pooling_bias", jnp.sum(pooled_grad.astype(f32), axis=0, keepdims=True))
        put("pooling", tn(pooled_grad, ref.grouped[...]))
        if linked:
            scatter_stage("pooling", 0)
        for k in range(3):
            put_third(
                6, k, nn(pooled_grad, get("pooling")[:, k * D : (k + 1) * D])
            )
        put_rows(slice(SEQ + 6, SEQ + 8), jnp.zeros((2, D), f32))
        if linked:
            scatter_stage("upsample", 1)

        def backward(i, carry):
            rows = at_rows(i, RB)
            block_grad = ref.cotangent[rows, :].astype(f32) + rows_of(shifted_rows(i))
            branch_grad = block_grad.astype(bf16)
            ref.branch_grad[rows, :] = branch_grad
            add_part(0, branch_grad.astype(f32))
            inner_grad = (nn(branch_grad, get("contract")) * ref.slope[rows, :].astype(f32)).astype(
                bf16
            )
            ref.slope[rows, :] = inner_grad
            add_part(1, inner_grad.astype(f32))
            second_grad = nn(inner_grad, get("expand"))
            normal = ref.normal[rows, :]
            add_part(2, second_grad * normal)
            add_part(3, second_grad)
            first_grad = block_grad + norm_backward(
                normal, ref.inverse[rows, :1], vec(ref.vectors, "gain_two"), second_grad
            )
            ref.first_grad[rows, :] = first_grad
            attended_grad = first_grad.astype(bf16)
            ref.attended_grad[rows, :] = attended_grad
            add_part(4, attended_grad.astype(f32))
            ref.mixed_grad[rows, :] = nn(attended_grad, get("mixing")).astype(bf16)
            at_step(i, 0, scatter_stage, "pooling", 1)
            at_step(i, 3, scatter_stage, "upsample", 2)
            at_step(i, 5, scatter_stage, "pooling", 2)
            return carry

        lax.fori_loop(0, SEQ // RB, backward, 0)
        send_out("first_grad").start()
        send_out("mixed_grad").start()
        put_part("contract_bias", 0)
        put_part("hidden", 1)
        put_part("gain_two", 2)
        put_part("shift_two", 3)
        put_part("mixing_bias", 4)
        put("contract", tn(ref.branch_grad[...], ref.activated[...]))
        if linked:
            scatter_stage("upsample", 3)
        put("expand", tn(ref.slope[...], ref.second_low[...]))
        put("mixing", tn(ref.attended_grad[...], ref.mixed[...]))
        if linked:
            scatter_stage("pooling", 3)
            _, _, x, y, core = scatter.bits
            partial = pltpu.make_async_copy(
                ref.own.at[:, :, x, y, core], ref.partial, ref.partial_sem
            )
            partial.start()
            partial.wait()
            for i in range(4):
                gather.drain(i, first=1)
        for name in outgoing:
            send_out(name).wait()

    return call(body, ins, outs, scratch, **params)


BACK_FIRST = (0, 0, 3, 0, 0, 0)
BACK_DURING = {
    2: ((0, 1),),
    7: ((0, 2), (1, 1)),
    14: ((0, 3), (1, 2), (2, 4)),
    18: ((0, 4), (1, 3)),
    23: ((1, 4),),
}


def back(plan, linked, ins):
    outs = {"token_grad": ((SEQ, D), f32, VMEM)}
    late_rows = ("tokens", "mixed_grad", "mixed", "value", "key", "query_u", "query_v", "first_grad")
    scratch = {
        "angles": VMEM((SEQ, D), f32),
        "key_table": VMEM((SEQ, 128 + D), bf16),
        "prob_grad": VMEM((2, QB, SEQ), f32),
        "total_grad": VMEM((2, QB, SEQ), bf16),
        "probs": VMEM((4, QB, PW), bf16),
        "key_acc": VMEM((128, SEQ), f32),
        "value_acc": VMEM((128, SEQ), f32),
        "joined_grad": VMEM((SEQ, 3 * D), bf16),
        "normed_low": VMEM((SEQ, D), bf16),
        "position_grad": VMEM((D, D), f32),
        "parts": VMEM((2, 8, D), f32),
        "all_sums": VMEM((16, FF), f32),
        "probs_sem": pltpu.SemaphoreType.DMA((4,)),
        "load_sem": pltpu.SemaphoreType.DMA((2,)),
        "row_sem": pltpu.SemaphoreType.DMA((len(late_rows),)),
    }
    scratch |= {n: VMEM((SEQ, D), f32 if n == "first_grad" else bf16) for n in late_rows}
    params = {}
    project_shape = plan.full_shape("project") if linked else (3 * D, D)
    position_shape = plan.full_shape("position") if linked else (D, D)
    scratch |= {"project": VMEM(project_shape, bf16), "position": VMEM(position_shape, bf16)}
    if linked:
        early_names = ("contract", "expand", "mixing")
        early = [plan.span("contract", "contract", 0), plan.span("mixing", "expand", 0)]
        late = [plan.span("pooling", "upsample", 0), plan.span("position", "position", 0)]
        row, rows = plan.span("project", "project", 0)
        late += [(row, rows // 2), (row + rows // 2, rows // 2)]
        pieces = split_pieces(early + late)
        count = COPIES * len(pieces)
        own_rows = plan.rows
        outs["vector_out"] = ((8, 128), f32, VMEM)
        outs["flat_out"] = ((own_rows, 128), f32, ANY)
        scratch |= {
            "own": VMEM(CUBE + (own_rows, 128), bf16),
            "land": VMEM(CUBE + (own_rows, 128), bf16),
            "flat": VMEM((own_rows, 128), f32),
            "vector_own": VMEM(CUBE + (8, 128), f32),
            "land_dp": VMEM((3, 2, 2, 2, 8, 128), f32),
            "land_fsdp": VMEM((7, 8, 128), f32),
            "vector_sem": pltpu.SemaphoreType.DMA((4, 8)),
            "send_sem": pltpu.SemaphoreType.DMA((count,)),
            "recv_sem": pltpu.SemaphoreType.DMA((count,)),
            "own_sem": pltpu.SemaphoreType.DMA((4,)),
        }
        params = dict(collective_id=2, has_side_effects=True)
    else:
        outs["project_grad"] = ((3 * D, D), bf16, VMEM)
        outs["position_grad_out"] = ((D, D), bf16, VMEM)
        outs["sums_out"] = ((16, FF), f32, VMEM)

    def body(ref):
        def row_copy(name):
            return pltpu.make_async_copy(
                getattr(ref, name + "_in"), getattr(ref, name), ref.row_sem.at[late_rows.index(name)]
            )

        for name in late_rows[:7]:
            row_copy(name).start()
        if linked:
            load_weight(plan, "project", ref.blocks, ref.project, ref.load_sem.at[0], VECTOR_ROWS)
            load_weight(plan, "position", ref.blocks, ref.position, ref.load_sem.at[1], VECTOR_ROWS)
            matrix = Scatter(ref.own, ref.land, ref.flat, pieces, ref.send_sem, ref.recv_sem)
            vector = AxisScatter(
                ref.vector_own, ref.land_dp, ref.land_fsdp, ref.vector_out, ref.vector_sem
            )
            axis_signal()

            def run(events):
                for chunk, stage in events:
                    for piece in (2 * chunk, 2 * chunk + 1):
                        matrix.advance(piece, stage, first=BACK_FIRST[chunk])

            for i, name in enumerate(early_names):
                c = plan.shard[name][1]
                for y, core, row, column in plan.blocks(name, 0):
                    pltpu.make_async_copy(
                        getattr(ref, name + "_grad").at[:, :, :, :, pl.ds(column, 128)],
                        ref.own.at[:, :, :, y, core, pl.ds(row, c), :],
                        ref.own_sem.at[i],
                    ).start()
            _, _, x, y, core = matrix.bits
            row, rows = late[0]
            partial = pltpu.make_async_copy(
                ref.partial, ref.own.at[:, :, x, y, core, pl.ds(row, rows), :], ref.own_sem.at[3]
            )
            partial.start()
        else:
            for i, name in enumerate(("project", "position")):
                pltpu.make_async_copy(
                    getattr(ref, name + "_full"), getattr(ref, name), ref.load_sem.at[i]
                ).start()

        def in_copy(head, slot):
            return pltpu.make_async_copy(
                ref.probs_in.at[head], ref.probs.at[slot], ref.probs_sem.at[slot]
            )

        for e in range(2):
            in_copy(e, e).start()

        def table_of(rows, sine, cosine):
            ref.key_table[rows, 128 : 128 + HALF] = sine
            ref.key_table[rows, 128 + HALF :] = cosine

        expand_angles(ref.coarse, ref.angles, table_of)

        def norm_rows(rows):
            return norm_parts(ref.tokens[rows, :].astype(f32))

        def low_rows(i, carry):
            rows = at_rows(i, RB)
            normal, _ = norm_rows(rows)
            ref.normed_low[rows, :] = (
                normal * vec(ref.vectors, "gain_one") + vec(ref.vectors, "shift_one")
            ).astype(bf16)
            return carry

        row_copy("tokens").wait()
        lax.fori_loop(0, SEQ // RB, low_rows, 0)
        ref.all_sums[...] = ref.sums[...]
        ref.parts[...] = jnp.zeros_like(ref.parts)
        if linked:
            axis_wait()
            partial.wait()
            run([(2, 3)])
            for i, name in enumerate(early_names):
                row, rows = plan.span(name, name, 0)
                whole = ref.own.at[:, :, :, :, :, pl.ds(row, rows), :]
                wait_whole(whole, ref.own_sem.at[i])
                if i == 0:
                    run([(0, 0)])
            run([(1, 0)])
        wait_whole(ref.project, ref.load_sem.at[0])
        wait_whole(ref.position, ref.load_sem.at[1])
        position = ref.position.reshape(D, D)
        for name in late_rows[1:7]:
            row_copy(name).wait()
        row_copy("first_grad").start()

        def pair(hp, carry):
            start = pl.multiple_of(hp * 128, 128)
            lanes = pl.ds(start, 128)
            base = lax.rem(hp, 2) * 2
            for e in range(2):
                in_copy(0, base + e).wait()

            @pl.when(hp < HEADS // 2 - 1)
            def _():
                for e in range(2):
                    in_copy(hp * 2 + 2 + e, 2 - base + e).start()

            ref.key_table[:, :128] = ref.key[:, lanes]
            content_sum = jnp.zeros((1, 128), f32)
            position_sum = jnp.zeros((1, 128), f32)
            for b in range(BLOCKS):
                row, width = b * QB, (b + 1) * QB
                rows = slice(row, row + QB)
                span = slice(POFF[b], POFF[b] + width)
                by_content, by_position = [], None
                for e in range(2):
                    upstream = keep_head(ref.mixed_grad[rows, lanes], e)
                    row_dot = jnp.sum(
                        upstream.astype(f32) * ref.mixed[rows, lanes].astype(f32),
                        axis=1,
                        keepdims=True,
                    )
                    ref.prob_grad[e, :, :width] = nt(upstream, ref.value[:width, lanes]) - row_dot
                    for sub in range(QB // SB):
                        used = row + (sub + 1) * SB
                        for g in range(SB // CH):
                            at = slice(sub * SB + g * CH, sub * SB + (g + 1) * CH)
                            p = ref.probs[base + e, at, POFF[b] : POFF[b] + used].astype(f32)
                            ref.total_grad[e, at, :used] = (
                                p * ref.prob_grad[e, at, :used] * HEAD_DIM ** (-0.5)
                            ).astype(bf16)
                        if used < width:
                            ref.total_grad[e, sub * SB : (sub + 1) * SB, used:width] = jnp.zeros(
                                (SB, width - used), bf16
                            )
                    scored = ref.total_grad[e, :, :width]
                    turned = nn(scored, ref.key_table[:width, :])
                    by_content.append(turned[:, :128])
                    low, high = rotate(
                        turned[:, 128:], ref.angles[rows, :HALF], ref.angles[rows, HALF:]
                    )
                    spread = jnp.concatenate([low, high], axis=1).astype(bf16)
                    own = (lax.broadcasted_iota(jnp.int32, (128, D), 0) // HEAD_DIM) == e
                    part = nt(spread, jnp.where(own, position[lanes, :], 0).astype(bf16))
                    by_position = part if by_position is None else by_position + part
                    part = tn(keep_head(ref.query_v[rows, lanes], e), spread)
                    if b == 0 and e == 0:
                        ref.position_grad[lanes, :] = part
                    else:
                        ref.position_grad[lanes, :] += part
                    to_key = tn(keep_head(ref.query_u[rows, lanes], e), scored)
                    to_value = tn(upstream, ref.probs[base + e, :, span])
                    if e == 0:
                        if b > 0:
                            ref.key_acc[:, :row] += to_key[:, :row]
                            ref.value_acc[:, :row] += to_value[:, :row]
                        ref.key_acc[:, row:width] = to_key[:, row:]
                        ref.value_acc[:, row:width] = to_value[:, row:]
                    else:
                        ref.key_acc[:, :width] += to_key
                        ref.value_acc[:, :width] += to_value
                    for when, events in BACK_DURING.items():
                        if linked and when % 6 == b * 2 + e:
                            run_at(hp, when // 6, lambda events=events: run(events))
                by_content = jnp.where(head_lanes(QB, 0), by_content[0], by_content[1])
                ref.joined_grad[rows, lanes] = (by_content + by_position).astype(bf16)
                content_sum += jnp.sum(by_content, axis=0, keepdims=True)
                position_sum += jnp.sum(by_position, axis=0, keepdims=True)
            ref.joined_grad[:, pl.ds(start + D, 128)] = ref.key_acc[...].T.astype(bf16)
            ref.joined_grad[:, pl.ds(start + 2 * D, 128)] = ref.value_acc[...].T.astype(bf16)
            r = VECTOR_ROW["content"]
            ref.all_sums[r : r + 1, lanes] = content_sum
            r = VECTOR_ROW["position_bias"]
            ref.all_sums[r : r + 1, lanes] = position_sum
            return carry

        lax.fori_loop(0, HEADS // 2, pair, 0)

        row_copy("first_grad").wait()
        if linked:
            put_blocks(plan, "position", ref.own, 0, lambda columns: ref.position_grad[:, columns])
            run([(3, 0)])
        for part in range(3):
            columns = slice(part * D, (part + 1) * D)
            grad = tn(ref.joined_grad[:, columns], ref.normed_low[...]).astype(bf16)
            if linked:
                ref.project_full[columns, :] = grad
            else:
                ref.project_grad[columns, :] = grad
        if linked:
            put_blocks(plan, "project", ref.own, 0, lambda columns: ref.project_full[:, columns])
            run([(4, 0), (5, 0), (3, 1)])
        else:
            ref.position_grad_out[...] = ref.position_grad[...].astype(bf16)

        def norm_back(i, carry):
            rows = at_rows(i, RB)
            normal, inverse = norm_rows(rows)
            upstream = nn(ref.joined_grad[rows, :], full(ref.project))
            ref.parts[0, :, :] += eight_rows(upstream * normal)
            ref.parts[1, :, :] += eight_rows(upstream)
            ref.token_grad[rows, :] = ref.first_grad[rows, :] + norm_backward(
                normal, inverse, vec(ref.vectors, "gain_one"), upstream
            )
            if linked:
                run_at(i, 1, lambda: run([(4, 1)]))
                run_at(i, 2, lambda: run([(5, 1)]))
                run_at(i, 3, lambda: run([(3, 2)]))
                run_at(i, 5, lambda: run([(4, 2)]))
            return carry

        lax.fori_loop(0, SEQ // RB, norm_back, 0)
        for slot, name in enumerate(("gain_one", "shift_one")):
            r = VECTOR_ROW[name]
            ref.all_sums[r : r + 1, :D] = jnp.sum(ref.parts[slot], axis=0, keepdims=True)
        if linked:
            pack_vectors(ref.all_sums, ref.vector_own)
            vector.first()
            run([(5, 2), (3, 3), (4, 3)])
            vector.second()
            run([(5, 3), (3, 4)])
            vector.last()
            run([(4, 4), (5, 4)])
            done = pltpu.make_async_copy(ref.flat, ref.flat_out, ref.own_sem.at[0])
            done.start()
            done.wait()
        else:
            ref.sums_out[...] = ref.all_sums[...]

    if linked:
        scratch["project_full"] = VMEM((3 * D, D), bf16)
    return call(body, ins, outs, scratch, **params)


PARTS = 4


def finish(plan, flat, vectors, rows):
    outs = {n + "_out": (plan.held_shape(n), f32, VMEM) for n in WEIGHTS}
    outs |= {n + "_out": ((VECTOR_SIZE[n] // 32,), f32, VMEM) for n in VECTORS}
    outs |= {n + "_copy": (v.shape, v.dtype, ANY) for n, v in rows.items()}
    ins = {"flat": (flat, VMEM), "vectors": (vectors, VMEM)}
    ins |= {n: (v, ANY) for n, v in rows.items()}
    scratch = {n + "_held": VMEM(v.shape, v.dtype) for n, v in rows.items()}
    scratch["in_sem"] = pltpu.SemaphoreType.DMA((len(rows) * PARTS,))
    scratch["out_sem"] = pltpu.SemaphoreType.DMA((len(rows) * PARTS,))

    def body(ref):
        loads, copies = [], []
        for n in rows:
            for part in range(PARTS):
                at = pl.ds(part * (SEQ // PARTS), SEQ // PARTS)
                held = getattr(ref, n + "_held").at[at]
                slot = len(loads)
                loads.append(
                    pltpu.make_async_copy(getattr(ref, n).at[at], held, ref.in_sem.at[slot])
                )
                copies.append(
                    pltpu.make_async_copy(
                        held, getattr(ref, n + "_copy").at[at], ref.out_sem.at[slot]
                    )
                )
        for load in loads:
            load.start()
        for load, copy in zip(loads, copies):
            load.wait()
            copy.start()
        for name in WEIGHTS:
            put_shard(plan, name, ref.flat, 0, getattr(ref, name + "_out"))
        for name, (line, offset, size) in vector_places().items():
            getattr(ref, name + "_out")[...] = ref.vectors[line, offset : offset + size]
        for copy in copies:
            copy.wait()

    return call(body, ins, outs, scratch)


def make_local(dp, fsdp):
    plan = Plan(dp, fsdp)
    linked = (dp, fsdp) == (4, 8)

    def gathered(weights):
        out = {}
        for name, shard in zip(WEIGHTS, weights):
            part = lax.all_gather(shard, "dp", axis=0, tiled=True)
            out[name + "_full"] = lax.all_gather(part, "fsdp", axis=1, tiled=True).T
        return out

    def gathered_vectors(vectors):
        rows = []
        for name, shard in zip(VECTORS, vectors):
            whole = lax.all_gather(shard, ("dp", "fsdp"), axis=0, tiled=True).astype(f32)
            rows.append(jnp.pad(whole, (0, FF - VECTOR_SIZE[name])))
        rows += [jnp.zeros((FF,), f32)] * (16 - len(rows))
        return jnp.stack(rows)

    def local(tokens, cotangent, *params):
        assert tokens.shape[0] == SEQ
        weights, vectors = params[:7], params[7:]
        given = dict(zip(VECTORS, vectors))
        coarse = coarse_angles()
        ins = {"tokens": (tokens, VMEM), "coarse": (coarse, VMEM)}
        if linked:
            ins |= {n + "_shard": (given[n], VMEM) for n in VECTORS}
            for n, w in zip(WEIGHTS, weights):
                ins[n + "_shard"] = (w.T if w.shape[1] % 128 else w, VMEM)
        else:
            whole = gathered(weights)
            ins["given_vectors"] = (gathered_vectors(vectors), VMEM)
            ins["project"] = (whole["project_full"], VMEM)
            ins["position"] = (whole["position_full"], VMEM)
        one = front(plan, linked, ins)

        ins = {
            "tokens": (tokens, VMEM),
            "cotangent": (cotangent, VMEM),
            "mixed": (one.mixed_out, VMEM),
            "vectors": (one.vectors, VMEM),
        }
        if linked:
            ins["blocks"] = (one.blocks, ANY)
        else:
            ins |= {n + "_full": (whole[n + "_full"], ANY) for n in MIDDLE}
        two = middle(plan, linked, ins)

        ins = {
            "tokens_in": (tokens, ANY),
            "coarse": (coarse, VMEM),
            "vectors": (one.vectors, VMEM),
            "query_u_in": (one.query_u_out, ANY),
            "query_v_in": (one.query_v_out, ANY),
            "key_in": (one.key_out, ANY),
            "value_in": (one.value_out, ANY),
            "mixed_in": (one.mixed_out, ANY),
            "mixed_grad_in": (two.mixed_grad_out, ANY),
            "first_grad_in": (two.first_grad_out, ANY),
            "sums": (two.sums, VMEM),
            "probs_in": (one.probs_out, ANY),
        }
        if linked:
            ins["blocks"] = (two.blocks_out, ANY)
            for n in ("contract", "expand", "mixing"):
                ins[n + "_grad"] = (getattr(two, n + "_grad_out"), ANY)
            ins["partial"] = (two.partial, ANY)
        else:
            ins |= {n + "_full": (whole[n + "_full"], ANY) for n in ("project", "position")}
        three = back(plan, linked, ins)

        if linked:
            last = finish(
                plan,
                three.flat_out,
                three.vector_out,
                {"output": two.output_out, "token_grad": three.token_grad},
            )
            output, token_grad = last.output_copy, last.token_grad_copy
            matrices = []
            for n in WEIGHTS:
                grad = getattr(last, n + "_out")
                matrices.append(grad if grad.shape == plan.shard[n] else grad.T)
            small = [getattr(last, n + "_out") for n in VECTORS]
        else:
            output, token_grad = two.output_out, three.token_grad
            grads = {n: getattr(two, n + "_grad_out") for n in MIDDLE}
            grads["project"] = three.project_grad
            grads["position"] = three.position_grad_out
            matrices = []
            for name in WEIGHTS:
                part = lax.psum_scatter(
                    grads[name].T, "fsdp", scatter_dimension=1, tiled=True
                )
                part = lax.psum_scatter(part, "dp", scatter_dimension=0, tiled=True)
                matrices.append(part.astype(f32))
            small = []
            for name in VECTORS:
                sums = three.sums_out[VECTOR_ROW[name], : VECTOR_SIZE[name]]
                small.append(
                    lax.psum_scatter(sums, ("dp", "fsdp"), scatter_dimension=0, tiled=True)
                )
        return (output, token_grad, *matrices, *small)

    return local


def solution(mesh):
    rows = P(("dp", "fsdp"), None)
    matrix = P("dp", "fsdp")
    vector = P(("dp", "fsdp"))
    return jax.shard_map(
        make_local(mesh.shape["dp"], mesh.shape["fsdp"]),
        mesh=mesh,
        in_specs=(rows,) * 2 + (matrix,) * 7 + (vector,) * 11,
        out_specs=(rows,) * 2 + (matrix,) * 7 + (vector,) * 11,
        check_vma=False,
    )
```

```python
import math
from types import SimpleNamespace

import jax
import jax.numpy as jnp
from jax import lax
from jax.experimental import pallas as pl
from jax.experimental.pallas import tpu as pltpu
from jax.sharding import PartitionSpec as P

D = 512
HALF = D // 2
HEADS = 8
HEAD_DIM = 64
FF = 2048
SEQ = 1152
THIRD = SEQ // 3
QB = 384
SB = 128
CH = 16
RB = 128
MB = 192
BLOCKS = SEQ // QB
POFF = [sum((b + 1) * QB for b in range(n)) for n in range(BLOCKS + 1)]
PW = POFF[BLOCKS]
EXP_SCALE = HEAD_DIM ** (-0.5) * math.log2(math.e)
ANGLE_STEP = 32
epsilon = 1e-05
bf16 = jnp.bfloat16
f32 = jnp.float32
MESH = pl.DeviceIdType.MESH
VMEM_LIMIT = 63 << 20

WEIGHTS = ("project", "position", "mixing", "expand", "contract", "pooling", "upsample")
WEIGHT_SHAPE = {
    "project": (D, 3 * D),
    "position": (D, D),
    "mixing": (D, D),
    "expand": (D, FF),
    "contract": (FF, D),
    "pooling": (3 * D, D),
    "upsample": (D, 3 * D),
}
VECTORS = (
    "gain_one",
    "shift_one",
    "content",
    "position_bias",
    "mixing_bias",
    "gain_two",
    "shift_two",
    "hidden",
    "contract_bias",
    "pooling_bias",
    "upsample_bias",
)
VECTOR_SIZE = {n: D for n in VECTORS} | {"hidden": FF, "upsample_bias": 3 * D}
VECTOR_ROW = {n: i for i, n in enumerate(VECTORS)}
PACKED_VECTORS = ("hidden", "upsample_bias", "gain_one") + tuple(
    n for n in VECTORS if n not in ("hidden", "upsample_bias", "gain_one")
)


def nn(a, b):
    return lax.dot_general(a, b, (((1,), (0,)), ((), ())), preferred_element_type=f32)


def nt(a, b):
    return lax.dot_general(a, b, (((1,), (1,)), ((), ())), preferred_element_type=f32)


def tn(a, b):
    return lax.dot_general(a, b, (((0,), (0,)), ((), ())), preferred_element_type=f32)


def at_rows(step, rows):
    return pl.ds(pl.multiple_of(step * rows, rows), rows)


def eight_rows(values):
    rows, columns = values.shape
    return jnp.sum(values.reshape(rows // 8, 8, columns), axis=0)


def call(body, ins, outs, scratch, alias=None, **params):
    names = [*ins, *outs, *scratch]

    def kernel(*refs):
        body(SimpleNamespace(**dict(zip(names, refs))))

    results = pl.pallas_call(
        kernel,
        out_shape=[jax.ShapeDtypeStruct(s, t) for s, t, _ in outs.values()],
        in_specs=[pl.BlockSpec(memory_space=m) for _, m in ins.values()],
        out_specs=[pl.BlockSpec(memory_space=m) for _, _, m in outs.values()],
        scratch_shapes=list(scratch.values()),
        input_output_aliases=alias or {},
        compiler_params=pltpu.CompilerParams(vmem_limit_bytes=VMEM_LIMIT, **params),
    )(*[a for a, _ in ins.values()])
    return SimpleNamespace(**dict(zip(outs, results)))


VMEM = pltpu.VMEM
ANY = pl.ANY


BIT_AXIS = ("fsdp", "fsdp", "fsdp", "dp", "dp")
BIT_MASK = (4, 2, 1, 2, 1)
CUBE = (2,) * 5
GATHER_ORDER = ((2, 3, 4), (3, 2, 4))
SCATTER_ORDER = ((4, 3, 2), (4, 2, 3))
STAGES = 4
COPIES = 6


def my_bits():
    fs = lax.axis_index("fsdp")
    dp = lax.axis_index("dp")
    return (
        lax.rem(fs // 4, 2),
        lax.rem(fs // 2, 2),
        lax.rem(fs, 2),
        lax.rem(dp // 2, 2),
        lax.rem(dp, 2),
    )


def partner(*flipped):
    place = {"fsdp": lax.axis_index("fsdp"), "dp": lax.axis_index("dp")}
    bits = my_bits()
    for bit in flipped:
        place[BIT_AXIS[bit]] += BIT_MASK[bit] * (1 - 2 * bits[bit])
    return (place["dp"], place["fsdp"])


LINE_FLIPS = ((1,), (0,), (0, 1))


def flipped_bits(flips):
    return tuple(1 - b if k in flips else b for k, b in enumerate(my_bits()))


def partner_signal():
    sem = pltpu.get_barrier_semaphore()
    for flips in LINE_FLIPS + ((2,), (3,), (4,)):
        pl.semaphore_signal(sem, inc=1, device_id=partner(*flips), device_id_type=MESH)


def partner_wait():
    pl.semaphore_wait(pltpu.get_barrier_semaphore(), 6)


def run_at(step, number, action):
    if isinstance(step, int):
        if step == number:
            action()
        return

    @pl.when(step == number)
    def _():
        action()


class Gather:
    def __init__(self, buf, pieces, send_sem, recv_sem, mine=None):
        self.buf, self.pieces, self.mine = buf, pieces, mine
        self.send_sem, self.recv_sem = send_sem, recv_sem
        self.bits = my_bits()

    def copy(self, source, target, sem, device):
        return pltpu.make_async_remote_copy(
            src_ref=source,
            dst_ref=target,
            send_sem=self.send_sem.at[sem],
            recv_sem=self.recv_sem.at[sem],
            device_id=device,
            device_id_type=MESH,
        )

    def copies(self, i, stage):
        row, rows, kind = self.pieces[i]
        part = (pl.ds(row, rows),)
        if stage == 0:
            target = self.buf.at[self.bits + part]
            source = target if self.mine is None else self.mine.at[part]
            return [
                self.copy(source, target, i * COPIES + n, partner(*flips))
                for n, flips in enumerate(LINE_FLIPS)
            ]
        order = GATHER_ORDER[kind]
        free = (0, 1) + order[: stage - 1]
        index = tuple(slice(None) if k in free else self.bits[k] for k in range(5))
        ref = self.buf.at[index + part]
        return [self.copy(ref, ref, i * COPIES + 2 + stage, partner(order[stage - 1]))]

    def advance(self, i, stage, first=0, last=STAGES):
        if stage > first:
            for copy in self.copies(i, stage - 1):
                copy.wait_recv()
        if stage < last:
            for copy in self.copies(i, stage):
                copy.start()

    def drain(self, i, first=0, last=STAGES):
        for stage in range(first, last):
            for copy in self.copies(i, stage):
                copy.wait_send()


class Scatter:
    def __init__(self, own, land, out, pieces, send_sem, recv_sem):
        self.own, self.land, self.out, self.pieces = own, land, out, pieces
        self.send_sem, self.recv_sem = send_sem, recv_sem
        self.bits = my_bits()

    def index(self, order, stage, side):
        out = []
        for k in range(5):
            if k in order[:stage]:
                out.append(1 - self.bits[k] if side in ("land", "target") else self.bits[k])
            elif k in order[stage : stage + 1]:
                out.append(1 - self.bits[k] if side in ("send", "target") else self.bits[k])
            else:
                out.append(slice(None))
        return tuple(out)

    def copy(self, source, target, sem, device):
        return pltpu.make_async_remote_copy(
            src_ref=source,
            dst_ref=target,
            send_sem=self.send_sem.at[sem],
            recv_sem=self.recv_sem.at[sem],
            device_id=device,
            device_id_type=MESH,
        )

    def copies(self, i, stage):
        row, rows, kind = self.pieces[i]
        order = SCATTER_ORDER[kind]
        part = (pl.ds(row, rows),)
        if stage == 3:
            place = self.bits[:2] + tuple(1 - b for b in self.bits[2:])
            return [
                self.copy(
                    self.own.at[flipped_bits(flips) + part],
                    self.land.at[place + part],
                    i * COPIES + 3 + n,
                    partner(*flips),
                )
                for n, flips in enumerate(LINE_FLIPS)
            ]
        return [
            self.copy(
                self.own.at[self.index(order, stage, "send") + part],
                self.land.at[self.index(order, stage, "target") + part],
                i * COPIES + stage,
                partner(order[stage]),
            )
        ]

    def add(self, i, stage):
        row, rows, kind = self.pieces[i]
        order = SCATTER_ORDER[kind]
        part = (pl.ds(row, rows), slice(None))
        if stage == 3:
            total = self.own[self.bits + part].astype(f32)
            for flips in LINE_FLIPS:
                place = flipped_bits(flips)[:2] + tuple(1 - b for b in self.bits[2:])
                total = total + self.land[place + part].astype(f32)
            self.out[pl.ds(row, rows), :] = total
            return
        mine = self.own.at[self.index(order, stage, "own")]
        came = self.land.at[self.index(order, stage, "land")]
        free = 4 - stage

        def body(j, carry):
            at = tuple(lax.rem(j // 2 ** (free - 1 - q), 2) for q in range(free)) + part
            mine[at] = mine[at] + came[at]
            return carry

        lax.fori_loop(0, 2**free, body, 0)

    def advance(self, i, stage, first=0, last=STAGES):
        if stage > first:
            for copy in self.copies(i, stage - 1):
                copy.wait()
            self.add(i, stage - 1)
        if stage < last:
            for copy in self.copies(i, stage):
                copy.start()


def split_pieces(chunks):
    pieces = []
    for row, rows in chunks:
        half = (rows // 2 + 15) // 16 * 16
        pieces.append((row, half, 0))
        pieces.append((row + half, rows - half, 1))
    return pieces


class AxisScatter:
    def __init__(self, own, land_dp, land_fsdp, out, sems):
        self.own, self.land_dp, self.land_fsdp, self.out = own, land_dp, land_fsdp, out
        self.sems = sems
        self.fs, self.dp = lax.axis_index("fsdp"), lax.axis_index("dp")

    def bits(self, fs, dp):
        return (lax.rem(fs // 4, 2), lax.rem(fs // 2, 2), lax.rem(fs, 2)), (
            lax.rem(dp // 2, 2),
            lax.rem(dp, 2),
        )

    def dp_copy(self, step):
        other = lax.rem(self.dp + step, 4)
        _, (y, core) = self.bits(self.fs, other)
        return pltpu.make_async_remote_copy(
            src_ref=self.own.at[:, :, :, y, core],
            dst_ref=self.land_dp.at[step - 1],
            send_sem=self.sems.at[0, step],
            recv_sem=self.sems.at[1, step],
            device_id=(other, self.fs),
            device_id_type=MESH,
        )

    def fsdp_copy(self, step):
        other = lax.rem(self.fs + step, 8)
        (zh, zl, x), (y, core) = self.bits(other, self.dp)
        return pltpu.make_async_remote_copy(
            src_ref=self.own.at[zh, zl, x, y, core],
            dst_ref=self.land_fsdp.at[step - 1],
            send_sem=self.sems.at[2, step],
            recv_sem=self.sems.at[3, step],
            device_id=(self.dp, other),
            device_id_type=MESH,
        )

    def first(self):
        for step in range(1, 4):
            self.dp_copy(step).start()

    def second(self):
        for step in range(1, 4):
            self.dp_copy(step).wait()
        _, (y, core) = self.bits(self.fs, self.dp)
        mine = self.own.at[:, :, :, y, core]
        mine[...] = mine[...] + self.land_dp[0] + self.land_dp[1] + self.land_dp[2]
        for step in range(1, 8):
            self.fsdp_copy(step).start()

    def last(self):
        for step in range(1, 8):
            self.fsdp_copy(step).wait()
        (zh, zl, x), (y, core) = self.bits(self.fs, self.dp)
        total = self.own[zh, zl, x, y, core]
        for step in range(7):
            total = total + self.land_fsdp[step]
        self.out[...] = total


def axis_signal():
    fs, dp = lax.axis_index("fsdp"), lax.axis_index("dp")
    sem = pltpu.get_barrier_semaphore()
    for step in range(1, 4):
        to = (lax.rem(dp + step, 4), fs)
        pl.semaphore_signal(sem, inc=1, device_id=to, device_id_type=MESH)
    for step in range(1, 8):
        to = (dp, lax.rem(fs + step, 8))
        pl.semaphore_signal(sem, inc=1, device_id=to, device_id_type=MESH)


def axis_wait():
    pl.semaphore_wait(pltpu.get_barrier_semaphore(), 10)


class Plan:
    def __init__(self, dp, fsdp):
        self.shard = {n: (WEIGHT_SHAPE[n][0] // dp, WEIGHT_SHAPE[n][1] // fsdp) for n in WEIGHTS}
        self.row, at = {}, 0
        for name in WEIGHTS:
            self.row[name] = at
            at += self.shard[name][0] * self.shard[name][1] // 128
        self.rows = at

    def span(self, first, last, shift):
        r, c = self.shard[last]
        end = self.row[last] + r * c // 128
        return (self.row[first] + shift, end - self.row[first])

    def full_shape(self, name):
        return (2, 2, 2, self.shard[name][1], WEIGHT_SHAPE[name][0])

    def held_shape(self, name):
        r, c = self.shard[name]
        return (c, r) if c % 128 else (r, c)

    def blocks(self, name, shift):
        r, c = self.shard[name]
        return [
            (y, core, shift + self.row[name] + q * c, (y * 2 + core) * r + q * 128)
            for y in range(2)
            for core in range(2)
            for q in range(r // 128)
        ]


def put_blocks(plan, name, own, shift, values_of):
    c = plan.shard[name][1]
    for y, core, at, column in plan.blocks(name, shift):
        values = values_of(slice(column, column + 128)).astype(bf16)
        own[:, :, :, y, core, at : at + c, :] = values.reshape(2, 2, 2, c, 128)


def put_shard(plan, name, flat, shift, target):
    r, c = plan.shard[name]
    for q in range(r // 128):
        at = shift + plan.row[name] + q * c
        if c % 128:
            target[:, q * 128 : (q + 1) * 128] = flat[at : at + c, :]
        else:
            target[q * 128 : (q + 1) * 128, :] = flat[at : at + c, :].T


def load_weight(plan, name, buf, target, sem, shift):
    c = plan.shard[name][1]
    for y, core, row, column in plan.blocks(name, shift):
        pltpu.make_async_copy(
            buf.at[:, :, :, y, core, pl.ds(row, c), :],
            target.at[:, :, :, :, pl.ds(column, 128)],
            sem,
        ).start()


def wait_whole(target, sem):
    pltpu.make_async_copy(target, target, sem).wait()


def full(ref):
    values = ref[...]
    return values.reshape(-1, values.shape[-1])


def vector_places():
    places, at = {}, 0
    for name in PACKED_VECTORS:
        size = VECTOR_SIZE[name] // 32
        places[name] = (at // 128, at % 128, size)
        at += size
    return places


def block_owner(first, size):
    row = lax.broadcasted_iota(jnp.int32, (32, D), 0)
    lane = lax.broadcasted_iota(jnp.int32, (32, D), 1) + first
    return lane // size == lax.rem(row, 4) * 8 + row // 4


def iota(shape, axis):
    return lax.broadcasted_iota(jnp.int32, shape, axis)


def narrow_vectors():
    places = vector_places()
    return [
        (places[n][0], places[n][1] // 16, VECTOR_ROW[n])
        for n in VECTORS
        if VECTOR_SIZE[n] == D
    ]


def spread_rule(size, offset, first):
    return (iota((128, D), 0) - offset == lax.rem(iota((128, D), 1) + first, size)).astype(bf16)


def gather_rule(size, offset, first):
    return (iota((D, 128), 1) - offset == lax.rem(iota((D, 128), 0) + first, size)).astype(bf16)


def unpack_vectors(blocks, target):
    flat = blocks[...].reshape(32 * 16, 128)
    own = []
    for line in range(2):
        pick = (iota((32, 512), 1) == iota((32, 512), 0) * 16 + line).astype(bf16)
        own.append(nn(pick, flat))
    group = iota((32, 128), 1) // 16
    narrow = narrow_vectors()
    stacked = jnp.concatenate([jnp.where(group == g, own[line], 0.0) for line, g, _ in narrow])
    same = (lax.rem(iota((128, D), 0), 16) == lax.rem(iota((128, D), 1), 16)).astype(bf16)
    wide = nn(stacked.astype(bf16), same)

    def put(row, first, values, size):
        kept = jnp.where(block_owner(first, size), values, 0.0)
        target[row : row + 1, first : first + D] = jnp.sum(kept, axis=0, keepdims=True)

    for n, (_, _, row) in enumerate(narrow):
        put(row, 0, wide[n * 32 : (n + 1) * 32], 16)
    line = own[0].astype(bf16)
    values = nn(line, spread_rule(64, 0, 0))
    for first in range(0, FF, D):
        put(VECTOR_ROW["hidden"], first, values, 64)
    for first in range(0, 3 * D, D):
        put(VECTOR_ROW["upsample_bias"], first, nn(line, spread_rule(48, 64, first)), 48)


def pack_vectors(source, target):
    def take(row, first, size):
        values = jnp.broadcast_to(source[row : row + 1, first : first + D], (32, D))
        return jnp.where(block_owner(first, size), values, 0.0)

    def collect(values, rule):
        total = jnp.zeros((values.shape[0], 128), f32)
        for _ in range(3):
            term = values.astype(bf16)
            total += nn(term, rule)
            values = values - term.astype(f32)
        return total

    narrow = narrow_vectors()
    stacked = jnp.concatenate([take(row, 0, 16) for _, _, row in narrow])
    same = (lax.rem(iota((D, 128), 1), 16) == lax.rem(iota((D, 128), 0), 16)).astype(bf16)
    close = collect(stacked, same)
    group = iota((32, 128), 1) // 16
    lines = [jnp.zeros((32, 128), f32), jnp.zeros((32, 128), f32)]
    for n, (line, g, _) in enumerate(narrow):
        lines[line] += jnp.where(group == g, close[n * 32 : (n + 1) * 32], 0.0)
    hidden = take(VECTOR_ROW["hidden"], 0, 64)
    for first in range(D, FF, D):
        hidden += take(VECTOR_ROW["hidden"], first, 64)
    lines[0] += collect(hidden, gather_rule(64, 0, 0))
    for first in range(0, 3 * D, D):
        values = take(VECTOR_ROW["upsample_bias"], first, 48)
        lines[0] += collect(values, gather_rule(48, 64, first))
    both = jnp.concatenate([lines[0][:, None, :], lines[1][:, None, :]], axis=1)
    both = jnp.concatenate([both, jnp.zeros((32, 6, 128), f32)], axis=1)
    target[...] = both.reshape(CUBE + (8, 128))


def coarse_angles():
    ratios = jnp.arange(0, D, 2).astype(f32) / D
    inverse = 1.0 / 10000.0**ratios
    steps = SEQ // ANGLE_STEP
    places = jnp.concatenate(
        [jnp.arange(steps) * ANGLE_STEP, jnp.zeros((-steps % 8,), jnp.int32), jnp.arange(ANGLE_STEP)]
    ).astype(f32)
    angles = places[:, None] * inverse[None, :]
    return jnp.concatenate([jnp.sin(angles), jnp.cos(angles)], axis=1)


def expand_angles(coarse, angles, table_of):
    steps = SEQ // ANGLE_STEP
    start = steps + -steps % 8

    def body(q, carry):
        high_sin, high_cos = coarse[pl.ds(q, 1), :HALF], coarse[pl.ds(q, 1), HALF:]
        low_sin, low_cos = coarse[start:, :HALF], coarse[start:, HALF:]
        sine = high_sin * low_cos + high_cos * low_sin
        cosine = high_cos * low_cos - high_sin * low_sin
        rows = at_rows(q, ANGLE_STEP)
        angles[rows, :HALF] = sine
        angles[rows, HALF:] = cosine
        table_of(rows, sine.astype(bf16), cosine.astype(bf16))
        return carry

    lax.fori_loop(0, steps, body, 0)


def head_lanes(rows, head):
    return (lax.broadcasted_iota(jnp.int32, (rows, 128), 1) // HEAD_DIM) == head


def keep_head(values, head):
    return jnp.where(head_lanes(values.shape[0], head), values, 0).astype(bf16)


def rotate(pair, sines, cosines):
    low, high = pair[:, :HALF], pair[:, HALF:]
    return high * sines - low * cosines, low * sines + high * cosines


def norm_parts(values):
    row_mean = jnp.mean(values, axis=-1, keepdims=True)
    centred = values - row_mean
    variance = jnp.mean(centred * centred, axis=-1, keepdims=True)
    inv_std = lax.rsqrt(variance + epsilon)
    return centred * inv_std, inv_std


def norm_backward(normal, inv_std, gain, upstream):
    scaled = upstream * gain
    scaled_mean = jnp.mean(scaled, axis=-1, keepdims=True)
    cross_mean = jnp.mean(scaled * normal, axis=-1, keepdims=True)
    return inv_std * (scaled - scaled_mean - normal * cross_mean)


def vec(ref, name):
    r = VECTOR_ROW[name]
    return ref[r : r + 1, : VECTOR_SIZE[name]]


VECTOR_ROWS = 16


FRONT_ROWS = ("query_u", "query_v", "key", "value", "mixed")
CHUNK_LAST = (4, 4, 4, 4, 1, 1)
FIRST = ((0, 0), (1, 0))
BEFORE = ((0, 1), (1, 1), (2, 0), (0, 2), (1, 2), (0, 3), (1, 3), (2, 1), (3, 0), (0, 4), (1, 4))
AFTER = ((2, 2), (3, 1), (4, 0), (5, 0))
DURING = {
    8: ((2, 3), (3, 2), (4, 1), (5, 1)),
    16: ((3, 3),),
    23: ((2, 4), (3, 4)),
}


def front(plan, linked, ins):
    outs = {
        "vectors": ((16, FF), f32, VMEM),
    }
    outs |= {n + "_out": ((SEQ, D), bf16, ANY) for n in FRONT_ROWS}
    outs |= {
        "probs_out": ((HEADS, QB, PW), bf16, ANY),
    }
    scratch = {
        "normal": VMEM((SEQ, D), f32),
        "angles": VMEM((SEQ, D), f32),
        "key_table": VMEM((SEQ, 128 + D), bf16),
        "score": VMEM((2, QB, SEQ), f32),
        "turned": VMEM((2, QB, 128 + D), bf16),
        "probs": VMEM((2, QB, PW), bf16),
        "probs_sem": pltpu.SemaphoreType.DMA((2,)),
        "out_sem": pltpu.SemaphoreType.DMA((len(FRONT_ROWS),)),
    }
    scratch |= {n: VMEM((SEQ, D), bf16) for n in FRONT_ROWS}
    params = {}
    if linked:
        rows = VECTOR_ROWS + plan.rows
        chunks = [
            (0, 128),
            (128, VECTOR_ROWS + plan.span("project", "position", 0)[1] - 128),
            plan.span("mixing", "expand", VECTOR_ROWS),
            plan.span("contract", "contract", VECTOR_ROWS),
            plan.span("pooling", "pooling", VECTOR_ROWS),
            plan.span("upsample", "upsample", VECTOR_ROWS),
        ]
        pieces = split_pieces(chunks)
        outs["blocks"] = (CUBE + (rows, 128), bf16, ANY)
        scratch |= {
            "mine": VMEM((rows, 128), bf16),
            "project": VMEM(plan.full_shape("project"), bf16),
            "position": VMEM(plan.full_shape("position"), bf16),
            "vector_blocks": VMEM(CUBE + (VECTOR_ROWS, 128), bf16),
            "vector_lines": VMEM((VECTOR_ROWS, 128), f32),
            "send_sem": pltpu.SemaphoreType.DMA((COPIES * len(pieces),)),
            "recv_sem": pltpu.SemaphoreType.DMA((COPIES * len(pieces),)),
            "load_sem": pltpu.SemaphoreType.DMA((4,)),
        }
        params = dict(collective_id=0, has_side_effects=True)

    def body(ref):
        if linked:
            partner_signal()
            gather = Gather(ref.blocks, pieces, ref.send_sem, ref.recv_sem, ref.mine)

            def run(events):
                for chunk, stage in events:
                    for piece in (2 * chunk, 2 * chunk + 1):
                        gather.advance(piece, stage, last=CHUNK_LAST[chunk])

            def pack(name):
                r, c = plan.shard[name]
                shard = getattr(ref, name + "_shard")
                for q in range(r // 128):
                    at = VECTOR_ROWS + plan.row[name] + q * c
                    if c % 128:
                        ref.mine[at : at + c, :] = shard[:, q * 128 : (q + 1) * 128]
                    else:
                        ref.mine[at : at + c, :] = shard[q * 128 : (q + 1) * 128, :].T

            ref.vector_lines[...] = jnp.zeros_like(ref.vector_lines)
            for name, (line, offset, size) in vector_places().items():
                entries = getattr(ref, name + "_shard")[...].astype(f32).reshape(1, size)
                ref.vector_lines[line : line + 1, offset : offset + size] = entries
            ref.mine[:VECTOR_ROWS, :] = ref.vector_lines[...].astype(bf16)
            for name in ("project", "position"):
                pack(name)
            partner_wait()
            run(FIRST)
            for name in WEIGHTS[2:]:
                pack(name)
            own = pltpu.make_async_copy(
                ref.mine, ref.blocks.at[gather.bits], ref.load_sem.at[0]
            )
            own.start()

        def first_norm(i, carry):
            rows = at_rows(i, RB)
            ref.normal[rows, :] = norm_parts(ref.tokens[rows, :].astype(f32))[0]
            return carry

        lax.fori_loop(0, SEQ // RB, first_norm, 0)

        def table_of(rows, sine, cosine):
            ref.key_table[rows, 128 : 128 + HALF] = sine
            ref.key_table[rows, 128 + HALF :] = cosine

        expand_angles(ref.coarse, ref.angles, table_of)

        if linked:
            own.wait()
            run(BEFORE)
            load_weight(plan, "project", ref.blocks, ref.project, ref.load_sem.at[1], VECTOR_ROWS)
            load_weight(plan, "position", ref.blocks, ref.position, ref.load_sem.at[3], VECTOR_ROWS)
            small = pltpu.make_async_copy(
                ref.blocks.at[:, :, :, :, :, pl.ds(0, VECTOR_ROWS), :],
                ref.vector_blocks,
                ref.load_sem.at[2],
            )
            small.start()
            small.wait()
            unpack_vectors(ref.vector_blocks, ref.vectors)
            wait_whole(ref.project, ref.load_sem.at[1])
        else:
            ref.vectors[...] = ref.given_vectors[...]

        def project_rows(b, carry):
            rows = at_rows(b, QB)
            normed = ref.normal[rows, :] * vec(ref.vectors, "gain_one") + vec(
                ref.vectors, "shift_one"
            )
            joined = nt(normed.astype(bf16), full(ref.project))
            ref.query_u[rows, :] = (joined[:, :D] + vec(ref.vectors, "content")).astype(bf16)
            ref.query_v[rows, :] = (joined[:, :D] + vec(ref.vectors, "position_bias")).astype(bf16)
            ref.key[rows, :] = joined[:, D : 2 * D].astype(bf16)
            ref.value[rows, :] = joined[:, 2 * D :].astype(bf16)
            return carry

        lax.fori_loop(0, BLOCKS, project_rows, 0)

        def row_copy(i):
            name = FRONT_ROWS[i]
            return pltpu.make_async_copy(
                getattr(ref, name), getattr(ref, name + "_out"), ref.out_sem.at[i]
            )

        for i in range(4):
            row_copy(i).start()

        if linked:
            run(AFTER)
            wait_whole(ref.position, ref.load_sem.at[3])
            position = ref.position.reshape(D, D)
        else:
            position = ref.position

        def out_copy(head, slot):
            return pltpu.make_async_copy(
                ref.probs.at[slot], ref.probs_out.at[head], ref.probs_sem.at[slot]
            )

        def scores(lanes, b, e):
            row, width = b * QB, (b + 1) * QB
            rows = slice(row, row + QB)
            spread = nn(keep_head(ref.query_v[rows, lanes], e), position[lanes, :])
            low, high = rotate(spread, ref.angles[rows, :HALF], ref.angles[rows, HALF:])
            ref.turned[e, :, :128] = keep_head(ref.query_u[rows, lanes], e)
            ref.turned[e, :, 128 : 128 + HALF] = low.astype(bf16)
            ref.turned[e, :, 128 + HALF :] = high.astype(bf16)
            ref.score[e, :, :width] = nt(ref.turned[e], ref.key_table[:width, :])

        def softmax(b, e):
            row, width = b * QB, (b + 1) * QB
            for sub in range(QB // SB):
                used = row + (sub + 1) * SB
                for g in range(SB // CH):
                    at = slice(sub * SB + g * CH, sub * SB + (g + 1) * CH)
                    tiles = [
                        ref.score[e, at, i * 128 : (i + 1) * 128] for i in range(used // 128)
                    ]
                    lane = lax.broadcasted_iota(jnp.int32, (CH, SB), 1)
                    place = lax.broadcasted_iota(jnp.int32, (CH, SB), 0) + g * CH
                    tiles[-1] = jnp.where(lane <= place, tiles[-1], -1e30)
                    top = tiles[0]
                    for tile in tiles[1:]:
                        top = jnp.maximum(top, tile)
                    top = jnp.max(top, axis=1, keepdims=True)
                    tiles = [jnp.exp2((tile - top) * EXP_SCALE) for tile in tiles]
                    total = tiles[0]
                    for tile in tiles[1:]:
                        total = total + tile
                    scale = 1.0 / jnp.sum(total, axis=1, keepdims=True)
                    for i, tile in enumerate(tiles):
                        lanes = slice(POFF[b] + i * 128, POFF[b] + (i + 1) * 128)
                        ref.probs[e, at, lanes] = (tile * scale).astype(bf16)
                if used < width:
                    ref.probs[e, sub * SB : (sub + 1) * SB, POFF[b] + used : POFF[b] + width] = (
                        jnp.zeros((SB, width - used), bf16)
                    )

        def pair(turn, inner):
            hp = turn * 2 + inner
            lanes = pl.ds(pl.multiple_of(hp * 128, 128), 128)
            ref.key_table[:, :128] = ref.key[:, lanes]

            if inner > 0:
                for e in range(2):
                    out_copy(0, e).wait()
            else:

                @pl.when(turn > 0)
                def _():
                    for e in range(2):
                        out_copy(0, e).wait()


            for b in range(BLOCKS):
                for e in range(2):
                    scores(lanes, b, e)
                    softmax(b, e)
                    for when, events in DURING.items():
                        if linked and when % 12 == inner * 6 + b * 2 + e:
                            run_at(turn, when // 12, lambda events=events: run(events))
                row, width = b * QB, (b + 1) * QB
                values = ref.value[:width, lanes]
                span = slice(POFF[b], POFF[b] + width)
                ref.mixed[row : row + QB, lanes] = jnp.where(
                    head_lanes(QB, 0),
                    nn(ref.probs[0, :, span], values),
                    nn(ref.probs[1, :, span], values),
                ).astype(bf16)
            for e in range(2):
                out_copy(hp * 2 + e, e).start()

        def two_pairs(turn, carry):
            pair(turn, 0)
            pair(turn, 1)
            return carry

        lax.fori_loop(0, HEADS // 4, two_pairs, 0)
        row_copy(4).start()
        for e in range(2):
            out_copy(0, e).wait()
        if linked:
            for i in range(len(pieces)):
                gather.drain(i, last=CHUNK_LAST[i // 2])
        for i in range(5):
            row_copy(i).wait()

    return call(body, ins, outs, scratch, **params)


MIDDLE = ("mixing", "expand", "contract", "pooling", "upsample")


def middle(plan, linked, ins):
    def weight_shape(name):
        return plan.full_shape(name) if linked else WEIGHT_SHAPE[name][::-1]

    outs = {
        "output_out": ((SEQ, D), bf16, ANY),
        "first_grad_out": ((SEQ, D), f32, ANY),
        "mixed_grad_out": ((SEQ, D), bf16, ANY),
        "sums": ((16, FF), f32, VMEM),
    }
    summed = ("pooling", "upsample") if linked else ()
    kept = [n for n in MIDDLE if n not in summed]
    outs |= {n + "_grad_out": (weight_shape(n), bf16, ANY) for n in kept}
    params = {}
    scratch = {n: VMEM(weight_shape(n), bf16) for n in MIDDLE}
    scratch |= {
        "normal": VMEM((SEQ, D), f32),
        "inverse": VMEM((SEQ, 128), f32),
        "second_low": VMEM((SEQ, D), bf16),
        "activated": VMEM((SEQ, FF), bf16),
        "slope": VMEM((SEQ, FF), bf16),
        "tiles": VMEM((D // 128, SEQ + 16, 128), f32),
        "grouped": VMEM((THIRD, 3 * D), bf16),
        "up_rows": VMEM((THIRD, 3 * D), bf16),
        "branch_grad": VMEM((SEQ, D), bf16),
        "attended_grad": VMEM((SEQ, D), bf16),
        "parts": VMEM((5, 8, FF), f32),
        "output": VMEM((SEQ, D), bf16),
        "first_grad": VMEM((SEQ, D), f32),
        "mixed_grad": VMEM((SEQ, D), bf16),
        "sem": pltpu.SemaphoreType.DMA((len(MIDDLE),)),
        "out_sem": pltpu.SemaphoreType.DMA((3 + len(kept),)),
    }
    scratch |= {n + "_grad": VMEM(weight_shape(n), bf16) for n in kept}
    if linked:
        gather_pieces = split_pieces(
            [plan.span(n, n, VECTOR_ROWS) for n in ("pooling", "upsample")]
        )
        base = -plan.row["pooling"]
        pieces = split_pieces([plan.span(n, n, base) for n in summed])
        rows = plan.span("pooling", "upsample", base)[1]
        outs["blocks_out"] = (CUBE + (VECTOR_ROWS + plan.rows, 128), bf16, ANY)
        outs["partial"] = ((2, 2, rows, 128), bf16, ANY)
        scratch |= {
            "own": VMEM(CUBE + (rows, 128), bf16),
            "land": VMEM(CUBE + (rows, 128), bf16),
            "partial_sem": pltpu.SemaphoreType.DMA,
            "gather_send": pltpu.SemaphoreType.DMA((4 * COPIES,)),
            "gather_recv": pltpu.SemaphoreType.DMA((4 * COPIES,)),
            "send_sem": pltpu.SemaphoreType.DMA((4 * COPIES,)),
            "recv_sem": pltpu.SemaphoreType.DMA((4 * COPIES,)),
        }
        params = dict(
            collective_id=1,
            has_side_effects=True,
            alias={list(ins).index("blocks"): list(outs).index("blocks_out")},
        )

    def body(ref):
        def fetch(name):
            i = MIDDLE.index(name)
            if linked:
                load_weight(
                    plan, name, ref.blocks_out, getattr(ref, name), ref.sem.at[i], VECTOR_ROWS
                )
            else:
                pltpu.make_async_copy(
                    getattr(ref, name + "_full"), getattr(ref, name), ref.sem.at[i]
                ).start()

        gather_stage = scatter_stage = None
        if linked:
            gather = Gather(ref.blocks_out, gather_pieces, ref.gather_send, ref.gather_recv)
            scatter = Scatter(ref.own, ref.land, None, pieces, ref.send_sem, ref.recv_sem)
            partner_signal()

            def gather_stage(stage):
                for i in range(4):
                    gather.advance(i, stage, first=1)

            def scatter_stage(name, stage):
                for half in range(2):
                    scatter.advance(summed.index(name) * 2 + half, stage, last=3)

        for name in ("mixing", "expand", "contract"):
            fetch(name)
        if linked:
            partner_wait()
            gather_stage(1)
        else:
            fetch("pooling")
            fetch("upsample")

        outgoing = ["output", "first_grad", "mixed_grad"] + [n + "_grad" for n in kept]

        def send_out(name):
            return pltpu.make_async_copy(
                getattr(ref, name),
                getattr(ref, name + "_out"),
                ref.out_sem.at[outgoing.index(name)],
            )

        def at_step(i, number, action, *args):
            if linked:
                run_at(i, number, lambda: action(*args))

        def ready(name):
            wait_whole(getattr(ref, name), ref.sem.at[MIDDLE.index(name)])

        def get(name):
            return full(getattr(ref, name))

        def put(name, values):
            if name in summed:
                put_blocks(plan, name, ref.own, base, lambda columns: values[:, columns])
                return
            target = getattr(ref, name + "_grad")
            target[...] = values.astype(bf16).reshape(target.shape)
            send_out(name + "_grad").start()

        def third(start, k):
            return jnp.concatenate(
                [ref.tiles[t, pl.ds(start + k, THIRD, stride=3), :] for t in range(D // 128)],
                axis=1,
            )

        def put_third(start, k, values):
            for t in range(D // 128):
                ref.tiles[t, pl.ds(start + k, THIRD, stride=3), :] = values[
                    :, t * 128 : (t + 1) * 128
                ]

        def rows_of(rows):
            return jnp.concatenate([ref.tiles[t, rows, :] for t in range(D // 128)], axis=1)

        def put_rows(rows, values):
            for t in range(D // 128):
                ref.tiles[t, rows, :] = values[:, t * 128 : (t + 1) * 128]

        def shifted_rows(i):
            return pl.ds(pl.multiple_of(i * MB + 8, 8), MB)

        ref.parts[...] = jnp.zeros_like(ref.parts)
        ref.sums[...] = jnp.zeros_like(ref.sums)

        def add_part(slot, values):
            columns = values.shape[1]
            ref.parts[slot, :, :columns] += eight_rows(values)

        def put_sum(name, values):
            r = VECTOR_ROW[name]
            ref.sums[r : r + 1, : values.shape[1]] = values

        def put_part(name, slot):
            columns = VECTOR_SIZE[name]
            put_sum(name, jnp.sum(ref.parts[slot, :, :columns], axis=0, keepdims=True))

        for name in ("mixing", "expand", "contract"):
            ready(name)

        def forward(i, carry):
            rows = at_rows(i, MB)
            attended = nt(ref.mixed[rows, :], get("mixing")) + vec(ref.vectors, "mixing_bias")
            first = ref.tokens[rows, :].astype(f32) + attended
            normal, inverse = norm_parts(first)
            ref.normal[rows, :] = normal
            ref.inverse[rows, :] = jnp.broadcast_to(inverse, (MB, 128))
            low = (
                normal * vec(ref.vectors, "gain_two") + vec(ref.vectors, "shift_two")
            ).astype(bf16)
            ref.second_low[rows, :] = low
            inner = nt(low, get("expand")) + vec(ref.vectors, "hidden")
            phi = 0.5 * (1.0 + lax.erf(inner * 2.0 ** (-0.5)))
            act = (inner * phi).astype(bf16)
            ref.activated[rows, :] = act
            bell = jnp.exp(-0.5 * inner * inner) * (2.0 * math.pi) ** (-0.5)
            ref.slope[rows, :] = (phi + inner * bell).astype(bf16)
            block = first + nt(act, get("contract")) + vec(ref.vectors, "contract_bias")
            put_rows(shifted_rows(i), block)
            at_step(i, 1, gather_stage, 2)
            at_step(i, 4, gather_stage, 3)
            return carry

        lax.fori_loop(0, SEQ // MB, forward, 0)

        put_rows(slice(0, 8), jnp.zeros((8, D), f32))
        for k in range(3):
            ref.grouped[:, k * D : (k + 1) * D] = third(6, k).astype(bf16)
        if linked:
            gather_stage(4)
            fetch("pooling")
            fetch("upsample")
        ready("pooling")
        pooled = (
            nt(ref.grouped[...], get("pooling")) + vec(ref.vectors, "pooling_bias")
        ).astype(bf16)
        ready("upsample")
        for k in range(3):
            columns = slice(k * D, (k + 1) * D)
            upward = nt(pooled, get("upsample")[columns, :]) + vec(ref.vectors, "upsample_bias")[
                :, columns
            ]
            put_third(8, k, third(8, k) + upward)

        def write_output(i, carry):
            ref.output[at_rows(i, MB), :] = rows_of(shifted_rows(i)).astype(bf16)
            put_rows(shifted_rows(i), ref.cotangent[at_rows(i, MB), :].astype(f32))
            return carry

        lax.fori_loop(0, SEQ // MB, write_output, 0)

        send_out("output").start()

        for k in range(3):
            ref.up_rows[:, k * D : (k + 1) * D] = third(8, k).astype(bf16)
        up_rows = ref.up_rows[...]
        put_sum("upsample_bias", jnp.sum(up_rows.astype(f32), axis=0, keepdims=True))
        put("upsample", tn(up_rows, pooled))
        if linked:
            scatter_stage("upsample", 0)
        pooled_grad = nn(up_rows, get("upsample")).astype(bf16)
        put_sum("pooling_bias", jnp.sum(pooled_grad.astype(f32), axis=0, keepdims=True))
        put("pooling", tn(pooled_grad, ref.grouped[...]))
        if linked:
            scatter_stage("pooling", 0)
        for k in range(3):
            put_third(
                6, k, nn(pooled_grad, get("pooling")[:, k * D : (k + 1) * D])
            )
        put_rows(slice(SEQ + 6, SEQ + 8), jnp.zeros((2, D), f32))
        if linked:
            scatter_stage("upsample", 1)

        def backward(i, carry):
            rows = at_rows(i, MB)
            block_grad = ref.cotangent[rows, :].astype(f32) + rows_of(shifted_rows(i))
            branch_grad = block_grad.astype(bf16)
            ref.branch_grad[rows, :] = branch_grad
            add_part(0, branch_grad.astype(f32))
            inner_grad = (nn(branch_grad, get("contract")) * ref.slope[rows, :].astype(f32)).astype(
                bf16
            )
            ref.slope[rows, :] = inner_grad
            add_part(1, inner_grad.astype(f32))
            second_grad = nn(inner_grad, get("expand"))
            normal = ref.normal[rows, :]
            add_part(2, second_grad * normal)
            add_part(3, second_grad)
            first_grad = block_grad + norm_backward(
                normal, ref.inverse[rows, :1], vec(ref.vectors, "gain_two"), second_grad
            )
            ref.first_grad[rows, :] = first_grad
            attended_grad = first_grad.astype(bf16)
            ref.attended_grad[rows, :] = attended_grad
            add_part(4, attended_grad.astype(f32))
            ref.mixed_grad[rows, :] = nn(attended_grad, get("mixing")).astype(bf16)
            at_step(i, 0, scatter_stage, "pooling", 1)
            at_step(i, 3, scatter_stage, "upsample", 2)
            at_step(i, 5, scatter_stage, "pooling", 2)
            return carry

        lax.fori_loop(0, SEQ // MB, backward, 0)
        send_out("first_grad").start()
        send_out("mixed_grad").start()
        put_part("contract_bias", 0)
        put_part("hidden", 1)
        put_part("gain_two", 2)
        put_part("shift_two", 3)
        put_part("mixing_bias", 4)

        def contract_part(part, carry):
            columns = pl.ds(pl.multiple_of(part * D, D), D)
            values = tn(ref.branch_grad[...], ref.activated[:, columns]).astype(bf16)
            target = ref.contract_grad.at[..., columns]
            target[...] = values.reshape(target.shape)
            return carry

        lax.fori_loop(0, FF // D, contract_part, 0)
        send_out("contract_grad").start()
        if linked:
            scatter_stage("upsample", 3)

        def expand_part(part, carry):
            columns = pl.ds(pl.multiple_of(part * D, D), D)
            values = tn(ref.slope[:, columns], ref.second_low[...]).astype(bf16)
            if linked:
                target = ref.expand_grad.at[part // 2, lax.rem(part, 2)]
            else:
                target = ref.expand_grad.at[columns]
            target[...] = values.reshape(target.shape)
            return carry

        lax.fori_loop(0, FF // D, expand_part, 0)
        send_out("expand_grad").start()
        put("mixing", tn(ref.attended_grad[...], ref.mixed[...]))
        if linked:
            scatter_stage("pooling", 3)
            _, _, x, y, core = scatter.bits
            partial = pltpu.make_async_copy(
                ref.own.at[:, :, x, y, core], ref.partial, ref.partial_sem
            )
            partial.start()
            partial.wait()
            for i in range(4):
                gather.drain(i, first=1)
        for name in outgoing:
            send_out(name).wait()

    return call(body, ins, outs, scratch, **params)


BACK_FIRST = (0, 0, 3, 0, 0, 0)
BACK_DURING = {
    2: ((0, 1),),
    7: ((0, 2), (1, 1)),
    14: ((0, 3), (1, 2), (2, 4)),
    18: ((0, 4), (1, 3)),
    23: ((1, 4),),
}


def back(plan, linked, ins):
    outs = {"token_grad": ((SEQ, D), f32, VMEM)}
    late_rows = ("tokens", "mixed_grad", "mixed", "value", "key", "query_u", "query_v", "first_grad")
    scratch = {
        "angles": VMEM((SEQ, D), f32),
        "key_table": VMEM((SEQ, 128 + D), bf16),
        "prob_grad": VMEM((2, QB, SEQ), f32),
        "total_grad": VMEM((2, QB, SEQ), bf16),
        "probs": VMEM((4, QB, PW), bf16),
        "key_acc": VMEM((128, SEQ), f32),
        "value_acc": VMEM((128, SEQ), f32),
        "joined_grad": VMEM((SEQ, 3 * D), bf16),
        "normed_low": VMEM((SEQ, D), bf16),
        "position_grad": VMEM((D, D), f32),
        "parts": VMEM((2, 8, D), f32),
        "all_sums": VMEM((16, FF), f32),
        "probs_sem": pltpu.SemaphoreType.DMA((4,)),
        "load_sem": pltpu.SemaphoreType.DMA((2,)),
        "row_sem": pltpu.SemaphoreType.DMA((len(late_rows),)),
    }
    scratch |= {n: VMEM((SEQ, D), f32 if n == "first_grad" else bf16) for n in late_rows}
    params = {}
    project_shape = plan.full_shape("project") if linked else (3 * D, D)
    position_shape = plan.full_shape("position") if linked else (D, D)
    scratch |= {"project": VMEM(project_shape, bf16), "position": VMEM(position_shape, bf16)}
    if linked:
        early_names = ("contract", "expand", "mixing")
        early = [plan.span("contract", "contract", 0), plan.span("mixing", "expand", 0)]
        late = [plan.span("pooling", "upsample", 0), plan.span("position", "position", 0)]
        row, rows = plan.span("project", "project", 0)
        late += [(row, rows // 2), (row + rows // 2, rows // 2)]
        pieces = split_pieces(early + late)
        count = COPIES * len(pieces)
        own_rows = plan.rows
        outs["vector_out"] = ((8, 128), f32, VMEM)
        outs["flat_out"] = ((own_rows, 128), f32, ANY)
        scratch |= {
            "own": VMEM(CUBE + (own_rows, 128), bf16),
            "land": VMEM(CUBE + (own_rows, 128), bf16),
            "flat": VMEM((own_rows, 128), f32),
            "vector_own": VMEM(CUBE + (8, 128), f32),
            "land_dp": VMEM((3, 2, 2, 2, 8, 128), f32),
            "land_fsdp": VMEM((7, 8, 128), f32),
            "vector_sem": pltpu.SemaphoreType.DMA((4, 8)),
            "send_sem": pltpu.SemaphoreType.DMA((count,)),
            "recv_sem": pltpu.SemaphoreType.DMA((count,)),
            "own_sem": pltpu.SemaphoreType.DMA((4,)),
        }
        params = dict(collective_id=2, has_side_effects=True)
    else:
        outs["project_grad"] = ((3 * D, D), bf16, VMEM)
        outs["position_grad_out"] = ((D, D), bf16, VMEM)
        outs["sums_out"] = ((16, FF), f32, VMEM)

    def body(ref):
        def row_copy(name):
            return pltpu.make_async_copy(
                getattr(ref, name + "_in"), getattr(ref, name), ref.row_sem.at[late_rows.index(name)]
            )

        for name in late_rows[:7]:
            row_copy(name).start()
        if linked:
            load_weight(plan, "project", ref.blocks, ref.project, ref.load_sem.at[0], VECTOR_ROWS)
            load_weight(plan, "position", ref.blocks, ref.position, ref.load_sem.at[1], VECTOR_ROWS)
            matrix = Scatter(ref.own, ref.land, ref.flat, pieces, ref.send_sem, ref.recv_sem)
            vector = AxisScatter(
                ref.vector_own, ref.land_dp, ref.land_fsdp, ref.vector_out, ref.vector_sem
            )
            axis_signal()

            def run(events):
                for chunk, stage in events:
                    for piece in (2 * chunk, 2 * chunk + 1):
                        matrix.advance(piece, stage, first=BACK_FIRST[chunk])

            for i, name in enumerate(early_names):
                c = plan.shard[name][1]
                for y, core, row, column in plan.blocks(name, 0):
                    pltpu.make_async_copy(
                        getattr(ref, name + "_grad").at[:, :, :, :, pl.ds(column, 128)],
                        ref.own.at[:, :, :, y, core, pl.ds(row, c), :],
                        ref.own_sem.at[i],
                    ).start()
            _, _, x, y, core = matrix.bits
            row, rows = late[0]
            partial = pltpu.make_async_copy(
                ref.partial, ref.own.at[:, :, x, y, core, pl.ds(row, rows), :], ref.own_sem.at[3]
            )
            partial.start()
        else:
            for i, name in enumerate(("project", "position")):
                pltpu.make_async_copy(
                    getattr(ref, name + "_full"), getattr(ref, name), ref.load_sem.at[i]
                ).start()

        def in_copy(head, slot):
            return pltpu.make_async_copy(
                ref.probs_in.at[head], ref.probs.at[slot], ref.probs_sem.at[slot]
            )

        for e in range(2):
            in_copy(e, e).start()

        def table_of(rows, sine, cosine):
            ref.key_table[rows, 128 : 128 + HALF] = sine
            ref.key_table[rows, 128 + HALF :] = cosine

        expand_angles(ref.coarse, ref.angles, table_of)

        def norm_rows(rows):
            return norm_parts(ref.tokens[rows, :].astype(f32))

        def low_rows(i, carry):
            rows = at_rows(i, RB)
            normal, _ = norm_rows(rows)
            ref.normed_low[rows, :] = (
                normal * vec(ref.vectors, "gain_one") + vec(ref.vectors, "shift_one")
            ).astype(bf16)
            return carry

        row_copy("tokens").wait()
        lax.fori_loop(0, SEQ // RB, low_rows, 0)
        ref.all_sums[...] = ref.sums[...]
        ref.parts[...] = jnp.zeros_like(ref.parts)
        if linked:
            axis_wait()
            partial.wait()
            run([(2, 3)])
            for i, name in enumerate(early_names):
                row, rows = plan.span(name, name, 0)
                whole = ref.own.at[:, :, :, :, :, pl.ds(row, rows), :]
                wait_whole(whole, ref.own_sem.at[i])
                if i == 0:
                    run([(0, 0)])
            run([(1, 0)])
        wait_whole(ref.project, ref.load_sem.at[0])
        wait_whole(ref.position, ref.load_sem.at[1])
        position = ref.position.reshape(D, D)
        for name in late_rows[1:7]:
            row_copy(name).wait()
        row_copy("first_grad").start()

        def pair(hp, carry):
            start = pl.multiple_of(hp * 128, 128)
            lanes = pl.ds(start, 128)
            base = lax.rem(hp, 2) * 2
            for e in range(2):
                in_copy(0, base + e).wait()

            @pl.when(hp < HEADS // 2 - 1)
            def _():
                for e in range(2):
                    in_copy(hp * 2 + 2 + e, 2 - base + e).start()

            ref.key_table[:, :128] = ref.key[:, lanes]
            content_sum = jnp.zeros((1, 128), f32)
            position_sum = jnp.zeros((1, 128), f32)
            for b in range(BLOCKS):
                row, width = b * QB, (b + 1) * QB
                rows = slice(row, row + QB)
                span = slice(POFF[b], POFF[b] + width)
                by_content, by_position = [], None
                for e in range(2):
                    upstream = keep_head(ref.mixed_grad[rows, lanes], e)
                    row_dot = jnp.sum(
                        upstream.astype(f32) * ref.mixed[rows, lanes].astype(f32),
                        axis=1,
                        keepdims=True,
                    )
                    ref.prob_grad[e, :, :width] = nt(upstream, ref.value[:width, lanes]) - row_dot
                    for sub in range(QB // SB):
                        used = row + (sub + 1) * SB
                        for g in range(SB // CH):
                            at = slice(sub * SB + g * CH, sub * SB + (g + 1) * CH)
                            p = ref.probs[base + e, at, POFF[b] : POFF[b] + used].astype(f32)
                            ref.total_grad[e, at, :used] = (
                                p * ref.prob_grad[e, at, :used] * HEAD_DIM ** (-0.5)
                            ).astype(bf16)
                        if used < width:
                            ref.total_grad[e, sub * SB : (sub + 1) * SB, used:width] = jnp.zeros(
                                (SB, width - used), bf16
                            )
                    scored = ref.total_grad[e, :, :width]
                    turned = nn(scored, ref.key_table[:width, :])
                    by_content.append(turned[:, :128])
                    low, high = rotate(
                        turned[:, 128:], ref.angles[rows, :HALF], ref.angles[rows, HALF:]
                    )
                    spread = jnp.concatenate([low, high], axis=1).astype(bf16)
                    own = (lax.broadcasted_iota(jnp.int32, (128, D), 0) // HEAD_DIM) == e
                    part = nt(spread, jnp.where(own, position[lanes, :], 0).astype(bf16))
                    by_position = part if by_position is None else by_position + part
                    part = tn(keep_head(ref.query_v[rows, lanes], e), spread)
                    if b == 0 and e == 0:
                        ref.position_grad[lanes, :] = part
                    else:
                        ref.position_grad[lanes, :] += part
                    to_key = tn(keep_head(ref.query_u[rows, lanes], e), scored)
                    to_value = tn(upstream, ref.probs[base + e, :, span])
                    if e == 0:
                        if b > 0:
                            ref.key_acc[:, :row] += to_key[:, :row]
                            ref.value_acc[:, :row] += to_value[:, :row]
                        ref.key_acc[:, row:width] = to_key[:, row:]
                        ref.value_acc[:, row:width] = to_value[:, row:]
                    else:
                        ref.key_acc[:, :width] += to_key
                        ref.value_acc[:, :width] += to_value
                    for when, events in BACK_DURING.items():
                        if linked and when % 6 == b * 2 + e:
                            run_at(hp, when // 6, lambda events=events: run(events))
                by_content = jnp.where(head_lanes(QB, 0), by_content[0], by_content[1])
                ref.joined_grad[rows, lanes] = (by_content + by_position).astype(bf16)
                content_sum += jnp.sum(by_content, axis=0, keepdims=True)
                position_sum += jnp.sum(by_position, axis=0, keepdims=True)
            ref.joined_grad[:, pl.ds(start + D, 128)] = ref.key_acc[...].T.astype(bf16)
            ref.joined_grad[:, pl.ds(start + 2 * D, 128)] = ref.value_acc[...].T.astype(bf16)
            r = VECTOR_ROW["content"]
            ref.all_sums[r : r + 1, lanes] = content_sum
            r = VECTOR_ROW["position_bias"]
            ref.all_sums[r : r + 1, lanes] = position_sum
            return carry

        lax.fori_loop(0, HEADS // 2, pair, 0)

        row_copy("first_grad").wait()
        if linked:
            put_blocks(plan, "position", ref.own, 0, lambda columns: ref.position_grad[:, columns])
            run([(3, 0)])
        def project_part(part, carry):
            columns = pl.ds(pl.multiple_of(part * D, D), D)
            grad = tn(ref.joined_grad[:, columns], ref.normed_low[...]).astype(bf16)
            if linked:
                ref.project_full[columns, :] = grad
            else:
                ref.project_grad[columns, :] = grad
            return carry

        lax.fori_loop(0, 3, project_part, 0)
        if linked:
            put_blocks(plan, "project", ref.own, 0, lambda columns: ref.project_full[:, columns])
            run([(4, 0), (5, 0), (3, 1)])
        else:
            ref.position_grad_out[...] = ref.position_grad[...].astype(bf16)

        def norm_back(i, carry):
            rows = at_rows(i, RB)
            normal, inverse = norm_rows(rows)
            upstream = nn(ref.joined_grad[rows, :], full(ref.project))
            ref.parts[0, :, :] += eight_rows(upstream * normal)
            ref.parts[1, :, :] += eight_rows(upstream)
            ref.token_grad[rows, :] = ref.first_grad[rows, :] + norm_backward(
                normal, inverse, vec(ref.vectors, "gain_one"), upstream
            )
            if linked:
                run_at(i, 1, lambda: run([(4, 1)]))
                run_at(i, 3, lambda: run([(5, 1)]))
                run_at(i, 5, lambda: run([(3, 2)]))
                run_at(i, 7, lambda: run([(4, 2)]))
            return carry

        lax.fori_loop(0, SEQ // RB, norm_back, 0)
        for slot, name in enumerate(("gain_one", "shift_one")):
            r = VECTOR_ROW[name]
            ref.all_sums[r : r + 1, :D] = jnp.sum(ref.parts[slot], axis=0, keepdims=True)
        if linked:
            pack_vectors(ref.all_sums, ref.vector_own)
            vector.first()
            run([(5, 2), (3, 3), (4, 3)])
            vector.second()
            run([(5, 3), (3, 4)])
            vector.last()
            run([(4, 4), (5, 4)])
            done = pltpu.make_async_copy(ref.flat, ref.flat_out, ref.own_sem.at[0])
            done.start()
            done.wait()
        else:
            ref.sums_out[...] = ref.all_sums[...]

    if linked:
        scratch["project_full"] = VMEM((3 * D, D), bf16)
    return call(body, ins, outs, scratch, **params)


PARTS = 4


def finish(plan, flat, vectors, rows):
    outs = {n + "_out": (plan.held_shape(n), f32, VMEM) for n in WEIGHTS}
    outs |= {n + "_out": ((VECTOR_SIZE[n] // 32,), f32, VMEM) for n in VECTORS}
    outs |= {n + "_copy": (v.shape, v.dtype, ANY) for n, v in rows.items()}
    ins = {"flat": (flat, VMEM), "vectors": (vectors, VMEM)}
    ins |= {n: (v, ANY) for n, v in rows.items()}
    scratch = {n + "_held": VMEM(v.shape, v.dtype) for n, v in rows.items()}
    scratch["in_sem"] = pltpu.SemaphoreType.DMA((len(rows) * PARTS,))
    scratch["out_sem"] = pltpu.SemaphoreType.DMA((len(rows) * PARTS,))

    def body(ref):
        loads, copies = [], []
        for n in rows:
            for part in range(PARTS):
                at = pl.ds(part * (SEQ // PARTS), SEQ // PARTS)
                held = getattr(ref, n + "_held").at[at]
                slot = len(loads)
                loads.append(
                    pltpu.make_async_copy(getattr(ref, n).at[at], held, ref.in_sem.at[slot])
                )
                copies.append(
                    pltpu.make_async_copy(
                        held, getattr(ref, n + "_copy").at[at], ref.out_sem.at[slot]
                    )
                )
        for load in loads:
            load.start()
        for load, copy in zip(loads, copies):
            load.wait()
            copy.start()
        for name in WEIGHTS:
            put_shard(plan, name, ref.flat, 0, getattr(ref, name + "_out"))
        for name, (line, offset, size) in vector_places().items():
            getattr(ref, name + "_out")[...] = ref.vectors[line, offset : offset + size]
        for copy in copies:
            copy.wait()

    return call(body, ins, outs, scratch)


def make_local(dp, fsdp):
    plan = Plan(dp, fsdp)
    linked = (dp, fsdp) == (4, 8)

    def gathered(weights):
        out = {}
        for name, shard in zip(WEIGHTS, weights):
            part = lax.all_gather(shard, "dp", axis=0, tiled=True)
            out[name + "_full"] = lax.all_gather(part, "fsdp", axis=1, tiled=True).T
        return out

    def gathered_vectors(vectors):
        rows = []
        for name, shard in zip(VECTORS, vectors):
            whole = lax.all_gather(shard, ("dp", "fsdp"), axis=0, tiled=True).astype(f32)
            rows.append(jnp.pad(whole, (0, FF - VECTOR_SIZE[name])))
        rows += [jnp.zeros((FF,), f32)] * (16 - len(rows))
        return jnp.stack(rows)

    def local(tokens, cotangent, *params):
        assert tokens.shape[0] == SEQ
        weights, vectors = params[:7], params[7:]
        given = dict(zip(VECTORS, vectors))
        coarse = coarse_angles()
        ins = {"tokens": (tokens, VMEM), "coarse": (coarse, VMEM)}
        if linked:
            ins |= {n + "_shard": (given[n], VMEM) for n in VECTORS}
            for n, w in zip(WEIGHTS, weights):
                ins[n + "_shard"] = (w.T if w.shape[1] % 128 else w, VMEM)
        else:
            whole = gathered(weights)
            ins["given_vectors"] = (gathered_vectors(vectors), VMEM)
            ins["project"] = (whole["project_full"], VMEM)
            ins["position"] = (whole["position_full"], VMEM)
        one = front(plan, linked, ins)

        ins = {
            "tokens": (tokens, VMEM),
            "cotangent": (cotangent, VMEM),
            "mixed": (one.mixed_out, VMEM),
            "vectors": (one.vectors, VMEM),
        }
        if linked:
            ins["blocks"] = (one.blocks, ANY)
        else:
            ins |= {n + "_full": (whole[n + "_full"], ANY) for n in MIDDLE}
        two = middle(plan, linked, ins)

        ins = {
            "tokens_in": (tokens, ANY),
            "coarse": (coarse, VMEM),
            "vectors": (one.vectors, VMEM),
            "query_u_in": (one.query_u_out, ANY),
            "query_v_in": (one.query_v_out, ANY),
            "key_in": (one.key_out, ANY),
            "value_in": (one.value_out, ANY),
            "mixed_in": (one.mixed_out, ANY),
            "mixed_grad_in": (two.mixed_grad_out, ANY),
            "first_grad_in": (two.first_grad_out, ANY),
            "sums": (two.sums, VMEM),
            "probs_in": (one.probs_out, ANY),
        }
        if linked:
            ins["blocks"] = (two.blocks_out, ANY)
            for n in ("contract", "expand", "mixing"):
                ins[n + "_grad"] = (getattr(two, n + "_grad_out"), ANY)
            ins["partial"] = (two.partial, ANY)
        else:
            ins |= {n + "_full": (whole[n + "_full"], ANY) for n in ("project", "position")}
        three = back(plan, linked, ins)

        if linked:
            last = finish(
                plan,
                three.flat_out,
                three.vector_out,
                {"output": two.output_out, "token_grad": three.token_grad},
            )
            output, token_grad = last.output_copy, last.token_grad_copy
            matrices = []
            for n in WEIGHTS:
                grad = getattr(last, n + "_out")
                matrices.append(grad if grad.shape == plan.shard[n] else grad.T)
            small = [getattr(last, n + "_out") for n in VECTORS]
        else:
            output, token_grad = two.output_out, three.token_grad
            grads = {n: getattr(two, n + "_grad_out") for n in MIDDLE}
            grads["project"] = three.project_grad
            grads["position"] = three.position_grad_out
            matrices = []
            for name in WEIGHTS:
                part = lax.psum_scatter(
                    grads[name].T, "fsdp", scatter_dimension=1, tiled=True
                )
                part = lax.psum_scatter(part, "dp", scatter_dimension=0, tiled=True)
                matrices.append(part.astype(f32))
            small = []
            for name in VECTORS:
                sums = three.sums_out[VECTOR_ROW[name], : VECTOR_SIZE[name]]
                small.append(
                    lax.psum_scatter(sums, ("dp", "fsdp"), scatter_dimension=0, tiled=True)
                )
        return (output, token_grad, *matrices, *small)

    return local


def solution(mesh):
    rows = P(("dp", "fsdp"), None)
    matrix = P("dp", "fsdp")
    vector = P(("dp", "fsdp"))
    return jax.shard_map(
        make_local(mesh.shape["dp"], mesh.shape["fsdp"]),
        mesh=mesh,
        in_specs=(rows,) * 2 + (matrix,) * 7 + (vector,) * 11,
        out_specs=(rows,) * 2 + (matrix,) * 7 + (vector,) * 11,
        check_vma=False,
    )
```

```python
import math
from types import SimpleNamespace

import jax
import jax.numpy as jnp
import numpy as np
from jax import lax
from jax.experimental import pallas as pl
from jax.experimental.pallas import tpu as pltpu
from jax.sharding import PartitionSpec as P

D = 512
HALF = D // 2
HEADS = 8
HEAD_DIM = 64
FF = 2048
SEQ = 1152
THIRD = SEQ // 3
QB = 384
SB = 128
CH = 16
RB = 128
MB = 192
BLOCKS = SEQ // QB
POFF = [sum((b + 1) * QB for b in range(n)) for n in range(BLOCKS + 1)]
PW = POFF[BLOCKS]
EXP_SCALE = HEAD_DIM ** (-0.5) * math.log2(math.e)
ANGLE_STEP = 32
epsilon = 1e-05
bf16 = jnp.bfloat16
f32 = jnp.float32
MESH = pl.DeviceIdType.MESH
VMEM_LIMIT = 63 << 20

WEIGHTS = ("project", "position", "mixing", "expand", "contract", "pooling", "upsample")
WEIGHT_SHAPE = {
    "project": (D, 3 * D),
    "position": (D, D),
    "mixing": (D, D),
    "expand": (D, FF),
    "contract": (FF, D),
    "pooling": (3 * D, D),
    "upsample": (D, 3 * D),
}
VECTORS = (
    "gain_one",
    "shift_one",
    "content",
    "position_bias",
    "mixing_bias",
    "gain_two",
    "shift_two",
    "hidden",
    "contract_bias",
    "pooling_bias",
    "upsample_bias",
)
VECTOR_SIZE = {n: D for n in VECTORS} | {"hidden": FF, "upsample_bias": 3 * D}
VECTOR_ROW = {n: i for i, n in enumerate(VECTORS)}
PACKED_VECTORS = ("hidden", "upsample_bias", "gain_one") + tuple(
    n for n in VECTORS if n not in ("hidden", "upsample_bias", "gain_one")
)


def nn(a, b):
    return lax.dot_general(a, b, (((1,), (0,)), ((), ())), preferred_element_type=f32)


def nt(a, b):
    return lax.dot_general(a, b, (((1,), (1,)), ((), ())), preferred_element_type=f32)


def tn(a, b):
    return lax.dot_general(a, b, (((0,), (0,)), ((), ())), preferred_element_type=f32)


def at_rows(step, rows):
    return pl.ds(pl.multiple_of(step * rows, rows), rows)


def eight_rows(values):
    rows, columns = values.shape
    return jnp.sum(values.reshape(rows // 8, 8, columns), axis=0)


def call(body, ins, outs, scratch, alias=None, **params):
    names = [*ins, *outs, *scratch]

    def kernel(*refs):
        body(SimpleNamespace(**dict(zip(names, refs))))

    results = pl.pallas_call(
        kernel,
        out_shape=[jax.ShapeDtypeStruct(s, t) for s, t, _ in outs.values()],
        in_specs=[pl.BlockSpec(memory_space=m) for _, m in ins.values()],
        out_specs=[pl.BlockSpec(memory_space=m) for _, _, m in outs.values()],
        scratch_shapes=list(scratch.values()),
        input_output_aliases=alias or {},
        compiler_params=pltpu.CompilerParams(vmem_limit_bytes=VMEM_LIMIT, **params),
    )(*[a for a, _ in ins.values()])
    return SimpleNamespace(**dict(zip(outs, results)))


VMEM = pltpu.VMEM
ANY = pl.ANY


BIT_AXIS = ("fsdp", "fsdp", "fsdp", "dp", "dp")
BIT_MASK = (4, 2, 1, 2, 1)
CUBE = (2,) * 5
GATHER_ORDER = ((2, 3, 4), (3, 2, 4))
SCATTER_ORDER = ((4, 3, 2), (4, 2, 3))
STAGES = 4
COPIES = 6


def my_bits():
    fs = lax.axis_index("fsdp")
    dp = lax.axis_index("dp")
    return (
        lax.rem(fs // 4, 2),
        lax.rem(fs // 2, 2),
        lax.rem(fs, 2),
        lax.rem(dp // 2, 2),
        lax.rem(dp, 2),
    )


def partner(*flipped):
    place = {"fsdp": lax.axis_index("fsdp"), "dp": lax.axis_index("dp")}
    bits = my_bits()
    for bit in flipped:
        place[BIT_AXIS[bit]] += BIT_MASK[bit] * (1 - 2 * bits[bit])
    return (place["dp"], place["fsdp"])


LINE_FLIPS = ((1,), (0,), (0, 1))


def flipped_bits(flips):
    return tuple(1 - b if k in flips else b for k, b in enumerate(my_bits()))


def partner_signal():
    sem = pltpu.get_barrier_semaphore()
    for flips in LINE_FLIPS + ((2,), (3,), (4,)):
        pl.semaphore_signal(sem, inc=1, device_id=partner(*flips), device_id_type=MESH)


def partner_wait():
    pl.semaphore_wait(pltpu.get_barrier_semaphore(), 6)


def run_at(step, number, action):
    if isinstance(step, int):
        if step == number:
            action()
        return

    @pl.when(step == number)
    def _():
        action()


class Gather:
    def __init__(self, buf, pieces, send_sem, recv_sem, mine=None):
        self.buf, self.pieces, self.mine = buf, pieces, mine
        self.send_sem, self.recv_sem = send_sem, recv_sem
        self.bits = my_bits()

    def copy(self, source, target, sem, device):
        return pltpu.make_async_remote_copy(
            src_ref=source,
            dst_ref=target,
            send_sem=self.send_sem.at[sem],
            recv_sem=self.recv_sem.at[sem],
            device_id=device,
            device_id_type=MESH,
        )

    def copies(self, i, stage):
        row, rows, kind = self.pieces[i]
        part = (pl.ds(row, rows),)
        if stage == 0:
            target = self.buf.at[self.bits + part]
            source = target if self.mine is None else self.mine.at[part]
            return [
                self.copy(source, target, i * COPIES + n, partner(*flips))
                for n, flips in enumerate(LINE_FLIPS)
            ]
        order = GATHER_ORDER[kind]
        free = (0, 1) + order[: stage - 1]
        index = tuple(slice(None) if k in free else self.bits[k] for k in range(5))
        ref = self.buf.at[index + part]
        return [self.copy(ref, ref, i * COPIES + 2 + stage, partner(order[stage - 1]))]

    def advance(self, i, stage, first=0, last=STAGES):
        if stage > first:
            for copy in self.copies(i, stage - 1):
                copy.wait_recv()
        if stage < last:
            for copy in self.copies(i, stage):
                copy.start()

    def drain(self, i, first=0, last=STAGES):
        for stage in range(first, last):
            for copy in self.copies(i, stage):
                copy.wait_send()


class Scatter:
    def __init__(self, own, land, out, pieces, send_sem, recv_sem):
        self.own, self.land, self.out, self.pieces = own, land, out, pieces
        self.send_sem, self.recv_sem = send_sem, recv_sem
        self.bits = my_bits()

    def index(self, order, stage, side):
        out = []
        for k in range(5):
            if k in order[:stage]:
                out.append(1 - self.bits[k] if side in ("land", "target") else self.bits[k])
            elif k in order[stage : stage + 1]:
                out.append(1 - self.bits[k] if side in ("send", "target") else self.bits[k])
            else:
                out.append(slice(None))
        return tuple(out)

    def copy(self, source, target, sem, device):
        return pltpu.make_async_remote_copy(
            src_ref=source,
            dst_ref=target,
            send_sem=self.send_sem.at[sem],
            recv_sem=self.recv_sem.at[sem],
            device_id=device,
            device_id_type=MESH,
        )

    def copies(self, i, stage):
        row, rows, kind = self.pieces[i]
        order = SCATTER_ORDER[kind]
        part = (pl.ds(row, rows),)
        if stage == 3:
            place = self.bits[:2] + tuple(1 - b for b in self.bits[2:])
            return [
                self.copy(
                    self.own.at[flipped_bits(flips) + part],
                    self.land.at[place + part],
                    i * COPIES + 3 + n,
                    partner(*flips),
                )
                for n, flips in enumerate(LINE_FLIPS)
            ]
        return [
            self.copy(
                self.own.at[self.index(order, stage, "send") + part],
                self.land.at[self.index(order, stage, "target") + part],
                i * COPIES + stage,
                partner(order[stage]),
            )
        ]

    def add(self, i, stage):
        row, rows, kind = self.pieces[i]
        order = SCATTER_ORDER[kind]
        part = (pl.ds(row, rows), slice(None))
        if stage == 3:
            total = self.own[self.bits + part].astype(f32)
            for flips in LINE_FLIPS:
                place = flipped_bits(flips)[:2] + tuple(1 - b for b in self.bits[2:])
                total = total + self.land[place + part].astype(f32)
            self.out[pl.ds(row, rows), :] = total
            return
        mine = self.own.at[self.index(order, stage, "own")]
        came = self.land.at[self.index(order, stage, "land")]
        free = 4 - stage

        def body(j, carry):
            at = tuple(lax.rem(j // 2 ** (free - 1 - q), 2) for q in range(free)) + part
            mine[at] = mine[at] + came[at]
            return carry

        lax.fori_loop(0, 2**free, body, 0, unroll=2)

    def advance(self, i, stage, first=0, last=STAGES):
        if stage > first:
            for copy in self.copies(i, stage - 1):
                copy.wait()
            self.add(i, stage - 1)
        if stage < last:
            for copy in self.copies(i, stage):
                copy.start()


def split_pieces(chunks):
    pieces = []
    for row, rows in chunks:
        half = (rows // 2 + 15) // 16 * 16
        pieces.append((row, half, 0))
        pieces.append((row + half, rows - half, 1))
    return pieces


class AxisScatter:
    def __init__(self, own, land_dp, land_fsdp, out, sems):
        self.own, self.land_dp, self.land_fsdp, self.out = own, land_dp, land_fsdp, out
        self.sems = sems
        self.fs, self.dp = lax.axis_index("fsdp"), lax.axis_index("dp")

    def bits(self, fs, dp):
        return (lax.rem(fs // 4, 2), lax.rem(fs // 2, 2), lax.rem(fs, 2)), (
            lax.rem(dp // 2, 2),
            lax.rem(dp, 2),
        )

    def dp_copy(self, step):
        other = lax.rem(self.dp + step, 4)
        _, (y, core) = self.bits(self.fs, other)
        return pltpu.make_async_remote_copy(
            src_ref=self.own.at[:, :, :, y, core],
            dst_ref=self.land_dp.at[step - 1],
            send_sem=self.sems.at[0, step],
            recv_sem=self.sems.at[1, step],
            device_id=(other, self.fs),
            device_id_type=MESH,
        )

    def fsdp_copy(self, step):
        other = lax.rem(self.fs + step, 8)
        (zh, zl, x), (y, core) = self.bits(other, self.dp)
        return pltpu.make_async_remote_copy(
            src_ref=self.own.at[zh, zl, x, y, core],
            dst_ref=self.land_fsdp.at[step - 1],
            send_sem=self.sems.at[2, step],
            recv_sem=self.sems.at[3, step],
            device_id=(self.dp, other),
            device_id_type=MESH,
        )

    def first(self):
        for step in range(1, 4):
            self.dp_copy(step).start()

    def second(self):
        for step in range(1, 4):
            self.dp_copy(step).wait()
        _, (y, core) = self.bits(self.fs, self.dp)
        mine = self.own.at[:, :, :, y, core]
        mine[...] = mine[...] + self.land_dp[0] + self.land_dp[1] + self.land_dp[2]
        for step in range(1, 8):
            self.fsdp_copy(step).start()

    def last(self):
        for step in range(1, 8):
            self.fsdp_copy(step).wait()
        (zh, zl, x), (y, core) = self.bits(self.fs, self.dp)
        total = self.own[zh, zl, x, y, core]
        for step in range(7):
            total = total + self.land_fsdp[step]
        self.out[...] = total


def axis_signal():
    fs, dp = lax.axis_index("fsdp"), lax.axis_index("dp")
    sem = pltpu.get_barrier_semaphore()
    for step in range(1, 4):
        to = (lax.rem(dp + step, 4), fs)
        pl.semaphore_signal(sem, inc=1, device_id=to, device_id_type=MESH)
    for step in range(1, 8):
        to = (dp, lax.rem(fs + step, 8))
        pl.semaphore_signal(sem, inc=1, device_id=to, device_id_type=MESH)


def axis_wait():
    pl.semaphore_wait(pltpu.get_barrier_semaphore(), 10)


class Plan:
    def __init__(self, dp, fsdp):
        self.shard = {n: (WEIGHT_SHAPE[n][0] // dp, WEIGHT_SHAPE[n][1] // fsdp) for n in WEIGHTS}
        self.row, at = {}, 0
        for name in WEIGHTS:
            self.row[name] = at
            at += self.shard[name][0] * self.shard[name][1] // 128
        self.rows = at

    def span(self, first, last, shift):
        r, c = self.shard[last]
        end = self.row[last] + r * c // 128
        return (self.row[first] + shift, end - self.row[first])

    def full_shape(self, name):
        return (2, 2, 2, self.shard[name][1], WEIGHT_SHAPE[name][0])

    def held_shape(self, name):
        r, c = self.shard[name]
        return (c, r) if c % 128 else (r, c)

    def blocks(self, name, shift):
        r, c = self.shard[name]
        return [
            (y, core, shift + self.row[name] + q * c, (y * 2 + core) * r + q * 128)
            for y in range(2)
            for core in range(2)
            for q in range(r // 128)
        ]


def put_blocks(plan, name, own, shift, values_of):
    c = plan.shard[name][1]
    for y, core, at, column in plan.blocks(name, shift):
        values = values_of(slice(column, column + 128)).astype(bf16)
        own[:, :, :, y, core, at : at + c, :] = values.reshape(2, 2, 2, c, 128)


def put_shard(plan, name, flat, shift, target):
    r, c = plan.shard[name]
    for q in range(r // 128):
        at = shift + plan.row[name] + q * c
        if c % 128:
            target[:, q * 128 : (q + 1) * 128] = flat[at : at + c, :]
        else:
            target[q * 128 : (q + 1) * 128, :] = flat[at : at + c, :].T


def load_weight(plan, name, buf, target, sem, shift):
    c = plan.shard[name][1]
    for y, core, row, column in plan.blocks(name, shift):
        pltpu.make_async_copy(
            buf.at[:, :, :, y, core, pl.ds(row, c), :],
            target.at[:, :, :, :, pl.ds(column, 128)],
            sem,
        ).start()


def wait_whole(target, sem):
    pltpu.make_async_copy(target, target, sem).wait()


def full(ref):
    values = ref[...]
    return values.reshape(-1, values.shape[-1])


def vector_places():
    places, at = {}, 0
    for name in PACKED_VECTORS:
        size = VECTOR_SIZE[name] // 32
        places[name] = (at // 128, at % 128, size)
        at += size
    return places


def block_owner(first, size):
    row = lax.broadcasted_iota(jnp.int32, (32, D), 0)
    lane = lax.broadcasted_iota(jnp.int32, (32, D), 1) + first
    return lane // size == lax.rem(row, 4) * 8 + row // 4


def iota(shape, axis):
    return lax.broadcasted_iota(jnp.int32, shape, axis)


def narrow_vectors():
    places = vector_places()
    return [
        (places[n][0], places[n][1] // 16, VECTOR_ROW[n])
        for n in VECTORS
        if VECTOR_SIZE[n] == D
    ]


def spread_rule(size, offset, first):
    return (iota((128, D), 0) - offset == lax.rem(iota((128, D), 1) + first, size)).astype(bf16)


def gather_rule(size, offset, first):
    return (iota((D, 128), 1) - offset == lax.rem(iota((D, 128), 0) + first, size)).astype(bf16)


def unpack_vectors(blocks, target):
    flat = blocks[...].reshape(32 * 16, 128)
    own = []
    for line in range(2):
        pick = (iota((32, 512), 1) == iota((32, 512), 0) * 16 + line).astype(bf16)
        own.append(nn(pick, flat))
    group = iota((32, 128), 1) // 16
    narrow = narrow_vectors()
    stacked = jnp.concatenate([jnp.where(group == g, own[line], 0.0) for line, g, _ in narrow])
    same = (lax.rem(iota((128, D), 0), 16) == lax.rem(iota((128, D), 1), 16)).astype(bf16)
    wide = nn(stacked.astype(bf16), same)

    def put(row, first, values, size):
        kept = jnp.where(block_owner(first, size), values, 0.0)
        target[row : row + 1, first : first + D] = jnp.sum(kept, axis=0, keepdims=True)

    for n, (_, _, row) in enumerate(narrow):
        put(row, 0, wide[n * 32 : (n + 1) * 32], 16)
    line = own[0].astype(bf16)
    values = nn(line, spread_rule(64, 0, 0))
    for first in range(0, FF, D):
        put(VECTOR_ROW["hidden"], first, values, 64)
    for first in range(0, 3 * D, D):
        put(VECTOR_ROW["upsample_bias"], first, nn(line, spread_rule(48, 64, first)), 48)


def pack_vectors(source, target):
    def take(row, first, size):
        values = jnp.broadcast_to(source[row : row + 1, first : first + D], (32, D))
        return jnp.where(block_owner(first, size), values, 0.0)

    def collect(values, rule):
        total = jnp.zeros((values.shape[0], 128), f32)
        for _ in range(3):
            term = values.astype(bf16)
            total += nn(term, rule)
            values = values - term.astype(f32)
        return total

    narrow = narrow_vectors()
    stacked = jnp.concatenate([take(row, 0, 16) for _, _, row in narrow])
    same = (lax.rem(iota((D, 128), 1), 16) == lax.rem(iota((D, 128), 0), 16)).astype(bf16)
    close = collect(stacked, same)
    group = iota((32, 128), 1) // 16
    lines = [jnp.zeros((32, 128), f32), jnp.zeros((32, 128), f32)]
    for n, (line, g, _) in enumerate(narrow):
        lines[line] += jnp.where(group == g, close[n * 32 : (n + 1) * 32], 0.0)
    hidden = take(VECTOR_ROW["hidden"], 0, 64)
    for first in range(D, FF, D):
        hidden += take(VECTOR_ROW["hidden"], first, 64)
    lines[0] += collect(hidden, gather_rule(64, 0, 0))
    for first in range(0, 3 * D, D):
        values = take(VECTOR_ROW["upsample_bias"], first, 48)
        lines[0] += collect(values, gather_rule(48, 64, first))
    both = jnp.concatenate([lines[0][:, None, :], lines[1][:, None, :]], axis=1)
    both = jnp.concatenate([both, jnp.zeros((32, 6, 128), f32)], axis=1)
    target[...] = both.reshape(CUBE + (8, 128))


ANGLE_STEPS = SEQ // ANGLE_STEP
FINE_ROW = ANGLE_STEPS + -ANGLE_STEPS % 8
COARSE_ROWS = FINE_ROW + ANGLE_STEP


def angle_rates():
    ratios = np.arange(0, D, 2).astype(np.float32) / np.float32(D)
    rates = np.float32(1.0) / np.power(np.float32(10000.0), ratios)
    return jnp.asarray(np.broadcast_to(rates, (8, HALF)).astype(np.float32))


def coarse_angles(rates, coarse):
    row = lax.broadcasted_iota(jnp.int32, (COARSE_ROWS, HALF), 0)
    place = jnp.where(row < FINE_ROW, row * ANGLE_STEP, row - FINE_ROW).astype(f32)
    angles = place * rates[0:1, :]
    coarse[:, :HALF] = jnp.sin(angles)
    coarse[:, HALF:] = jnp.cos(angles)


def expand_angles(coarse, angles, table_of):
    steps, start = ANGLE_STEPS, FINE_ROW

    def body(q, carry):
        high_sin, high_cos = coarse[pl.ds(q, 1), :HALF], coarse[pl.ds(q, 1), HALF:]
        low_sin, low_cos = coarse[start:, :HALF], coarse[start:, HALF:]
        sine = high_sin * low_cos + high_cos * low_sin
        cosine = high_cos * low_cos - high_sin * low_sin
        rows = at_rows(q, ANGLE_STEP)
        angles[rows, :HALF] = sine
        angles[rows, HALF:] = cosine
        table_of(rows, sine.astype(bf16), cosine.astype(bf16))
        return carry

    lax.fori_loop(0, steps, body, 0)


def head_lanes(rows, head):
    return (lax.broadcasted_iota(jnp.int32, (rows, 128), 1) // HEAD_DIM) == head


def keep_head(values, head):
    return jnp.where(head_lanes(values.shape[0], head), values, 0).astype(bf16)


def rotate(pair, sines, cosines):
    low, high = pair[:, :HALF], pair[:, HALF:]
    return high * sines - low * cosines, low * sines + high * cosines


def norm_parts(values):
    row_mean = jnp.mean(values, axis=-1, keepdims=True)
    centred = values - row_mean
    variance = jnp.mean(centred * centred, axis=-1, keepdims=True)
    inv_std = lax.rsqrt(variance + epsilon)
    return centred * inv_std, inv_std


def norm_backward(normal, inv_std, gain, upstream):
    scaled = upstream * gain
    scaled_mean = jnp.mean(scaled, axis=-1, keepdims=True)
    cross_mean = jnp.mean(scaled * normal, axis=-1, keepdims=True)
    return inv_std * (scaled - scaled_mean - normal * cross_mean)


def vec(ref, name):
    r = VECTOR_ROW[name]
    return ref[r : r + 1, : VECTOR_SIZE[name]]


VECTOR_ROWS = 16


FRONT_ROWS = ("query_u", "query_v", "key", "value", "mixed")
CHUNK_LAST = (4, 4, 4, 4, 2, 2)
FIRST = ((0, 0), (1, 0))
BEFORE = ((0, 1), (1, 1), (2, 0), (0, 2), (1, 2), (0, 3), (1, 3), (2, 1), (3, 0), (0, 4), (1, 4))
AFTER = ((2, 2), (3, 1), (4, 0), (5, 0))
DURING = {
    11: ((2, 3), (3, 2), (4, 1), (5, 1)),
    17: ((3, 3),),
    23: ((2, 4), (3, 4), (4, 2), (5, 2)),
}


def front(plan, linked, ins):
    outs = {
        "vectors": ((16, FF), f32, VMEM),
        "coarse": ((COARSE_ROWS, D), f32, VMEM),
    }
    outs |= {n + "_out": ((SEQ, D), bf16, ANY) for n in FRONT_ROWS}
    outs |= {
        "probs_out": ((HEADS, QB, PW), bf16, ANY),
    }
    scratch = {
        "normal": VMEM((SEQ, D), f32),
        "angles": VMEM((SEQ, D), f32),
        "key_table": VMEM((SEQ, 128 + D), bf16),
        "score": VMEM((2, QB, SEQ), f32),
        "turned": VMEM((2, QB, 128 + D), bf16),
        "probs": VMEM((2, QB, PW), bf16),
        "probs_sem": pltpu.SemaphoreType.DMA((2,)),
        "out_sem": pltpu.SemaphoreType.DMA((len(FRONT_ROWS),)),
    }
    scratch |= {n: VMEM((SEQ, D), bf16) for n in FRONT_ROWS}
    params = {}
    if linked:
        rows = VECTOR_ROWS + plan.rows
        chunks = [
            (0, 128),
            (128, VECTOR_ROWS + plan.span("project", "position", 0)[1] - 128),
            plan.span("mixing", "expand", VECTOR_ROWS),
            plan.span("contract", "contract", VECTOR_ROWS),
            plan.span("pooling", "pooling", VECTOR_ROWS),
            plan.span("upsample", "upsample", VECTOR_ROWS),
        ]
        pieces = split_pieces(chunks)
        outs["blocks"] = (CUBE + (rows, 128), bf16, ANY)
        scratch |= {
            "mine": VMEM((rows, 128), bf16),
            "project": VMEM(plan.full_shape("project"), bf16),
            "position": VMEM(plan.full_shape("position"), bf16),
            "vector_blocks": VMEM(CUBE + (VECTOR_ROWS, 128), bf16),
            "vector_lines": VMEM((VECTOR_ROWS, 128), f32),
            "send_sem": pltpu.SemaphoreType.DMA((COPIES * len(pieces),)),
            "recv_sem": pltpu.SemaphoreType.DMA((COPIES * len(pieces),)),
            "load_sem": pltpu.SemaphoreType.DMA((4,)),
        }
        params = dict(collective_id=0, has_side_effects=True)

    def body(ref):
        if linked:
            partner_signal()
            gather = Gather(ref.blocks, pieces, ref.send_sem, ref.recv_sem, ref.mine)

            def run(events):
                for chunk, stage in events:
                    for piece in (2 * chunk, 2 * chunk + 1):
                        gather.advance(piece, stage, last=CHUNK_LAST[chunk])

            def pack(name):
                r, c = plan.shard[name]
                shard = getattr(ref, name + "_shard")
                for q in range(r // 128):
                    at = VECTOR_ROWS + plan.row[name] + q * c
                    if c % 128:
                        ref.mine[at : at + c, :] = shard[:, q * 128 : (q + 1) * 128]
                    else:
                        ref.mine[at : at + c, :] = shard[q * 128 : (q + 1) * 128, :].T

            ref.vector_lines[...] = jnp.zeros_like(ref.vector_lines)
            for name, (line, offset, size) in vector_places().items():
                entries = getattr(ref, name + "_shard")[...].astype(f32).reshape(1, size)
                ref.vector_lines[line : line + 1, offset : offset + size] = entries
            ref.mine[:VECTOR_ROWS, :] = ref.vector_lines[...].astype(bf16)
            for name in ("project", "position"):
                pack(name)
            partner_wait()
            run(FIRST)
            for name in WEIGHTS[2:]:
                pack(name)
            own = pltpu.make_async_copy(
                ref.mine, ref.blocks.at[gather.bits], ref.load_sem.at[0]
            )
            own.start()

        def first_norm(i, carry):
            rows = at_rows(i, RB)
            ref.normal[rows, :] = norm_parts(ref.tokens[rows, :].astype(f32))[0]
            return carry

        lax.fori_loop(0, SEQ // RB, first_norm, 0)

        def table_of(rows, sine, cosine):
            ref.key_table[rows, 128 : 128 + HALF] = sine
            ref.key_table[rows, 128 + HALF :] = cosine

        coarse_angles(ref.rates, ref.coarse)
        expand_angles(ref.coarse, ref.angles, table_of)

        if linked:
            own.wait()
            run(BEFORE)
            load_weight(plan, "project", ref.blocks, ref.project, ref.load_sem.at[1], VECTOR_ROWS)
            load_weight(plan, "position", ref.blocks, ref.position, ref.load_sem.at[3], VECTOR_ROWS)
            small = pltpu.make_async_copy(
                ref.blocks.at[:, :, :, :, :, pl.ds(0, VECTOR_ROWS), :],
                ref.vector_blocks,
                ref.load_sem.at[2],
            )
            small.start()
            small.wait()
            unpack_vectors(ref.vector_blocks, ref.vectors)
            wait_whole(ref.project, ref.load_sem.at[1])
        else:
            ref.vectors[...] = ref.given_vectors[...]

        def project_rows(b, carry):
            rows = at_rows(b, QB)
            normed = ref.normal[rows, :] * vec(ref.vectors, "gain_one") + vec(
                ref.vectors, "shift_one"
            )
            joined = nt(normed.astype(bf16), full(ref.project))
            ref.query_u[rows, :] = (joined[:, :D] + vec(ref.vectors, "content")).astype(bf16)
            ref.query_v[rows, :] = (joined[:, :D] + vec(ref.vectors, "position_bias")).astype(bf16)
            ref.key[rows, :] = joined[:, D : 2 * D].astype(bf16)
            ref.value[rows, :] = joined[:, 2 * D :].astype(bf16)
            return carry

        lax.fori_loop(0, BLOCKS, project_rows, 0)

        def row_copy(i):
            name = FRONT_ROWS[i]
            return pltpu.make_async_copy(
                getattr(ref, name), getattr(ref, name + "_out"), ref.out_sem.at[i]
            )

        for i in range(4):
            row_copy(i).start()

        if linked:
            run(AFTER)
            wait_whole(ref.position, ref.load_sem.at[3])
            position = ref.position.reshape(D, D)
        else:
            position = ref.position

        def out_copy(head, slot):
            return pltpu.make_async_copy(
                ref.probs.at[slot], ref.probs_out.at[head], ref.probs_sem.at[slot]
            )

        def scores(lanes, b, e):
            row, width = b * QB, (b + 1) * QB
            rows = slice(row, row + QB)
            spread = nn(keep_head(ref.query_v[rows, lanes], e), position[lanes, :])
            low, high = rotate(spread, ref.angles[rows, :HALF], ref.angles[rows, HALF:])
            ref.turned[e, :, :128] = keep_head(ref.query_u[rows, lanes], e)
            ref.turned[e, :, 128 : 128 + HALF] = low.astype(bf16)
            ref.turned[e, :, 128 + HALF :] = high.astype(bf16)
            ref.score[e, :, :width] = nt(ref.turned[e], ref.key_table[:width, :])

        def softmax(b, e):
            row, width = b * QB, (b + 1) * QB
            for sub in range(QB // SB):
                used = row + (sub + 1) * SB
                for g in range(SB // CH):
                    at = slice(sub * SB + g * CH, sub * SB + (g + 1) * CH)
                    tiles = [
                        ref.score[e, at, i * 128 : (i + 1) * 128] for i in range(used // 128)
                    ]
                    lane = lax.broadcasted_iota(jnp.int32, (CH, SB), 1)
                    place = lax.broadcasted_iota(jnp.int32, (CH, SB), 0) + g * CH
                    tiles[-1] = jnp.where(lane <= place, tiles[-1], -1e30)
                    top = tiles[0]
                    for tile in tiles[1:]:
                        top = jnp.maximum(top, tile)
                    top = jnp.max(top, axis=1, keepdims=True)
                    tiles = [jnp.exp2((tile - top) * EXP_SCALE) for tile in tiles]
                    total = tiles[0]
                    for tile in tiles[1:]:
                        total = total + tile
                    scale = 1.0 / jnp.sum(total, axis=1, keepdims=True)
                    for i, tile in enumerate(tiles):
                        lanes = slice(POFF[b] + i * 128, POFF[b] + (i + 1) * 128)
                        ref.probs[e, at, lanes] = (tile * scale).astype(bf16)
                if used < width:
                    ref.probs[e, sub * SB : (sub + 1) * SB, POFF[b] + used : POFF[b] + width] = (
                        jnp.zeros((SB, width - used), bf16)
                    )

        def pair(turn, inner):
            hp = turn * 2 + inner
            lanes = pl.ds(pl.multiple_of(hp * 128, 128), 128)
            ref.key_table[:, :128] = ref.key[:, lanes]

            if inner > 0:
                for e in range(2):
                    out_copy(0, e).wait()
            else:

                @pl.when(turn > 0)
                def _():
                    for e in range(2):
                        out_copy(0, e).wait()


            for b in range(BLOCKS):
                for e in range(2):
                    scores(lanes, b, e)
                    softmax(b, e)
                    for when, events in DURING.items():
                        if linked and when % 12 == inner * 6 + b * 2 + e:
                            run_at(turn, when // 12, lambda events=events: run(events))
                row, width = b * QB, (b + 1) * QB
                values = ref.value[:width, lanes]
                span = slice(POFF[b], POFF[b] + width)
                ref.mixed[row : row + QB, lanes] = jnp.where(
                    head_lanes(QB, 0),
                    nn(ref.probs[0, :, span], values),
                    nn(ref.probs[1, :, span], values),
                ).astype(bf16)
            for e in range(2):
                out_copy(hp * 2 + e, e).start()

        def two_pairs(turn, carry):
            pair(turn, 0)
            pair(turn, 1)
            return carry

        lax.fori_loop(0, HEADS // 4, two_pairs, 0)
        row_copy(4).start()
        for e in range(2):
            out_copy(0, e).wait()
        if linked:
            for i in range(len(pieces)):
                gather.drain(i, last=CHUNK_LAST[i // 2])
        for i in range(5):
            row_copy(i).wait()

    return call(body, ins, outs, scratch, **params)


MIDDLE = ("mixing", "expand", "contract", "pooling", "upsample")


def middle(plan, linked, ins):
    def weight_shape(name):
        return plan.full_shape(name) if linked else WEIGHT_SHAPE[name][::-1]

    outs = {
        "output_out": ((SEQ, D), bf16, ANY),
        "first_grad_out": ((SEQ, D), f32, ANY),
        "mixed_grad_out": ((SEQ, D), bf16, ANY),
        "sums": ((16, FF), f32, VMEM),
    }
    summed = ("pooling", "upsample") if linked else ()
    kept = [n for n in MIDDLE if n not in summed]
    outs |= {n + "_grad_out": (weight_shape(n), bf16, ANY) for n in kept}
    params = {}
    scratch = {n: VMEM(weight_shape(n), bf16) for n in MIDDLE}
    scratch |= {
        "normal": VMEM((SEQ, D), f32),
        "inverse": VMEM((SEQ, 128), f32),
        "second_low": VMEM((SEQ, D), bf16),
        "activated": VMEM((SEQ, FF), bf16),
        "slope": VMEM((SEQ, FF), bf16),
        "tiles": VMEM((D // 128, SEQ + 16, 128), f32),
        "grouped": VMEM((THIRD, 3 * D), bf16),
        "up_rows": VMEM((THIRD, 3 * D), bf16),
        "branch_grad": VMEM((SEQ, D), bf16),
        "attended_grad": VMEM((SEQ, D), bf16),
        "parts": VMEM((5, 8, FF), f32),
        "output": VMEM((SEQ, D), bf16),
        "first_grad": VMEM((SEQ, D), f32),
        "mixed_grad": VMEM((SEQ, D), bf16),
        "sem": pltpu.SemaphoreType.DMA((len(MIDDLE),)),
        "row_sem": pltpu.SemaphoreType.DMA((3,)),
        "tokens": VMEM((SEQ, D), bf16),
        "cotangent": VMEM((SEQ, D), bf16),
        "mixed": VMEM((SEQ, D), bf16),
        "out_sem": pltpu.SemaphoreType.DMA((3 + len(kept),)),
    }
    scratch |= {n + "_grad": VMEM(weight_shape(n), bf16) for n in kept}
    if linked:
        gather_pieces = split_pieces(
            [plan.span(n, n, VECTOR_ROWS) for n in ("pooling", "upsample")]
        )
        base = -plan.row["pooling"]
        pieces = split_pieces([plan.span(n, n, base) for n in summed])
        rows = plan.span("pooling", "upsample", base)[1]
        outs["blocks_out"] = (CUBE + (VECTOR_ROWS + plan.rows, 128), bf16, ANY)
        outs["partial"] = ((2, 2, rows, 128), bf16, ANY)
        scratch |= {
            "own": VMEM(CUBE + (rows, 128), bf16),
            "land": VMEM(CUBE + (rows, 128), bf16),
            "partial_sem": pltpu.SemaphoreType.DMA,
            "gather_send": pltpu.SemaphoreType.DMA((4 * COPIES,)),
            "gather_recv": pltpu.SemaphoreType.DMA((4 * COPIES,)),
            "send_sem": pltpu.SemaphoreType.DMA((4 * COPIES,)),
            "recv_sem": pltpu.SemaphoreType.DMA((4 * COPIES,)),
        }
        params = dict(
            collective_id=1,
            has_side_effects=True,
            alias={list(ins).index("blocks"): list(outs).index("blocks_out")},
        )

    def body(ref):
        def fetch(name):
            i = MIDDLE.index(name)
            if linked:
                load_weight(
                    plan, name, ref.blocks_out, getattr(ref, name), ref.sem.at[i], VECTOR_ROWS
                )
            else:
                pltpu.make_async_copy(
                    getattr(ref, name + "_full"), getattr(ref, name), ref.sem.at[i]
                ).start()

        gather_stage = scatter_stage = None
        if linked:
            gather = Gather(ref.blocks_out, gather_pieces, ref.gather_send, ref.gather_recv)
            scatter = Scatter(ref.own, ref.land, None, pieces, ref.send_sem, ref.recv_sem)
            partner_signal()

            def gather_stage(stage):
                for i in range(4):
                    gather.advance(i, stage, first=2)

            def scatter_stage(name, stage):
                for half in range(2):
                    scatter.advance(summed.index(name) * 2 + half, stage, last=3)

        arriving = ("mixed", "tokens", "cotangent")

        def row_copy(name):
            return pltpu.make_async_copy(
                getattr(ref, name + "_in"), getattr(ref, name), ref.row_sem.at[arriving.index(name)]
            )

        row_copy("mixed").start()
        row_copy("tokens").start()
        for name in ("mixing", "expand", "contract"):
            fetch(name)
        if linked:
            partner_wait()
            gather_stage(2)
        else:
            fetch("pooling")
            fetch("upsample")

        outgoing = ["output", "first_grad", "mixed_grad"] + [n + "_grad" for n in kept]

        def send_out(name):
            return pltpu.make_async_copy(
                getattr(ref, name),
                getattr(ref, name + "_out"),
                ref.out_sem.at[outgoing.index(name)],
            )

        def at_step(i, number, action, *args):
            if linked:
                run_at(i, number, lambda: action(*args))

        def ready(name):
            wait_whole(getattr(ref, name), ref.sem.at[MIDDLE.index(name)])

        def get(name):
            return full(getattr(ref, name))

        def put(name, values):
            if name in summed:
                put_blocks(plan, name, ref.own, base, lambda columns: values[:, columns])
                return
            target = getattr(ref, name + "_grad")
            target[...] = values.astype(bf16).reshape(target.shape)
            send_out(name + "_grad").start()

        def third(start, k):
            return jnp.concatenate(
                [ref.tiles[t, pl.ds(start + k, THIRD, stride=3), :] for t in range(D // 128)],
                axis=1,
            )

        def put_third(start, k, values):
            for t in range(D // 128):
                ref.tiles[t, pl.ds(start + k, THIRD, stride=3), :] = values[
                    :, t * 128 : (t + 1) * 128
                ]

        def rows_of(rows):
            return jnp.concatenate([ref.tiles[t, rows, :] for t in range(D // 128)], axis=1)

        def put_rows(rows, values):
            for t in range(D // 128):
                ref.tiles[t, rows, :] = values[:, t * 128 : (t + 1) * 128]

        def shifted_rows(i):
            return pl.ds(pl.multiple_of(i * MB + 8, 8), MB)

        ref.parts[...] = jnp.zeros_like(ref.parts)
        ref.sums[...] = jnp.zeros_like(ref.sums)

        def add_part(slot, values):
            columns = values.shape[1]
            ref.parts[slot, :, :columns] += eight_rows(values)

        def put_sum(name, values):
            r = VECTOR_ROW[name]
            ref.sums[r : r + 1, : values.shape[1]] = values

        def put_part(name, slot):
            columns = VECTOR_SIZE[name]
            put_sum(name, jnp.sum(ref.parts[slot, :, :columns], axis=0, keepdims=True))

        row_copy("cotangent").start()
        row_copy("mixed").wait()
        row_copy("tokens").wait()
        for name in ("mixing", "expand", "contract"):
            ready(name)

        def forward(i, carry):
            rows = at_rows(i, MB)
            attended = nt(ref.mixed[rows, :], get("mixing")) + vec(ref.vectors, "mixing_bias")
            first = ref.tokens[rows, :].astype(f32) + attended
            normal, inverse = norm_parts(first)
            ref.normal[rows, :] = normal
            ref.inverse[rows, :] = jnp.broadcast_to(inverse, (MB, 128))
            low = (
                normal * vec(ref.vectors, "gain_two") + vec(ref.vectors, "shift_two")
            ).astype(bf16)
            ref.second_low[rows, :] = low
            inner = nt(low, get("expand")) + vec(ref.vectors, "hidden")
            phi = 0.5 * (1.0 + lax.erf(inner * 2.0 ** (-0.5)))
            act = (inner * phi).astype(bf16)
            ref.activated[rows, :] = act
            bell = jnp.exp(-0.5 * inner * inner) * (2.0 * math.pi) ** (-0.5)
            ref.slope[rows, :] = (phi + inner * bell).astype(bf16)
            block = first + nt(act, get("contract")) + vec(ref.vectors, "contract_bias")
            put_rows(shifted_rows(i), block)
            at_step(i, 4, gather_stage, 3)
            return carry

        lax.fori_loop(0, SEQ // MB, forward, 0)

        put_rows(slice(0, 8), jnp.zeros((8, D), f32))
        for k in range(3):
            ref.grouped[:, k * D : (k + 1) * D] = third(6, k).astype(bf16)
        if linked:
            gather_stage(4)
            fetch("pooling")
            fetch("upsample")
        ready("pooling")
        pooled = (
            nt(ref.grouped[...], get("pooling")) + vec(ref.vectors, "pooling_bias")
        ).astype(bf16)
        ready("upsample")
        for k in range(3):
            columns = slice(k * D, (k + 1) * D)
            upward = nt(pooled, get("upsample")[columns, :]) + vec(ref.vectors, "upsample_bias")[
                :, columns
            ]
            put_third(8, k, third(8, k) + upward)

        row_copy("cotangent").wait()

        def write_output(i, carry):
            ref.output[at_rows(i, MB), :] = rows_of(shifted_rows(i)).astype(bf16)
            put_rows(shifted_rows(i), ref.cotangent[at_rows(i, MB), :].astype(f32))
            return carry

        lax.fori_loop(0, SEQ // MB, write_output, 0)

        send_out("output").start()

        for k in range(3):
            ref.up_rows[:, k * D : (k + 1) * D] = third(8, k).astype(bf16)
        up_rows = ref.up_rows[...]
        put_sum("upsample_bias", jnp.sum(up_rows.astype(f32), axis=0, keepdims=True))
        put("upsample", tn(up_rows, pooled))
        if linked:
            scatter_stage("upsample", 0)
        pooled_grad = nn(up_rows, get("upsample")).astype(bf16)
        put_sum("pooling_bias", jnp.sum(pooled_grad.astype(f32), axis=0, keepdims=True))
        put("pooling", tn(pooled_grad, ref.grouped[...]))
        if linked:
            scatter_stage("pooling", 0)
        for k in range(3):
            put_third(
                6, k, nn(pooled_grad, get("pooling")[:, k * D : (k + 1) * D])
            )
        put_rows(slice(SEQ + 6, SEQ + 8), jnp.zeros((2, D), f32))
        if linked:
            scatter_stage("upsample", 1)

        def backward(i, carry):
            rows = at_rows(i, MB)
            block_grad = ref.cotangent[rows, :].astype(f32) + rows_of(shifted_rows(i))
            branch_grad = block_grad.astype(bf16)
            ref.branch_grad[rows, :] = branch_grad
            add_part(0, branch_grad.astype(f32))
            inner_grad = (nn(branch_grad, get("contract")) * ref.slope[rows, :].astype(f32)).astype(
                bf16
            )
            ref.slope[rows, :] = inner_grad
            add_part(1, inner_grad.astype(f32))
            second_grad = nn(inner_grad, get("expand"))
            normal = ref.normal[rows, :]
            add_part(2, second_grad * normal)
            add_part(3, second_grad)
            first_grad = block_grad + norm_backward(
                normal, ref.inverse[rows, :1], vec(ref.vectors, "gain_two"), second_grad
            )
            ref.first_grad[rows, :] = first_grad
            attended_grad = first_grad.astype(bf16)
            ref.attended_grad[rows, :] = attended_grad
            add_part(4, attended_grad.astype(f32))
            ref.mixed_grad[rows, :] = nn(attended_grad, get("mixing")).astype(bf16)
            at_step(i, 0, scatter_stage, "pooling", 1)
            at_step(i, 3, scatter_stage, "upsample", 2)
            at_step(i, 5, scatter_stage, "pooling", 2)
            return carry

        lax.fori_loop(0, SEQ // MB, backward, 0)
        send_out("first_grad").start()
        send_out("mixed_grad").start()
        put_part("contract_bias", 0)
        put_part("hidden", 1)
        put_part("gain_two", 2)
        put_part("shift_two", 3)
        put_part("mixing_bias", 4)

        def contract_part(part, carry):
            columns = pl.ds(pl.multiple_of(part * D, D), D)
            values = tn(ref.branch_grad[...], ref.activated[:, columns]).astype(bf16)
            target = ref.contract_grad.at[..., columns]
            target[...] = values.reshape(target.shape)
            return carry

        lax.fori_loop(0, FF // D, contract_part, 0)
        send_out("contract_grad").start()
        if linked:
            scatter_stage("upsample", 3)

        def expand_part(part, carry):
            columns = pl.ds(pl.multiple_of(part * D, D), D)
            values = tn(ref.slope[:, columns], ref.second_low[...]).astype(bf16)
            if linked:
                target = ref.expand_grad.at[part // 2, lax.rem(part, 2)]
            else:
                target = ref.expand_grad.at[columns]
            target[...] = values.reshape(target.shape)
            return carry

        lax.fori_loop(0, FF // D, expand_part, 0)
        send_out("expand_grad").start()
        put("mixing", tn(ref.attended_grad[...], ref.mixed[...]))
        if linked:
            scatter_stage("pooling", 3)
            _, _, x, y, core = scatter.bits
            partial = pltpu.make_async_copy(
                ref.own.at[:, :, x, y, core], ref.partial, ref.partial_sem
            )
            partial.start()
            partial.wait()
            for i in range(4):
                gather.drain(i, first=2)
        for name in outgoing:
            send_out(name).wait()

    return call(body, ins, outs, scratch, **params)


BACK_FIRST = (0, 0, 3, 0, 0, 0)
BACK_DURING = {
    2: ((0, 1),),
    7: ((0, 2), (1, 1)),
    14: ((0, 3), (1, 2), (2, 4)),
    18: ((0, 4), (1, 3)),
    23: ((1, 4),),
}


def back(plan, linked, ins):
    outs = {"token_grad_out": ((SEQ, D), f32, ANY)}
    late_rows = ("tokens", "mixed_grad", "mixed", "value", "key", "query_u", "query_v", "first_grad")
    scratch = {
        "angles": VMEM((SEQ, D), f32),
        "key_table": VMEM((SEQ, 128 + D), bf16),
        "prob_grad": VMEM((2, QB, SEQ), f32),
        "total_grad": VMEM((2, QB, SEQ), bf16),
        "probs": VMEM((4, QB, PW), bf16),
        "key_acc": VMEM((128, SEQ), f32),
        "value_acc": VMEM((128, SEQ), f32),
        "joined_grad": VMEM((SEQ, 3 * D), bf16),
        "normed_low": VMEM((SEQ, D), bf16),
        "position_grad": VMEM((D, D), f32),
        "parts": VMEM((2, 8, D), f32),
        "all_sums": VMEM((16, FF), f32),
        "probs_sem": pltpu.SemaphoreType.DMA((4,)),
        "load_sem": pltpu.SemaphoreType.DMA((2,)),
        "token_grad": VMEM((SEQ, D), f32),
        "token_sem": pltpu.SemaphoreType.DMA,
        "row_sem": pltpu.SemaphoreType.DMA((len(late_rows),)),
    }
    scratch |= {n: VMEM((SEQ, D), f32 if n == "first_grad" else bf16) for n in late_rows}
    params = {}
    project_shape = plan.full_shape("project") if linked else (3 * D, D)
    position_shape = plan.full_shape("position") if linked else (D, D)
    scratch |= {"project": VMEM(project_shape, bf16), "position": VMEM(position_shape, bf16)}
    if linked:
        early_names = ("contract", "expand", "mixing")
        early = [plan.span("contract", "contract", 0), plan.span("mixing", "expand", 0)]
        late = [plan.span("pooling", "upsample", 0), plan.span("position", "position", 0)]
        row, rows = plan.span("project", "project", 0)
        late += [(row, rows // 2), (row + rows // 2, rows // 2)]
        pieces = split_pieces(early + late)
        count = COPIES * len(pieces)
        own_rows = plan.rows
        outs["vector_out"] = ((8, 128), f32, VMEM)
        outs["flat_out"] = ((own_rows, 128), f32, ANY)
        scratch |= {
            "own": VMEM(CUBE + (own_rows, 128), bf16),
            "land": VMEM(CUBE + (own_rows, 128), bf16),
            "flat": VMEM((own_rows, 128), f32),
            "vector_own": VMEM(CUBE + (8, 128), f32),
            "land_dp": VMEM((3, 2, 2, 2, 8, 128), f32),
            "land_fsdp": VMEM((7, 8, 128), f32),
            "vector_sem": pltpu.SemaphoreType.DMA((4, 8)),
            "send_sem": pltpu.SemaphoreType.DMA((count,)),
            "recv_sem": pltpu.SemaphoreType.DMA((count,)),
            "own_sem": pltpu.SemaphoreType.DMA((4,)),
        }
        params = dict(collective_id=2, has_side_effects=True)
    else:
        outs["project_grad"] = ((3 * D, D), bf16, VMEM)
        outs["position_grad_out"] = ((D, D), bf16, VMEM)
        outs["sums_out"] = ((16, FF), f32, VMEM)

    def body(ref):
        def row_copy(name):
            return pltpu.make_async_copy(
                getattr(ref, name + "_in"), getattr(ref, name), ref.row_sem.at[late_rows.index(name)]
            )

        for name in late_rows[:7]:
            row_copy(name).start()
        if linked:
            load_weight(plan, "project", ref.blocks, ref.project, ref.load_sem.at[0], VECTOR_ROWS)
            load_weight(plan, "position", ref.blocks, ref.position, ref.load_sem.at[1], VECTOR_ROWS)
            matrix = Scatter(ref.own, ref.land, ref.flat, pieces, ref.send_sem, ref.recv_sem)
            vector = AxisScatter(
                ref.vector_own, ref.land_dp, ref.land_fsdp, ref.vector_out, ref.vector_sem
            )
            axis_signal()

            def run(events):
                for chunk, stage in events:
                    for piece in (2 * chunk, 2 * chunk + 1):
                        matrix.advance(piece, stage, first=BACK_FIRST[chunk])

            for i, name in enumerate(early_names):
                c = plan.shard[name][1]
                for y, core, row, column in plan.blocks(name, 0):
                    pltpu.make_async_copy(
                        getattr(ref, name + "_grad").at[:, :, :, :, pl.ds(column, 128)],
                        ref.own.at[:, :, :, y, core, pl.ds(row, c), :],
                        ref.own_sem.at[i],
                    ).start()
            _, _, x, y, core = matrix.bits
            row, rows = late[0]
            partial = pltpu.make_async_copy(
                ref.partial, ref.own.at[:, :, x, y, core, pl.ds(row, rows), :], ref.own_sem.at[3]
            )
            partial.start()
        else:
            for i, name in enumerate(("project", "position")):
                pltpu.make_async_copy(
                    getattr(ref, name + "_full"), getattr(ref, name), ref.load_sem.at[i]
                ).start()

        def in_copy(head, slot):
            return pltpu.make_async_copy(
                ref.probs_in.at[head], ref.probs.at[slot], ref.probs_sem.at[slot]
            )

        for e in range(2):
            in_copy(e, e).start()

        def table_of(rows, sine, cosine):
            ref.key_table[rows, 128 : 128 + HALF] = sine
            ref.key_table[rows, 128 + HALF :] = cosine

        expand_angles(ref.coarse, ref.angles, table_of)

        def norm_rows(rows):
            return norm_parts(ref.tokens[rows, :].astype(f32))

        def low_rows(i, carry):
            rows = at_rows(i, RB)
            normal, _ = norm_rows(rows)
            ref.normed_low[rows, :] = (
                normal * vec(ref.vectors, "gain_one") + vec(ref.vectors, "shift_one")
            ).astype(bf16)
            return carry

        row_copy("tokens").wait()
        lax.fori_loop(0, SEQ // RB, low_rows, 0)
        ref.all_sums[...] = ref.sums[...]
        ref.parts[...] = jnp.zeros_like(ref.parts)
        if linked:
            axis_wait()
            partial.wait()
            run([(2, 3)])
            for i, name in enumerate(early_names):
                row, rows = plan.span(name, name, 0)
                whole = ref.own.at[:, :, :, :, :, pl.ds(row, rows), :]
                wait_whole(whole, ref.own_sem.at[i])
                if i == 0:
                    run([(0, 0)])
            run([(1, 0)])
        wait_whole(ref.project, ref.load_sem.at[0])
        wait_whole(ref.position, ref.load_sem.at[1])
        position = ref.position.reshape(D, D)
        for name in late_rows[1:7]:
            row_copy(name).wait()
        row_copy("first_grad").start()

        def pair(hp, carry):
            start = pl.multiple_of(hp * 128, 128)
            lanes = pl.ds(start, 128)
            base = lax.rem(hp, 2) * 2
            for e in range(2):
                in_copy(0, base + e).wait()

            @pl.when(hp < HEADS // 2 - 1)
            def _():
                for e in range(2):
                    in_copy(hp * 2 + 2 + e, 2 - base + e).start()

            ref.key_table[:, :128] = ref.key[:, lanes]
            content_sum = jnp.zeros((1, 128), f32)
            position_sum = jnp.zeros((1, 128), f32)
            for b in range(BLOCKS):
                row, width = b * QB, (b + 1) * QB
                rows = slice(row, row + QB)
                span = slice(POFF[b], POFF[b] + width)
                by_content, by_position = [], None
                for e in range(2):
                    upstream = keep_head(ref.mixed_grad[rows, lanes], e)
                    row_dot = jnp.sum(
                        upstream.astype(f32) * ref.mixed[rows, lanes].astype(f32),
                        axis=1,
                        keepdims=True,
                    )
                    ref.prob_grad[e, :, :width] = nt(upstream, ref.value[:width, lanes]) - row_dot
                    for sub in range(QB // SB):
                        used = row + (sub + 1) * SB
                        for g in range(SB // CH):
                            at = slice(sub * SB + g * CH, sub * SB + (g + 1) * CH)
                            p = ref.probs[base + e, at, POFF[b] : POFF[b] + used].astype(f32)
                            ref.total_grad[e, at, :used] = (
                                p * ref.prob_grad[e, at, :used] * HEAD_DIM ** (-0.5)
                            ).astype(bf16)
                        if used < width:
                            ref.total_grad[e, sub * SB : (sub + 1) * SB, used:width] = jnp.zeros(
                                (SB, width - used), bf16
                            )
                    scored = ref.total_grad[e, :, :width]
                    turned = nn(scored, ref.key_table[:width, :])
                    by_content.append(turned[:, :128])
                    low, high = rotate(
                        turned[:, 128:], ref.angles[rows, :HALF], ref.angles[rows, HALF:]
                    )
                    spread = jnp.concatenate([low, high], axis=1).astype(bf16)
                    own = (lax.broadcasted_iota(jnp.int32, (128, D), 0) // HEAD_DIM) == e
                    part = nt(spread, jnp.where(own, position[lanes, :], 0).astype(bf16))
                    by_position = part if by_position is None else by_position + part
                    part = tn(keep_head(ref.query_v[rows, lanes], e), spread)
                    if b == 0 and e == 0:
                        ref.position_grad[lanes, :] = part
                    else:
                        ref.position_grad[lanes, :] += part
                    to_key = tn(keep_head(ref.query_u[rows, lanes], e), scored)
                    to_value = tn(upstream, ref.probs[base + e, :, span])
                    if e == 0:
                        if b > 0:
                            ref.key_acc[:, :row] += to_key[:, :row]
                            ref.value_acc[:, :row] += to_value[:, :row]
                        ref.key_acc[:, row:width] = to_key[:, row:]
                        ref.value_acc[:, row:width] = to_value[:, row:]
                    else:
                        ref.key_acc[:, :width] += to_key
                        ref.value_acc[:, :width] += to_value
                    for when, events in BACK_DURING.items():
                        if linked and when % 6 == b * 2 + e:
                            run_at(hp, when // 6, lambda events=events: run(events))
                by_content = jnp.where(head_lanes(QB, 0), by_content[0], by_content[1])
                ref.joined_grad[rows, lanes] = (by_content + by_position).astype(bf16)
                content_sum += jnp.sum(by_content, axis=0, keepdims=True)
                position_sum += jnp.sum(by_position, axis=0, keepdims=True)
            ref.joined_grad[:, pl.ds(start + D, 128)] = ref.key_acc[...].T.astype(bf16)
            ref.joined_grad[:, pl.ds(start + 2 * D, 128)] = ref.value_acc[...].T.astype(bf16)
            r = VECTOR_ROW["content"]
            ref.all_sums[r : r + 1, lanes] = content_sum
            r = VECTOR_ROW["position_bias"]
            ref.all_sums[r : r + 1, lanes] = position_sum
            return carry

        lax.fori_loop(0, HEADS // 2, pair, 0)

        row_copy("first_grad").wait()
        if linked:
            put_blocks(plan, "position", ref.own, 0, lambda columns: ref.position_grad[:, columns])
            run([(3, 0)])
        def project_part(part, carry):
            columns = pl.ds(pl.multiple_of(part * D, D), D)
            grad = tn(ref.joined_grad[:, columns], ref.normed_low[...]).astype(bf16)
            if linked:
                ref.project_full[columns, :] = grad
            else:
                ref.project_grad[columns, :] = grad
            return carry

        lax.fori_loop(0, 3, project_part, 0)
        if linked:
            put_blocks(plan, "project", ref.own, 0, lambda columns: ref.project_full[:, columns])
            run([(4, 0), (5, 0), (3, 1)])
        else:
            ref.position_grad_out[...] = ref.position_grad[...].astype(bf16)

        def norm_back(i, carry):
            rows = at_rows(i, RB)
            normal, inverse = norm_rows(rows)
            upstream = nn(ref.joined_grad[rows, :], full(ref.project))
            ref.parts[0, :, :] += eight_rows(upstream * normal)
            ref.parts[1, :, :] += eight_rows(upstream)
            ref.token_grad[rows, :] = ref.first_grad[rows, :] + norm_backward(
                normal, inverse, vec(ref.vectors, "gain_one"), upstream
            )
            if linked:
                run_at(i, 1, lambda: run([(4, 1)]))
                run_at(i, 3, lambda: run([(5, 1)]))
                run_at(i, 5, lambda: run([(3, 2)]))
                run_at(i, 7, lambda: run([(4, 2)]))
            return carry

        lax.fori_loop(0, SEQ // RB, norm_back, 0)
        token_copy = pltpu.make_async_copy(ref.token_grad, ref.token_grad_out, ref.token_sem)
        token_copy.start()
        for slot, name in enumerate(("gain_one", "shift_one")):
            r = VECTOR_ROW[name]
            ref.all_sums[r : r + 1, :D] = jnp.sum(ref.parts[slot], axis=0, keepdims=True)
        if linked:
            pack_vectors(ref.all_sums, ref.vector_own)
            vector.first()
            run([(5, 2), (3, 3), (4, 3)])
            vector.second()
            run([(5, 3), (3, 4)])
            vector.last()
            run([(4, 4), (5, 4)])
            done = pltpu.make_async_copy(ref.flat, ref.flat_out, ref.own_sem.at[0])
            done.start()
            done.wait()
        else:
            ref.sums_out[...] = ref.all_sums[...]
        token_copy.wait()

    if linked:
        scratch["project_full"] = VMEM((3 * D, D), bf16)
    return call(body, ins, outs, scratch, **params)


PARTS = 4


def finish(plan, flat, vectors, rows):
    outs = {n + "_out": (plan.held_shape(n), f32, VMEM) for n in WEIGHTS}
    outs |= {n + "_out": ((VECTOR_SIZE[n] // 32,), f32, VMEM) for n in VECTORS}
    outs |= {n + "_copy": (v.shape, v.dtype, ANY) for n, v in rows.items()}
    ins = {"flat": (flat, VMEM), "vectors": (vectors, VMEM)}
    ins |= {n: (v, ANY) for n, v in rows.items()}
    scratch = {n + "_held": VMEM(v.shape, v.dtype) for n, v in rows.items()}
    scratch["in_sem"] = pltpu.SemaphoreType.DMA((len(rows) * PARTS,))
    scratch["out_sem"] = pltpu.SemaphoreType.DMA((len(rows) * PARTS,))

    def body(ref):
        loads, copies = [], []
        for n in rows:
            for part in range(PARTS):
                at = pl.ds(part * (SEQ // PARTS), SEQ // PARTS)
                held = getattr(ref, n + "_held").at[at]
                slot = len(loads)
                loads.append(
                    pltpu.make_async_copy(getattr(ref, n).at[at], held, ref.in_sem.at[slot])
                )
                copies.append(
                    pltpu.make_async_copy(
                        held, getattr(ref, n + "_copy").at[at], ref.out_sem.at[slot]
                    )
                )
        for load in loads:
            load.start()
        for load, copy in zip(loads, copies):
            load.wait()
            copy.start()
        for name in WEIGHTS:
            put_shard(plan, name, ref.flat, 0, getattr(ref, name + "_out"))
        for name, (line, offset, size) in vector_places().items():
            getattr(ref, name + "_out")[...] = ref.vectors[line, offset : offset + size]
        for copy in copies:
            copy.wait()

    return call(body, ins, outs, scratch)


def make_local(dp, fsdp):
    plan = Plan(dp, fsdp)
    linked = (dp, fsdp) == (4, 8)

    def gathered(weights):
        out = {}
        for name, shard in zip(WEIGHTS, weights):
            part = lax.all_gather(shard, "dp", axis=0, tiled=True)
            out[name + "_full"] = lax.all_gather(part, "fsdp", axis=1, tiled=True).T
        return out

    def gathered_vectors(vectors):
        rows = []
        for name, shard in zip(VECTORS, vectors):
            whole = lax.all_gather(shard, ("dp", "fsdp"), axis=0, tiled=True).astype(f32)
            rows.append(jnp.pad(whole, (0, FF - VECTOR_SIZE[name])))
        rows += [jnp.zeros((FF,), f32)] * (16 - len(rows))
        return jnp.stack(rows)

    def local(tokens, cotangent, *params):
        assert tokens.shape[0] == SEQ
        weights, vectors = params[:7], params[7:]
        given = dict(zip(VECTORS, vectors))
        rates = angle_rates()
        ins = {"tokens": (tokens, VMEM), "rates": (rates, VMEM)}
        if linked:
            ins |= {n + "_shard": (given[n], VMEM) for n in VECTORS}
            for n, w in zip(WEIGHTS, weights):
                ins[n + "_shard"] = (w.T if w.shape[1] % 128 else w, VMEM)
        else:
            whole = gathered(weights)
            ins["given_vectors"] = (gathered_vectors(vectors), VMEM)
            ins["project"] = (whole["project_full"], VMEM)
            ins["position"] = (whole["position_full"], VMEM)
        one = front(plan, linked, ins)

        ins = {
            "tokens_in": (tokens, ANY),
            "cotangent_in": (cotangent, ANY),
            "mixed_in": (one.mixed_out, ANY),
            "vectors": (one.vectors, VMEM),
        }
        if linked:
            ins["blocks"] = (one.blocks, ANY)
        else:
            ins |= {n + "_full": (whole[n + "_full"], ANY) for n in MIDDLE}
        two = middle(plan, linked, ins)

        ins = {
            "tokens_in": (tokens, ANY),
            "coarse": (one.coarse, VMEM),
            "vectors": (one.vectors, VMEM),
            "query_u_in": (one.query_u_out, ANY),
            "query_v_in": (one.query_v_out, ANY),
            "key_in": (one.key_out, ANY),
            "value_in": (one.value_out, ANY),
            "mixed_in": (one.mixed_out, ANY),
            "mixed_grad_in": (two.mixed_grad_out, ANY),
            "first_grad_in": (two.first_grad_out, ANY),
            "sums": (two.sums, VMEM),
            "probs_in": (one.probs_out, ANY),
        }
        if linked:
            ins["blocks"] = (two.blocks_out, ANY)
            for n in ("contract", "expand", "mixing"):
                ins[n + "_grad"] = (getattr(two, n + "_grad_out"), ANY)
            ins["partial"] = (two.partial, ANY)
        else:
            ins |= {n + "_full": (whole[n + "_full"], ANY) for n in ("project", "position")}
        three = back(plan, linked, ins)

        if linked:
            last = finish(
                plan,
                three.flat_out,
                three.vector_out,
                {"output": two.output_out, "token_grad": three.token_grad_out},
            )
            output, token_grad = last.output_copy, last.token_grad_copy
            matrices = []
            for n in WEIGHTS:
                grad = getattr(last, n + "_out")
                matrices.append(grad if grad.shape == plan.shard[n] else grad.T)
            small = [getattr(last, n + "_out") for n in VECTORS]
        else:
            output, token_grad = two.output_out, three.token_grad_out
            grads = {n: getattr(two, n + "_grad_out") for n in MIDDLE}
            grads["project"] = three.project_grad
            grads["position"] = three.position_grad_out
            matrices = []
            for name in WEIGHTS:
                part = lax.psum_scatter(
                    grads[name].T, "fsdp", scatter_dimension=1, tiled=True
                )
                part = lax.psum_scatter(part, "dp", scatter_dimension=0, tiled=True)
                matrices.append(part.astype(f32))
            small = []
            for name in VECTORS:
                sums = three.sums_out[VECTOR_ROW[name], : VECTOR_SIZE[name]]
                small.append(
                    lax.psum_scatter(sums, ("dp", "fsdp"), scatter_dimension=0, tiled=True)
                )
        return (output, token_grad, *matrices, *small)

    return local


def solution(mesh):
    rows = P(("dp", "fsdp"), None)
    matrix = P("dp", "fsdp")
    vector = P(("dp", "fsdp"))
    return jax.shard_map(
        make_local(mesh.shape["dp"], mesh.shape["fsdp"]),
        mesh=mesh,
        in_specs=(rows,) * 2 + (matrix,) * 7 + (vector,) * 11,
        out_specs=(rows,) * 2 + (matrix,) * 7 + (vector,) * 11,
        check_vma=False,
    )
```

```python
import math
from types import SimpleNamespace

import jax
import jax.numpy as jnp
import numpy as np
from jax import lax
from jax.experimental import pallas as pl
from jax.experimental.pallas import tpu as pltpu
from jax.sharding import PartitionSpec as P

D = 512
HALF = D // 2
HEADS = 8
HEAD_DIM = 64
FF = 2048
SEQ = 1152
THIRD = SEQ // 3
QB = 384
SB = 128
CH = 16
RB = 128
MB = 192
BLOCKS = SEQ // QB
POFF = [sum((b + 1) * QB for b in range(n)) for n in range(BLOCKS + 1)]
PW = POFF[BLOCKS]
EXP_SCALE = HEAD_DIM ** (-0.5) * math.log2(math.e)
ANGLE_STEP = 32
epsilon = 1e-05
bf16 = jnp.bfloat16
f32 = jnp.float32
MESH = pl.DeviceIdType.MESH
VMEM_LIMIT = 63 << 20

WEIGHTS = ("project", "position", "mixing", "expand", "contract", "pooling", "upsample")
WEIGHT_SHAPE = {
    "project": (D, 3 * D),
    "position": (D, D),
    "mixing": (D, D),
    "expand": (D, FF),
    "contract": (FF, D),
    "pooling": (3 * D, D),
    "upsample": (D, 3 * D),
}
VECTORS = (
    "gain_one",
    "shift_one",
    "content",
    "position_bias",
    "mixing_bias",
    "gain_two",
    "shift_two",
    "hidden",
    "contract_bias",
    "pooling_bias",
    "upsample_bias",
)
VECTOR_SIZE = {n: D for n in VECTORS} | {"hidden": FF, "upsample_bias": 3 * D}
VECTOR_ROW = {n: i for i, n in enumerate(VECTORS)}
PACKED_VECTORS = ("hidden", "upsample_bias", "gain_one") + tuple(
    n for n in VECTORS if n not in ("hidden", "upsample_bias", "gain_one")
)


def nn(a, b):
    return lax.dot_general(a, b, (((1,), (0,)), ((), ())), preferred_element_type=f32)


def nt(a, b):
    return lax.dot_general(a, b, (((1,), (1,)), ((), ())), preferred_element_type=f32)


def tn(a, b):
    return lax.dot_general(a, b, (((0,), (0,)), ((), ())), preferred_element_type=f32)


def at_rows(step, rows):
    return pl.ds(pl.multiple_of(step * rows, rows), rows)


def eight_rows(values):
    rows, columns = values.shape
    return jnp.sum(values.reshape(rows // 8, 8, columns), axis=0)


def call(body, ins, outs, scratch, alias=None, **params):
    names = [*ins, *outs, *scratch]

    def kernel(*refs):
        body(SimpleNamespace(**dict(zip(names, refs))))

    results = pl.pallas_call(
        kernel,
        out_shape=[jax.ShapeDtypeStruct(s, t) for s, t, _ in outs.values()],
        in_specs=[pl.BlockSpec(memory_space=m) for _, m in ins.values()],
        out_specs=[pl.BlockSpec(memory_space=m) for _, _, m in outs.values()],
        scratch_shapes=list(scratch.values()),
        input_output_aliases=alias or {},
        compiler_params=pltpu.CompilerParams(vmem_limit_bytes=VMEM_LIMIT, **params),
    )(*[a for a, _ in ins.values()])
    return SimpleNamespace(**dict(zip(outs, results)))


VMEM = pltpu.VMEM
ANY = pl.ANY


BIT_AXIS = ("fsdp", "fsdp", "fsdp", "dp", "dp")
BIT_MASK = (4, 2, 1, 2, 1)
CUBE = (2,) * 5
GATHER_ORDER = ((2, 3, 4), (3, 2, 4))
SCATTER_ORDER = ((4, 3, 2), (4, 2, 3))
STAGES = 4
COPIES = 6


def my_bits():
    fs = lax.axis_index("fsdp")
    dp = lax.axis_index("dp")
    return (
        lax.rem(fs // 4, 2),
        lax.rem(fs // 2, 2),
        lax.rem(fs, 2),
        lax.rem(dp // 2, 2),
        lax.rem(dp, 2),
    )


def partner(*flipped):
    place = {"fsdp": lax.axis_index("fsdp"), "dp": lax.axis_index("dp")}
    bits = my_bits()
    for bit in flipped:
        place[BIT_AXIS[bit]] += BIT_MASK[bit] * (1 - 2 * bits[bit])
    return (place["dp"], place["fsdp"])


LINE_FLIPS = ((1,), (0,), (0, 1))


def flipped_bits(flips):
    return tuple(1 - b if k in flips else b for k, b in enumerate(my_bits()))


def partner_signal():
    sem = pltpu.get_barrier_semaphore()
    for flips in LINE_FLIPS + ((2,), (3,), (4,)):
        pl.semaphore_signal(sem, inc=1, device_id=partner(*flips), device_id_type=MESH)


def partner_wait():
    pl.semaphore_wait(pltpu.get_barrier_semaphore(), 6)


def run_at(step, number, action):
    if isinstance(step, int):
        if step == number:
            action()
        return

    @pl.when(step == number)
    def _():
        action()


class Gather:
    def __init__(self, buf, pieces, send_sem, recv_sem, mine=None):
        self.buf, self.pieces, self.mine = buf, pieces, mine
        self.send_sem, self.recv_sem = send_sem, recv_sem
        self.bits = my_bits()

    def copy(self, source, target, sem, device):
        return pltpu.make_async_remote_copy(
            src_ref=source,
            dst_ref=target,
            send_sem=self.send_sem.at[sem],
            recv_sem=self.recv_sem.at[sem],
            device_id=device,
            device_id_type=MESH,
        )

    def copies(self, i, stage):
        row, rows, kind = self.pieces[i]
        part = (pl.ds(row, rows),)
        if stage == 0:
            target = self.buf.at[self.bits + part]
            source = target if self.mine is None else self.mine.at[part]
            return [
                self.copy(source, target, i * COPIES + n, partner(*flips))
                for n, flips in enumerate(LINE_FLIPS)
            ]
        order = GATHER_ORDER[kind]
        free = (0, 1) + order[: stage - 1]
        index = tuple(slice(None) if k in free else self.bits[k] for k in range(5))
        ref = self.buf.at[index + part]
        return [self.copy(ref, ref, i * COPIES + 2 + stage, partner(order[stage - 1]))]

    def advance(self, i, stage, first=0, last=STAGES):
        if stage > first:
            for copy in self.copies(i, stage - 1):
                copy.wait_recv()
        if stage < last:
            for copy in self.copies(i, stage):
                copy.start()

    def drain(self, i, first=0, last=STAGES):
        for stage in range(first, last):
            for copy in self.copies(i, stage):
                copy.wait_send()


class Scatter:
    def __init__(self, own, land, out, pieces, send_sem, recv_sem):
        self.own, self.land, self.out, self.pieces = own, land, out, pieces
        self.send_sem, self.recv_sem = send_sem, recv_sem
        self.bits = my_bits()

    def index(self, order, stage, side):
        out = []
        for k in range(5):
            if k in order[:stage]:
                out.append(1 - self.bits[k] if side in ("land", "target") else self.bits[k])
            elif k in order[stage : stage + 1]:
                out.append(1 - self.bits[k] if side in ("send", "target") else self.bits[k])
            else:
                out.append(slice(None))
        return tuple(out)

    def copy(self, source, target, sem, device):
        return pltpu.make_async_remote_copy(
            src_ref=source,
            dst_ref=target,
            send_sem=self.send_sem.at[sem],
            recv_sem=self.recv_sem.at[sem],
            device_id=device,
            device_id_type=MESH,
        )

    def copies(self, i, stage):
        row, rows, kind = self.pieces[i]
        order = SCATTER_ORDER[kind]
        part = (pl.ds(row, rows),)
        if stage == 3:
            place = self.bits[:2] + tuple(1 - b for b in self.bits[2:])
            return [
                self.copy(
                    self.own.at[flipped_bits(flips) + part],
                    self.land.at[place + part],
                    i * COPIES + 3 + n,
                    partner(*flips),
                )
                for n, flips in enumerate(LINE_FLIPS)
            ]
        return [
            self.copy(
                self.own.at[self.index(order, stage, "send") + part],
                self.land.at[self.index(order, stage, "target") + part],
                i * COPIES + stage,
                partner(order[stage]),
            )
        ]

    def add(self, i, stage):
        row, rows, kind = self.pieces[i]
        order = SCATTER_ORDER[kind]
        part = (pl.ds(row, rows), slice(None))
        if stage == 3:
            total = self.own[self.bits + part].astype(f32)
            for flips in LINE_FLIPS:
                place = flipped_bits(flips)[:2] + tuple(1 - b for b in self.bits[2:])
                total = total + self.land[place + part].astype(f32)
            self.out[pl.ds(row, rows), :] = total
            return
        mine = self.own.at[self.index(order, stage, "own")]
        came = self.land.at[self.index(order, stage, "land")]
        free = 4 - stage

        def body(j, carry):
            at = tuple(lax.rem(j // 2 ** (free - 1 - q), 2) for q in range(free)) + part
            mine[at] = mine[at] + came[at]
            return carry

        lax.fori_loop(0, 2**free, body, 0, unroll=2)

    def advance(self, i, stage, first=0, last=STAGES):
        if stage > first:
            for copy in self.copies(i, stage - 1):
                copy.wait()
            self.add(i, stage - 1)
        if stage < last:
            for copy in self.copies(i, stage):
                copy.start()


def split_pieces(chunks):
    pieces = []
    for row, rows in chunks:
        half = (rows // 2 + 15) // 16 * 16
        pieces.append((row, half, 0))
        pieces.append((row + half, rows - half, 1))
    return pieces


class AxisScatter:
    def __init__(self, own, land_dp, land_fsdp, out, sems):
        self.own, self.land_dp, self.land_fsdp, self.out = own, land_dp, land_fsdp, out
        self.sems = sems
        self.fs, self.dp = lax.axis_index("fsdp"), lax.axis_index("dp")

    def bits(self, fs, dp):
        return (lax.rem(fs // 4, 2), lax.rem(fs // 2, 2), lax.rem(fs, 2)), (
            lax.rem(dp // 2, 2),
            lax.rem(dp, 2),
        )

    def dp_copy(self, step):
        other = lax.rem(self.dp + step, 4)
        _, (y, core) = self.bits(self.fs, other)
        return pltpu.make_async_remote_copy(
            src_ref=self.own.at[:, :, :, y, core],
            dst_ref=self.land_dp.at[step - 1],
            send_sem=self.sems.at[0, step],
            recv_sem=self.sems.at[1, step],
            device_id=(other, self.fs),
            device_id_type=MESH,
        )

    def fsdp_copy(self, step):
        other = lax.rem(self.fs + step, 8)
        (zh, zl, x), (y, core) = self.bits(other, self.dp)
        return pltpu.make_async_remote_copy(
            src_ref=self.own.at[zh, zl, x, y, core],
            dst_ref=self.land_fsdp.at[step - 1],
            send_sem=self.sems.at[2, step],
            recv_sem=self.sems.at[3, step],
            device_id=(self.dp, other),
            device_id_type=MESH,
        )

    def first(self):
        for step in range(1, 4):
            self.dp_copy(step).start()

    def second(self):
        for step in range(1, 4):
            self.dp_copy(step).wait()
        _, (y, core) = self.bits(self.fs, self.dp)
        mine = self.own.at[:, :, :, y, core]
        mine[...] = mine[...] + self.land_dp[0] + self.land_dp[1] + self.land_dp[2]
        for step in range(1, 8):
            self.fsdp_copy(step).start()

    def last(self):
        for step in range(1, 8):
            self.fsdp_copy(step).wait()
        (zh, zl, x), (y, core) = self.bits(self.fs, self.dp)
        total = self.own[zh, zl, x, y, core]
        for step in range(7):
            total = total + self.land_fsdp[step]
        self.out[...] = total


def axis_signal():
    fs, dp = lax.axis_index("fsdp"), lax.axis_index("dp")
    sem = pltpu.get_barrier_semaphore()
    for step in range(1, 4):
        to = (lax.rem(dp + step, 4), fs)
        pl.semaphore_signal(sem, inc=1, device_id=to, device_id_type=MESH)
    for step in range(1, 8):
        to = (dp, lax.rem(fs + step, 8))
        pl.semaphore_signal(sem, inc=1, device_id=to, device_id_type=MESH)


def axis_wait():
    pl.semaphore_wait(pltpu.get_barrier_semaphore(), 10)


class Plan:
    def __init__(self, dp, fsdp):
        self.shard = {n: (WEIGHT_SHAPE[n][0] // dp, WEIGHT_SHAPE[n][1] // fsdp) for n in WEIGHTS}
        self.row, at = {}, 0
        for name in WEIGHTS:
            self.row[name] = at
            at += self.shard[name][0] * self.shard[name][1] // 128
        self.rows = at

    def span(self, first, last, shift):
        r, c = self.shard[last]
        end = self.row[last] + r * c // 128
        return (self.row[first] + shift, end - self.row[first])

    def full_shape(self, name):
        return (2, 2, 2, self.shard[name][1], WEIGHT_SHAPE[name][0])

    def held_shape(self, name):
        r, c = self.shard[name]
        return (c, r) if c % 128 else (r, c)

    def blocks(self, name, shift):
        r, c = self.shard[name]
        return [
            (y, core, shift + self.row[name] + q * c, (y * 2 + core) * r + q * 128)
            for y in range(2)
            for core in range(2)
            for q in range(r // 128)
        ]


def put_blocks(plan, name, own, shift, values_of):
    c = plan.shard[name][1]
    for y, core, at, column in plan.blocks(name, shift):
        values = values_of(slice(column, column + 128)).astype(bf16)
        own[:, :, :, y, core, at : at + c, :] = values.reshape(2, 2, 2, c, 128)


def put_shard(plan, name, flat, shift, target):
    r, c = plan.shard[name]
    for q in range(r // 128):
        at = shift + plan.row[name] + q * c
        if c % 128:
            target[:, q * 128 : (q + 1) * 128] = flat[at : at + c, :]
        else:
            target[q * 128 : (q + 1) * 128, :] = flat[at : at + c, :].T


def load_weight(plan, name, buf, target, sem, shift):
    c = plan.shard[name][1]
    for y, core, row, column in plan.blocks(name, shift):
        pltpu.make_async_copy(
            buf.at[:, :, :, y, core, pl.ds(row, c), :],
            target.at[:, :, :, :, pl.ds(column, 128)],
            sem,
        ).start()


def wait_whole(target, sem):
    pltpu.make_async_copy(target, target, sem).wait()


def full(ref):
    values = ref[...]
    return values.reshape(-1, values.shape[-1])


def vector_places():
    places, at = {}, 0
    for name in PACKED_VECTORS:
        size = VECTOR_SIZE[name] // 32
        places[name] = (at // 128, at % 128, size)
        at += size
    return places


def block_owner(first, size):
    row = lax.broadcasted_iota(jnp.int32, (32, D), 0)
    lane = lax.broadcasted_iota(jnp.int32, (32, D), 1) + first
    return lane // size == lax.rem(row, 4) * 8 + row // 4


def iota(shape, axis):
    return lax.broadcasted_iota(jnp.int32, shape, axis)


def narrow_vectors():
    places = vector_places()
    return [
        (places[n][0], places[n][1] // 16, VECTOR_ROW[n])
        for n in VECTORS
        if VECTOR_SIZE[n] == D
    ]


def spread_rule(size, offset, first):
    return (iota((128, D), 0) - offset == lax.rem(iota((128, D), 1) + first, size)).astype(bf16)


def gather_rule(size, offset, first):
    return (iota((D, 128), 1) - offset == lax.rem(iota((D, 128), 0) + first, size)).astype(bf16)


def unpack_vectors(blocks, target):
    flat = blocks[...].reshape(32 * 16, 128)
    own = []
    for line in range(2):
        pick = (iota((32, 512), 1) == iota((32, 512), 0) * 16 + line).astype(bf16)
        own.append(nn(pick, flat))
    group = iota((32, 128), 1) // 16
    narrow = narrow_vectors()
    stacked = jnp.concatenate([jnp.where(group == g, own[line], 0.0) for line, g, _ in narrow])
    same = (lax.rem(iota((128, D), 0), 16) == lax.rem(iota((128, D), 1), 16)).astype(bf16)
    wide = nn(stacked.astype(bf16), same)

    def put(row, first, values, size):
        kept = jnp.where(block_owner(first, size), values, 0.0)
        target[row : row + 1, first : first + D] = jnp.sum(kept, axis=0, keepdims=True)

    for n, (_, _, row) in enumerate(narrow):
        put(row, 0, wide[n * 32 : (n + 1) * 32], 16)
    line = own[0].astype(bf16)
    values = nn(line, spread_rule(64, 0, 0))
    for first in range(0, FF, D):
        put(VECTOR_ROW["hidden"], first, values, 64)
    for first in range(0, 3 * D, D):
        put(VECTOR_ROW["upsample_bias"], first, nn(line, spread_rule(48, 64, first)), 48)


def pack_vectors(source, target):
    def take(row, first, size):
        values = jnp.broadcast_to(source[row : row + 1, first : first + D], (32, D))
        return jnp.where(block_owner(first, size), values, 0.0)

    def collect(values, rule):
        total = jnp.zeros((values.shape[0], 128), f32)
        for _ in range(3):
            term = values.astype(bf16)
            total += nn(term, rule)
            values = values - term.astype(f32)
        return total

    narrow = narrow_vectors()
    stacked = jnp.concatenate([take(row, 0, 16) for _, _, row in narrow])
    same = (lax.rem(iota((D, 128), 1), 16) == lax.rem(iota((D, 128), 0), 16)).astype(bf16)
    close = collect(stacked, same)
    group = iota((32, 128), 1) // 16
    lines = [jnp.zeros((32, 128), f32), jnp.zeros((32, 128), f32)]
    for n, (line, g, _) in enumerate(narrow):
        lines[line] += jnp.where(group == g, close[n * 32 : (n + 1) * 32], 0.0)
    hidden = take(VECTOR_ROW["hidden"], 0, 64)
    for first in range(D, FF, D):
        hidden += take(VECTOR_ROW["hidden"], first, 64)
    lines[0] += collect(hidden, gather_rule(64, 0, 0))
    for first in range(0, 3 * D, D):
        values = take(VECTOR_ROW["upsample_bias"], first, 48)
        lines[0] += collect(values, gather_rule(48, 64, first))
    both = jnp.concatenate([lines[0][:, None, :], lines[1][:, None, :]], axis=1)
    both = jnp.concatenate([both, jnp.zeros((32, 6, 128), f32)], axis=1)
    target[...] = both.reshape(CUBE + (8, 128))


ANGLE_STEPS = SEQ // ANGLE_STEP
FINE_ROW = ANGLE_STEPS + -ANGLE_STEPS % 8
COARSE_ROWS = FINE_ROW + ANGLE_STEP


def angle_rates():
    ratios = np.arange(0, D, 2).astype(np.float32) / np.float32(D)
    rates = np.float32(1.0) / np.power(np.float32(10000.0), ratios)
    return jnp.asarray(np.broadcast_to(rates, (8, HALF)).astype(np.float32))


def coarse_angles(rates, coarse):
    row = lax.broadcasted_iota(jnp.int32, (COARSE_ROWS, HALF), 0)
    place = jnp.where(row < FINE_ROW, row * ANGLE_STEP, row - FINE_ROW).astype(f32)
    angles = place * rates[0:1, :]
    coarse[:, :HALF] = jnp.sin(angles)
    coarse[:, HALF:] = jnp.cos(angles)


def expand_angles(coarse, angles, table_of):
    steps, start = ANGLE_STEPS, FINE_ROW

    def body(q, carry):
        high_sin, high_cos = coarse[pl.ds(q, 1), :HALF], coarse[pl.ds(q, 1), HALF:]
        low_sin, low_cos = coarse[start:, :HALF], coarse[start:, HALF:]
        sine = high_sin * low_cos + high_cos * low_sin
        cosine = high_cos * low_cos - high_sin * low_sin
        rows = at_rows(q, ANGLE_STEP)
        angles[rows, :HALF] = sine
        angles[rows, HALF:] = cosine
        table_of(rows, sine.astype(bf16), cosine.astype(bf16))
        return carry

    lax.fori_loop(0, steps, body, 0)


def head_lanes(rows, head):
    return (lax.broadcasted_iota(jnp.int32, (rows, 128), 1) // HEAD_DIM) == head


def keep_head(values, head):
    return jnp.where(head_lanes(values.shape[0], head), values, 0).astype(bf16)


def rotate(pair, sines, cosines):
    low, high = pair[:, :HALF], pair[:, HALF:]
    return high * sines - low * cosines, low * sines + high * cosines


def norm_parts(values):
    row_mean = jnp.mean(values, axis=-1, keepdims=True)
    centred = values - row_mean
    variance = jnp.mean(centred * centred, axis=-1, keepdims=True)
    inv_std = lax.rsqrt(variance + epsilon)
    return centred * inv_std, inv_std


def norm_backward(normal, inv_std, gain, upstream):
    scaled = upstream * gain
    scaled_mean = jnp.mean(scaled, axis=-1, keepdims=True)
    cross_mean = jnp.mean(scaled * normal, axis=-1, keepdims=True)
    return inv_std * (scaled - scaled_mean - normal * cross_mean)


def vec(ref, name):
    r = VECTOR_ROW[name]
    return ref[r : r + 1, : VECTOR_SIZE[name]]


VECTOR_ROWS = 16


FRONT_ROWS = ("query_u", "query_v", "key", "value", "mixed")
CHUNK_LAST = (4, 4, 4, 4, 2, 2)
FIRST = ((0, 0), (1, 0))
BEFORE = ((0, 1), (1, 1), (2, 0), (0, 2), (1, 2), (0, 3), (1, 3), (2, 1), (3, 0), (0, 4), (1, 4))
AFTER = ((2, 2), (3, 1), (4, 0), (5, 0))
DURING = {
    11: ((2, 3), (3, 2), (4, 1), (5, 1)),
    17: ((3, 3),),
    23: ((2, 4), (3, 4), (4, 2), (5, 2)),
}


def front(plan, linked, ins):
    outs = {
        "vectors": ((16, FF), f32, VMEM),
        "coarse": ((COARSE_ROWS, D), f32, VMEM),
    }
    outs |= {n + "_out": ((SEQ, D), bf16, ANY) for n in FRONT_ROWS}
    outs |= {
        "probs_out": ((HEADS, QB, PW), bf16, ANY),
    }
    scratch = {
        "normal": VMEM((SEQ, D), f32),
        "angles": VMEM((SEQ, D), f32),
        "key_table": VMEM((SEQ, 128 + D), bf16),
        "score": VMEM((2, QB, SEQ), f32),
        "turned": VMEM((2, QB, 128 + D), bf16),
        "probs": VMEM((2, QB, PW), bf16),
        "probs_sem": pltpu.SemaphoreType.DMA((2,)),
        "out_sem": pltpu.SemaphoreType.DMA((len(FRONT_ROWS),)),
        "tokens": VMEM((SEQ, D), bf16),
        "token_sem": pltpu.SemaphoreType.DMA,
    }
    scratch |= {n: VMEM((SEQ, D), bf16) for n in FRONT_ROWS}
    params = {}
    if linked:
        rows = VECTOR_ROWS + plan.rows
        chunks = [
            (0, 128),
            (128, VECTOR_ROWS + plan.span("project", "position", 0)[1] - 128),
            plan.span("mixing", "expand", VECTOR_ROWS),
            plan.span("contract", "contract", VECTOR_ROWS),
            plan.span("pooling", "pooling", VECTOR_ROWS),
            plan.span("upsample", "upsample", VECTOR_ROWS),
        ]
        pieces = split_pieces(chunks)
        outs["blocks"] = (CUBE + (rows, 128), bf16, ANY)
        scratch |= {
            "mine": VMEM((rows, 128), bf16),
            "project": VMEM(plan.full_shape("project"), bf16),
            "position": VMEM(plan.full_shape("position"), bf16),
            "vector_blocks": VMEM(CUBE + (VECTOR_ROWS, 128), bf16),
            "vector_lines": VMEM((VECTOR_ROWS, 128), f32),
            "send_sem": pltpu.SemaphoreType.DMA((COPIES * len(pieces),)),
            "recv_sem": pltpu.SemaphoreType.DMA((COPIES * len(pieces),)),
            "load_sem": pltpu.SemaphoreType.DMA((4,)),
        }
        params = dict(collective_id=0, has_side_effects=True)

    def body(ref):
        token_load = pltpu.make_async_copy(ref.tokens_in, ref.tokens, ref.token_sem)
        token_load.start()
        if linked:
            partner_signal()
            gather = Gather(ref.blocks, pieces, ref.send_sem, ref.recv_sem, ref.mine)

            def run(events):
                for chunk, stage in events:
                    for piece in (2 * chunk, 2 * chunk + 1):
                        gather.advance(piece, stage, last=CHUNK_LAST[chunk])

            def pack(name):
                r, c = plan.shard[name]
                shard = getattr(ref, name + "_shard")
                for q in range(r // 128):
                    at = VECTOR_ROWS + plan.row[name] + q * c
                    if c % 128:
                        ref.mine[at : at + c, :] = shard[:, q * 128 : (q + 1) * 128]
                    else:
                        ref.mine[at : at + c, :] = shard[q * 128 : (q + 1) * 128, :].T

            ref.vector_lines[...] = jnp.zeros_like(ref.vector_lines)
            for name, (line, offset, size) in vector_places().items():
                entries = getattr(ref, name + "_shard")[...].astype(f32).reshape(1, size)
                ref.vector_lines[line : line + 1, offset : offset + size] = entries
            ref.mine[:VECTOR_ROWS, :] = ref.vector_lines[...].astype(bf16)
            for name in ("project", "position"):
                pack(name)
            partner_wait()
            run(FIRST)
            for name in WEIGHTS[2:]:
                pack(name)
            own = pltpu.make_async_copy(
                ref.mine, ref.blocks.at[gather.bits], ref.load_sem.at[0]
            )
            own.start()

        token_load.wait()

        def first_norm(i, carry):
            rows = at_rows(i, RB)
            ref.normal[rows, :] = norm_parts(ref.tokens[rows, :].astype(f32))[0]
            return carry

        lax.fori_loop(0, SEQ // RB, first_norm, 0)

        def table_of(rows, sine, cosine):
            ref.key_table[rows, 128 : 128 + HALF] = sine
            ref.key_table[rows, 128 + HALF :] = cosine

        coarse_angles(ref.rates, ref.coarse)
        expand_angles(ref.coarse, ref.angles, table_of)

        if linked:
            own.wait()
            run(BEFORE)
            load_weight(plan, "project", ref.blocks, ref.project, ref.load_sem.at[1], VECTOR_ROWS)
            load_weight(plan, "position", ref.blocks, ref.position, ref.load_sem.at[3], VECTOR_ROWS)
            small = pltpu.make_async_copy(
                ref.blocks.at[:, :, :, :, :, pl.ds(0, VECTOR_ROWS), :],
                ref.vector_blocks,
                ref.load_sem.at[2],
            )
            small.start()
            small.wait()
            unpack_vectors(ref.vector_blocks, ref.vectors)
            wait_whole(ref.project, ref.load_sem.at[1])
        else:
            ref.vectors[...] = ref.given_vectors[...]

        def project_rows(b, carry):
            rows = at_rows(b, QB)
            normed = ref.normal[rows, :] * vec(ref.vectors, "gain_one") + vec(
                ref.vectors, "shift_one"
            )
            joined = nt(normed.astype(bf16), full(ref.project))
            ref.query_u[rows, :] = (joined[:, :D] + vec(ref.vectors, "content")).astype(bf16)
            ref.query_v[rows, :] = (joined[:, :D] + vec(ref.vectors, "position_bias")).astype(bf16)
            ref.key[rows, :] = joined[:, D : 2 * D].astype(bf16)
            ref.value[rows, :] = joined[:, 2 * D :].astype(bf16)
            return carry

        lax.fori_loop(0, BLOCKS, project_rows, 0)

        def row_copy(i):
            name = FRONT_ROWS[i]
            return pltpu.make_async_copy(
                getattr(ref, name), getattr(ref, name + "_out"), ref.out_sem.at[i]
            )

        for i in range(4):
            row_copy(i).start()

        if linked:
            run(AFTER)
            wait_whole(ref.position, ref.load_sem.at[3])
            position = ref.position.reshape(D, D)
        else:
            position = ref.position

        def out_copy(head, slot):
            return pltpu.make_async_copy(
                ref.probs.at[slot], ref.probs_out.at[head], ref.probs_sem.at[slot]
            )

        def scores(lanes, b, e):
            row, width = b * QB, (b + 1) * QB
            rows = slice(row, row + QB)
            spread = nn(keep_head(ref.query_v[rows, lanes], e), position[lanes, :])
            low, high = rotate(spread, ref.angles[rows, :HALF], ref.angles[rows, HALF:])
            ref.turned[e, :, :128] = keep_head(ref.query_u[rows, lanes], e)
            ref.turned[e, :, 128 : 128 + HALF] = low.astype(bf16)
            ref.turned[e, :, 128 + HALF :] = high.astype(bf16)
            ref.score[e, :, :width] = nt(ref.turned[e], ref.key_table[:width, :])

        def softmax(b, e):
            row, width = b * QB, (b + 1) * QB
            for sub in range(QB // SB):
                used = row + (sub + 1) * SB
                for g in range(SB // CH):
                    at = slice(sub * SB + g * CH, sub * SB + (g + 1) * CH)
                    tiles = [
                        ref.score[e, at, i * 128 : (i + 1) * 128] for i in range(used // 128)
                    ]
                    lane = lax.broadcasted_iota(jnp.int32, (CH, SB), 1)
                    place = lax.broadcasted_iota(jnp.int32, (CH, SB), 0) + g * CH
                    tiles[-1] = jnp.where(lane <= place, tiles[-1], -1e30)
                    top = tiles[0]
                    for tile in tiles[1:]:
                        top = jnp.maximum(top, tile)
                    top = jnp.max(top, axis=1, keepdims=True)
                    tiles = [jnp.exp2((tile - top) * EXP_SCALE) for tile in tiles]
                    total = tiles[0]
                    for tile in tiles[1:]:
                        total = total + tile
                    scale = 1.0 / jnp.sum(total, axis=1, keepdims=True)
                    for i, tile in enumerate(tiles):
                        lanes = slice(POFF[b] + i * 128, POFF[b] + (i + 1) * 128)
                        ref.probs[e, at, lanes] = (tile * scale).astype(bf16)
                if used < width:
                    ref.probs[e, sub * SB : (sub + 1) * SB, POFF[b] + used : POFF[b] + width] = (
                        jnp.zeros((SB, width - used), bf16)
                    )

        def pair(turn, inner):
            hp = turn * 2 + inner
            lanes = pl.ds(pl.multiple_of(hp * 128, 128), 128)
            ref.key_table[:, :128] = ref.key[:, lanes]

            if inner > 0:
                for e in range(2):
                    out_copy(0, e).wait()
            else:

                @pl.when(turn > 0)
                def _():
                    for e in range(2):
                        out_copy(0, e).wait()


            for b in range(BLOCKS):
                for e in range(2):
                    scores(lanes, b, e)
                    softmax(b, e)
                    for when, events in DURING.items():
                        if linked and when % 12 == inner * 6 + b * 2 + e:
                            run_at(turn, when // 12, lambda events=events: run(events))
                row, width = b * QB, (b + 1) * QB
                values = ref.value[:width, lanes]
                span = slice(POFF[b], POFF[b] + width)
                ref.mixed[row : row + QB, lanes] = jnp.where(
                    head_lanes(QB, 0),
                    nn(ref.probs[0, :, span], values),
                    nn(ref.probs[1, :, span], values),
                ).astype(bf16)
            for e in range(2):
                out_copy(hp * 2 + e, e).start()

        def two_pairs(turn, carry):
            pair(turn, 0)
            pair(turn, 1)
            return carry

        lax.fori_loop(0, HEADS // 4, two_pairs, 0)
        row_copy(4).start()
        for e in range(2):
            out_copy(0, e).wait()
        if linked:
            for i in range(len(pieces)):
                gather.drain(i, last=CHUNK_LAST[i // 2])
        for i in range(5):
            row_copy(i).wait()

    return call(body, ins, outs, scratch, **params)


MIDDLE = ("mixing", "expand", "contract", "pooling", "upsample")


def middle(plan, linked, ins):
    def weight_shape(name):
        return plan.full_shape(name) if linked else WEIGHT_SHAPE[name][::-1]

    outs = {
        "output_out": ((SEQ, D), bf16, ANY),
        "first_grad_out": ((SEQ, D), f32, ANY),
        "mixed_grad_out": ((SEQ, D), bf16, ANY),
        "sums": ((16, FF), f32, VMEM),
    }
    summed = ("pooling", "upsample") if linked else ()
    kept = [n for n in MIDDLE if n not in summed]
    outs |= {n + "_grad_out": (weight_shape(n), bf16, ANY) for n in kept}
    params = {}
    scratch = {n: VMEM(weight_shape(n), bf16) for n in MIDDLE}
    scratch |= {
        "normal": VMEM((SEQ, D), f32),
        "inverse": VMEM((SEQ, 128), f32),
        "second_low": VMEM((SEQ, D), bf16),
        "activated": VMEM((SEQ, FF), bf16),
        "slope": VMEM((SEQ, FF), bf16),
        "tiles": VMEM((D // 128, SEQ + 16, 128), f32),
        "grouped": VMEM((THIRD, 3 * D), bf16),
        "up_rows": VMEM((THIRD, 3 * D), bf16),
        "branch_grad": VMEM((SEQ, D), bf16),
        "attended_grad": VMEM((SEQ, D), bf16),
        "parts": VMEM((5, 8, FF), f32),
        "output": VMEM((SEQ, D), bf16),
        "first_grad": VMEM((SEQ, D), f32),
        "mixed_grad": VMEM((SEQ, D), bf16),
        "sem": pltpu.SemaphoreType.DMA((len(MIDDLE),)),
        "row_sem": pltpu.SemaphoreType.DMA((3,)),
        "tokens": VMEM((SEQ, D), bf16),
        "cotangent": VMEM((SEQ, D), bf16),
        "mixed": VMEM((SEQ, D), bf16),
        "out_sem": pltpu.SemaphoreType.DMA((3 + len(kept),)),
    }
    scratch |= {n + "_grad": VMEM(weight_shape(n), bf16) for n in kept}
    if linked:
        gather_pieces = split_pieces(
            [plan.span(n, n, VECTOR_ROWS) for n in ("pooling", "upsample")]
        )
        base = -plan.row["pooling"]
        pieces = split_pieces([plan.span(n, n, base) for n in summed])
        rows = plan.span("pooling", "upsample", base)[1]
        outs["blocks_out"] = (CUBE + (VECTOR_ROWS + plan.rows, 128), bf16, ANY)
        outs["partial"] = ((2, 2, rows, 128), bf16, ANY)
        scratch |= {
            "own": VMEM(CUBE + (rows, 128), bf16),
            "land": VMEM(CUBE + (rows, 128), bf16),
            "partial_sem": pltpu.SemaphoreType.DMA,
            "gather_send": pltpu.SemaphoreType.DMA((4 * COPIES,)),
            "gather_recv": pltpu.SemaphoreType.DMA((4 * COPIES,)),
            "send_sem": pltpu.SemaphoreType.DMA((4 * COPIES,)),
            "recv_sem": pltpu.SemaphoreType.DMA((4 * COPIES,)),
        }
        params = dict(
            collective_id=1,
            has_side_effects=True,
            alias={list(ins).index("blocks"): list(outs).index("blocks_out")},
        )

    def body(ref):
        def fetch(name):
            i = MIDDLE.index(name)
            if linked:
                load_weight(
                    plan, name, ref.blocks_out, getattr(ref, name), ref.sem.at[i], VECTOR_ROWS
                )
            else:
                pltpu.make_async_copy(
                    getattr(ref, name + "_full"), getattr(ref, name), ref.sem.at[i]
                ).start()

        gather_stage = scatter_stage = None
        if linked:
            gather = Gather(ref.blocks_out, gather_pieces, ref.gather_send, ref.gather_recv)
            scatter = Scatter(ref.own, ref.land, None, pieces, ref.send_sem, ref.recv_sem)
            partner_signal()

            def gather_stage(stage):
                for i in range(4):
                    gather.advance(i, stage, first=2)

            def scatter_stage(name, stage):
                for half in range(2):
                    scatter.advance(summed.index(name) * 2 + half, stage, last=3)

        arriving = ("mixed", "tokens", "cotangent")

        def row_copy(name):
            return pltpu.make_async_copy(
                getattr(ref, name + "_in"), getattr(ref, name), ref.row_sem.at[arriving.index(name)]
            )

        row_copy("mixed").start()
        row_copy("tokens").start()
        for name in ("mixing", "expand", "contract"):
            fetch(name)
        if linked:
            partner_wait()
            gather_stage(2)
        else:
            fetch("pooling")
            fetch("upsample")

        outgoing = ["output", "first_grad", "mixed_grad"] + [n + "_grad" for n in kept]

        def send_out(name):
            return pltpu.make_async_copy(
                getattr(ref, name),
                getattr(ref, name + "_out"),
                ref.out_sem.at[outgoing.index(name)],
            )

        def at_step(i, number, action, *args):
            if linked:
                run_at(i, number, lambda: action(*args))

        def ready(name):
            wait_whole(getattr(ref, name), ref.sem.at[MIDDLE.index(name)])

        def get(name):
            return full(getattr(ref, name))

        def put(name, values):
            if name in summed:
                put_blocks(plan, name, ref.own, base, lambda columns: values[:, columns])
                return
            target = getattr(ref, name + "_grad")
            target[...] = values.astype(bf16).reshape(target.shape)
            send_out(name + "_grad").start()

        def third(start, k):
            return jnp.concatenate(
                [ref.tiles[t, pl.ds(start + k, THIRD, stride=3), :] for t in range(D // 128)],
                axis=1,
            )

        def put_third(start, k, values):
            for t in range(D // 128):
                ref.tiles[t, pl.ds(start + k, THIRD, stride=3), :] = values[
                    :, t * 128 : (t + 1) * 128
                ]

        def rows_of(rows):
            return jnp.concatenate([ref.tiles[t, rows, :] for t in range(D // 128)], axis=1)

        def put_rows(rows, values):
            for t in range(D // 128):
                ref.tiles[t, rows, :] = values[:, t * 128 : (t + 1) * 128]

        def shifted_rows(i):
            return pl.ds(pl.multiple_of(i * MB + 8, 8), MB)

        ref.parts[...] = jnp.zeros_like(ref.parts)
        ref.sums[...] = jnp.zeros_like(ref.sums)

        def add_part(slot, values):
            columns = values.shape[1]
            ref.parts[slot, :, :columns] += eight_rows(values)

        def put_sum(name, values):
            r = VECTOR_ROW[name]
            ref.sums[r : r + 1, : values.shape[1]] = values

        def put_part(name, slot):
            columns = VECTOR_SIZE[name]
            put_sum(name, jnp.sum(ref.parts[slot, :, :columns], axis=0, keepdims=True))

        row_copy("cotangent").start()
        row_copy("mixed").wait()
        row_copy("tokens").wait()
        for name in ("mixing", "expand", "contract"):
            ready(name)

        def forward(i, carry):
            rows = at_rows(i, MB)
            attended = nt(ref.mixed[rows, :], get("mixing")) + vec(ref.vectors, "mixing_bias")
            first = ref.tokens[rows, :].astype(f32) + attended
            normal, inverse = norm_parts(first)
            ref.normal[rows, :] = normal
            ref.inverse[rows, :] = jnp.broadcast_to(inverse, (MB, 128))
            low = (
                normal * vec(ref.vectors, "gain_two") + vec(ref.vectors, "shift_two")
            ).astype(bf16)
            ref.second_low[rows, :] = low
            inner = nt(low, get("expand")) + vec(ref.vectors, "hidden")
            phi = 0.5 * (1.0 + lax.erf(inner * 2.0 ** (-0.5)))
            act = (inner * phi).astype(bf16)
            ref.activated[rows, :] = act
            bell = jnp.exp(-0.5 * inner * inner) * (2.0 * math.pi) ** (-0.5)
            ref.slope[rows, :] = (phi + inner * bell).astype(bf16)
            block = first + nt(act, get("contract")) + vec(ref.vectors, "contract_bias")
            put_rows(shifted_rows(i), block)
            at_step(i, 4, gather_stage, 3)
            return carry

        lax.fori_loop(0, SEQ // MB, forward, 0)

        put_rows(slice(0, 8), jnp.zeros((8, D), f32))
        for k in range(3):
            ref.grouped[:, k * D : (k + 1) * D] = third(6, k).astype(bf16)
        if linked:
            gather_stage(4)
            fetch("pooling")
            fetch("upsample")
        ready("pooling")
        pooled = (
            nt(ref.grouped[...], get("pooling")) + vec(ref.vectors, "pooling_bias")
        ).astype(bf16)
        ready("upsample")
        for k in range(3):
            columns = slice(k * D, (k + 1) * D)
            upward = nt(pooled, get("upsample")[columns, :]) + vec(ref.vectors, "upsample_bias")[
                :, columns
            ]
            put_third(8, k, third(8, k) + upward)

        row_copy("cotangent").wait()

        def write_output(i, carry):
            ref.output[at_rows(i, MB), :] = rows_of(shifted_rows(i)).astype(bf16)
            put_rows(shifted_rows(i), ref.cotangent[at_rows(i, MB), :].astype(f32))
            return carry

        lax.fori_loop(0, SEQ // MB, write_output, 0)

        send_out("output").start()

        for k in range(3):
            ref.up_rows[:, k * D : (k + 1) * D] = third(8, k).astype(bf16)
        up_rows = ref.up_rows[...]
        put_sum("upsample_bias", jnp.sum(up_rows.astype(f32), axis=0, keepdims=True))
        put("upsample", tn(up_rows, pooled))
        if linked:
            scatter_stage("upsample", 0)
        pooled_grad = nn(up_rows, get("upsample")).astype(bf16)
        put_sum("pooling_bias", jnp.sum(pooled_grad.astype(f32), axis=0, keepdims=True))
        put("pooling", tn(pooled_grad, ref.grouped[...]))
        if linked:
            scatter_stage("pooling", 0)
        for k in range(3):
            put_third(
                6, k, nn(pooled_grad, get("pooling")[:, k * D : (k + 1) * D])
            )
        put_rows(slice(SEQ + 6, SEQ + 8), jnp.zeros((2, D), f32))
        if linked:
            scatter_stage("upsample", 1)

        def backward(i, carry):
            rows = at_rows(i, MB)
            block_grad = ref.cotangent[rows, :].astype(f32) + rows_of(shifted_rows(i))
            branch_grad = block_grad.astype(bf16)
            ref.branch_grad[rows, :] = branch_grad
            add_part(0, branch_grad.astype(f32))
            inner_grad = (nn(branch_grad, get("contract")) * ref.slope[rows, :].astype(f32)).astype(
                bf16
            )
            ref.slope[rows, :] = inner_grad
            add_part(1, inner_grad.astype(f32))
            second_grad = nn(inner_grad, get("expand"))
            normal = ref.normal[rows, :]
            add_part(2, second_grad * normal)
            add_part(3, second_grad)
            first_grad = block_grad + norm_backward(
                normal, ref.inverse[rows, :1], vec(ref.vectors, "gain_two"), second_grad
            )
            ref.first_grad[rows, :] = first_grad
            attended_grad = first_grad.astype(bf16)
            ref.attended_grad[rows, :] = attended_grad
            add_part(4, attended_grad.astype(f32))
            ref.mixed_grad[rows, :] = nn(attended_grad, get("mixing")).astype(bf16)
            at_step(i, 0, scatter_stage, "pooling", 1)
            at_step(i, 3, scatter_stage, "upsample", 2)
            at_step(i, 5, scatter_stage, "pooling", 2)
            return carry

        lax.fori_loop(0, SEQ // MB, backward, 0)
        send_out("first_grad").start()
        send_out("mixed_grad").start()
        put_part("contract_bias", 0)
        put_part("hidden", 1)
        put_part("gain_two", 2)
        put_part("shift_two", 3)
        put_part("mixing_bias", 4)

        def contract_part(part, carry):
            columns = pl.ds(pl.multiple_of(part * D, D), D)
            values = tn(ref.branch_grad[...], ref.activated[:, columns]).astype(bf16)
            target = ref.contract_grad.at[..., columns]
            target[...] = values.reshape(target.shape)
            return carry

        lax.fori_loop(0, FF // D, contract_part, 0)
        send_out("contract_grad").start()
        if linked:
            scatter_stage("upsample", 3)

        def expand_part(part, carry):
            columns = pl.ds(pl.multiple_of(part * D, D), D)
            values = tn(ref.slope[:, columns], ref.second_low[...]).astype(bf16)
            if linked:
                target = ref.expand_grad.at[part // 2, lax.rem(part, 2)]
            else:
                target = ref.expand_grad.at[columns]
            target[...] = values.reshape(target.shape)
            return carry

        lax.fori_loop(0, FF // D, expand_part, 0)
        send_out("expand_grad").start()
        put("mixing", tn(ref.attended_grad[...], ref.mixed[...]))
        if linked:
            scatter_stage("pooling", 3)
            _, _, x, y, core = scatter.bits
            partial = pltpu.make_async_copy(
                ref.own.at[:, :, x, y, core], ref.partial, ref.partial_sem
            )
            partial.start()
            partial.wait()
            for i in range(4):
                gather.drain(i, first=2)
        for name in outgoing:
            send_out(name).wait()

    return call(body, ins, outs, scratch, **params)


BACK_FIRST = (0, 0, 3, 0, 0, 0)
BACK_DURING = {
    2: ((0, 1),),
    7: ((0, 2), (1, 1)),
    14: ((0, 3), (1, 2), (2, 4)),
    18: ((0, 4), (1, 3)),
    23: ((1, 4),),
}


def back(plan, linked, ins):
    outs = {"token_grad_out": ((SEQ, D), f32, ANY)}
    late_rows = ("tokens", "mixed_grad", "mixed", "value", "key", "query_u", "query_v", "first_grad")
    scratch = {
        "angles": VMEM((SEQ, D), f32),
        "key_table": VMEM((SEQ, 128 + D), bf16),
        "prob_grad": VMEM((2, QB, SEQ), f32),
        "total_grad": VMEM((2, QB, SEQ), bf16),
        "probs": VMEM((4, QB, PW), bf16),
        "key_acc": VMEM((128, SEQ), f32),
        "value_acc": VMEM((128, SEQ), f32),
        "joined_grad": VMEM((SEQ, 3 * D), bf16),
        "normed_low": VMEM((SEQ, D), bf16),
        "position_grad": VMEM((D, D), f32),
        "parts": VMEM((2, 8, D), f32),
        "all_sums": VMEM((16, FF), f32),
        "probs_sem": pltpu.SemaphoreType.DMA((4,)),
        "load_sem": pltpu.SemaphoreType.DMA((2,)),
        "token_grad": VMEM((SEQ, D), f32),
        "token_sem": pltpu.SemaphoreType.DMA,
        "row_sem": pltpu.SemaphoreType.DMA((len(late_rows),)),
    }
    scratch |= {n: VMEM((SEQ, D), f32 if n == "first_grad" else bf16) for n in late_rows}
    params = {}
    project_shape = plan.full_shape("project") if linked else (3 * D, D)
    position_shape = plan.full_shape("position") if linked else (D, D)
    scratch |= {"project": VMEM(project_shape, bf16), "position": VMEM(position_shape, bf16)}
    if linked:
        early_names = ("contract", "expand", "mixing")
        early = [plan.span("contract", "contract", 0), plan.span("mixing", "expand", 0)]
        late = [plan.span("pooling", "upsample", 0), plan.span("position", "position", 0)]
        row, rows = plan.span("project", "project", 0)
        late += [(row, rows // 2), (row + rows // 2, rows // 2)]
        pieces = split_pieces(early + late)
        count = COPIES * len(pieces)
        own_rows = plan.rows
        outs["vector_out"] = ((8, 128), f32, VMEM)
        outs["flat_out"] = ((own_rows, 128), f32, ANY)
        scratch |= {
            "own": VMEM(CUBE + (own_rows, 128), bf16),
            "land": VMEM(CUBE + (own_rows, 128), bf16),
            "flat": VMEM((own_rows, 128), f32),
            "vector_own": VMEM(CUBE + (8, 128), f32),
            "land_dp": VMEM((3, 2, 2, 2, 8, 128), f32),
            "land_fsdp": VMEM((7, 8, 128), f32),
            "vector_sem": pltpu.SemaphoreType.DMA((4, 8)),
            "send_sem": pltpu.SemaphoreType.DMA((count,)),
            "recv_sem": pltpu.SemaphoreType.DMA((count,)),
            "own_sem": pltpu.SemaphoreType.DMA((4,)),
        }
        params = dict(collective_id=2, has_side_effects=True)
    else:
        outs["project_grad"] = ((3 * D, D), bf16, VMEM)
        outs["position_grad_out"] = ((D, D), bf16, VMEM)
        outs["sums_out"] = ((16, FF), f32, VMEM)

    def body(ref):
        def row_copy(name):
            return pltpu.make_async_copy(
                getattr(ref, name + "_in"), getattr(ref, name), ref.row_sem.at[late_rows.index(name)]
            )

        for name in late_rows[:7]:
            row_copy(name).start()
        if linked:
            load_weight(plan, "project", ref.blocks, ref.project, ref.load_sem.at[0], VECTOR_ROWS)
            load_weight(plan, "position", ref.blocks, ref.position, ref.load_sem.at[1], VECTOR_ROWS)
            matrix = Scatter(ref.own, ref.land, ref.flat, pieces, ref.send_sem, ref.recv_sem)
            vector = AxisScatter(
                ref.vector_own, ref.land_dp, ref.land_fsdp, ref.vector_out, ref.vector_sem
            )
            axis_signal()

            def run(events):
                for chunk, stage in events:
                    for piece in (2 * chunk, 2 * chunk + 1):
                        matrix.advance(piece, stage, first=BACK_FIRST[chunk])

            for i, name in enumerate(early_names):
                c = plan.shard[name][1]
                for y, core, row, column in plan.blocks(name, 0):
                    pltpu.make_async_copy(
                        getattr(ref, name + "_grad").at[:, :, :, :, pl.ds(column, 128)],
                        ref.own.at[:, :, :, y, core, pl.ds(row, c), :],
                        ref.own_sem.at[i],
                    ).start()
            _, _, x, y, core = matrix.bits
            row, rows = late[0]
            partial = pltpu.make_async_copy(
                ref.partial, ref.own.at[:, :, x, y, core, pl.ds(row, rows), :], ref.own_sem.at[3]
            )
            partial.start()
        else:
            for i, name in enumerate(("project", "position")):
                pltpu.make_async_copy(
                    getattr(ref, name + "_full"), getattr(ref, name), ref.load_sem.at[i]
                ).start()

        def in_copy(head, slot):
            return pltpu.make_async_copy(
                ref.probs_in.at[head], ref.probs.at[slot], ref.probs_sem.at[slot]
            )

        for e in range(2):
            in_copy(e, e).start()

        def table_of(rows, sine, cosine):
            ref.key_table[rows, 128 : 128 + HALF] = sine
            ref.key_table[rows, 128 + HALF :] = cosine

        expand_angles(ref.coarse, ref.angles, table_of)

        def norm_rows(rows):
            return norm_parts(ref.tokens[rows, :].astype(f32))

        def low_rows(i, carry):
            rows = at_rows(i, RB)
            normal, _ = norm_rows(rows)
            ref.normed_low[rows, :] = (
                normal * vec(ref.vectors, "gain_one") + vec(ref.vectors, "shift_one")
            ).astype(bf16)
            return carry

        row_copy("tokens").wait()
        lax.fori_loop(0, SEQ // RB, low_rows, 0)
        ref.all_sums[...] = ref.sums[...]
        ref.parts[...] = jnp.zeros_like(ref.parts)
        if linked:
            axis_wait()
            partial.wait()
            run([(2, 3)])
            for i, name in enumerate(early_names):
                row, rows = plan.span(name, name, 0)
                whole = ref.own.at[:, :, :, :, :, pl.ds(row, rows), :]
                wait_whole(whole, ref.own_sem.at[i])
                if i == 0:
                    run([(0, 0)])
            run([(1, 0)])
        wait_whole(ref.project, ref.load_sem.at[0])
        wait_whole(ref.position, ref.load_sem.at[1])
        position = ref.position.reshape(D, D)
        for name in late_rows[1:7]:
            row_copy(name).wait()
        row_copy("first_grad").start()

        def pair(hp, carry):
            start = pl.multiple_of(hp * 128, 128)
            lanes = pl.ds(start, 128)
            base = lax.rem(hp, 2) * 2
            for e in range(2):
                in_copy(0, base + e).wait()

            @pl.when(hp < HEADS // 2 - 1)
            def _():
                for e in range(2):
                    in_copy(hp * 2 + 2 + e, 2 - base + e).start()

            ref.key_table[:, :128] = ref.key[:, lanes]
            content_sum = jnp.zeros((1, 128), f32)
            position_sum = jnp.zeros((1, 128), f32)
            for b in range(BLOCKS):
                row, width = b * QB, (b + 1) * QB
                rows = slice(row, row + QB)
                span = slice(POFF[b], POFF[b] + width)
                by_content, by_position = [], None
                for e in range(2):
                    upstream = keep_head(ref.mixed_grad[rows, lanes], e)
                    row_dot = jnp.sum(
                        upstream.astype(f32) * ref.mixed[rows, lanes].astype(f32),
                        axis=1,
                        keepdims=True,
                    )
                    ref.prob_grad[e, :, :width] = nt(upstream, ref.value[:width, lanes]) - row_dot
                    for sub in range(QB // SB):
                        used = row + (sub + 1) * SB
                        for g in range(SB // CH):
                            at = slice(sub * SB + g * CH, sub * SB + (g + 1) * CH)
                            p = ref.probs[base + e, at, POFF[b] : POFF[b] + used].astype(f32)
                            ref.total_grad[e, at, :used] = (
                                p * ref.prob_grad[e, at, :used] * HEAD_DIM ** (-0.5)
                            ).astype(bf16)
                        if used < width:
                            ref.total_grad[e, sub * SB : (sub + 1) * SB, used:width] = jnp.zeros(
                                (SB, width - used), bf16
                            )
                    scored = ref.total_grad[e, :, :width]
                    turned = nn(scored, ref.key_table[:width, :])
                    by_content.append(turned[:, :128])
                    low, high = rotate(
                        turned[:, 128:], ref.angles[rows, :HALF], ref.angles[rows, HALF:]
                    )
                    spread = jnp.concatenate([low, high], axis=1).astype(bf16)
                    own = (lax.broadcasted_iota(jnp.int32, (128, D), 0) // HEAD_DIM) == e
                    part = nt(spread, jnp.where(own, position[lanes, :], 0).astype(bf16))
                    by_position = part if by_position is None else by_position + part
                    part = tn(keep_head(ref.query_v[rows, lanes], e), spread)
                    if b == 0 and e == 0:
                        ref.position_grad[lanes, :] = part
                    else:
                        ref.position_grad[lanes, :] += part
                    to_key = tn(keep_head(ref.query_u[rows, lanes], e), scored)
                    to_value = tn(upstream, ref.probs[base + e, :, span])
                    if e == 0:
                        if b > 0:
                            ref.key_acc[:, :row] += to_key[:, :row]
                            ref.value_acc[:, :row] += to_value[:, :row]
                        ref.key_acc[:, row:width] = to_key[:, row:]
                        ref.value_acc[:, row:width] = to_value[:, row:]
                    else:
                        ref.key_acc[:, :width] += to_key
                        ref.value_acc[:, :width] += to_value
                    for when, events in BACK_DURING.items():
                        if linked and when % 6 == b * 2 + e:
                            run_at(hp, when // 6, lambda events=events: run(events))
                by_content = jnp.where(head_lanes(QB, 0), by_content[0], by_content[1])
                ref.joined_grad[rows, lanes] = (by_content + by_position).astype(bf16)
                content_sum += jnp.sum(by_content, axis=0, keepdims=True)
                position_sum += jnp.sum(by_position, axis=0, keepdims=True)
            ref.joined_grad[:, pl.ds(start + D, 128)] = ref.key_acc[...].T.astype(bf16)
            ref.joined_grad[:, pl.ds(start + 2 * D, 128)] = ref.value_acc[...].T.astype(bf16)
            r = VECTOR_ROW["content"]
            ref.all_sums[r : r + 1, lanes] = content_sum
            r = VECTOR_ROW["position_bias"]
            ref.all_sums[r : r + 1, lanes] = position_sum
            return carry

        lax.fori_loop(0, HEADS // 2, pair, 0)

        row_copy("first_grad").wait()
        if linked:
            put_blocks(plan, "position", ref.own, 0, lambda columns: ref.position_grad[:, columns])
            run([(3, 0)])
        def project_part(part, carry):
            columns = pl.ds(pl.multiple_of(part * D, D), D)
            grad = tn(ref.joined_grad[:, columns], ref.normed_low[...]).astype(bf16)
            if linked:
                ref.project_full[columns, :] = grad
            else:
                ref.project_grad[columns, :] = grad
            return carry

        lax.fori_loop(0, 3, project_part, 0)
        if linked:
            put_blocks(plan, "project", ref.own, 0, lambda columns: ref.project_full[:, columns])
            run([(4, 0), (5, 0), (3, 1)])
        else:
            ref.position_grad_out[...] = ref.position_grad[...].astype(bf16)

        def norm_back(i, carry):
            rows = at_rows(i, RB)
            normal, inverse = norm_rows(rows)
            upstream = nn(ref.joined_grad[rows, :], full(ref.project))
            ref.parts[0, :, :] += eight_rows(upstream * normal)
            ref.parts[1, :, :] += eight_rows(upstream)
            ref.token_grad[rows, :] = ref.first_grad[rows, :] + norm_backward(
                normal, inverse, vec(ref.vectors, "gain_one"), upstream
            )
            if linked:
                run_at(i, 1, lambda: run([(4, 1)]))
                run_at(i, 3, lambda: run([(5, 1)]))
                run_at(i, 5, lambda: run([(3, 2)]))
                run_at(i, 7, lambda: run([(4, 2)]))
            return carry

        lax.fori_loop(0, SEQ // RB, norm_back, 0)
        token_copy = pltpu.make_async_copy(ref.token_grad, ref.token_grad_out, ref.token_sem)
        token_copy.start()
        for slot, name in enumerate(("gain_one", "shift_one")):
            r = VECTOR_ROW[name]
            ref.all_sums[r : r + 1, :D] = jnp.sum(ref.parts[slot], axis=0, keepdims=True)
        if linked:
            pack_vectors(ref.all_sums, ref.vector_own)
            vector.first()
            run([(5, 2), (3, 3), (4, 3)])
            vector.second()
            run([(5, 3), (3, 4)])
            vector.last()
            run([(4, 4), (5, 4)])
            done = pltpu.make_async_copy(ref.flat, ref.flat_out, ref.own_sem.at[0])
            done.start()
            done.wait()
        else:
            ref.sums_out[...] = ref.all_sums[...]
        token_copy.wait()

    if linked:
        scratch["project_full"] = VMEM((3 * D, D), bf16)
    return call(body, ins, outs, scratch, **params)


PARTS = 4


def finish(plan, flat, vectors, rows):
    outs = {n + "_out": (plan.held_shape(n), f32, VMEM) for n in WEIGHTS}
    outs |= {n + "_out": ((VECTOR_SIZE[n] // 32,), f32, VMEM) for n in VECTORS}
    outs |= {n + "_copy": (v.shape, v.dtype, ANY) for n, v in rows.items()}
    ins = {"flat_in": (flat, ANY), "vectors_in": (vectors, ANY)}
    ins |= {n: (v, ANY) for n, v in rows.items()}
    scratch = {n + "_held": VMEM(v.shape, v.dtype) for n, v in rows.items()}
    scratch |= {"flat": VMEM(flat.shape, f32), "vectors": VMEM(vectors.shape, f32)}
    scratch["small_sem"] = pltpu.SemaphoreType.DMA((2,))
    scratch["in_sem"] = pltpu.SemaphoreType.DMA((len(rows) * PARTS,))
    scratch["out_sem"] = pltpu.SemaphoreType.DMA((len(rows) * PARTS,))

    def body(ref):
        loads, copies = [], []
        for n in rows:
            for part in range(PARTS):
                at = pl.ds(part * (SEQ // PARTS), SEQ // PARTS)
                held = getattr(ref, n + "_held").at[at]
                slot = len(loads)
                loads.append(
                    pltpu.make_async_copy(getattr(ref, n).at[at], held, ref.in_sem.at[slot])
                )
                copies.append(
                    pltpu.make_async_copy(
                        held, getattr(ref, n + "_copy").at[at], ref.out_sem.at[slot]
                    )
                )
        small = [
            pltpu.make_async_copy(ref.vectors_in, ref.vectors, ref.small_sem.at[0]),
            pltpu.make_async_copy(ref.flat_in, ref.flat, ref.small_sem.at[1]),
        ]
        for load in small + loads:
            load.start()
        for load in small:
            load.wait()
        for name in WEIGHTS:
            put_shard(plan, name, ref.flat, 0, getattr(ref, name + "_out"))
        for name, (line, offset, size) in vector_places().items():
            getattr(ref, name + "_out")[...] = ref.vectors[line, offset : offset + size]
        for load, copy in zip(loads, copies):
            load.wait()
            copy.start()
        for copy in copies:
            copy.wait()

    return call(body, ins, outs, scratch)


def make_local(dp, fsdp):
    plan = Plan(dp, fsdp)
    linked = (dp, fsdp) == (4, 8)

    def gathered(weights):
        out = {}
        for name, shard in zip(WEIGHTS, weights):
            part = lax.all_gather(shard, "dp", axis=0, tiled=True)
            out[name + "_full"] = lax.all_gather(part, "fsdp", axis=1, tiled=True).T
        return out

    def gathered_vectors(vectors):
        rows = []
        for name, shard in zip(VECTORS, vectors):
            whole = lax.all_gather(shard, ("dp", "fsdp"), axis=0, tiled=True).astype(f32)
            rows.append(jnp.pad(whole, (0, FF - VECTOR_SIZE[name])))
        rows += [jnp.zeros((FF,), f32)] * (16 - len(rows))
        return jnp.stack(rows)

    def local(tokens, cotangent, *params):
        assert tokens.shape[0] == SEQ
        weights, vectors = params[:7], params[7:]
        given = dict(zip(VECTORS, vectors))
        rates = angle_rates()
        ins = {"tokens_in": (tokens, ANY), "rates": (rates, VMEM)}
        if linked:
            ins |= {n + "_shard": (given[n], VMEM) for n in VECTORS}
            for n, w in zip(WEIGHTS, weights):
                ins[n + "_shard"] = (w.T if w.shape[1] % 128 else w, VMEM)
        else:
            whole = gathered(weights)
            ins["given_vectors"] = (gathered_vectors(vectors), VMEM)
            ins["project"] = (whole["project_full"], VMEM)
            ins["position"] = (whole["position_full"], VMEM)
        one = front(plan, linked, ins)

        ins = {
            "tokens_in": (tokens, ANY),
            "cotangent_in": (cotangent, ANY),
            "mixed_in": (one.mixed_out, ANY),
            "vectors": (one.vectors, VMEM),
        }
        if linked:
            ins["blocks"] = (one.blocks, ANY)
        else:
            ins |= {n + "_full": (whole[n + "_full"], ANY) for n in MIDDLE}
        two = middle(plan, linked, ins)

        ins = {
            "tokens_in": (tokens, ANY),
            "coarse": (one.coarse, VMEM),
            "vectors": (one.vectors, VMEM),
            "query_u_in": (one.query_u_out, ANY),
            "query_v_in": (one.query_v_out, ANY),
            "key_in": (one.key_out, ANY),
            "value_in": (one.value_out, ANY),
            "mixed_in": (one.mixed_out, ANY),
            "mixed_grad_in": (two.mixed_grad_out, ANY),
            "first_grad_in": (two.first_grad_out, ANY),
            "sums": (two.sums, VMEM),
            "probs_in": (one.probs_out, ANY),
        }
        if linked:
            ins["blocks"] = (two.blocks_out, ANY)
            for n in ("contract", "expand", "mixing"):
                ins[n + "_grad"] = (getattr(two, n + "_grad_out"), ANY)
            ins["partial"] = (two.partial, ANY)
        else:
            ins |= {n + "_full": (whole[n + "_full"], ANY) for n in ("project", "position")}
        three = back(plan, linked, ins)

        if linked:
            last = finish(
                plan,
                three.flat_out,
                three.vector_out,
                {"output": two.output_out, "token_grad": three.token_grad_out},
            )
            output, token_grad = last.output_copy, last.token_grad_copy
            matrices = []
            for n in WEIGHTS:
                grad = getattr(last, n + "_out")
                matrices.append(grad if grad.shape == plan.shard[n] else grad.T)
            small = [getattr(last, n + "_out") for n in VECTORS]
        else:
            output, token_grad = two.output_out, three.token_grad_out
            grads = {n: getattr(two, n + "_grad_out") for n in MIDDLE}
            grads["project"] = three.project_grad
            grads["position"] = three.position_grad_out
            matrices = []
            for name in WEIGHTS:
                part = lax.psum_scatter(
                    grads[name].T, "fsdp", scatter_dimension=1, tiled=True
                )
                part = lax.psum_scatter(part, "dp", scatter_dimension=0, tiled=True)
                matrices.append(part.astype(f32))
            small = []
            for name in VECTORS:
                sums = three.sums_out[VECTOR_ROW[name], : VECTOR_SIZE[name]]
                small.append(
                    lax.psum_scatter(sums, ("dp", "fsdp"), scatter_dimension=0, tiled=True)
                )
        return (output, token_grad, *matrices, *small)

    return local


def solution(mesh):
    rows = P(("dp", "fsdp"), None)
    matrix = P("dp", "fsdp")
    vector = P(("dp", "fsdp"))
    return jax.shard_map(
        make_local(mesh.shape["dp"], mesh.shape["fsdp"]),
        mesh=mesh,
        in_specs=(rows,) * 2 + (matrix,) * 7 + (vector,) * 11,
        out_specs=(rows,) * 2 + (matrix,) * 7 + (vector,) * 11,
        check_vma=False,
    )
```
